32 devices in a mesh: blocks: 2 (over x), mode: 16 (over z, y, core).
Axes of the slice: x: 2, y: 2, z: 4, core: 2. Of those that a mesh axis runs over, the one named last changes fastest.
Arguments:
- right_side: float32 [2, 8, 1024, 1024], P(None, 'blocks', 'mode'), parts along dimension 1, may hold values from -6 to 6
- classes: int32 [8, 1024, 1024], P('blocks', 'mode'), parts along dimension 0, may hold values from 0 to 7
- noise_table: float32 [8], replicated, may hold values from 0.05 to 1
- kernel_first: bfloat16 [1024, 1024], replicated, may hold values from -1 to 3, as said below
- kernel_second: bfloat16 [1024, 1024], replicated, may hold values from -1 to 3, as said below
- basis_first: bfloat16 [1024, 1024], replicated, may hold values from -1 to 2, as said below
- basis_second: bfloat16 [1024, 1024], replicated, may hold values from -1 to 2, as said below
- eigen_first: float32 [1024], replicated, may hold values from 0.5 to 4
- eigen_second: float32 [1024], P('mode'), may hold values from 0.5 to 4
Outputs:
- solution_field: float32 [2, 8, 1024, 1024], P(None, 'blocks', 'mode'), parts along dimension 1
- residual: float32 [2, 8, 1024, 1024], P(None, 'blocks', 'mode'), parts along dimension 1
The draws below stay inside these ranges and needn't reach their ends.
There are 2 independent parts, one for each index of `blocks`. The reference program is written for one: setup_inputs(seed, part) draws one part's arguments, and reference() takes and returns one part's arrays. A program takes and returns all parts, laid end to end along the dimension named above; an argument that names none is the same for every part. Nothing has to cross between parts.
Inputs may be any that keep to these rules, and one draw needn't show every extreme that they name: `kernel_first`: symmetric positive definite. `kernel_second`: symmetric positive definite. `basis_first`: nonsingular. `basis_second`: nonsingular.
All inputs are finite; a program needn't handle non-finite values.
Results may differ from the reference program's by a relative error of at most 0.0003.
Values sent between devices are 32-bit elements; how exact they have to be, the bound alone decides.
No kernel may reach another device: no remote copies, remote signals or barrier semaphores. Data moves between devices by JAX's collectives and lax.ppermute only.
A program may use at most 128 MiB of HBM per device.

```python
import math
import jax
import jax.numpy as jnp
from jax import lax

N1 = 1024
N2 = 1024
PLANES = 4
SAMPLES = 2
NCLASS = 8
ITERS = 2


def make_kernel(key, width):
    gauss = jax.random.normal(key, (width, width), jnp.float32) / jnp.sqrt(jnp.float32(width))
    product = jnp.dot(gauss, gauss.T, precision=lax.Precision.HIGHEST)
    return (product + 0.5 * jnp.eye(width, dtype=jnp.float32)).astype(jnp.bfloat16)


def make_basis(key, width):
    gauss = jax.random.normal(key, (width, width), jnp.float32) / jnp.sqrt(jnp.float32(width))
    return (jnp.eye(width, dtype=jnp.float32) + 0.3 * gauss).astype(jnp.bfloat16)


def draw_kernel_first(key, part):
    return make_kernel(jax.random.fold_in(key, 11), N1)


def draw_kernel_second(key, part):
    return make_kernel(jax.random.fold_in(key, 12), N2)


def draw_basis_first(key, part):
    return make_basis(jax.random.fold_in(key, 13), N1)


def draw_basis_second(key, part):
    return make_basis(jax.random.fold_in(key, 14), N2)


def with_ends(drawn, stream_key, smallest, top_value):
    spot = [jax.random.randint(jax.random.fold_in(stream_key, axis), (), 0, length) for axis, length in enumerate(drawn.shape)]
    main_axis = drawn.shape.index(max(drawn.shape))
    neighbour = spot[:main_axis] + [(spot[main_axis] + 1) % drawn.shape[main_axis]] + spot[main_axis + 1:]
    return drawn.at[tuple(spot)].set(smallest).at[tuple(neighbour)].set(top_value)


def steps_of(key, shape, cuts, least, high):
    def one(position, blocks):
        draws = jax.random.uniform(jax.random.fold_in(jax.random.fold_in(key, 6), position), (blocks,), jnp.float32, least / len(cuts), high / len(cuts))
        return jnp.repeat(jnp.exp(draws), shape[position] // blocks).reshape((-1,) + (1,) * (len(shape) - position - 1))

    loudness = one(*cuts[0])
    for cut in cuts[1:]:
        loudness = loudness * one(*cut)
    return loudness


def bell_draw(key, shape, scale, most, split=(), kind=jnp.bfloat16):
    result = jax.random.normal(key, shape, jnp.float32) * scale
    if len(split) > 0:
        result = steps_of(key, shape, split, -0.22, 0.18) * result
    return jnp.clip(result, min=-most, max=most).astype(kind)


def setup_inputs(seed: int = 0, part: int = 0) -> dict:
    streams_of = jax.random.split(jax.random.key(seed), 10)
    own_keys = jax.random.split(jax.random.fold_in(streams_of[9], part), 10)
    right_side = bell_draw(own_keys[0], (SAMPLES, PLANES, N1, N2), 1.0, 6.0, ((2, 16),), jnp.float32)
    classes = with_ends(jax.random.randint(own_keys[1], (PLANES, N1, N2), 0, NCLASS), jax.random.fold_in(own_keys[1], 1), 0, NCLASS - 1).astype(jnp.int32)
    noise_table = jnp.clip(jnp.exp(jax.random.uniform(streams_of[2], (NCLASS,), jnp.float32, math.log(0.05), math.log(1.0))), 0.05, 1.0)
    kernel_first = draw_kernel_first(jax.random.fold_in(streams_of[9], 71), part)
    kernel_second = draw_kernel_second(jax.random.fold_in(streams_of[9], 71), part)
    basis_first = draw_basis_first(jax.random.fold_in(streams_of[9], 71), part)
    basis_second = draw_basis_second(jax.random.fold_in(streams_of[9], 71), part)
    eigen_first = jnp.clip(jnp.exp(jax.random.uniform(streams_of[7], (N1,), jnp.float32, math.log(0.5), math.log(4.0))), 0.5, 4.0)
    eigen_second = jnp.clip(jnp.exp(math.log(4.0) - 2.0794415 * jax.random.uniform(streams_of[8], (N2,), jnp.float32) ** steps_of(streams_of[8], (N2,), ((0, 16),), -0.2, 0.2)), 0.5, 4.0)
    return {"right_side": right_side, "classes": classes, "noise_table": noise_table, "kernel_first": kernel_first, "kernel_second": kernel_second, "basis_first": basis_first, "basis_second": basis_second, "eigen_first": eigen_first, "eigen_second": eigen_second}


def first(matrix, field):
    return jnp.einsum('ik,spkj->spij', matrix.astype(jnp.float32), field, precision=lax.Precision.HIGHEST)


def second(matrix, field):
    return jnp.einsum('jk,spik->spij', matrix.astype(jnp.float32), field, precision=lax.Precision.HIGHEST)


def reference(right_side, classes, noise_table, kernel_first, kernel_second, basis_first, basis_second, eigen_first, eigen_second):
    noise = noise_table[classes]
    mean_noise = jnp.mean(noise_table)
    weights = 1.0 / (eigen_first[:, None] * eigen_second[None, :] + mean_noise)

    def operate(field):
        return first(kernel_first, second(kernel_second, field)) + noise[None] * field

    def precond(field):
        inner = first(basis_first.T, second(basis_second.T, field)) * weights
        return first(basis_first, second(basis_second, inner))

    solution_field = jnp.zeros_like(right_side)
    residual = right_side
    z_field = precond(residual)
    direction = z_field
    gamma = jnp.sum(residual * z_field)
    for step in range(ITERS):
        image = operate(direction)
        alpha = gamma / jnp.sum(direction * image)
        solution_field = solution_field + alpha * direction
        residual = residual - alpha * image
        if step + 1 < ITERS:
            z_field = precond(residual)
            gamma_new = jnp.sum(residual * z_field)
            direction = z_field + (gamma_new / gamma) * direction
            gamma = gamma_new
    return solution_field, residual
```

```python
import functools

import jax
import jax.numpy as jnp
from jax import lax
from jax.experimental import pallas as pl
from jax.experimental.pallas import tpu as pltpu
from jax.sharding import PartitionSpec as P

NCLASS = 8
ITERS = 2
F32 = jnp.float32
BF16 = jnp.bfloat16


def along_rows(matrix, field):
    return jnp.einsum("jk,sprk->sprj", matrix, field, precision=lax.Precision.HIGHEST)


def rows_to_send(matrix, field, groups):
    result = jnp.einsum("kj,sprk->jspr", matrix, field, precision=lax.Precision.HIGHEST)
    return result.reshape(groups, -1)


def received_to_columns(matrix, received, shape5):
    groups, cols, samples, planes, rows = shape5
    block = received.reshape(shape5)
    reshaped = matrix.reshape(groups, rows, matrix.shape[1])
    return jnp.einsum("mri,mcspr->cspi", reshaped, block, precision=lax.Precision.HIGHEST)


def along_columns(matrix, columns):
    return jnp.einsum("ik,cspk->cspi", matrix, columns, precision=lax.Precision.HIGHEST)


def columns_to_send(matrix, columns, groups, rows):
    reshaped = matrix.reshape(groups, rows, matrix.shape[1])
    result = jnp.einsum("mrk,cspk->mcspr", reshaped, columns, precision=lax.Precision.HIGHEST)
    return result.reshape(groups, -1)


def received_to_rows(matrix, received, shape5):
    groups, cols, samples, planes, rows = shape5
    block = received.reshape(shape5)
    reshaped = matrix.reshape(matrix.shape[0], groups, cols)
    return jnp.einsum("jmc,mcspr->sprj", reshaped, block, precision=lax.Precision.HIGHEST)


def general_body(
    right_side,
    classes,
    noise_table,
    kernel_first,
    kernel_second,
    basis_first,
    basis_second,
    eigen_first,
    eigen_second,
):
    groups = lax.axis_size("mode")
    samples, planes, rows, width_two = right_side.shape
    cols = eigen_second.shape[0]
    shape5 = (groups, cols, samples, planes, rows)
    kern_one = kernel_first.astype(F32)
    kern_two = kernel_second.astype(F32)
    base_one = basis_first.astype(F32)
    base_two = basis_second.astype(F32)
    noise = jnp.zeros(classes.shape, F32)
    for level in range(NCLASS):
        noise = noise + jnp.where(classes == level, noise_table[level], 0.0)
    noise = noise[None]
    mean_noise = jnp.mean(noise_table)
    col_weights = 1.0 / (eigen_second[:, None] * eigen_first[None, :] + mean_noise)
    col_weights = col_weights[:, None, None, :]

    def exchange(outgoing):
        return lax.all_to_all(outgoing, "mode", split_axis=0, concat_axis=0, tiled=True)

    def precond_apply(field):
        incoming = exchange(rows_to_send(base_two, field, groups))
        weighted = received_to_columns(base_one, incoming, shape5) * col_weights
        columns = along_columns(base_one, weighted)
        back = exchange(columns_to_send(base_one, weighted, groups, rows))
        kernel_back = exchange(columns_to_send(kern_one, columns, groups, rows))
        z_field = received_to_rows(base_two, back, shape5)
        image = (
            along_rows(kern_two, received_to_rows(base_two, kernel_back, shape5)) + noise * z_field
        )
        return (z_field, image)

    def inner(left, right):
        return lax.psum(jnp.sum(left * right), "mode")

    solution_field = jnp.zeros_like(right_side)
    residual = right_side
    z_field, image = precond_apply(residual)
    direction, along = (z_field, image)
    gamma = inner(residual, z_field)
    for step in range(ITERS):
        alpha = gamma / inner(direction, along)
        solution_field = solution_field + alpha * direction
        residual = residual - alpha * along
        if step + 1 < ITERS:
            z_field, image = precond_apply(residual)
            gamma_new = inner(residual, z_field)
            ratio = gamma_new / gamma
            direction = z_field + ratio * direction
            along = image + ratio * along
            gamma = gamma_new
    return (solution_field, residual)


def split(value):
    high = value.astype(BF16)
    low = (value - high.astype(F32)).astype(BF16)
    return high, low


def times_right(value, matrix, contract):
    high, low = split(value)
    dims = (((1,), (contract,)), ((), ()))
    both = jnp.concatenate([high, low], axis=0)
    result = lax.dot_general(both, matrix, dims, preferred_element_type=F32)
    return result[: value.shape[0]] + result[value.shape[0] :]


def times_left(matrix, value):
    high, low = split(value)
    dims = (((1,), (0,)), ((), ()))
    return lax.dot_general(matrix, high, dims, preferred_element_type=F32) + lax.dot_general(
        matrix, low, dims, preferred_element_type=F32
    )


def fold(value):
    total = jnp.sum(value, axis=0, keepdims=True)
    return functools.reduce(
        jnp.add, [total[:, at : at + 128] for at in range(0, total.shape[1], 128)]
    )


def params(dims):
    return pltpu.CompilerParams(
        dimension_semantics=("arbitrary",) * dims, vmem_limit_bytes=56 * 1024 * 1024
    )


def outgoing_kernel(table_ref, right_ref, class_ref, basis_ref, out_ref):
    samples, _, rows, width = right_ref.shape
    cores = out_ref.shape[1] // samples
    half = width // cores
    field = right_ref[...].reshape(samples * rows, width)
    mapped = times_right(field, basis_ref[...], 0)
    level = class_ref[0]
    noise = jnp.full(level.shape, table_ref[0], F32)
    for index in range(1, NCLASS):
        noise = jnp.where(level == index, table_ref[index], noise)
    share = rows // cores
    for sample in range(samples):
        for core in range(cores):
            out_ref[0, sample * cores + core, :rows, :] = mapped[
                sample * rows : (sample + 1) * rows, core * half : (core + 1) * half
            ]
            out_ref[0, sample * cores + core, rows:, :] = noise[
                core * share : (core + 1) * share, sample * half : (sample + 1) * half
            ]


def column_kernel(first_call, place_ref, *refs):
    if first_call:
        (field_ref, weight_ref, turned_ref, basis_ref, kernel_ref) = refs[:5]
        (spectral_ref, keep_ref, send_ref, sum_ref, scratch_ref) = refs[5:]
    else:
        (held_ref, got_ref, before_ref, weight_ref, turned_ref, basis_ref, kernel_ref) = refs[:7]
        (keep_ref, send_ref, sum_ref, scratch_ref) = refs[7:]
    groups, rows, chunk = scratch_ref.shape
    share = rows // 2
    core = place_ref[0]
    mine = pl.ds(pl.multiple_of(core * share, share), share)
    theirs = pl.ds(pl.multiple_of((1 - core) * share, share), share)
    if first_call:
        field = field_ref[...].reshape(groups * rows, chunk)
    else:
        scratch_ref[:, mine, :] = held_ref[...]
        scratch_ref[:, theirs, :] = got_ref[...]
        field = scratch_ref[...].reshape(groups * rows, chunk)
    spectral = times_left(turned_ref[...], field)
    weighted = spectral * weight_ref[...]
    if first_call:
        spectral_ref[...] = spectral
        sums = [fold(spectral * weighted)]
    else:
        sums = [fold(before_ref[...] * weighted), fold(spectral * weighted)]
    block = jnp.concatenate(sums + [jnp.zeros((8 - len(sums), 128), F32)], axis=0)

    @pl.when(pl.program_id(0) == 0)
    def _():
        sum_ref[...] = block

    @pl.when(pl.program_id(0) != 0)
    def _():
        sum_ref[...] += block

    column = times_left(basis_ref[...], weighted)
    scratch_ref[...] = column.reshape(groups, rows, chunk)
    keep_ref[0] = scratch_ref[:, mine, :]
    send_ref[0] = scratch_ref[:, theirs, :]
    image = times_left(kernel_ref[...], column)
    scratch_ref[...] = image.reshape(groups, rows, chunk)
    keep_ref[1] = scratch_ref[:, mine, :]
    send_ref[1] = scratch_ref[:, theirs, :]


def row_kernel(first_call, place_ref, keep_ref, got_ref, near_ref, far_ref, basis_ref, kernel_ref, *refs):
    if first_call:
        (z_ref, image_ref, back_keep_ref, back_send_ref, scratch_ref) = refs
    else:
        (one_ref, two_ref, z_ref, image_ref, sum_ref, scratch_ref) = refs
    height, width = scratch_ref.shape
    half = width // 2
    groups, share = z_ref.shape[:2]
    core = place_ref[0]
    sample = place_ref[1]
    mine = pl.ds(pl.multiple_of(core * half, half), half)
    theirs = pl.ds(pl.multiple_of((1 - core) * half, half), half)

    def whole(index):
        scratch_ref[:, mine] = keep_ref[index].reshape(height, half)
        scratch_ref[:, theirs] = got_ref[index].reshape(height, half)
        return scratch_ref[...]

    basis = basis_ref[...]
    z_field = times_right(whole(0), basis, 1)
    image = times_right(times_right(whole(1), basis, 1), kernel_ref[...], 1)
    scratch_ref[:, pl.ds(pl.multiple_of(sample * half, half), half)] = near_ref[...].reshape(
        height, half
    )
    scratch_ref[:, pl.ds(pl.multiple_of((1 - sample) * half, half), half)] = far_ref[
        ...
    ].reshape(height, half)
    image = image + scratch_ref[...] * z_field
    z_ref[...] = z_field.reshape(z_ref.shape)
    image_ref[...] = image.reshape(image_ref.shape)
    if first_call:
        scratch_ref[...] = times_right(image, basis, 0)
        back_keep_ref[...] = scratch_ref[:, mine].reshape(back_keep_ref.shape)
        back_send_ref[...] = scratch_ref[:, theirs].reshape(back_send_ref.shape)
    else:

        @pl.when(pl.program_id(0) == 0)
        def _():
            first = jnp.concatenate(
                [one_ref[0:1], two_ref[0:2], jnp.zeros((5, 128), F32)], axis=0
            )
            sum_ref[...] = jnp.broadcast_to(first[None], sum_ref.shape)

        last = jnp.concatenate(
            [jnp.zeros((3, 128), F32), fold(z_field * image), jnp.zeros((4, 128), F32)], axis=0
        )
        sum_ref[...] += jnp.broadcast_to(last[None], sum_ref.shape)


def combine_kernel(sum_ref, z_ref, image_ref, f_ref, f_image_ref, out_ref):
    total = jnp.sum(sum_ref[...], axis=0)
    total = jnp.sum(total, axis=1, keepdims=True)
    g00, g01, g11, h11 = (total[at : at + 1] for at in range(4))
    alpha = g00 / g01
    turn = alpha * g11 / g01
    gamma = alpha * alpha * g11 - g00
    curvature = alpha * alpha * h11 - turn * turn * g01
    step = gamma / curvature
    on_z = alpha + step * turn
    on_f = -(alpha * step)
    share = z_ref.shape[1]
    out_ref[:, :share, :] = on_z[None] * z_ref[...] + on_f[None] * f_ref[...]
    out_ref[:, share:, :] = on_z[None] * image_ref[...] + on_f[None] * f_image_ref[...]


def finish_kernel(got_ref, right_ref, solution_ref, residual_ref):
    cores, double = got_ref.shape[:2]
    share = double // 2
    for core in range(cores):
        at = slice(core * share, (core + 1) * share)
        solution_ref[0, 0, at, :] = got_ref[core, :share, :]
        residual_ref[0, 0, at, :] = right_ref[0, 0, at, :] - got_ref[core, share:, :]


def paired_body(
    right_side,
    classes,
    noise_table,
    kernel_first,
    kernel_second,
    basis_first,
    basis_second,
    eigen_first,
    eigen_second,
):
    groups = lax.axis_size("mode")
    samples, planes, rows, width = right_side.shape
    height = groups * rows
    cores = 2
    half = width // cores
    share = rows // cores
    tall = rows + share
    index = lax.axis_index("mode")
    core = index % cores
    sample = (index // cores) % samples
    place = jnp.stack([core, sample]).astype(jnp.int32)

    def shape_of(*shape):
        return jax.ShapeDtypeStruct(shape, F32)

    smem = pl.BlockSpec(memory_space=pltpu.SMEM)

    def full(*shape):
        return pl.BlockSpec(shape, lambda *at: (0,) * len(shape))

    core_swap = [(at, at ^ 1) for at in range(groups)]
    sample_swap = [(at, at ^ cores) for at in range(groups)]

    outgoing = pl.pallas_call(
        outgoing_kernel,
        grid=(planes,),
        in_specs=[
            smem,
            pl.BlockSpec((samples, 1, rows, width), lambda p: (0, p, 0, 0)),
            pl.BlockSpec((1, rows, width), lambda p: (p, 0, 0)),
            full(width, width),
        ],
        out_specs=pl.BlockSpec((1, samples * cores, tall, half), lambda p: (p, 0, 0, 0)),
        out_shape=shape_of(planes, samples * cores, tall, half),
        compiler_params=params(1),
        name="outgoing",
    )(noise_table, right_side, classes, basis_second)
    arrived = lax.all_to_all(
        outgoing.reshape(groups, tall, half), "mode", split_axis=0, concat_axis=0, tiled=True
    )

    eigen = eigen_second.reshape(1, -1)
    reach = 1
    while reach < groups:
        other = lax.ppermute(eigen, "mode", [(at, at ^ reach) for at in range(groups)])
        low = (index // reach) % 2 == 0
        eigen = jnp.where(
            low,
            jnp.concatenate([eigen, other], axis=1),
            jnp.concatenate([other, eigen], axis=1),
        )
        reach *= 2
    eigen = lax.dynamic_slice(eigen, (0, core * half), (1, half))
    weights = 1.0 / (eigen_first[:, None] * eigen + jnp.mean(noise_table))
    turned = basis_first.T

    near = arrived[:, rows:, :]
    far = lax.ppermute(near, "mode", sample_swap)

    chunk = half // 2
    steps = half // chunk
    tile = pl.BlockSpec((height, chunk), lambda j: (0, j))
    piece = pl.BlockSpec((groups, share, chunk), lambda j: (0, 0, j))
    pieces = pl.BlockSpec((2, groups, share, chunk), lambda j: (0, 0, 0, j))
    square = full(height, height)
    row_square = full(width, width)
    scratch = [pltpu.VMEM((groups, rows, chunk), F32)]
    spectral, keep, send, sum_one = pl.pallas_call(
        functools.partial(column_kernel, True),
        grid=(steps,),
        in_specs=[
            smem,
            pl.BlockSpec((groups, rows, chunk), lambda j: (0, 0, j)),
            tile,
            square,
            square,
            square,
        ],
        out_specs=[tile, pieces, pieces, full(8, 128)],
        out_shape=[
            shape_of(height, half),
            shape_of(2, groups, share, half),
            shape_of(2, groups, share, half),
            shape_of(8, 128),
        ],
        scratch_shapes=scratch,
        compiler_params=params(1),
        name="columns_one",
    )(place, arrived, weights, turned, basis_first, kernel_first)
    got = lax.ppermute(send, "mode", core_swap)

    part = groups // 2
    row_pieces = pl.BlockSpec((2, part, share, half), lambda i: (0, i, 0, 0))
    row_piece = pl.BlockSpec((part, share, half), lambda i: (i, 0, 0))
    row_whole = pl.BlockSpec((part, share, width), lambda i: (i, 0, 0))
    row_scratch = [pltpu.VMEM((part * share, width), F32)]
    row_specs = [smem, row_pieces, row_pieces, row_piece, row_piece, row_square, row_square]
    z_field, image, back_keep, back_send = pl.pallas_call(
        functools.partial(row_kernel, True),
        grid=(2,),
        in_specs=row_specs,
        out_specs=[row_whole, row_whole, row_piece, row_piece],
        out_shape=[
            shape_of(groups, share, width),
            shape_of(groups, share, width),
            shape_of(groups, share, half),
            shape_of(groups, share, half),
        ],
        scratch_shapes=row_scratch,
        compiler_params=params(1),
        name="rows_one",
    )(place, keep, got, near, far, basis_second, kernel_second)
    back_got = lax.ppermute(back_send, "mode", core_swap)

    keep, send, sum_two = pl.pallas_call(
        functools.partial(column_kernel, False),
        grid=(steps,),
        in_specs=[smem, piece, piece, tile, tile, square, square, square],
        out_specs=[pieces, pieces, full(8, 128)],
        out_shape=[
            shape_of(2, groups, share, half),
            shape_of(2, groups, share, half),
            shape_of(8, 128),
        ],
        scratch_shapes=scratch,
        compiler_params=params(1),
        name="columns_two",
    )(place, back_keep, back_got, spectral, weights, turned, basis_first, kernel_first)
    got = lax.ppermute(send, "mode", core_swap)

    f_field, f_image, sums = pl.pallas_call(
        functools.partial(row_kernel, False),
        grid=(2,),
        in_specs=row_specs + [full(8, 128), full(8, 128)],
        out_specs=[row_whole, row_whole, full(groups, 8, 128)],
        out_shape=[
            shape_of(groups, share, width),
            shape_of(groups, share, width),
            shape_of(groups, 8, 128),
        ],
        scratch_shapes=row_scratch,
        compiler_params=params(1),
        name="rows_two",
    )(place, keep, got, near, far, basis_second, kernel_second, sum_one, sum_two)
    sums = lax.all_to_all(sums, "mode", split_axis=0, concat_axis=0, tiled=True)

    few = groups // 8
    few_spec = pl.BlockSpec((few, share, width), lambda i: (i, 0, 0))
    answer = pl.pallas_call(
        combine_kernel,
        grid=(8,),
        in_specs=[full(groups, 8, 128)] + [few_spec] * 4,
        out_specs=pl.BlockSpec((few, rows, width), lambda i: (i, 0, 0)),
        out_shape=shape_of(groups, rows, width),
        compiler_params=params(1),
        name="combine",
    )(sums, z_field, image, f_field, f_image)
    answer = lax.all_to_all(answer, "mode", split_axis=0, concat_axis=0, tiled=True)

    block = pl.BlockSpec((1, 1, rows, width), lambda p, s: (s, p, 0, 0))
    return tuple(
        pl.pallas_call(
            finish_kernel,
            grid=(planes, samples),
            in_specs=[
                pl.BlockSpec((cores, rows, width), lambda p, s: (p * samples + s, 0, 0)),
                block,
            ],
            out_specs=[block, block],
            out_shape=[shape_of(*right_side.shape)] * 2,
            compiler_params=params(2),
            name="finish",
        )(answer, right_side)
    )


def body(right_side, classes, *rest):
    groups = lax.axis_size("mode")
    samples, planes, rows, width = right_side.shape
    paired = (
        groups == 2 * samples * planes
        and samples == 2
        and rows % 16 == 0
        and width % 512 == 0
        and groups % 8 == 0
    )
    chosen = paired_body if paired else general_body
    return chosen(right_side, classes, *rest)


def solution(mesh):
    in_specs = (
        P(None, "blocks", "mode", None),
        P("blocks", "mode", None),
        P(),
        P(),
        P(),
        P(),
        P(),
        P(),
        P("mode"),
    )
    out_specs = (P(None, "blocks", "mode", None), P(None, "blocks", "mode", None))
    return jax.shard_map(body, mesh=mesh, in_specs=in_specs, out_specs=out_specs, check_vma=False)
```

```python
import functools

import jax
import jax.numpy as jnp
from jax import lax
from jax.experimental import pallas as pl
from jax.experimental.pallas import tpu as pltpu
from jax.sharding import PartitionSpec as P


NCLASS = 8
ITERS = 2
F32 = jnp.float32
BF16 = jnp.bfloat16


def along_rows(matrix, field):
    return jnp.einsum("jk,sprk->sprj", matrix, field, precision=lax.Precision.HIGHEST)


def rows_to_send(matrix, field, groups):
    result = jnp.einsum("kj,sprk->jspr", matrix, field, precision=lax.Precision.HIGHEST)
    return result.reshape(groups, -1)


def received_to_columns(matrix, received, shape5):
    groups, _, _, _, rows = shape5
    block = received.reshape(shape5)
    reshaped = matrix.reshape(groups, rows, matrix.shape[1])
    return jnp.einsum("mri,mcspr->cspi", reshaped, block, precision=lax.Precision.HIGHEST)


def along_columns(matrix, columns):
    return jnp.einsum("ik,cspk->cspi", matrix, columns, precision=lax.Precision.HIGHEST)


def columns_to_send(matrix, columns, groups, rows):
    reshaped = matrix.reshape(groups, rows, matrix.shape[1])
    result = jnp.einsum("mrk,cspk->mcspr", reshaped, columns, precision=lax.Precision.HIGHEST)
    return result.reshape(groups, -1)


def received_to_rows(matrix, received, shape5):
    groups, cols, _, _, _ = shape5
    block = received.reshape(shape5)
    reshaped = matrix.reshape(matrix.shape[0], groups, cols)
    return jnp.einsum("jmc,mcspr->sprj", reshaped, block, precision=lax.Precision.HIGHEST)


def general_body(
    right_side,
    classes,
    noise_table,
    kernel_first,
    kernel_second,
    basis_first,
    basis_second,
    eigen_first,
    eigen_second,
):
    groups = lax.axis_size("mode")
    samples, planes, rows, _ = right_side.shape
    cols = eigen_second.shape[0]
    shape5 = (groups, cols, samples, planes, rows)
    kern_one = kernel_first.astype(F32)
    kern_two = kernel_second.astype(F32)
    base_one = basis_first.astype(F32)
    base_two = basis_second.astype(F32)
    noise = jnp.zeros(classes.shape, F32)
    for level in range(NCLASS):
        noise = noise + jnp.where(classes == level, noise_table[level], 0.0)
    noise = noise[None]
    mean_noise = jnp.mean(noise_table)
    col_weights = 1.0 / (eigen_second[:, None] * eigen_first[None, :] + mean_noise)
    col_weights = col_weights[:, None, None, :]

    def exchange(outgoing):
        return lax.all_to_all(outgoing, "mode", split_axis=0, concat_axis=0, tiled=True)

    def precond_apply(field):
        incoming = exchange(rows_to_send(base_two, field, groups))
        weighted = received_to_columns(base_one, incoming, shape5) * col_weights
        columns = along_columns(base_one, weighted)
        back = exchange(columns_to_send(base_one, weighted, groups, rows))
        kernel_back = exchange(columns_to_send(kern_one, columns, groups, rows))
        z_field = received_to_rows(base_two, back, shape5)
        image = (
            along_rows(kern_two, received_to_rows(base_two, kernel_back, shape5)) + noise * z_field
        )
        return (z_field, image)

    def inner(left, right):
        return lax.psum(jnp.sum(left * right), "mode")

    solution_field = jnp.zeros_like(right_side)
    residual = right_side
    z_field, image = precond_apply(residual)
    direction, along = (z_field, image)
    gamma = inner(residual, z_field)
    for step in range(ITERS):
        alpha = gamma / inner(direction, along)
        solution_field = solution_field + alpha * direction
        residual = residual - alpha * along
        if step + 1 < ITERS:
            z_field, image = precond_apply(residual)
            gamma_new = inner(residual, z_field)
            ratio = gamma_new / gamma
            direction = z_field + ratio * direction
            along = image + ratio * along
            gamma = gamma_new
    return (solution_field, residual)


def split(value):
    high = value.astype(BF16)
    low = (value - high.astype(F32)).astype(BF16)
    return high, low


def times_right(value, matrix, contract):
    high, low = split(value)
    dims = (((1,), (contract,)), ((), ()))
    both = jnp.concatenate([high, low], axis=0)
    result = lax.dot_general(both, matrix, dims, preferred_element_type=F32)
    return result[: value.shape[0]] + result[value.shape[0] :]


def times_left(matrix, value):
    high, low = split(value)
    dims = (((1,), (0,)), ((), ()))
    both = jnp.concatenate([high, low], axis=1)
    result = lax.dot_general(matrix, both, dims, preferred_element_type=F32)
    return result[:, : value.shape[1]] + result[:, value.shape[1] :]


def fold(value):
    total = jnp.sum(value, axis=0, keepdims=True)
    return functools.reduce(
        jnp.add, [total[:, at : at + 128] for at in range(0, total.shape[1], 128)]
    )


def params(dims, mebibytes):
    return pltpu.CompilerParams(
        dimension_semantics=("arbitrary",) * dims, vmem_limit_bytes=mebibytes * 1024 * 1024
    )


def outgoing_kernel(table_ref, right_ref, class_ref, basis_ref, out_ref):
    samples, _, rows, width = right_ref.shape
    cores = out_ref.shape[1] // samples
    half = width // cores
    field = right_ref[...].reshape(samples * rows, width)
    mapped = times_right(field, basis_ref[...], 0)
    level = class_ref[0]
    noise = jnp.full(level.shape, table_ref[0], F32)
    for index in range(1, NCLASS):
        noise = jnp.where(level == index, table_ref[index], noise)
    share = rows // cores
    for sample in range(samples):
        for core in range(cores):
            out_ref[0, sample * cores + core, :rows, :] = mapped[
                sample * rows : (sample + 1) * rows, core * half : (core + 1) * half
            ]
            out_ref[0, sample * cores + core, rows:, :] = noise[
                core * share : (core + 1) * share, sample * half : (sample + 1) * half
            ]


def column_kernel(first_call, place_ref, *refs):
    if first_call:
        (field_ref, weight_ref, turned_ref, basis_ref, kernel_ref) = refs[:5]
        (spectral_ref, keep_ref, send_ref, sum_ref, scratch_ref) = refs[5:]
    else:
        (held_ref, got_ref, before_ref, weight_ref, turned_ref, basis_ref, kernel_ref) = refs[:7]
        (keep_ref, send_ref, sum_ref, scratch_ref) = refs[7:]
    groups, rows, chunk = scratch_ref.shape
    share = rows // 2
    core = place_ref[0]
    mine = pl.ds(pl.multiple_of(core * share, share), share)
    theirs = pl.ds(pl.multiple_of((1 - core) * share, share), share)
    if first_call:
        field = field_ref[...].reshape(groups * rows, chunk)
    else:
        scratch_ref[:, mine, :] = held_ref[...]
        scratch_ref[:, theirs, :] = got_ref[...]
        field = scratch_ref[...].reshape(groups * rows, chunk)
    spectral = times_left(turned_ref[...], field)
    weighted = spectral * weight_ref[...]
    if first_call:
        spectral_ref[...] = spectral
        sums = [fold(spectral * weighted)]
    else:
        sums = [fold(before_ref[...] * weighted), fold(spectral * weighted)]
    block = jnp.concatenate(sums + [jnp.zeros((8 - len(sums), 128), F32)], axis=0)

    @pl.when(pl.program_id(0) == 0)
    def _():
        sum_ref[...] = block

    @pl.when(pl.program_id(0) != 0)
    def _():
        sum_ref[...] += block

    column = times_left(basis_ref[...], weighted)
    scratch_ref[...] = column.reshape(groups, rows, chunk)
    keep_ref[0] = scratch_ref[:, mine, :]
    send_ref[0] = scratch_ref[:, theirs, :]
    image = times_left(kernel_ref[...], column)
    scratch_ref[...] = image.reshape(groups, rows, chunk)
    keep_ref[1] = scratch_ref[:, mine, :]
    send_ref[1] = scratch_ref[:, theirs, :]


def row_kernel(first_call, place_ref, keep_ref, got_ref, near_ref, far_ref, basis_ref, kernel_ref, *refs):
    if first_call:
        (z_ref, image_ref, back_keep_ref, back_send_ref, scratch_ref) = refs
    else:
        (one_ref, two_ref, z_ref, image_ref, sum_ref, scratch_ref) = refs
    height, width = scratch_ref.shape
    half = width // 2
    core = place_ref[0]
    sample = place_ref[1]
    mine = pl.ds(pl.multiple_of(core * half, half), half)
    theirs = pl.ds(pl.multiple_of((1 - core) * half, half), half)

    def whole(index):
        scratch_ref[:, mine] = keep_ref[index].reshape(height, half)
        scratch_ref[:, theirs] = got_ref[index].reshape(height, half)
        return scratch_ref[...]

    basis = basis_ref[...]
    z_field = times_right(whole(0), basis, 1)
    image = times_right(times_right(whole(1), basis, 1), kernel_ref[...], 1)
    scratch_ref[:, pl.ds(pl.multiple_of(sample * half, half), half)] = near_ref[...].reshape(
        height, half
    )
    scratch_ref[:, pl.ds(pl.multiple_of((1 - sample) * half, half), half)] = far_ref[
        ...
    ].reshape(height, half)
    image = image + scratch_ref[...] * z_field
    z_ref[...] = z_field.reshape(z_ref.shape)
    image_ref[...] = image.reshape(image_ref.shape)
    if first_call:
        scratch_ref[...] = times_right(image, basis, 0)
        back_keep_ref[...] = scratch_ref[:, mine].reshape(back_keep_ref.shape)
        back_send_ref[...] = scratch_ref[:, theirs].reshape(back_send_ref.shape)
    else:

        @pl.when(pl.program_id(0) == 0)
        def _():
            first = jnp.concatenate(
                [one_ref[0:1], two_ref[0:2], jnp.zeros((5, 128), F32)], axis=0
            )
            sum_ref[...] = jnp.broadcast_to(first[None], sum_ref.shape)

        last = jnp.concatenate(
            [jnp.zeros((3, 128), F32), fold(z_field * image), jnp.zeros((4, 128), F32)], axis=0
        )
        sum_ref[...] += jnp.broadcast_to(last[None], sum_ref.shape)


def combine_kernel(sum_ref, z_ref, image_ref, f_ref, f_image_ref, out_ref):
    total = jnp.sum(sum_ref[...], axis=0)
    total = jnp.sum(total, axis=1, keepdims=True)
    g00, g01, g11, h11 = (total[at : at + 1] for at in range(4))
    alpha = g00 / g01
    turn = alpha * g11 / g01
    gamma = alpha * alpha * g11 - g00
    curvature = alpha * alpha * h11 - turn * turn * g01
    step = gamma / curvature
    on_z = alpha + step * turn
    on_f = -(alpha * step)
    share = z_ref.shape[1]
    out_ref[:, :share, :] = on_z[None] * z_ref[...] + on_f[None] * f_ref[...]
    out_ref[:, share:, :] = on_z[None] * image_ref[...] + on_f[None] * f_image_ref[...]


def finish_kernel(got_ref, right_ref, solution_ref, residual_ref):
    count, rows = got_ref.shape[:2]
    samples = right_ref.shape[0]
    cores = count // samples
    share = rows // cores
    for sample in range(samples):
        for core in range(cores):
            at = slice(core * share, (core + 1) * share)
            block = sample * cores + core
            solution_ref[sample, 0, at, :] = got_ref[block, :share, :]
            residual_ref[sample, 0, at, :] = (
                right_ref[sample, 0, at, :] - got_ref[block, share:, :]
            )


def paired_body(
    right_side,
    classes,
    noise_table,
    kernel_first,
    kernel_second,
    basis_first,
    basis_second,
    eigen_first,
    eigen_second,
):
    groups = lax.axis_size("mode")
    samples, planes, rows, width = right_side.shape
    height = groups * rows
    cores = 2
    half = width // cores
    share = rows // cores
    tall = rows + share
    index = lax.axis_index("mode")
    core = index % cores
    sample = (index // cores) % samples
    place = jnp.stack([core, sample]).astype(jnp.int32)

    def shape_of(*shape):
        return jax.ShapeDtypeStruct(shape, F32)

    smem = pl.BlockSpec(memory_space=pltpu.SMEM)

    def full(*shape):
        return pl.BlockSpec(
            shape, lambda *at: (0,) * len(shape), pipeline_mode=pl.Buffered(1)
        )

    def whole_out(*shape):
        return pl.BlockSpec(shape, lambda *at: (0,) * len(shape))

    core_swap = [(at, at ^ 1) for at in range(groups)]
    sample_swap = [(at, at ^ cores) for at in range(groups)]

    outgoing = pl.pallas_call(
        outgoing_kernel,
        grid=(planes,),
        in_specs=[
            smem,
            pl.BlockSpec((samples, 1, rows, width), lambda p: (0, p, 0, 0)),
            pl.BlockSpec((1, rows, width), lambda p: (p, 0, 0)),
            full(width, width),
        ],
        out_specs=pl.BlockSpec((1, samples * cores, tall, half), lambda p: (p, 0, 0, 0)),
        out_shape=shape_of(planes, samples * cores, tall, half),
        compiler_params=params(1, 16),
        name="outgoing",
    )(noise_table, right_side, classes, basis_second)
    arrived = lax.all_to_all(
        outgoing.reshape(groups, tall, half), "mode", split_axis=0, concat_axis=0, tiled=True
    )

    eigen = eigen_second.reshape(1, -1)
    reach = 1
    while reach < groups:
        other = lax.ppermute(eigen, "mode", [(at, at ^ reach) for at in range(groups)])
        low = (index // reach) % 2 == 0
        eigen = jnp.where(
            low,
            jnp.concatenate([eigen, other], axis=1),
            jnp.concatenate([other, eigen], axis=1),
        )
        reach *= 2
    eigen = lax.dynamic_slice(eigen, (0, core * half), (1, half))
    weights = 1.0 / (eigen_first[:, None] * eigen + jnp.mean(noise_table))
    turned = basis_first.T

    near = arrived[:, rows:, :]
    far = lax.ppermute(near, "mode", sample_swap)

    chunk = half // 2
    steps = half // chunk
    tile = pl.BlockSpec((height, chunk), lambda j: (0, j))
    piece = pl.BlockSpec((groups, share, chunk), lambda j: (0, 0, j))
    pieces = pl.BlockSpec((2, groups, share, chunk), lambda j: (0, 0, 0, j))
    square = full(height, height)
    row_square = full(width, width)
    scratch = [pltpu.VMEM((groups, rows, chunk), F32)]
    spectral, keep, send, sum_one = pl.pallas_call(
        functools.partial(column_kernel, True),
        grid=(steps,),
        in_specs=[
            smem,
            pl.BlockSpec((groups, rows, chunk), lambda j: (0, 0, j)),
            tile,
            square,
            square,
            square,
        ],
        out_specs=[tile, pieces, pieces, whole_out(8, 128)],
        out_shape=[
            shape_of(height, half),
            shape_of(2, groups, share, half),
            shape_of(2, groups, share, half),
            shape_of(8, 128),
        ],
        scratch_shapes=scratch,
        compiler_params=params(1, 32),
        name="columns_one",
    )(place, arrived, weights, turned, basis_first, kernel_first)
    got = lax.ppermute(send, "mode", core_swap)

    part = groups // 2
    row_pieces = pl.BlockSpec((2, part, share, half), lambda i: (0, i, 0, 0))
    row_piece = pl.BlockSpec((part, share, half), lambda i: (i, 0, 0))
    row_whole = pl.BlockSpec((part, share, width), lambda i: (i, 0, 0))
    row_scratch = [pltpu.VMEM((part * share, width), F32)]
    row_specs = [smem, row_pieces, row_pieces, row_piece, row_piece, row_square, row_square]
    z_field, image, back_keep, back_send = pl.pallas_call(
        functools.partial(row_kernel, True),
        grid=(2,),
        in_specs=row_specs,
        out_specs=[row_whole, row_whole, row_piece, row_piece],
        out_shape=[
            shape_of(groups, share, width),
            shape_of(groups, share, width),
            shape_of(groups, share, half),
            shape_of(groups, share, half),
        ],
        scratch_shapes=row_scratch,
        compiler_params=params(1, 32),
        name="rows_one",
    )(place, keep, got, near, far, basis_second, kernel_second)
    back_got = lax.ppermute(back_send, "mode", core_swap)

    keep, send, sum_two = pl.pallas_call(
        functools.partial(column_kernel, False),
        grid=(steps,),
        in_specs=[smem, piece, piece, tile, tile, square, square, square],
        out_specs=[pieces, pieces, whole_out(8, 128)],
        out_shape=[
            shape_of(2, groups, share, half),
            shape_of(2, groups, share, half),
            shape_of(8, 128),
        ],
        scratch_shapes=scratch,
        compiler_params=params(1, 32),
        name="columns_two",
    )(place, back_keep, back_got, spectral, weights, turned, basis_first, kernel_first)
    got = lax.ppermute(send, "mode", core_swap)

    f_field, f_image, sums = pl.pallas_call(
        functools.partial(row_kernel, False),
        grid=(2,),
        in_specs=row_specs + [full(8, 128), full(8, 128)],
        out_specs=[row_whole, row_whole, whole_out(groups, 8, 128)],
        out_shape=[
            shape_of(groups, share, width),
            shape_of(groups, share, width),
            shape_of(groups, 8, 128),
        ],
        scratch_shapes=row_scratch,
        compiler_params=params(1, 32),
        name="rows_two",
    )(place, keep, got, near, far, basis_second, kernel_second, sum_one, sum_two)
    sums = lax.all_to_all(sums, "mode", split_axis=0, concat_axis=0, tiled=True)

    few = groups // 4
    few_spec = pl.BlockSpec((few, share, width), lambda i: (i, 0, 0))
    answer = pl.pallas_call(
        combine_kernel,
        grid=(4,),
        in_specs=[full(groups, 8, 128)] + [few_spec] * 4,
        out_specs=pl.BlockSpec((few, rows, width), lambda i: (i, 0, 0)),
        out_shape=shape_of(groups, rows, width),
        compiler_params=params(1, 20),
        name="combine",
    )(sums, z_field, image, f_field, f_image)
    answer = lax.all_to_all(answer, "mode", split_axis=0, concat_axis=0, tiled=True)

    block = pl.BlockSpec((samples, 1, rows, width), lambda p: (0, p, 0, 0))
    return tuple(
        pl.pallas_call(
            finish_kernel,
            grid=(planes,),
            in_specs=[
                pl.BlockSpec((samples * cores, rows, width), lambda p: (p, 0, 0)),
                block,
            ],
            out_specs=[block, block],
            out_shape=[shape_of(*right_side.shape)] * 2,
            compiler_params=params(1, 20),
            name="finish",
        )(answer, right_side)
    )


def body(right_side, classes, *rest):
    groups = lax.axis_size("mode")
    samples, planes, rows, width = right_side.shape
    paired = (
        groups == 2 * samples * planes
        and samples == 2
        and rows % 16 == 0
        and width % 512 == 0
        and groups % 8 == 0
    )
    chosen = paired_body if paired else general_body
    return chosen(right_side, classes, *rest)


def solution(mesh):
    in_specs = (
        P(None, "blocks", "mode", None),
        P("blocks", "mode", None),
        P(),
        P(),
        P(),
        P(),
        P(),
        P(),
        P("mode"),
    )
    out_specs = (P(None, "blocks", "mode", None), P(None, "blocks", "mode", None))
    return jax.shard_map(body, mesh=mesh, in_specs=in_specs, out_specs=out_specs, check_vma=False)
```

```python
import functools

import jax
import jax.numpy as jnp
from jax import lax
from jax.experimental import pallas as pl
from jax.experimental.pallas import tpu as pltpu
from jax.sharding import PartitionSpec as P


NCLASS = 8
ITERS = 2
F32 = jnp.float32
BF16 = jnp.bfloat16


def along_rows(matrix, field):
    return jnp.einsum("jk,sprk->sprj", matrix, field, precision=lax.Precision.HIGHEST)


def rows_to_send(matrix, field, groups):
    result = jnp.einsum("kj,sprk->jspr", matrix, field, precision=lax.Precision.HIGHEST)
    return result.reshape(groups, -1)


def received_to_columns(matrix, received, shape5):
    groups, _, _, _, rows = shape5
    block = received.reshape(shape5)
    reshaped = matrix.reshape(groups, rows, matrix.shape[1])
    return jnp.einsum("mri,mcspr->cspi", reshaped, block, precision=lax.Precision.HIGHEST)


def along_columns(matrix, columns):
    return jnp.einsum("ik,cspk->cspi", matrix, columns, precision=lax.Precision.HIGHEST)


def columns_to_send(matrix, columns, groups, rows):
    reshaped = matrix.reshape(groups, rows, matrix.shape[1])
    result = jnp.einsum("mrk,cspk->mcspr", reshaped, columns, precision=lax.Precision.HIGHEST)
    return result.reshape(groups, -1)


def received_to_rows(matrix, received, shape5):
    groups, cols, _, _, _ = shape5
    block = received.reshape(shape5)
    reshaped = matrix.reshape(matrix.shape[0], groups, cols)
    return jnp.einsum("jmc,mcspr->sprj", reshaped, block, precision=lax.Precision.HIGHEST)


def general_body(
    right_side,
    classes,
    noise_table,
    kernel_first,
    kernel_second,
    basis_first,
    basis_second,
    eigen_first,
    eigen_second,
):
    groups = lax.axis_size("mode")
    samples, planes, rows, _ = right_side.shape
    cols = eigen_second.shape[0]
    shape5 = (groups, cols, samples, planes, rows)
    kern_one = kernel_first.astype(F32)
    kern_two = kernel_second.astype(F32)
    base_one = basis_first.astype(F32)
    base_two = basis_second.astype(F32)
    noise = jnp.zeros(classes.shape, F32)
    for level in range(NCLASS):
        noise = noise + jnp.where(classes == level, noise_table[level], 0.0)
    noise = noise[None]
    mean_noise = jnp.mean(noise_table)
    col_weights = 1.0 / (eigen_second[:, None] * eigen_first[None, :] + mean_noise)
    col_weights = col_weights[:, None, None, :]

    def exchange(outgoing):
        return lax.all_to_all(outgoing, "mode", split_axis=0, concat_axis=0, tiled=True)

    def precond_apply(field):
        incoming = exchange(rows_to_send(base_two, field, groups))
        weighted = received_to_columns(base_one, incoming, shape5) * col_weights
        columns = along_columns(base_one, weighted)
        back = exchange(columns_to_send(base_one, weighted, groups, rows))
        kernel_back = exchange(columns_to_send(kern_one, columns, groups, rows))
        z_field = received_to_rows(base_two, back, shape5)
        image = (
            along_rows(kern_two, received_to_rows(base_two, kernel_back, shape5)) + noise * z_field
        )
        return (z_field, image)

    def inner(left, right):
        return lax.psum(jnp.sum(left * right), "mode")

    solution_field = jnp.zeros_like(right_side)
    residual = right_side
    z_field, image = precond_apply(residual)
    direction, along = (z_field, image)
    gamma = inner(residual, z_field)
    for step in range(ITERS):
        alpha = gamma / inner(direction, along)
        solution_field = solution_field + alpha * direction
        residual = residual - alpha * along
        if step + 1 < ITERS:
            z_field, image = precond_apply(residual)
            gamma_new = inner(residual, z_field)
            ratio = gamma_new / gamma
            direction = z_field + ratio * direction
            along = image + ratio * along
            gamma = gamma_new
    return (solution_field, residual)


def split(value):
    high = value.astype(BF16)
    low = (value - high.astype(F32)).astype(BF16)
    return high, low


def times_right(value, matrix, contract):
    high, low = split(value)
    dims = (((1,), (contract,)), ((), ()))
    both = jnp.concatenate([high, low], axis=0)
    result = lax.dot_general(both, matrix, dims, preferred_element_type=F32)
    return result[: value.shape[0]] + result[value.shape[0] :]


def times_left(matrix, value):
    high, low = split(value)
    dims = (((1,), (0,)), ((), ()))
    both = jnp.concatenate([high, low], axis=1)
    result = lax.dot_general(matrix, both, dims, preferred_element_type=F32)
    return result[:, : value.shape[1]] + result[:, value.shape[1] :]


def fold(value):
    total = jnp.sum(value, axis=0, keepdims=True)
    return functools.reduce(
        jnp.add, [total[:, at : at + 128] for at in range(0, total.shape[1], 128)]
    )


def params(dims, mebibytes):
    return pltpu.CompilerParams(
        dimension_semantics=("arbitrary",) * dims, vmem_limit_bytes=mebibytes * 1024 * 1024
    )


def outgoing_kernel(table_ref, right_ref, class_ref, basis_ref, out_ref):
    samples, _, rows, width = right_ref.shape
    cores = out_ref.shape[1] // samples
    half = width // cores
    field = right_ref[...].reshape(samples * rows, width)
    mapped = times_right(field, basis_ref[...], 0)
    level = class_ref[0]
    noise = jnp.full(level.shape, table_ref[0], F32)
    for index in range(1, NCLASS):
        noise = jnp.where(level == index, table_ref[index], noise)
    share = rows // cores
    for sample in range(samples):
        for core in range(cores):
            out_ref[0, sample * cores + core, :rows, :] = mapped[
                sample * rows : (sample + 1) * rows, core * half : (core + 1) * half
            ]
            out_ref[0, sample * cores + core, rows:, :] = noise[
                core * share : (core + 1) * share, sample * half : (sample + 1) * half
            ]


def column_kernel(first_call, place_ref, *refs):
    if first_call:
        (field_ref, weight_ref, turned_ref, basis_ref, kernel_ref) = refs[:5]
        (spectral_ref, keep_ref, send_ref, sum_ref, scratch_ref) = refs[5:]
    else:
        (held_ref, got_ref, before_ref, weight_ref, turned_ref, basis_ref, kernel_ref) = refs[:7]
        (keep_ref, send_ref, sum_ref, scratch_ref) = refs[7:]
    groups, rows, chunk = scratch_ref.shape
    share = rows // 2
    core = place_ref[0]
    mine = pl.ds(pl.multiple_of(core * share, share), share)
    theirs = pl.ds(pl.multiple_of((1 - core) * share, share), share)
    if first_call:
        field = field_ref[...].reshape(groups * rows, chunk)
    else:
        scratch_ref[:, mine, :] = held_ref[...]
        scratch_ref[:, theirs, :] = got_ref[...]
        field = scratch_ref[...].reshape(groups * rows, chunk)
    spectral = times_left(turned_ref[...], field)
    weighted = spectral * weight_ref[...]
    if first_call:
        spectral_ref[...] = spectral
        sums = [fold(spectral * weighted)]
    else:
        sums = [fold(before_ref[...] * weighted), fold(spectral * weighted)]
    block = jnp.concatenate(sums + [jnp.zeros((8 - len(sums), 128), F32)], axis=0)

    @pl.when(pl.program_id(0) == 0)
    def _():
        sum_ref[...] = block

    @pl.when(pl.program_id(0) != 0)
    def _():
        sum_ref[...] += block

    column = times_left(basis_ref[...], weighted)
    scratch_ref[...] = column.reshape(groups, rows, chunk)
    keep_ref[0] = scratch_ref[:, mine, :]
    send_ref[0] = scratch_ref[:, theirs, :]
    image = times_left(kernel_ref[...], column)
    scratch_ref[...] = image.reshape(groups, rows, chunk)
    keep_ref[1] = scratch_ref[:, mine, :]
    send_ref[1] = scratch_ref[:, theirs, :]


def row_kernel(first_call, place_ref, keep_ref, got_ref, near_ref, far_ref, basis_ref, kernel_ref, *refs):
    if first_call:
        (z_ref, image_ref, back_keep_ref, back_send_ref, scratch_ref) = refs
    else:
        (one_ref, two_ref, z_ref, image_ref, sum_ref, scratch_ref) = refs
    height, width = scratch_ref.shape
    half = width // 2
    core = place_ref[0]
    sample = place_ref[1]
    mine = pl.ds(pl.multiple_of(core * half, half), half)
    theirs = pl.ds(pl.multiple_of((1 - core) * half, half), half)

    def whole(index):
        scratch_ref[:, mine] = keep_ref[index].reshape(height, half)
        scratch_ref[:, theirs] = got_ref[index].reshape(height, half)
        return scratch_ref[...]

    basis = basis_ref[...]
    z_field = times_right(whole(0), basis, 1)
    image = times_right(times_right(whole(1), basis, 1), kernel_ref[...], 1)
    scratch_ref[:, pl.ds(pl.multiple_of(sample * half, half), half)] = near_ref[...].reshape(
        height, half
    )
    scratch_ref[:, pl.ds(pl.multiple_of((1 - sample) * half, half), half)] = far_ref[
        ...
    ].reshape(height, half)
    image = image + scratch_ref[...] * z_field
    z_ref[...] = z_field.reshape(z_ref.shape)
    image_ref[...] = image.reshape(image_ref.shape)
    if first_call:
        scratch_ref[...] = times_right(image, basis, 0)
        back_keep_ref[...] = scratch_ref[:, mine].reshape(back_keep_ref.shape)
        back_send_ref[...] = scratch_ref[:, theirs].reshape(back_send_ref.shape)
    else:

        @pl.when(pl.program_id(0) == 0)
        def _():
            first = jnp.concatenate(
                [one_ref[0:1], two_ref[0:2], jnp.zeros((5, 128), F32)], axis=0
            )
            sum_ref[...] = jnp.broadcast_to(first[None], sum_ref.shape)

        last = jnp.concatenate(
            [jnp.zeros((3, 128), F32), fold(z_field * image), jnp.zeros((4, 128), F32)], axis=0
        )
        sum_ref[...] += jnp.broadcast_to(last[None], sum_ref.shape)


def combine_kernel(sum_ref, z_ref, image_ref, f_ref, f_image_ref, out_ref):
    total = jnp.sum(sum_ref[...], axis=0)
    total = jnp.sum(total, axis=1, keepdims=True)
    g00, g01, g11, h11 = (total[at : at + 1] for at in range(4))
    alpha = g00 / g01
    turn = alpha * g11 / g01
    gamma = alpha * alpha * g11 - g00
    curvature = alpha * alpha * h11 - turn * turn * g01
    step = gamma / curvature
    on_z = alpha + step * turn
    on_f = -(alpha * step)
    share = z_ref.shape[1]
    out_ref[:, :share, :] = on_z[None] * z_ref[...] + on_f[None] * f_ref[...]
    out_ref[:, share:, :] = on_z[None] * image_ref[...] + on_f[None] * f_image_ref[...]


def finish_kernel(got_ref, right_ref, solution_ref, residual_ref):
    count, rows = got_ref.shape[:2]
    samples = right_ref.shape[0]
    cores = count // samples
    share = rows // cores
    for sample in range(samples):
        for core in range(cores):
            at = slice(core * share, (core + 1) * share)
            block = sample * cores + core
            solution_ref[sample, 0, at, :] = got_ref[block, :share, :]
            residual_ref[sample, 0, at, :] = (
                right_ref[sample, 0, at, :] - got_ref[block, share:, :]
            )


def paired_body(
    right_side,
    classes,
    noise_table,
    kernel_first,
    kernel_second,
    basis_first,
    basis_second,
    eigen_first,
    eigen_second,
):
    groups = lax.axis_size("mode")
    samples, planes, rows, width = right_side.shape
    height = groups * rows
    cores = 2
    half = width // cores
    share = rows // cores
    tall = rows + share
    index = lax.axis_index("mode")
    core = index % cores
    sample = (index // cores) % samples
    place = jnp.stack([core, sample]).astype(jnp.int32)

    def shape_of(*shape):
        return jax.ShapeDtypeStruct(shape, F32)

    smem = pl.BlockSpec(memory_space=pltpu.SMEM)

    def full(*shape):
        return pl.BlockSpec(
            shape, lambda *at: (0,) * len(shape), pipeline_mode=pl.Buffered(1)
        )

    def whole_out(*shape):
        return pl.BlockSpec(shape, lambda *at: (0,) * len(shape))

    core_swap = [(at, at ^ 1) for at in range(groups)]
    sample_swap = [(at, at ^ cores) for at in range(groups)]

    outgoing = pl.pallas_call(
        outgoing_kernel,
        grid=(planes,),
        in_specs=[
            smem,
            pl.BlockSpec((samples, 1, rows, width), lambda p: (0, p, 0, 0)),
            pl.BlockSpec((1, rows, width), lambda p: (p, 0, 0)),
            full(width, width),
        ],
        out_specs=pl.BlockSpec((1, samples * cores, tall, half), lambda p: (p, 0, 0, 0)),
        out_shape=shape_of(planes, samples * cores, tall, half),
        compiler_params=params(1, 58),
        name="outgoing",
    )(noise_table, right_side, classes, basis_second)
    arrived = lax.all_to_all(
        outgoing.reshape(groups, tall, half), "mode", split_axis=0, concat_axis=0, tiled=True
    )

    eigen = eigen_second.reshape(1, -1)
    plane = index // (cores * samples)
    for reach in (1, cores):
        other = lax.ppermute(eigen, "mode", [(at, at ^ reach) for at in range(groups)])
        low = (index // reach) % 2 == 0
        eigen = jnp.where(
            low,
            jnp.concatenate([eigen, other], axis=1),
            jnp.concatenate([other, eigen], axis=1),
        )
    unit = cores * samples
    shifted = [eigen] + [
        lax.ppermute(eigen, "mode", [(at, (at + by * unit) % groups) for at in range(groups)])
        for by in range(1, planes)
    ]
    per_core = planes // cores
    eigen = jnp.concatenate(
        [
            functools.reduce(
                jnp.add,
                [
                    jnp.where((plane - by) % planes == core * per_core + at, shifted[by], 0.0)
                    for by in range(planes)
                ],
            )
            for at in range(per_core)
        ],
        axis=1,
    )
    weights = 1.0 / (eigen_first[:, None] * eigen + jnp.mean(noise_table))
    turned = basis_first.T

    near = arrived[:, rows:, :]
    far = lax.ppermute(near, "mode", sample_swap)

    chunk = half
    steps = half // chunk
    tile = pl.BlockSpec((height, chunk), lambda j: (0, j))
    piece = pl.BlockSpec((groups, share, chunk), lambda j: (0, 0, j))
    pieces = pl.BlockSpec((2, groups, share, chunk), lambda j: (0, 0, 0, j))
    square = full(height, height)
    row_square = full(width, width)
    scratch = [pltpu.VMEM((groups, rows, chunk), F32)]
    spectral, keep, send, sum_one = pl.pallas_call(
        functools.partial(column_kernel, True),
        grid=(steps,),
        in_specs=[
            smem,
            pl.BlockSpec((groups, rows, chunk), lambda j: (0, 0, j)),
            tile,
            square,
            square,
            square,
        ],
        out_specs=[tile, pieces, pieces, whole_out(8, 128)],
        out_shape=[
            shape_of(height, half),
            shape_of(2, groups, share, half),
            shape_of(2, groups, share, half),
            shape_of(8, 128),
        ],
        scratch_shapes=scratch,
        compiler_params=params(1, 14),
        name="columns_one",
    )(place, arrived, weights, turned, basis_first, kernel_first)
    got = lax.ppermute(send, "mode", core_swap)

    part = groups
    row_pieces = pl.BlockSpec((2, part, share, half), lambda i: (0, i, 0, 0))
    row_piece = pl.BlockSpec((part, share, half), lambda i: (i, 0, 0))
    row_whole = pl.BlockSpec((part, share, width), lambda i: (i, 0, 0))
    row_scratch = [pltpu.VMEM((part * share, width), F32)]
    row_specs = [smem, row_pieces, row_pieces, row_piece, row_piece, row_square, row_square]
    z_field, image, back_keep, back_send = pl.pallas_call(
        functools.partial(row_kernel, True),
        grid=(groups // part,),
        in_specs=row_specs,
        out_specs=[row_whole, row_whole, row_piece, row_piece],
        out_shape=[
            shape_of(groups, share, width),
            shape_of(groups, share, width),
            shape_of(groups, share, half),
            shape_of(groups, share, half),
        ],
        scratch_shapes=row_scratch,
        compiler_params=params(1, 12),
        name="rows_one",
    )(place, keep, got, near, far, basis_second, kernel_second)
    back_got = lax.ppermute(back_send, "mode", core_swap)

    keep, send, sum_two = pl.pallas_call(
        functools.partial(column_kernel, False),
        grid=(steps,),
        in_specs=[smem, piece, piece, tile, tile, square, square, square],
        out_specs=[pieces, pieces, whole_out(8, 128)],
        out_shape=[
            shape_of(2, groups, share, half),
            shape_of(2, groups, share, half),
            shape_of(8, 128),
        ],
        scratch_shapes=scratch,
        compiler_params=params(1, 14),
        name="columns_two",
    )(place, back_keep, back_got, spectral, weights, turned, basis_first, kernel_first)
    got = lax.ppermute(send, "mode", core_swap)

    f_field, f_image, sums = pl.pallas_call(
        functools.partial(row_kernel, False),
        grid=(groups // part,),
        in_specs=row_specs + [full(8, 128), full(8, 128)],
        out_specs=[row_whole, row_whole, whole_out(groups, 8, 128)],
        out_shape=[
            shape_of(groups, share, width),
            shape_of(groups, share, width),
            shape_of(groups, 8, 128),
        ],
        scratch_shapes=row_scratch,
        compiler_params=params(1, 12),
        name="rows_two",
    )(place, keep, got, near, far, basis_second, kernel_second, sum_one, sum_two)
    sums = lax.all_to_all(sums, "mode", split_axis=0, concat_axis=0, tiled=True)

    few = groups // 4
    few_spec = pl.BlockSpec((few, share, width), lambda i: (i, 0, 0))
    answer = pl.pallas_call(
        combine_kernel,
        grid=(4,),
        in_specs=[full(groups, 8, 128)] + [few_spec] * 4,
        out_specs=pl.BlockSpec((few, rows, width), lambda i: (i, 0, 0)),
        out_shape=shape_of(groups, rows, width),
        compiler_params=params(1, 6),
        name="combine",
    )(sums, z_field, image, f_field, f_image)
    answer = lax.all_to_all(answer, "mode", split_axis=0, concat_axis=0, tiled=True)

    block = pl.BlockSpec((samples, 1, rows, width), lambda p: (0, p, 0, 0))
    return tuple(
        pl.pallas_call(
            finish_kernel,
            grid=(planes,),
            in_specs=[
                pl.BlockSpec((samples * cores, rows, width), lambda p: (p, 0, 0)),
                block,
            ],
            out_specs=[block, block],
            out_shape=[shape_of(*right_side.shape)] * 2,
            compiler_params=params(1, 10),
            name="finish",
        )(answer, right_side)
    )


def body(right_side, classes, *rest):
    groups = lax.axis_size("mode")
    samples, planes, rows, width = right_side.shape
    paired = (
        groups == 2 * samples * planes
        and samples == 2
        and rows % 16 == 0
        and width % 512 == 0
        and groups % 8 == 0
        and planes % 2 == 0
    )
    chosen = paired_body if paired else general_body
    return chosen(right_side, classes, *rest)


def solution(mesh):
    in_specs = (
        P(None, "blocks", "mode", None),
        P("blocks", "mode", None),
        P(),
        P(),
        P(),
        P(),
        P(),
        P(),
        P("mode"),
    )
    out_specs = (P(None, "blocks", "mode", None), P(None, "blocks", "mode", None))
    return jax.shard_map(body, mesh=mesh, in_specs=in_specs, out_specs=out_specs, check_vma=False)
```

```python
import functools

import jax
import jax.numpy as jnp
from jax import lax
from jax.experimental import pallas as pl
from jax.experimental.pallas import tpu as pltpu
from jax.sharding import PartitionSpec as P


NCLASS = 8
ITERS = 2
F32 = jnp.float32
BF16 = jnp.bfloat16


def along_rows(matrix, field):
    return jnp.einsum("jk,sprk->sprj", matrix, field, precision=lax.Precision.HIGHEST)


def rows_to_send(matrix, field, groups):
    result = jnp.einsum("kj,sprk->jspr", matrix, field, precision=lax.Precision.HIGHEST)
    return result.reshape(groups, -1)


def received_to_columns(matrix, received, shape5):
    groups, _, _, _, rows = shape5
    block = received.reshape(shape5)
    reshaped = matrix.reshape(groups, rows, matrix.shape[1])
    return jnp.einsum("mri,mcspr->cspi", reshaped, block, precision=lax.Precision.HIGHEST)


def along_columns(matrix, columns):
    return jnp.einsum("ik,cspk->cspi", matrix, columns, precision=lax.Precision.HIGHEST)


def columns_to_send(matrix, columns, groups, rows):
    reshaped = matrix.reshape(groups, rows, matrix.shape[1])
    result = jnp.einsum("mrk,cspk->mcspr", reshaped, columns, precision=lax.Precision.HIGHEST)
    return result.reshape(groups, -1)


def received_to_rows(matrix, received, shape5):
    groups, cols, _, _, _ = shape5
    block = received.reshape(shape5)
    reshaped = matrix.reshape(matrix.shape[0], groups, cols)
    return jnp.einsum("jmc,mcspr->sprj", reshaped, block, precision=lax.Precision.HIGHEST)


def general_body(
    right_side,
    classes,
    noise_table,
    kernel_first,
    kernel_second,
    basis_first,
    basis_second,
    eigen_first,
    eigen_second,
):
    groups = lax.axis_size("mode")
    samples, planes, rows, _ = right_side.shape
    cols = eigen_second.shape[0]
    shape5 = (groups, cols, samples, planes, rows)
    kern_one = kernel_first.astype(F32)
    kern_two = kernel_second.astype(F32)
    base_one = basis_first.astype(F32)
    base_two = basis_second.astype(F32)
    noise = jnp.zeros(classes.shape, F32)
    for level in range(NCLASS):
        noise = noise + jnp.where(classes == level, noise_table[level], 0.0)
    noise = noise[None]
    mean_noise = jnp.mean(noise_table)
    col_weights = 1.0 / (eigen_second[:, None] * eigen_first[None, :] + mean_noise)
    col_weights = col_weights[:, None, None, :]

    def exchange(outgoing):
        return lax.all_to_all(outgoing, "mode", split_axis=0, concat_axis=0, tiled=True)

    def precond_apply(field):
        incoming = exchange(rows_to_send(base_two, field, groups))
        weighted = received_to_columns(base_one, incoming, shape5) * col_weights
        columns = along_columns(base_one, weighted)
        back = exchange(columns_to_send(base_one, weighted, groups, rows))
        kernel_back = exchange(columns_to_send(kern_one, columns, groups, rows))
        z_field = received_to_rows(base_two, back, shape5)
        image = (
            along_rows(kern_two, received_to_rows(base_two, kernel_back, shape5)) + noise * z_field
        )
        return (z_field, image)

    def inner(left, right):
        return lax.psum(jnp.sum(left * right), "mode")

    solution_field = jnp.zeros_like(right_side)
    residual = right_side
    z_field, image = precond_apply(residual)
    direction, along = (z_field, image)
    gamma = inner(residual, z_field)
    for step in range(ITERS):
        alpha = gamma / inner(direction, along)
        solution_field = solution_field + alpha * direction
        residual = residual - alpha * along
        if step + 1 < ITERS:
            z_field, image = precond_apply(residual)
            gamma_new = inner(residual, z_field)
            ratio = gamma_new / gamma
            direction = z_field + ratio * direction
            along = image + ratio * along
            gamma = gamma_new
    return (solution_field, residual)


def split(value):
    high = value.astype(BF16)
    low = (value - high.astype(F32)).astype(BF16)
    return high, low


def times_right(value, matrix, contract):
    high, low = split(value)
    dims = (((1,), (contract,)), ((), ()))
    both = jnp.concatenate([high, low], axis=0)
    result = lax.dot_general(both, matrix, dims, preferred_element_type=F32)
    return result[: value.shape[0]] + result[value.shape[0] :]


def times_left(matrix, value):
    high, low = split(value)
    dims = (((1,), (0,)), ((), ()))
    both = jnp.concatenate([high, low], axis=1)
    result = lax.dot_general(matrix, both, dims, preferred_element_type=F32)
    return result[:, : value.shape[1]] + result[:, value.shape[1] :]


def fold(value):
    total = jnp.sum(value, axis=0, keepdims=True)
    return functools.reduce(
        jnp.add, [total[:, at : at + 128] for at in range(0, total.shape[1], 128)]
    )


def params(dims, mebibytes):
    return pltpu.CompilerParams(
        dimension_semantics=("arbitrary",) * dims, vmem_limit_bytes=mebibytes * 1024 * 1024
    )


def outgoing_kernel(table_ref, right_ref, class_ref, basis_ref, out_ref):
    samples, _, rows, width = right_ref.shape
    cores = out_ref.shape[1] // samples
    half = width // cores
    field = right_ref[...].reshape(samples * rows, width)
    mapped = times_right(field, basis_ref[...], 0)
    level = class_ref[0]
    noise = jnp.full(level.shape, table_ref[0], F32)
    for index in range(1, NCLASS):
        noise = jnp.where(level == index, table_ref[index], noise)
    share = rows // cores
    for sample in range(samples):
        for core in range(cores):
            out_ref[0, sample * cores + core, :rows, :] = mapped[
                sample * rows : (sample + 1) * rows, core * half : (core + 1) * half
            ]
            out_ref[0, sample * cores + core, rows:, :] = noise[
                core * share : (core + 1) * share, sample * half : (sample + 1) * half
            ]


def both_shares(place_ref, share):
    core = place_ref[0]
    mine = pl.ds(pl.multiple_of(core * share, share), share)
    theirs = pl.ds(pl.multiple_of((1 - core) * share, share), share)
    return mine, theirs


def split_rows(place_ref, value, scratch_ref, keep_ref, send_ref):
    mine, theirs = both_shares(place_ref, scratch_ref.shape[1] // 2)
    scratch_ref[...] = value.reshape(scratch_ref.shape)
    keep_ref[...] = scratch_ref[:, mine, :]
    send_ref[...] = scratch_ref[:, theirs, :]


def store_sums(sum_ref, sums):
    rows = sum_ref.shape[0]
    sum_ref[...] = jnp.concatenate(sums + [jnp.zeros((rows - len(sums), 128), F32)], axis=0)


def first_column_kernel(
    place_ref,
    table_ref,
    field_ref,
    tall_ref,
    wide_ref,
    turned_ref,
    basis_ref,
    spectral_ref,
    weight_ref,
    column_ref,
    keep_ref,
    send_ref,
    sum_ref,
    scratch_ref,
):
    mean = functools.reduce(jnp.add, [table_ref[at] for at in range(NCLASS)]) * (1.0 / NCLASS)
    height, width = spectral_ref.shape
    for at in range(0, width, 128):
        lanes = slice(at, at + 128)
        weight_ref[:, lanes] = 1.0 / (tall_ref[...] * wide_ref[:, lanes] + mean)
    spectral = times_left(turned_ref[...], field_ref[...].reshape(height, width))
    weighted = spectral * weight_ref[...]
    spectral_ref[...] = spectral
    store_sums(sum_ref, [fold(spectral * weighted)])
    column = times_left(basis_ref[...], weighted)
    column_ref[...] = column
    split_rows(place_ref, column, scratch_ref, keep_ref, send_ref)


def next_column_kernel(
    place_ref,
    held_ref,
    got_ref,
    before_ref,
    weight_ref,
    turned_ref,
    basis_ref,
    column_ref,
    keep_ref,
    send_ref,
    sum_ref,
    scratch_ref,
):
    mine, theirs = both_shares(place_ref, scratch_ref.shape[1] // 2)
    scratch_ref[:, mine, :] = held_ref[...]
    scratch_ref[:, theirs, :] = got_ref[...]
    spectral = times_left(turned_ref[...], scratch_ref[...].reshape(column_ref.shape))
    weighted = spectral * weight_ref[...]
    store_sums(sum_ref, [fold(before_ref[...] * weighted), fold(spectral * weighted)])
    column = times_left(basis_ref[...], weighted)
    column_ref[...] = column
    split_rows(place_ref, column, scratch_ref, keep_ref, send_ref)


def column_image_kernel(place_ref, column_ref, kernel_ref, keep_ref, send_ref, scratch_ref):
    image = times_left(kernel_ref[...], column_ref[...])
    split_rows(place_ref, image, scratch_ref, keep_ref, send_ref)


def join_columns(place_ref, scratch_ref, keep_ref, got_ref):
    height, width = scratch_ref.shape
    mine, theirs = both_shares(place_ref, width // 2)
    scratch_ref[:, mine] = keep_ref[...].reshape(height, width // 2)
    scratch_ref[:, theirs] = got_ref[...].reshape(height, width // 2)
    return scratch_ref[...]


def row_kernel(place_ref, keep_ref, got_ref, basis_ref, z_ref, scratch_ref):
    field = join_columns(place_ref, scratch_ref, keep_ref, got_ref)
    z_ref[...] = times_right(field, basis_ref[...], 1).reshape(z_ref.shape)


def row_image(place_ref, keep_ref, got_ref, basis_ref, kernel_ref, scratch_ref):
    field = join_columns(place_ref, scratch_ref, keep_ref, got_ref)
    return times_right(times_right(field, basis_ref[...], 1), kernel_ref[...], 1)


def add_noise(place_ref, image, z_ref, near_ref, far_ref, scratch_ref):
    height, width = scratch_ref.shape
    half = width // 2
    sample = place_ref[1]
    near = pl.ds(pl.multiple_of(sample * half, half), half)
    far = pl.ds(pl.multiple_of((1 - sample) * half, half), half)
    scratch_ref[:, near] = near_ref[...].reshape(height, half)
    scratch_ref[:, far] = far_ref[...].reshape(height, half)
    return image + scratch_ref[...] * z_ref[...].reshape(height, width)


def first_image_kernel(
    place_ref, keep_ref, got_ref, basis_ref, kernel_ref, image_ref, scratch_ref
):
    image = row_image(place_ref, keep_ref, got_ref, basis_ref, kernel_ref, scratch_ref)
    image_ref[...] = image.reshape(image_ref.shape)


def return_kernel(
    place_ref,
    part_ref,
    z_ref,
    near_ref,
    far_ref,
    basis_ref,
    image_ref,
    keep_ref,
    send_ref,
    scratch_ref,
):
    image = part_ref[...].reshape(scratch_ref.shape)
    image = add_noise(place_ref, image, z_ref, near_ref, far_ref, scratch_ref)
    image_ref[...] = image.reshape(image_ref.shape)
    mine, theirs = both_shares(place_ref, scratch_ref.shape[1] // 2)
    scratch_ref[...] = times_right(image, basis_ref[...], 0)
    keep_ref[...] = scratch_ref[:, mine].reshape(keep_ref.shape)
    send_ref[...] = scratch_ref[:, theirs].reshape(send_ref.shape)


def last_image_kernel(
    place_ref,
    keep_ref,
    got_ref,
    z_ref,
    near_ref,
    far_ref,
    basis_ref,
    kernel_ref,
    one_ref,
    two_ref,
    image_ref,
    sum_ref,
    scratch_ref,
):
    image = row_image(place_ref, keep_ref, got_ref, basis_ref, kernel_ref, scratch_ref)
    image = add_noise(place_ref, image, z_ref, near_ref, far_ref, scratch_ref)
    image_ref[...] = image.reshape(image_ref.shape)
    last = fold(z_ref[...].reshape(image.shape) * image)
    total = jnp.concatenate(
        [one_ref[0:1], two_ref[0:2], last, jnp.zeros((4, 128), F32)], axis=0
    )
    sum_ref[...] = jnp.broadcast_to(total[None], sum_ref.shape)


def combine_kernel(sum_ref, z_ref, image_ref, f_ref, f_image_ref, out_ref):
    total = jnp.sum(sum_ref[...], axis=0)
    total = jnp.sum(total, axis=1, keepdims=True)
    g00, g01, g11, h11 = (total[at : at + 1] for at in range(4))
    alpha = g00 / g01
    turn = alpha * g11 / g01
    gamma = alpha * alpha * g11 - g00
    curvature = alpha * alpha * h11 - turn * turn * g01
    step = gamma / curvature
    on_z = alpha + step * turn
    on_f = -(alpha * step)
    share = z_ref.shape[1]
    out_ref[:, :share, :] = on_z[None] * z_ref[...] + on_f[None] * f_ref[...]
    out_ref[:, share:, :] = on_z[None] * image_ref[...] + on_f[None] * f_image_ref[...]


def finish_kernel(got_ref, right_ref, solution_ref, residual_ref):
    count, rows = got_ref.shape[:2]
    samples = right_ref.shape[0]
    cores = count // samples
    share = rows // cores
    for sample in range(samples):
        for core in range(cores):
            at = slice(core * share, (core + 1) * share)
            block = sample * cores + core
            solution_ref[sample, 0, at, :] = got_ref[block, :share, :]
            residual_ref[sample, 0, at, :] = (
                right_ref[sample, 0, at, :] - got_ref[block, share:, :]
            )


def paired_body(
    right_side,
    classes,
    noise_table,
    kernel_first,
    kernel_second,
    basis_first,
    basis_second,
    eigen_first,
    eigen_second,
):
    groups = lax.axis_size("mode")
    samples, planes, rows, width = right_side.shape
    height = groups * rows
    cores = 2
    half = width // cores
    share = rows // cores
    tall = rows + share
    index = lax.axis_index("mode")
    core = index % cores
    sample = (index // cores) % samples
    place = jnp.stack([core, sample]).astype(jnp.int32)

    def shape_of(*shape):
        return jax.ShapeDtypeStruct(shape, F32)

    smem = pl.BlockSpec(memory_space=pltpu.SMEM)

    def full(*shape):
        return pl.BlockSpec(
            shape, lambda *at: (0,) * len(shape), pipeline_mode=pl.Buffered(1)
        )

    def whole_out(*shape):
        return pl.BlockSpec(shape, lambda *at: (0,) * len(shape))

    core_swap = [(at, at ^ 1) for at in range(groups)]
    sample_swap = [(at, at ^ cores) for at in range(groups)]

    outgoing = pl.pallas_call(
        outgoing_kernel,
        grid=(planes,),
        in_specs=[
            smem,
            pl.BlockSpec((samples, 1, rows, width), lambda p: (0, p, 0, 0)),
            pl.BlockSpec((1, rows, width), lambda p: (p, 0, 0)),
            full(width, width),
        ],
        out_specs=pl.BlockSpec((1, samples * cores, tall, half), lambda p: (p, 0, 0, 0)),
        out_shape=shape_of(planes, samples * cores, tall, half),
        compiler_params=params(1, 58),
        name="outgoing",
    )(noise_table, right_side, classes, basis_second)
    arrived = lax.all_to_all(
        outgoing.reshape(groups, tall, half), "mode", split_axis=0, concat_axis=0, tiled=True
    )

    eigen = eigen_second.reshape(1, -1)
    plane = index // (cores * samples)
    for reach in (1, cores):
        other = lax.ppermute(eigen, "mode", [(at, at ^ reach) for at in range(groups)])
        low = (index // reach) % 2 == 0
        eigen = jnp.where(
            low,
            jnp.concatenate([eigen, other], axis=1),
            jnp.concatenate([other, eigen], axis=1),
        )
    unit = cores * samples
    shifted = [eigen] + [
        lax.ppermute(eigen, "mode", [(at, (at + by * unit) % groups) for at in range(groups)])
        for by in range(1, planes)
    ]
    per_core = planes // cores
    eigen = jnp.concatenate(
        [
            functools.reduce(
                jnp.add,
                [
                    jnp.where((plane - by) % planes == core * per_core + at, shifted[by], 0.0)
                    for by in range(planes)
                ],
            )
            for at in range(per_core)
        ],
        axis=1,
    )
    tall_eigen = jnp.broadcast_to(eigen_first[:, None], (height, 128))
    turned = basis_first.T

    near = arrived[:, rows:, :]
    far = lax.ppermute(near, "mode", sample_swap)

    def swap(value):
        return lax.ppermute(value, "mode", core_swap)

    def call(kernel, inputs, shapes, scratch_shape, specs=None):
        return pl.pallas_call(
            kernel,
            grid=(1,),
            in_specs=specs or [smem] + [full(*value.shape) for value in inputs[1:]],
            out_specs=[whole_out(*shape) for shape in shapes],
            out_shape=[shape_of(*shape) for shape in shapes],
            scratch_shapes=[pltpu.VMEM(scratch_shape, F32)],
            compiler_params=params(1, 12),
        )(*inputs)

    tile = (height, half)
    piece = (groups, share, half)
    whole = (groups, share, width)
    by_rows = (groups, rows, half)
    flat = (groups * share, width)
    sums_shape = (8, 128)

    spectral, weights, column, keep, send, sum_one = call(
        first_column_kernel,
        (place, noise_table, arrived, tall_eigen, eigen, turned, basis_first),
        (tile, tile, tile, piece, piece, sums_shape),
        by_rows,
        [smem, smem, full(groups, rows, half), full(height, 128), full(1, half)]
        + [full(height, height)] * 2,
    )
    got = swap(send)
    image_keep, image_send = call(
        column_image_kernel, (place, column, kernel_first), (piece, piece), by_rows
    )
    image_got = swap(image_send)
    (z_field,) = call(row_kernel, (place, keep, got, basis_second), (whole,), flat)
    (part,) = call(
        first_image_kernel,
        (place, image_keep, image_got, basis_second, kernel_second),
        (whole,),
        flat,
    )
    image, back_keep, back_send = call(
        return_kernel, (place, part, z_field, near, far, basis_second), (whole, piece, piece), flat
    )
    back_got = swap(back_send)

    column, keep, send, sum_two = call(
        next_column_kernel,
        (place, back_keep, back_got, spectral, weights, turned, basis_first),
        (tile, piece, piece, sums_shape),
        by_rows,
    )
    got = swap(send)
    image_keep, image_send = call(
        column_image_kernel, (place, column, kernel_first), (piece, piece), by_rows
    )
    image_got = swap(image_send)
    (f_field,) = call(row_kernel, (place, keep, got, basis_second), (whole,), flat)
    f_image, sums = call(
        last_image_kernel,
        (
            place,
            image_keep,
            image_got,
            f_field,
            near,
            far,
            basis_second,
            kernel_second,
            sum_one,
            sum_two,
        ),
        (whole, (groups, 8, 128)),
        flat,
    )
    sums = lax.all_to_all(sums, "mode", split_axis=0, concat_axis=0, tiled=True)

    few = groups // 4
    few_spec = pl.BlockSpec((few, share, width), lambda i: (i, 0, 0))
    answer = pl.pallas_call(
        combine_kernel,
        grid=(4,),
        in_specs=[full(groups, 8, 128)] + [few_spec] * 4,
        out_specs=pl.BlockSpec((few, rows, width), lambda i: (i, 0, 0)),
        out_shape=shape_of(groups, rows, width),
        compiler_params=params(1, 6),
        name="combine",
    )(sums, z_field, image, f_field, f_image)
    answer = lax.all_to_all(answer, "mode", split_axis=0, concat_axis=0, tiled=True)

    block = pl.BlockSpec((samples, 1, rows, width), lambda p: (0, p, 0, 0))
    return tuple(
        pl.pallas_call(
            finish_kernel,
            grid=(planes,),
            in_specs=[
                pl.BlockSpec((samples * cores, rows, width), lambda p: (p, 0, 0)),
                block,
            ],
            out_specs=[block, block],
            out_shape=[shape_of(*right_side.shape)] * 2,
            compiler_params=params(1, 10),
            name="finish",
        )(answer, right_side)
    )


def body(right_side, classes, *rest):
    groups = lax.axis_size("mode")
    samples, planes, rows, width = right_side.shape
    paired = (
        groups == 2 * samples * planes
        and samples == 2
        and rows % 16 == 0
        and width % 512 == 0
        and groups % 8 == 0
        and planes % 2 == 0
    )
    chosen = paired_body if paired else general_body
    return chosen(right_side, classes, *rest)


def solution(mesh):
    in_specs = (
        P(None, "blocks", "mode", None),
        P("blocks", "mode", None),
        P(),
        P(),
        P(),
        P(),
        P(),
        P(),
        P("mode"),
    )
    out_specs = (P(None, "blocks", "mode", None), P(None, "blocks", "mode", None))
    return jax.shard_map(body, mesh=mesh, in_specs=in_specs, out_specs=out_specs, check_vma=False)
```

```python
import functools

import jax
import jax.numpy as jnp
from jax import lax
from jax.experimental import pallas as pl
from jax.experimental.pallas import tpu as pltpu
from jax.sharding import PartitionSpec as P


NCLASS = 8
ITERS = 2
F32 = jnp.float32
BF16 = jnp.bfloat16


def along_rows(matrix, field):
    return jnp.einsum("jk,sprk->sprj", matrix, field, precision=lax.Precision.HIGHEST)


def rows_to_send(matrix, field, groups):
    result = jnp.einsum("kj,sprk->jspr", matrix, field, precision=lax.Precision.HIGHEST)
    return result.reshape(groups, -1)


def received_to_columns(matrix, received, shape5):
    groups, _, _, _, rows = shape5
    block = received.reshape(shape5)
    reshaped = matrix.reshape(groups, rows, matrix.shape[1])
    return jnp.einsum("mri,mcspr->cspi", reshaped, block, precision=lax.Precision.HIGHEST)


def along_columns(matrix, columns):
    return jnp.einsum("ik,cspk->cspi", matrix, columns, precision=lax.Precision.HIGHEST)


def columns_to_send(matrix, columns, groups, rows):
    reshaped = matrix.reshape(groups, rows, matrix.shape[1])
    result = jnp.einsum("mrk,cspk->mcspr", reshaped, columns, precision=lax.Precision.HIGHEST)
    return result.reshape(groups, -1)


def received_to_rows(matrix, received, shape5):
    groups, cols, _, _, _ = shape5
    block = received.reshape(shape5)
    reshaped = matrix.reshape(matrix.shape[0], groups, cols)
    return jnp.einsum("jmc,mcspr->sprj", reshaped, block, precision=lax.Precision.HIGHEST)


def general_body(
    right_side,
    classes,
    noise_table,
    kernel_first,
    kernel_second,
    basis_first,
    basis_second,
    eigen_first,
    eigen_second,
):
    groups = lax.axis_size("mode")
    samples, planes, rows, _ = right_side.shape
    cols = eigen_second.shape[0]
    shape5 = (groups, cols, samples, planes, rows)
    kern_one = kernel_first.astype(F32)
    kern_two = kernel_second.astype(F32)
    base_one = basis_first.astype(F32)
    base_two = basis_second.astype(F32)
    noise = jnp.zeros(classes.shape, F32)
    for level in range(NCLASS):
        noise = noise + jnp.where(classes == level, noise_table[level], 0.0)
    noise = noise[None]
    mean_noise = jnp.mean(noise_table)
    col_weights = 1.0 / (eigen_second[:, None] * eigen_first[None, :] + mean_noise)
    col_weights = col_weights[:, None, None, :]

    def exchange(outgoing):
        return lax.all_to_all(outgoing, "mode", split_axis=0, concat_axis=0, tiled=True)

    def precond_apply(field):
        incoming = exchange(rows_to_send(base_two, field, groups))
        weighted = received_to_columns(base_one, incoming, shape5) * col_weights
        columns = along_columns(base_one, weighted)
        back = exchange(columns_to_send(base_one, weighted, groups, rows))
        kernel_back = exchange(columns_to_send(kern_one, columns, groups, rows))
        z_field = received_to_rows(base_two, back, shape5)
        image = (
            along_rows(kern_two, received_to_rows(base_two, kernel_back, shape5)) + noise * z_field
        )
        return (z_field, image)

    def inner(left, right):
        return lax.psum(jnp.sum(left * right), "mode")

    solution_field = jnp.zeros_like(right_side)
    residual = right_side
    z_field, image = precond_apply(residual)
    direction, along = (z_field, image)
    gamma = inner(residual, z_field)
    for step in range(ITERS):
        alpha = gamma / inner(direction, along)
        solution_field = solution_field + alpha * direction
        residual = residual - alpha * along
        if step + 1 < ITERS:
            z_field, image = precond_apply(residual)
            gamma_new = inner(residual, z_field)
            ratio = gamma_new / gamma
            direction = z_field + ratio * direction
            along = image + ratio * along
            gamma = gamma_new
    return (solution_field, residual)


def split(value):
    high = value.astype(BF16)
    low = (value - high.astype(F32)).astype(BF16)
    return high, low


def times_right(value, matrix, contract):
    high, low = split(value)
    dims = (((1,), (contract,)), ((), ()))
    both = jnp.concatenate([high, low], axis=0)
    result = lax.dot_general(both, matrix, dims, preferred_element_type=F32)
    return result[: value.shape[0]] + result[value.shape[0] :]


def times_left(matrix, value):
    high, low = split(value)
    dims = (((1,), (0,)), ((), ()))
    both = jnp.concatenate([high, low], axis=1)
    result = lax.dot_general(matrix, both, dims, preferred_element_type=F32)
    return result[:, : value.shape[1]] + result[:, value.shape[1] :]


def fold(value):
    total = jnp.sum(value, axis=0, keepdims=True)
    return functools.reduce(
        jnp.add, [total[:, at : at + 128] for at in range(0, total.shape[1], 128)]
    )


def params(dims, mebibytes):
    return pltpu.CompilerParams(
        dimension_semantics=("arbitrary",) * dims, vmem_limit_bytes=mebibytes * 1024 * 1024
    )


def noise_kernel(place_ref, table_ref, class_ref, *out_refs):
    planes = class_ref.shape[0]
    for by, out_ref in enumerate(out_refs):
        level = class_ref[(place_ref[2] + by) % planes]
        noise = jnp.full(level.shape, table_ref[0], F32)
        for index in range(1, NCLASS):
            noise = jnp.where(level == index, table_ref[index], noise)
        out_ref[...] = noise


def follow_kernel(value_ref, *refs):
    refs[-1][...] = value_ref[...]


def outgoing_kernel(right_ref, basis_ref, out_ref):
    samples, _, rows, width = right_ref.shape
    cores = out_ref.shape[2]
    half = width // cores
    field = right_ref[...].reshape(samples * rows, width)
    mapped = times_right(field, basis_ref[...], 0)
    for sample in range(samples):
        for core in range(cores):
            out_ref[0, sample, core] = mapped[
                sample * rows : (sample + 1) * rows, core * half : (core + 1) * half
            ]


def both_shares(place_ref, share):
    core = place_ref[0]
    mine = pl.ds(pl.multiple_of(core * share, share), share)
    theirs = pl.ds(pl.multiple_of((1 - core) * share, share), share)
    return mine, theirs


def split_rows(place_ref, value, scratch_ref, keep_ref, send_ref):
    core = place_ref[0]
    scratch_ref[...] = value.reshape(scratch_ref.shape)
    keep_ref[...] = scratch_ref[:, core]
    send_ref[...] = scratch_ref[:, 1 - core]


def store_sums(sum_ref, sums):
    rows = sum_ref.shape[0]
    sum_ref[...] = jnp.concatenate(sums + [jnp.zeros((rows - len(sums), 128), F32)], axis=0)


def first_column_kernel(
    place_ref,
    table_ref,
    field_ref,
    tall_ref,
    wide_ref,
    turned_ref,
    basis_ref,
    spectral_ref,
    weight_ref,
    column_ref,
    keep_ref,
    send_ref,
    sum_ref,
    scratch_ref,
):
    mean = functools.reduce(jnp.add, [table_ref[at] for at in range(NCLASS)]) * (1.0 / NCLASS)
    height, width = spectral_ref.shape
    for at in range(0, width, 128):
        lanes = slice(at, at + 128)
        weight_ref[:, lanes] = 1.0 / (tall_ref[...] * wide_ref[:, lanes] + mean)
    spectral = times_left(turned_ref[...], field_ref[...].reshape(height, width))
    weighted = spectral * weight_ref[...]
    spectral_ref[...] = spectral
    store_sums(sum_ref, [fold(spectral * weighted)])
    column = times_left(basis_ref[...], weighted)
    column_ref[...] = column
    split_rows(place_ref, column, scratch_ref, keep_ref, send_ref)


def next_column_kernel(
    place_ref,
    held_ref,
    got_ref,
    before_ref,
    weight_ref,
    turned_ref,
    basis_ref,
    column_ref,
    keep_ref,
    send_ref,
    sum_ref,
    scratch_ref,
):
    core = place_ref[0]
    scratch_ref[:, core] = held_ref[...]
    scratch_ref[:, 1 - core] = got_ref[...]
    spectral = times_left(turned_ref[...], scratch_ref[...].reshape(column_ref.shape))
    weighted = spectral * weight_ref[...]
    store_sums(sum_ref, [fold(before_ref[...] * weighted), fold(spectral * weighted)])
    column = times_left(basis_ref[...], weighted)
    column_ref[...] = column
    split_rows(place_ref, column, scratch_ref, keep_ref, send_ref)


def column_image_kernel(place_ref, column_ref, kernel_ref, keep_ref, send_ref, scratch_ref):
    image = times_left(kernel_ref[...], column_ref[...])
    split_rows(place_ref, image, scratch_ref, keep_ref, send_ref)


def join_columns(place_ref, scratch_ref, keep_ref, got_ref):
    height, width = scratch_ref.shape
    mine, theirs = both_shares(place_ref, width // 2)
    scratch_ref[:, mine] = keep_ref[...].reshape(height, width // 2)
    scratch_ref[:, theirs] = got_ref[...].reshape(height, width // 2)
    return scratch_ref[...]


def row_kernel(place_ref, keep_ref, got_ref, basis_ref, z_ref, scratch_ref):
    field = join_columns(place_ref, scratch_ref, keep_ref, got_ref)
    z_ref[...] = times_right(field, basis_ref[...], 1).reshape(z_ref.shape)


def row_image(place_ref, keep_ref, got_ref, basis_ref, kernel_ref, scratch_ref):
    field = join_columns(place_ref, scratch_ref, keep_ref, got_ref)
    return times_right(times_right(field, basis_ref[...], 1), kernel_ref[...], 1)


def add_noise(place_ref, image, z_ref, noise_refs, image_ref):
    image_ref[...] = image.reshape(image_ref.shape)
    planes = len(noise_refs) // 2
    samples = image_ref.shape[0] // planes
    for by in range(planes):
        row = (place_ref[2] + planes - by) % planes
        for at, noise_ref in enumerate((noise_refs[by], noise_refs[planes + by])):
            sample = (place_ref[1] + at) % samples
            block = row * samples + sample
            image_ref[block] += noise_ref[...] * z_ref[block]


def first_image_kernel(
    place_ref, keep_ref, got_ref, basis_ref, kernel_ref, image_ref, scratch_ref
):
    image = row_image(place_ref, keep_ref, got_ref, basis_ref, kernel_ref, scratch_ref)
    image_ref[...] = image.reshape(image_ref.shape)


def return_kernel(place_ref, part_ref, z_ref, basis_ref, *refs):
    noise_refs, (image_ref, keep_ref, send_ref, scratch_ref) = refs[:-4], refs[-4:]
    add_noise(place_ref, part_ref[...], z_ref, noise_refs, image_ref)
    mine, theirs = both_shares(place_ref, scratch_ref.shape[1] // 2)
    scratch_ref[...] = times_right(image_ref[...].reshape(scratch_ref.shape), basis_ref[...], 0)
    keep_ref[...] = scratch_ref[:, mine].reshape(keep_ref.shape)
    send_ref[...] = scratch_ref[:, theirs].reshape(send_ref.shape)


def last_image_kernel(
    place_ref, keep_ref, got_ref, z_ref, basis_ref, kernel_ref, one_ref, two_ref, *refs
):
    noise_refs, (image_ref, sum_ref, scratch_ref) = refs[:-3], refs[-3:]
    image = row_image(place_ref, keep_ref, got_ref, basis_ref, kernel_ref, scratch_ref)
    add_noise(place_ref, image, z_ref, noise_refs, image_ref)
    last = fold((z_ref[...] * image_ref[...]).reshape(scratch_ref.shape))
    total = jnp.concatenate(
        [one_ref[0:1], two_ref[0:2], last, jnp.zeros((4, 128), F32)], axis=0
    )
    sum_ref[...] = jnp.broadcast_to(total[None], sum_ref.shape)


def combine_kernel(sum_ref, z_ref, image_ref, f_ref, f_image_ref, out_ref):
    total = jnp.sum(sum_ref[...], axis=0)
    total = jnp.sum(total, axis=1, keepdims=True)
    g00, g01, g11, h11 = (total[at : at + 1] for at in range(4))
    alpha = g00 / g01
    turn = alpha * g11 / g01
    gamma = alpha * alpha * g11 - g00
    curvature = alpha * alpha * h11 - turn * turn * g01
    step = gamma / curvature
    on_z = alpha + step * turn
    on_f = -(alpha * step)
    share = z_ref.shape[1]
    out_ref[:, :share, :] = on_z[None] * z_ref[...] + on_f[None] * f_ref[...]
    out_ref[:, share:, :] = on_z[None] * image_ref[...] + on_f[None] * f_image_ref[...]


def finish_kernel(got_ref, right_ref, solution_ref, residual_ref):
    samples = got_ref.shape[0]
    rows = got_ref.shape[1] // 2
    for sample in range(samples):
        solution_ref[sample, 0] = got_ref[sample, :rows, :]
        residual_ref[sample, 0] = right_ref[sample, 0] - got_ref[sample, rows:, :]


def paired_body(
    right_side,
    classes,
    noise_table,
    kernel_first,
    kernel_second,
    basis_first,
    basis_second,
    eigen_first,
    eigen_second,
):
    groups = lax.axis_size("mode")
    samples, planes, rows, width = right_side.shape
    height = groups * rows
    cores = 2
    half = width // cores
    blocks = groups // cores
    unit = cores * samples
    index = lax.axis_index("mode")
    core = index % cores
    sample = (index // cores) % samples
    plane = index // unit
    place = jnp.stack([core, sample, plane]).astype(jnp.int32)

    def shape_of(*shape):
        return jax.ShapeDtypeStruct(shape, F32)

    smem = pl.BlockSpec(memory_space=pltpu.SMEM)

    def full(*shape):
        return pl.BlockSpec(
            shape, lambda *at: (0,) * len(shape), pipeline_mode=pl.Buffered(1)
        )

    def whole_out(*shape):
        return pl.BlockSpec(shape, lambda *at: (0,) * len(shape))

    core_swap = [(at, at ^ 1) for at in range(groups)]
    sample_swap = [(at, at ^ cores) for at in range(groups)]

    noise = pl.pallas_call(
        noise_kernel,
        grid=(1,),
        in_specs=[smem, smem, full(planes, rows, width)],
        out_specs=[whole_out(rows, width)] * planes,
        out_shape=[shape_of(rows, width)] * planes,
        compiler_params=params(1, 8),
        name="noise",
    )(place, noise_table, classes)
    near = [noise[0]] + [
        lax.ppermute(noise[by], "mode", [(at, (at + by * unit) % groups) for at in range(groups)])
        for by in range(1, planes)
    ]
    far = [lax.ppermute(value, "mode", sample_swap) for value in near]
    noise = (*near, *far)

    outgoing = pl.pallas_call(
        outgoing_kernel,
        grid=(planes,),
        in_specs=[
            pl.BlockSpec((samples, 1, rows, width), lambda p: (0, p, 0, 0)),
            full(width, width),
        ],
        out_specs=pl.BlockSpec((1, samples, cores, rows, half), lambda p: (p, 0, 0, 0, 0)),
        out_shape=shape_of(planes, samples, cores, rows, half),
        compiler_params=params(1, 56),
        name="outgoing",
    )(right_side, basis_second)
    arrived = lax.all_to_all(
        outgoing.reshape(groups, rows, half), "mode", split_axis=0, concat_axis=0, tiled=True
    )

    eigen = eigen_second.reshape(1, -1)
    for reach in (1, cores):
        other = lax.ppermute(eigen, "mode", [(at, at ^ reach) for at in range(groups)])
        low = (index // reach) % 2 == 0
        eigen = jnp.where(
            low,
            jnp.concatenate([eigen, other], axis=1),
            jnp.concatenate([other, eigen], axis=1),
        )
    eigen = pl.pallas_call(
        follow_kernel,
        in_specs=[pl.BlockSpec(memory_space=pltpu.VMEM)]
        + [pl.BlockSpec(memory_space=pl.ANY)] * (planes - 1),
        out_specs=pl.BlockSpec(memory_space=pltpu.VMEM),
        out_shape=shape_of(*eigen.shape),
        compiler_params=pltpu.CompilerParams(vmem_limit_bytes=1024 * 1024),
        name="follow",
    )(eigen, *near[1:])
    shifted = [eigen] + [
        lax.ppermute(eigen, "mode", [(at, (at + by * unit) % groups) for at in range(groups)])
        for by in range(1, planes)
    ]
    per_core = planes // cores
    eigen = jnp.concatenate(
        [
            functools.reduce(
                jnp.add,
                [
                    jnp.where((plane - by) % planes == core * per_core + at, shifted[by], 0.0)
                    for by in range(planes)
                ],
            )
            for at in range(per_core)
        ],
        axis=1,
    )
    tall_eigen = jnp.broadcast_to(eigen_first[:, None], (height, 128))
    turned = basis_first.T

    def swap(value):
        return lax.ppermute(value, "mode", core_swap)

    def call(kernel, inputs, shapes, scratch_shape, specs=None):
        return pl.pallas_call(
            kernel,
            grid=(1,),
            in_specs=specs or [smem] + [full(*value.shape) for value in inputs[1:]],
            out_specs=[whole_out(*shape) for shape in shapes],
            out_shape=[shape_of(*shape) for shape in shapes],
            scratch_shapes=[pltpu.VMEM(scratch_shape, F32)],
            compiler_params=params(1, 12),
        )(*inputs)

    tile = (height, half)
    piece = (blocks, rows, half)
    whole = (blocks, rows, width)
    by_rows = (blocks, cores, rows, half)
    flat = (blocks * rows, width)
    sums_shape = (8, 128)

    spectral, weights, column, keep, send, sum_one = call(
        first_column_kernel,
        (place, noise_table, arrived, tall_eigen, eigen, turned, basis_first),
        (tile, tile, tile, piece, piece, sums_shape),
        by_rows,
        [smem, smem, full(groups, rows, half), full(height, 128), full(1, half)]
        + [full(height, height)] * 2,
    )
    got = swap(send)
    image_keep, image_send = call(
        column_image_kernel, (place, column, kernel_first), (piece, piece), by_rows
    )
    image_got = swap(image_send)
    (z_field,) = call(row_kernel, (place, keep, got, basis_second), (whole,), flat)
    (part,) = call(
        first_image_kernel,
        (place, image_keep, image_got, basis_second, kernel_second),
        (whole,),
        flat,
    )
    image, back_keep, back_send = call(
        return_kernel, (place, part, z_field, basis_second, *noise), (whole, piece, piece), flat
    )
    back_got = swap(back_send)

    column, keep, send, sum_two = call(
        next_column_kernel,
        (place, back_keep, back_got, spectral, weights, turned, basis_first),
        (tile, piece, piece, sums_shape),
        by_rows,
    )
    got = swap(send)
    image_keep, image_send = call(
        column_image_kernel, (place, column, kernel_first), (piece, piece), by_rows
    )
    image_got = swap(image_send)
    (f_field,) = call(row_kernel, (place, keep, got, basis_second), (whole,), flat)
    f_image, sums = call(
        last_image_kernel,
        (
            place,
            image_keep,
            image_got,
            f_field,
            basis_second,
            kernel_second,
            sum_one,
            sum_two,
            *noise,
        ),
        (whole, (groups, 8, 128)),
        flat,
    )
    sums = lax.all_to_all(sums, "mode", split_axis=0, concat_axis=0, tiled=True)

    few = blocks // 4
    few_spec = pl.BlockSpec((few, rows, width), lambda i: (i, 0, 0))
    answer = pl.pallas_call(
        combine_kernel,
        grid=(4,),
        in_specs=[full(groups, 8, 128)] + [few_spec] * 4,
        out_specs=pl.BlockSpec((few, 2 * rows, width), lambda i: (i, 0, 0)),
        out_shape=shape_of(blocks, 2 * rows, width),
        compiler_params=params(1, 6),
        name="combine",
    )(sums, z_field, image, f_field, f_image)
    answer = lax.all_to_all(
        answer,
        "mode",
        split_axis=0,
        concat_axis=0,
        axis_index_groups=[list(range(at, groups, cores)) for at in range(cores)],
        tiled=True,
    )

    block = pl.BlockSpec((samples, 1, rows, width), lambda p: (0, p, 0, 0))
    return tuple(
        pl.pallas_call(
            finish_kernel,
            grid=(planes,),
            in_specs=[
                pl.BlockSpec((samples, 2 * rows, width), lambda p: (p, 0, 0)),
                block,
            ],
            out_specs=[block, block],
            out_shape=[shape_of(*right_side.shape)] * 2,
            compiler_params=params(1, 10),
            name="finish",
        )(answer, right_side)
    )


def body(right_side, classes, *rest):
    groups = lax.axis_size("mode")
    samples, planes, rows, width = right_side.shape
    paired = (
        groups == 2 * samples * planes
        and samples == 2
        and rows % 8 == 0
        and width % 512 == 0
        and planes % 2 == 0
    )
    chosen = paired_body if paired else general_body
    return chosen(right_side, classes, *rest)


def solution(mesh):
    in_specs = (
        P(None, "blocks", "mode", None),
        P("blocks", "mode", None),
        P(),
        P(),
        P(),
        P(),
        P(),
        P(),
        P("mode"),
    )
    out_specs = (P(None, "blocks", "mode", None), P(None, "blocks", "mode", None))
    return jax.shard_map(body, mesh=mesh, in_specs=in_specs, out_specs=out_specs, check_vma=False)
```

```python
import functools

import jax
import jax.numpy as jnp
from jax import lax
from jax.experimental import pallas as pl
from jax.experimental.pallas import tpu as pltpu
from jax.sharding import PartitionSpec as P


NCLASS = 8
ITERS = 2
F32 = jnp.float32
BF16 = jnp.bfloat16


def along_rows(matrix, field):
    return jnp.einsum("jk,sprk->sprj", matrix, field, precision=lax.Precision.HIGHEST)


def rows_to_send(matrix, field, groups):
    result = jnp.einsum("kj,sprk->jspr", matrix, field, precision=lax.Precision.HIGHEST)
    return result.reshape(groups, -1)


def received_to_columns(matrix, received, shape5):
    groups, _, _, _, rows = shape5
    block = received.reshape(shape5)
    reshaped = matrix.reshape(groups, rows, matrix.shape[1])
    return jnp.einsum("mri,mcspr->cspi", reshaped, block, precision=lax.Precision.HIGHEST)


def along_columns(matrix, columns):
    return jnp.einsum("ik,cspk->cspi", matrix, columns, precision=lax.Precision.HIGHEST)


def columns_to_send(matrix, columns, groups, rows):
    reshaped = matrix.reshape(groups, rows, matrix.shape[1])
    result = jnp.einsum("mrk,cspk->mcspr", reshaped, columns, precision=lax.Precision.HIGHEST)
    return result.reshape(groups, -1)


def received_to_rows(matrix, received, shape5):
    groups, cols, _, _, _ = shape5
    block = received.reshape(shape5)
    reshaped = matrix.reshape(matrix.shape[0], groups, cols)
    return jnp.einsum("jmc,mcspr->sprj", reshaped, block, precision=lax.Precision.HIGHEST)


def general_body(
    right_side,
    classes,
    noise_table,
    kernel_first,
    kernel_second,
    basis_first,
    basis_second,
    eigen_first,
    eigen_second,
):
    groups = lax.axis_size("mode")
    samples, planes, rows, _ = right_side.shape
    cols = eigen_second.shape[0]
    shape5 = (groups, cols, samples, planes, rows)
    kern_one = kernel_first.astype(F32)
    kern_two = kernel_second.astype(F32)
    base_one = basis_first.astype(F32)
    base_two = basis_second.astype(F32)
    noise = jnp.zeros(classes.shape, F32)
    for level in range(NCLASS):
        noise = noise + jnp.where(classes == level, noise_table[level], 0.0)
    noise = noise[None]
    mean_noise = jnp.mean(noise_table)
    col_weights = 1.0 / (eigen_second[:, None] * eigen_first[None, :] + mean_noise)
    col_weights = col_weights[:, None, None, :]

    def exchange(outgoing):
        return lax.all_to_all(outgoing, "mode", split_axis=0, concat_axis=0, tiled=True)

    def precond_apply(field):
        incoming = exchange(rows_to_send(base_two, field, groups))
        weighted = received_to_columns(base_one, incoming, shape5) * col_weights
        columns = along_columns(base_one, weighted)
        back = exchange(columns_to_send(base_one, weighted, groups, rows))
        kernel_back = exchange(columns_to_send(kern_one, columns, groups, rows))
        z_field = received_to_rows(base_two, back, shape5)
        image = (
            along_rows(kern_two, received_to_rows(base_two, kernel_back, shape5)) + noise * z_field
        )
        return (z_field, image)

    def inner(left, right):
        return lax.psum(jnp.sum(left * right), "mode")

    solution_field = jnp.zeros_like(right_side)
    residual = right_side
    z_field, image = precond_apply(residual)
    direction, along = (z_field, image)
    gamma = inner(residual, z_field)
    for step in range(ITERS):
        alpha = gamma / inner(direction, along)
        solution_field = solution_field + alpha * direction
        residual = residual - alpha * along
        if step + 1 < ITERS:
            z_field, image = precond_apply(residual)
            gamma_new = inner(residual, z_field)
            ratio = gamma_new / gamma
            direction = z_field + ratio * direction
            along = image + ratio * along
            gamma = gamma_new
    return (solution_field, residual)


def split(value):
    high = value.astype(BF16)
    low = (value - high.astype(F32)).astype(BF16)
    return high, low


def times_right(value, matrix, contract):
    high, low = split(value)
    dims = (((1,), (contract,)), ((), ()))
    both = jnp.concatenate([high, low], axis=0)
    result = lax.dot_general(both, matrix, dims, preferred_element_type=F32)
    return result[: value.shape[0]] + result[value.shape[0] :]


def times_left(matrix, value):
    high, low = split(value)
    dims = (((1,), (0,)), ((), ()))
    both = jnp.concatenate([high, low], axis=1)
    result = lax.dot_general(matrix, both, dims, preferred_element_type=F32)
    return result[:, : value.shape[1]] + result[:, value.shape[1] :]


def fold(value):
    total = jnp.sum(value, axis=0, keepdims=True)
    return functools.reduce(
        jnp.add, [total[:, at : at + 128] for at in range(0, total.shape[1], 128)]
    )


def params(dims, mebibytes):
    return pltpu.CompilerParams(
        dimension_semantics=("arbitrary",) * dims, vmem_limit_bytes=mebibytes * 1024 * 1024
    )


def noise_kernel(shifts, place_ref, table_ref, class_ref, *out_refs):
    planes = class_ref.shape[0]
    for by, out_ref in zip(shifts, out_refs):
        level = class_ref[(place_ref[2] + by) % planes]
        noise = jnp.full(level.shape, table_ref[0], F32)
        for index in range(1, NCLASS):
            noise = jnp.where(level == index, table_ref[index], noise)
        out_ref[...] = noise


def follow_kernel(value_ref, *refs):
    refs[-1][...] = value_ref[...]


def prepare_kernel(
    first_ref, second_ref, kernel_ref, eigen_ref, _, turned_ref, high_ref, low_ref, tall_ref
):
    turned_ref[...] = first_ref[...].T
    tall_ref[...] = jnp.broadcast_to(eigen_ref[...], tall_ref.shape[::-1]).T
    dims = (((1,), (0,)), ((), ()))
    product = lax.dot_general(
        kernel_ref[...], second_ref[...], dims, preferred_element_type=F32
    )
    high_ref[...], low_ref[...] = split(product)


def outgoing_kernel(right_ref, basis_ref, out_ref):
    samples, _, rows, width = right_ref.shape
    cores = out_ref.shape[2]
    half = width // cores
    field = right_ref[...].reshape(samples * rows, width)
    mapped = times_right(field, basis_ref[...], 0)
    for sample in range(samples):
        for core in range(cores):
            out_ref[0, sample, core] = mapped[
                sample * rows : (sample + 1) * rows, core * half : (core + 1) * half
            ]


def both_shares(place_ref, share):
    core = place_ref[0]
    mine = pl.ds(pl.multiple_of(core * share, share), share)
    theirs = pl.ds(pl.multiple_of((1 - core) * share, share), share)
    return mine, theirs


def split_rows(place_ref, value, scratch_ref, keep_ref, send_ref):
    core = place_ref[0]
    scratch_ref[...] = value.reshape(scratch_ref.shape)
    keep_ref[...] = scratch_ref[:, core]
    send_ref[...] = scratch_ref[:, 1 - core]


def store_sums(sum_ref, sums):
    rows = sum_ref.shape[0]
    sum_ref[...] = jnp.concatenate(sums + [jnp.zeros((rows - len(sums), 128), F32)], axis=0)


def first_column_kernel(
    place_ref,
    table_ref,
    field_hbm,
    turned_hbm,
    basis_hbm,
    tall_ref,
    *refs,
):
    wide_refs, refs, local = refs[:-11], refs[-11:-4], refs[-4:]
    spectral_ref, weight_ref, column_ref, keep_ref, send_ref, sum_ref, scratch_ref = refs
    field_ref, turned_ref, basis_ref, done = local
    pairs = ((field_hbm, field_ref), (turned_hbm, turned_ref), (basis_hbm, basis_ref))
    copies = [
        pltpu.make_async_copy(source, target, done.at[at])
        for at, (source, target) in enumerate(pairs)
    ]
    for copy in copies:
        copy.start()
    mean = functools.reduce(jnp.add, [table_ref[at] for at in range(NCLASS)]) * (1.0 / NCLASS)
    height, width = spectral_ref.shape
    planes = len(wide_refs)
    part = wide_refs[0].shape[1]
    for block in range(width // part):
        wanted = place_ref[0] * (width // part) + block
        wide = jnp.zeros((1, part), F32)
        for by, wide_ref in enumerate(wide_refs):
            here = (place_ref[2] + planes - by) % planes == wanted
            wide = jnp.where(here, wide_ref[...], wide)
        for at in range(0, part, 128):
            lanes = slice(block * part + at, block * part + at + 128)
            weight_ref[:, lanes] = 1.0 / (tall_ref[...] * wide[:, at : at + 128] + mean)
    copies[0].wait()
    copies[1].wait()
    spectral = times_left(turned_ref[...], field_ref[...].reshape(height, width))
    weighted = spectral * weight_ref[...]
    spectral_ref[...] = spectral
    store_sums(sum_ref, [fold(spectral * weighted)])
    copies[2].wait()
    column = times_left(basis_ref[...], weighted)
    column_ref[...] = column
    split_rows(place_ref, column, scratch_ref, keep_ref, send_ref)


def next_column_kernel(
    place_ref,
    held_ref,
    got_ref,
    before_ref,
    weight_ref,
    turned_ref,
    basis_ref,
    column_ref,
    keep_ref,
    send_ref,
    sum_ref,
    scratch_ref,
):
    core = place_ref[0]
    scratch_ref[:, core] = held_ref[...]
    scratch_ref[:, 1 - core] = got_ref[...]
    spectral = times_left(turned_ref[...], scratch_ref[...].reshape(column_ref.shape))
    weighted = spectral * weight_ref[...]
    store_sums(sum_ref, [fold(before_ref[...] * weighted), fold(spectral * weighted)])
    column = times_left(basis_ref[...], weighted)
    column_ref[...] = column
    split_rows(place_ref, column, scratch_ref, keep_ref, send_ref)


def column_image_kernel(place_ref, column_ref, kernel_ref, keep_ref, send_ref, scratch_ref):
    image = times_left(kernel_ref[...], column_ref[...])
    split_rows(place_ref, image, scratch_ref, keep_ref, send_ref)


def join_columns(place_ref, scratch_ref, keep_ref, got_ref):
    height, width = scratch_ref.shape
    mine, theirs = both_shares(place_ref, width // 2)
    scratch_ref[:, mine] = keep_ref[...].reshape(height, width // 2)
    scratch_ref[:, theirs] = got_ref[...].reshape(height, width // 2)
    return scratch_ref[...]


def row_kernel(place_ref, keep_ref, got_ref, basis_ref, z_ref, scratch_ref):
    field = join_columns(place_ref, scratch_ref, keep_ref, got_ref)
    z_ref[...] = times_right(field, basis_ref[...], 1).reshape(z_ref.shape)


def row_image(place_ref, keep_ref, got_ref, high_ref, low_ref, scratch_ref):
    field = join_columns(place_ref, scratch_ref, keep_ref, got_ref)
    high, low = split(field)
    dims = (((1,), (1,)), ((), ()))
    both = jnp.concatenate([high, low], axis=0)
    result = lax.dot_general(both, high_ref[...], dims, preferred_element_type=F32)
    small = lax.dot_general(high, low_ref[...], dims, preferred_element_type=F32)
    return result[: field.shape[0]] + (result[field.shape[0] :] + small)


def first_image_kernel(place_ref, keep_ref, got_ref, high_ref, low_ref, image_ref, scratch_ref):
    image = row_image(place_ref, keep_ref, got_ref, high_ref, low_ref, scratch_ref)
    image_ref[...] = image.reshape(image_ref.shape)


def noise_image_kernel(place_ref, part_ref, z_ref, basis_ref, *refs):
    noise_refs, (noise_ref, image_ref, send_ref) = refs[:-3], refs[-3:]
    planes = len(noise_refs) // 2
    samples = image_ref.shape[0] // planes
    for by in range(planes):
        row = (place_ref[2] + planes - by) % planes
        for at, part in enumerate((noise_refs[by], noise_refs[planes + by])):
            noise_ref[row * samples + (place_ref[1] + at) % samples] = part[...]
    image_ref[...] = part_ref[...] + noise_ref[...] * z_ref[...]
    half = send_ref.shape[2]
    _, theirs = both_shares(place_ref, half)
    image = image_ref[...].reshape(-1, basis_ref.shape[0])
    send_ref[...] = times_right(image, basis_ref[:, theirs], 0).reshape(send_ref.shape)


def keep_kernel(place_ref, image_ref, basis_ref, keep_ref):
    mine, _ = both_shares(place_ref, keep_ref.shape[2])
    image = image_ref[...].reshape(-1, basis_ref.shape[0])
    keep_ref[...] = times_right(image, basis_ref[:, mine], 0).reshape(keep_ref.shape)


def last_image_kernel(
    place_ref,
    keep_ref,
    got_ref,
    z_ref,
    noise_ref,
    high_ref,
    low_ref,
    one_ref,
    two_ref,
    image_ref,
    sum_ref,
    scratch_ref,
):
    image = row_image(place_ref, keep_ref, got_ref, high_ref, low_ref, scratch_ref)
    field = z_ref[...].reshape(image.shape)
    image = image + noise_ref[...].reshape(image.shape) * field
    image_ref[...] = image.reshape(image_ref.shape)
    total = jnp.concatenate(
        [one_ref[0:1], two_ref[0:2], fold(field * image), jnp.zeros((4, 128), F32)], axis=0
    )
    sum_ref[...] = jnp.broadcast_to(total[None], sum_ref.shape)


def combine_kernel(sum_ref, z_ref, image_ref, f_ref, f_image_ref, out_ref):
    total = jnp.sum(sum_ref[...], axis=0)
    total = jnp.sum(total, axis=1, keepdims=True)
    g00, g01, g11, h11 = (total[at : at + 1] for at in range(4))
    alpha = g00 / g01
    turn = alpha * g11 / g01
    gamma = alpha * alpha * g11 - g00
    curvature = alpha * alpha * h11 - turn * turn * g01
    step = gamma / curvature
    on_z = alpha + step * turn
    on_f = -(alpha * step)
    share = z_ref.shape[1]
    out_ref[:, :share, :] = on_z[None] * z_ref[...] + on_f[None] * f_ref[...]
    out_ref[:, share:, :] = on_z[None] * image_ref[...] + on_f[None] * f_image_ref[...]


def finish_kernel(got_ref, right_ref, solution_ref, residual_ref):
    samples = got_ref.shape[0]
    rows = got_ref.shape[1] // 2
    for sample in range(samples):
        solution_ref[sample, 0] = got_ref[sample, :rows, :]
        residual_ref[sample, 0] = right_ref[sample, 0] - got_ref[sample, rows:, :]


def paired_body(
    right_side,
    classes,
    noise_table,
    kernel_first,
    kernel_second,
    basis_first,
    basis_second,
    eigen_first,
    eigen_second,
):
    groups = lax.axis_size("mode")
    samples, planes, rows, width = right_side.shape
    height = groups * rows
    cores = 2
    half = width // cores
    blocks = groups // cores
    unit = cores * samples
    index = lax.axis_index("mode")
    core = index % cores
    sample = (index // cores) % samples
    plane = index // unit
    place = jnp.stack([core, sample, plane]).astype(jnp.int32)

    def shape_of(*shape):
        return jax.ShapeDtypeStruct(shape, F32)

    smem = pl.BlockSpec(memory_space=pltpu.SMEM)

    def full(*shape):
        return pl.BlockSpec(
            shape, lambda *at: (0,) * len(shape), pipeline_mode=pl.Buffered(1)
        )

    def whole_out(*shape):
        return pl.BlockSpec(shape, lambda *at: (0,) * len(shape))

    core_swap = [(at, at ^ 1) for at in range(groups)]
    sample_swap = [(at, at ^ cores) for at in range(groups)]

    def noise_of(shifts):
        return pl.pallas_call(
            functools.partial(noise_kernel, shifts),
            grid=(1,),
            in_specs=[smem, smem, full(planes, rows, width)],
            out_specs=[whole_out(rows, width)] * len(shifts),
            out_shape=[shape_of(rows, width)] * len(shifts),
            compiler_params=params(1, 56),
        )(place, noise_table, classes)

    def plane_shift(value, by):
        pairs = [(at, (at + by * unit) % groups) for at in range(groups)]
        return lax.ppermute(value, "mode", pairs)

    ahead = planes // 2
    others = [by for by in range(planes) if by != ahead]
    near = [None] * planes
    near[ahead] = plane_shift(noise_of([ahead])[0], ahead)
    rest = noise_of(others)
    for by, value in zip(others, rest):
        near[by] = plane_shift(value, by) if by else value
    far = [lax.ppermute(value, "mode", sample_swap) for value in near]
    noise = (*near, *far)

    outgoing = pl.pallas_call(
        outgoing_kernel,
        grid=(planes,),
        in_specs=[
            pl.BlockSpec((samples, 1, rows, width), lambda p: (0, p, 0, 0)),
            full(width, width),
        ],
        out_specs=pl.BlockSpec((1, samples, cores, rows, half), lambda p: (p, 0, 0, 0, 0)),
        out_shape=shape_of(planes, samples, cores, rows, half),
        compiler_params=params(1, 56),
        name="outgoing",
    )(right_side, basis_second)
    arrived = lax.all_to_all(
        outgoing.reshape(groups, rows, half), "mode", split_axis=0, concat_axis=0, tiled=True
    )

    eigen = eigen_second.reshape(1, -1)
    for reach in (1, cores):
        other = lax.ppermute(eigen, "mode", [(at, at ^ reach) for at in range(groups)])
        low = (index // reach) % 2 == 0
        eigen = jnp.where(
            low,
            jnp.concatenate([eigen, other], axis=1),
            jnp.concatenate([other, eigen], axis=1),
        )
    eigen = pl.pallas_call(
        follow_kernel,
        in_specs=[pl.BlockSpec(memory_space=pltpu.VMEM)]
        + [pl.BlockSpec(memory_space=pl.ANY)] * (planes - 1),
        out_specs=pl.BlockSpec(memory_space=pltpu.VMEM),
        out_shape=shape_of(*eigen.shape),
        compiler_params=pltpu.CompilerParams(vmem_limit_bytes=1024 * 1024),
        name="follow",
    )(eigen, *near[1:])
    shifted = [eigen] + [
        lax.ppermute(eigen, "mode", [(at, (at + by * unit) % groups) for at in range(groups)])
        for by in range(1, planes)
    ]
    bf16_square = jax.ShapeDtypeStruct((height, height), BF16)
    turned, high, low, tall_eigen = pl.pallas_call(
        prepare_kernel,
        grid=(1,),
        in_specs=[full(height, height), full(width, width), full(width, width), full(1, height)]
        + [pl.BlockSpec(memory_space=pl.ANY)],
        out_specs=[whole_out(height, height)] * 3 + [whole_out(height, 128)],
        out_shape=[bf16_square] * 3 + [shape_of(height, 128)],
        compiler_params=params(1, 24),
        name="prepare",
    )(basis_first, basis_second, kernel_second, eigen_first.reshape(1, -1), eigen)

    def swap(value):
        return lax.ppermute(value, "mode", core_swap)

    def call(kernel, inputs, shapes, scratch_shape, specs=None, more=(), mebibytes=12):
        return pl.pallas_call(
            kernel,
            grid=(1,),
            in_specs=specs or [smem] + [full(*value.shape) for value in inputs[1:]],
            out_specs=[whole_out(*shape) for shape in shapes],
            out_shape=[shape_of(*shape) for shape in shapes],
            scratch_shapes=[*([pltpu.VMEM(scratch_shape, F32)] if scratch_shape else []), *more],
            compiler_params=params(1, mebibytes),
        )(*inputs)

    tile = (height, half)
    piece = (blocks, rows, half)
    whole = (blocks, rows, width)
    by_rows = (blocks, cores, rows, half)
    flat = (blocks * rows, width)
    sums_shape = (8, 128)

    spectral, weights, column, keep, send, sum_one = call(
        first_column_kernel,
        (
            place,
            noise_table,
            pltpu.with_memory_space_constraint(arrived, pltpu.HBM),
            pltpu.with_memory_space_constraint(turned, pltpu.HBM),
            pltpu.with_memory_space_constraint(basis_first, pltpu.HBM),
            tall_eigen,
            *shifted,
        ),
        (tile, tile, tile, piece, piece, sums_shape),
        by_rows,
        [smem, smem]
        + [pl.BlockSpec(memory_space=pltpu.HBM)] * 3
        + [full(height, 128)]
        + [full(*value.shape) for value in shifted],
        [
            pltpu.VMEM((groups, rows, half), F32),
            pltpu.VMEM((height, height), BF16),
            pltpu.VMEM((height, height), BF16),
            pltpu.SemaphoreType.DMA((3,)),
        ],
        18,
    )
    got = swap(send)
    image_keep, image_send = call(
        column_image_kernel, (place, column, kernel_first), (piece, piece), by_rows
    )
    image_got = swap(image_send)
    (z_field,) = call(row_kernel, (place, keep, got, basis_second), (whole,), flat)
    (part,) = call(first_image_kernel, (place, image_keep, image_got, high, low), (whole,), flat)
    noise, image, back_send = call(
        noise_image_kernel,
        (place, part, z_field, basis_second, *noise),
        (whole, whole, piece),
        None,
    )
    (back_keep,) = call(keep_kernel, (place, image, basis_second), (piece,), None)
    back_got = swap(back_send)

    column, keep, send, sum_two = call(
        next_column_kernel,
        (place, back_keep, back_got, spectral, weights, turned, basis_first),
        (tile, piece, piece, sums_shape),
        by_rows,
    )
    got = swap(send)
    image_keep, image_send = call(
        column_image_kernel, (place, column, kernel_first), (piece, piece), by_rows
    )
    image_got = swap(image_send)
    (f_field,) = call(row_kernel, (place, keep, got, basis_second), (whole,), flat)
    f_image, sums = call(
        last_image_kernel,
        (
            place,
            image_keep,
            image_got,
            f_field,
            noise,
            high,
            low,
            sum_one,
            sum_two,
        ),
        (whole, (groups, 8, 128)),
        flat,
    )
    sums = lax.all_to_all(sums, "mode", split_axis=0, concat_axis=0, tiled=True)

    few = blocks // 4
    few_spec = pl.BlockSpec((few, rows, width), lambda i: (i, 0, 0))
    answer = pl.pallas_call(
        combine_kernel,
        grid=(4,),
        in_specs=[full(groups, 8, 128)] + [few_spec] * 4,
        out_specs=pl.BlockSpec((few, 2 * rows, width), lambda i: (i, 0, 0)),
        out_shape=shape_of(blocks, 2 * rows, width),
        compiler_params=params(1, 6),
        name="combine",
    )(sums, z_field, image, f_field, f_image)
    answer = lax.all_to_all(
        answer,
        "mode",
        split_axis=0,
        concat_axis=0,
        axis_index_groups=[list(range(at, groups, cores)) for at in range(cores)],
        tiled=True,
    )

    block = pl.BlockSpec((samples, 1, rows, width), lambda p: (0, p, 0, 0))
    return tuple(
        pl.pallas_call(
            finish_kernel,
            grid=(planes,),
            in_specs=[
                pl.BlockSpec((samples, 2 * rows, width), lambda p: (p, 0, 0)),
                block,
            ],
            out_specs=[block, block],
            out_shape=[shape_of(*right_side.shape)] * 2,
            compiler_params=params(1, 10),
            name="finish",
        )(answer, right_side)
    )


def body(right_side, classes, *rest):
    groups = lax.axis_size("mode")
    samples, planes, rows, width = right_side.shape
    paired = (
        groups == 2 * samples * planes
        and samples == 2
        and rows % 8 == 0
        and width % 512 == 0
        and planes % 2 == 0
    )
    chosen = paired_body if paired else general_body
    return chosen(right_side, classes, *rest)


def solution(mesh):
    in_specs = (
        P(None, "blocks", "mode", None),
        P("blocks", "mode", None),
        P(),
        P(),
        P(),
        P(),
        P(),
        P(),
        P("mode"),
    )
    out_specs = (P(None, "blocks", "mode", None), P(None, "blocks", "mode", None))
    return jax.shard_map(body, mesh=mesh, in_specs=in_specs, out_specs=out_specs, check_vma=False)
```

```python
import functools

import jax
import jax.numpy as jnp
from jax import lax
from jax.experimental import pallas as pl
from jax.experimental.pallas import tpu as pltpu
from jax.sharding import PartitionSpec as P


NCLASS = 8
ITERS = 2
F32 = jnp.float32
BF16 = jnp.bfloat16


def along_rows(matrix, field):
    return jnp.einsum("jk,sprk->sprj", matrix, field, precision=lax.Precision.HIGHEST)


def rows_to_send(matrix, field, groups):
    result = jnp.einsum("kj,sprk->jspr", matrix, field, precision=lax.Precision.HIGHEST)
    return result.reshape(groups, -1)


def received_to_columns(matrix, received, shape5):
    groups, _, _, _, rows = shape5
    block = received.reshape(shape5)
    reshaped = matrix.reshape(groups, rows, matrix.shape[1])
    return jnp.einsum("mri,mcspr->cspi", reshaped, block, precision=lax.Precision.HIGHEST)


def along_columns(matrix, columns):
    return jnp.einsum("ik,cspk->cspi", matrix, columns, precision=lax.Precision.HIGHEST)


def columns_to_send(matrix, columns, groups, rows):
    reshaped = matrix.reshape(groups, rows, matrix.shape[1])
    result = jnp.einsum("mrk,cspk->mcspr", reshaped, columns, precision=lax.Precision.HIGHEST)
    return result.reshape(groups, -1)


def received_to_rows(matrix, received, shape5):
    groups, cols, _, _, _ = shape5
    block = received.reshape(shape5)
    reshaped = matrix.reshape(matrix.shape[0], groups, cols)
    return jnp.einsum("jmc,mcspr->sprj", reshaped, block, precision=lax.Precision.HIGHEST)


def general_body(
    right_side,
    classes,
    noise_table,
    kernel_first,
    kernel_second,
    basis_first,
    basis_second,
    eigen_first,
    eigen_second,
):
    groups = lax.axis_size("mode")
    samples, planes, rows, _ = right_side.shape
    cols = eigen_second.shape[0]
    shape5 = (groups, cols, samples, planes, rows)
    kern_one = kernel_first.astype(F32)
    kern_two = kernel_second.astype(F32)
    base_one = basis_first.astype(F32)
    base_two = basis_second.astype(F32)
    noise = jnp.zeros(classes.shape, F32)
    for level in range(NCLASS):
        noise = noise + jnp.where(classes == level, noise_table[level], 0.0)
    noise = noise[None]
    mean_noise = jnp.mean(noise_table)
    col_weights = 1.0 / (eigen_second[:, None] * eigen_first[None, :] + mean_noise)
    col_weights = col_weights[:, None, None, :]

    def exchange(outgoing):
        return lax.all_to_all(outgoing, "mode", split_axis=0, concat_axis=0, tiled=True)

    def precond_apply(field):
        incoming = exchange(rows_to_send(base_two, field, groups))
        weighted = received_to_columns(base_one, incoming, shape5) * col_weights
        columns = along_columns(base_one, weighted)
        back = exchange(columns_to_send(base_one, weighted, groups, rows))
        kernel_back = exchange(columns_to_send(kern_one, columns, groups, rows))
        z_field = received_to_rows(base_two, back, shape5)
        image = (
            along_rows(kern_two, received_to_rows(base_two, kernel_back, shape5)) + noise * z_field
        )
        return (z_field, image)

    def inner(left, right):
        return lax.psum(jnp.sum(left * right), "mode")

    solution_field = jnp.zeros_like(right_side)
    residual = right_side
    z_field, image = precond_apply(residual)
    direction, along = (z_field, image)
    gamma = inner(residual, z_field)
    for step in range(ITERS):
        alpha = gamma / inner(direction, along)
        solution_field = solution_field + alpha * direction
        residual = residual - alpha * along
        if step + 1 < ITERS:
            z_field, image = precond_apply(residual)
            gamma_new = inner(residual, z_field)
            ratio = gamma_new / gamma
            direction = z_field + ratio * direction
            along = image + ratio * along
            gamma = gamma_new
    return (solution_field, residual)


def split(value):
    high = value.astype(BF16)
    low = (value - high.astype(F32)).astype(BF16)
    return high, low


def times_right(value, matrix, contract):
    high, low = split(value)
    dims = (((1,), (contract,)), ((), ()))
    both = jnp.concatenate([high, low], axis=0)
    result = lax.dot_general(both, matrix, dims, preferred_element_type=F32)
    return result[: value.shape[0]] + result[value.shape[0] :]


def times_left(matrix, value):
    high, low = split(value)
    dims = (((1,), (0,)), ((), ()))
    both = jnp.concatenate([high, low], axis=1)
    result = lax.dot_general(matrix, both, dims, preferred_element_type=F32)
    return result[:, : value.shape[1]] + result[:, value.shape[1] :]


def fold(value):
    total = jnp.sum(value, axis=0, keepdims=True)
    return functools.reduce(
        jnp.add, [total[:, at : at + 128] for at in range(0, total.shape[1], 128)]
    )


def params(dims, mebibytes):
    return pltpu.CompilerParams(
        dimension_semantics=("arbitrary",) * dims, vmem_limit_bytes=mebibytes * 1024 * 1024
    )


def noise_kernel(shifts, unit, table_ref, class_hbm, *refs):
    out_refs, (class_ref, done) = refs[:-2], refs[-2:]
    planes = class_hbm.shape[0]
    plane = lax.axis_index("mode") // unit
    copies = [
        pltpu.make_async_copy(class_hbm.at[(plane + by) % planes], class_ref.at[at], done.at[at])
        for at, by in enumerate(shifts)
    ]
    for copy in copies:
        copy.start()
    for at, copy in enumerate(copies):
        copy.wait()
        level = class_ref[at]
        noise = jnp.full(level.shape, table_ref[0], F32)
        for index in range(1, NCLASS):
            noise = jnp.where(level == index, table_ref[index], noise)
        out_refs[at][...] = noise


def follow_kernel(value_ref, *refs):
    refs[-1][...] = value_ref[...]


def prepare_kernel(
    first_ref, second_ref, kernel_ref, eigen_ref, _, turned_ref, high_ref, low_ref, tall_ref
):
    turned_ref[...] = first_ref[...].T
    tall_ref[...] = jnp.broadcast_to(eigen_ref[...], tall_ref.shape[::-1]).T
    dims = (((1,), (0,)), ((), ()))
    product = lax.dot_general(
        kernel_ref[...], second_ref[...], dims, preferred_element_type=F32
    )
    high_ref[...], low_ref[...] = split(product)


def outgoing_kernel(right_ref, basis_ref, out_ref):
    samples, _, rows, width = right_ref.shape
    cores = out_ref.shape[2]
    half = width // cores
    field = right_ref[...].reshape(samples * rows, width)
    mapped = times_right(field, basis_ref[...], 0)
    for sample in range(samples):
        for core in range(cores):
            out_ref[0, sample, core] = mapped[
                sample * rows : (sample + 1) * rows, core * half : (core + 1) * half
            ]


def both_shares(place_ref, share):
    core = place_ref[0]
    mine = pl.ds(pl.multiple_of(core * share, share), share)
    theirs = pl.ds(pl.multiple_of((1 - core) * share, share), share)
    return mine, theirs


def split_rows(place_ref, value, scratch_ref, keep_ref, send_ref):
    core = place_ref[0]
    scratch_ref[...] = value.reshape(scratch_ref.shape)
    keep_ref[...] = scratch_ref[:, core]
    send_ref[...] = scratch_ref[:, 1 - core]


def store_sums(sum_ref, sums):
    rows = sum_ref.shape[0]
    sum_ref[...] = jnp.concatenate(sums + [jnp.zeros((rows - len(sums), 128), F32)], axis=0)


def first_column_kernel(
    place_ref,
    table_ref,
    field_hbm,
    turned_hbm,
    basis_hbm,
    tall_ref,
    *refs,
):
    wide_refs, refs, local = refs[:-11], refs[-11:-4], refs[-4:]
    spectral_ref, weight_ref, column_ref, keep_ref, send_ref, sum_ref, scratch_ref = refs
    field_ref, turned_ref, basis_ref, done = local
    middle = turned_ref.shape[0] // 2
    upper, lower = pl.ds(0, middle), pl.ds(middle, middle)
    pairs = (
        (field_hbm, field_ref),
        (turned_hbm.at[upper], turned_ref.at[upper]),
        (turned_hbm.at[lower], turned_ref.at[lower]),
        (basis_hbm, basis_ref),
    )
    copies = [
        pltpu.make_async_copy(source, target, done.at[at])
        for at, (source, target) in enumerate(pairs)
    ]
    for copy in copies:
        copy.start()
    mean = functools.reduce(jnp.add, [table_ref[at] for at in range(NCLASS)]) * (1.0 / NCLASS)
    height, width = spectral_ref.shape
    planes = len(wide_refs)
    part = wide_refs[0].shape[1]
    for block in range(width // part):
        wanted = place_ref[0] * (width // part) + block
        wide = jnp.zeros((1, part), F32)
        for by, wide_ref in enumerate(wide_refs):
            here = (place_ref[2] + planes - by) % planes == wanted
            wide = jnp.where(here, wide_ref[...], wide)
        for at in range(0, part, 128):
            lanes = slice(block * part + at, block * part + at + 128)
            weight_ref[:, lanes] = 1.0 / (tall_ref[...] * wide[:, at : at + 128] + mean)
    copies[0].wait()
    field = field_ref[...].reshape(height, width)
    copies[1].wait()
    above = times_left(turned_ref[:middle], field)
    copies[2].wait()
    spectral = jnp.concatenate([above, times_left(turned_ref[middle:], field)], axis=0)
    weighted = spectral * weight_ref[...]
    spectral_ref[...] = spectral
    store_sums(sum_ref, [fold(spectral * weighted)])
    copies[3].wait()
    column = times_left(basis_ref[...], weighted)
    column_ref[...] = column
    split_rows(place_ref, column, scratch_ref, keep_ref, send_ref)


def next_column_kernel(
    place_ref,
    held_ref,
    got_ref,
    before_ref,
    weight_ref,
    turned_ref,
    basis_ref,
    column_ref,
    keep_ref,
    send_ref,
    sum_ref,
    scratch_ref,
):
    core = place_ref[0]
    scratch_ref[:, core] = held_ref[...]
    scratch_ref[:, 1 - core] = got_ref[...]
    spectral = times_left(turned_ref[...], scratch_ref[...].reshape(column_ref.shape))
    weighted = spectral * weight_ref[...]
    store_sums(sum_ref, [fold(before_ref[...] * weighted), fold(spectral * weighted)])
    column = times_left(basis_ref[...], weighted)
    column_ref[...] = column
    split_rows(place_ref, column, scratch_ref, keep_ref, send_ref)


def column_image_kernel(place_ref, column_ref, kernel_ref, keep_ref, send_ref, scratch_ref):
    image = times_left(kernel_ref[...], column_ref[...])
    split_rows(place_ref, image, scratch_ref, keep_ref, send_ref)


def join_columns(place_ref, scratch_ref, keep_ref, got_ref):
    height, width = scratch_ref.shape
    mine, theirs = both_shares(place_ref, width // 2)
    scratch_ref[:, mine] = keep_ref[...].reshape(height, width // 2)
    scratch_ref[:, theirs] = got_ref[...].reshape(height, width // 2)
    return scratch_ref[...]


def row_kernel(place_ref, keep_ref, got_ref, basis_ref, z_ref, scratch_ref):
    field = join_columns(place_ref, scratch_ref, keep_ref, got_ref)
    z_ref[...] = times_right(field, basis_ref[...], 1).reshape(z_ref.shape)


def row_image(place_ref, keep_ref, got_ref, high_ref, low_ref, scratch_ref):
    field = join_columns(place_ref, scratch_ref, keep_ref, got_ref)
    high, low = split(field)
    dims = (((1,), (1,)), ((), ()))
    both = jnp.concatenate([high, low], axis=0)
    result = lax.dot_general(both, high_ref[...], dims, preferred_element_type=F32)
    small = lax.dot_general(high, low_ref[...], dims, preferred_element_type=F32)
    return result[: field.shape[0]] + (result[field.shape[0] :] + small)


def first_image_kernel(place_ref, keep_ref, got_ref, high_ref, low_ref, z_ref, *refs):
    parts, (image_ref, noise_ref, scratch_ref, done) = refs[:-4], refs[-4:]
    planes = len(parts) // 2
    samples = image_ref.shape[0] // planes
    copies = []
    for by in range(planes):
        row = (place_ref[2] + planes - by) % planes
        for at, part in enumerate((parts[by], parts[planes + by])):
            block = row * samples + (place_ref[1] + at) % samples
            here = done.at[2 * by + at]
            copies.append(pltpu.make_async_copy(part, noise_ref.at[block], here))
    for copy in copies:
        copy.start()
    image = row_image(place_ref, keep_ref, got_ref, high_ref, low_ref, scratch_ref)
    for copy in copies:
        copy.wait()
    image_ref[...] = image.reshape(image_ref.shape) + noise_ref[...] * z_ref[...]


def return_kernel(whose, place_ref, image_ref, basis_ref, out_ref):
    lanes = both_shares(place_ref, out_ref.shape[2])[whose]
    image = image_ref[...].reshape(-1, basis_ref.shape[0])
    out_ref[...] = times_right(image, basis_ref[:, lanes], 0).reshape(out_ref.shape)


def last_image_kernel(
    place_ref,
    keep_ref,
    got_ref,
    z_ref,
    noise_ref,
    high_ref,
    low_ref,
    one_ref,
    two_ref,
    image_ref,
    sum_ref,
    scratch_ref,
):
    image = row_image(place_ref, keep_ref, got_ref, high_ref, low_ref, scratch_ref)
    field = z_ref[...].reshape(image.shape)
    image = image + noise_ref[...].reshape(image.shape) * field
    image_ref[...] = image.reshape(image_ref.shape)
    total = jnp.concatenate(
        [one_ref[0:1], two_ref[0:2], fold(field * image), jnp.zeros((4, 128), F32)], axis=0
    )
    sum_ref[...] = jnp.broadcast_to(total[None], sum_ref.shape)


def combine_kernel(sum_ref, z_ref, image_ref, f_ref, f_image_ref, out_ref):
    total = jnp.sum(sum_ref[...], axis=0)
    total = jnp.sum(total, axis=1, keepdims=True)
    g00, g01, g11, h11 = (total[at : at + 1] for at in range(4))
    alpha = g00 / g01
    turn = alpha * g11 / g01
    gamma = alpha * alpha * g11 - g00
    curvature = alpha * alpha * h11 - turn * turn * g01
    step = gamma / curvature
    on_z = alpha + step * turn
    on_f = -(alpha * step)
    share = z_ref.shape[1]
    out_ref[:, :share, :] = on_z[None] * z_ref[...] + on_f[None] * f_ref[...]
    out_ref[:, share:, :] = on_z[None] * image_ref[...] + on_f[None] * f_image_ref[...]


def finish_kernel(got_ref, right_ref, solution_ref, residual_ref):
    samples = got_ref.shape[0]
    rows = got_ref.shape[1] // 2
    for sample in range(samples):
        solution_ref[sample, 0] = got_ref[sample, :rows, :]
        residual_ref[sample, 0] = right_ref[sample, 0] - got_ref[sample, rows:, :]


def paired_body(
    right_side,
    classes,
    noise_table,
    kernel_first,
    kernel_second,
    basis_first,
    basis_second,
    eigen_first,
    eigen_second,
):
    groups = lax.axis_size("mode")
    samples, planes, rows, width = right_side.shape
    height = groups * rows
    cores = 2
    half = width // cores
    blocks = groups // cores
    unit = cores * samples
    index = lax.axis_index("mode")
    core = index % cores
    sample = (index // cores) % samples
    plane = index // unit
    place = jnp.stack([core, sample, plane]).astype(jnp.int32)

    def shape_of(*shape):
        return jax.ShapeDtypeStruct(shape, F32)

    smem = pl.BlockSpec(memory_space=pltpu.SMEM)

    def full(*shape):
        return pl.BlockSpec(
            shape, lambda *at: (0,) * len(shape), pipeline_mode=pl.Buffered(1)
        )

    def whole_out(*shape):
        return pl.BlockSpec(shape, lambda *at: (0,) * len(shape))

    core_swap = [(at, at ^ 1) for at in range(groups)]
    sample_swap = [(at, at ^ cores) for at in range(groups)]

    def in_hbm(value):
        return pltpu.with_memory_space_constraint(value, pltpu.HBM)

    def noise_of(shifts):
        return pl.pallas_call(
            functools.partial(noise_kernel, shifts, unit),
            grid=(1,),
            in_specs=[smem, pl.BlockSpec(memory_space=pltpu.HBM)],
            out_specs=[whole_out(rows, width)] * len(shifts),
            out_shape=[shape_of(rows, width)] * len(shifts),
            scratch_shapes=[
                pltpu.VMEM((len(shifts), rows, width), jnp.int32),
                pltpu.SemaphoreType.DMA((len(shifts),)),
            ],
            compiler_params=params(1, 56),
        )(noise_table, in_hbm(classes))

    def plane_shift(value, by):
        pairs = [(at, (at + by * unit) % groups) for at in range(groups)]
        return lax.ppermute(value, "mode", pairs)

    ahead = planes // 2
    others = [by for by in range(planes) if by != ahead]
    near = [None] * planes
    near[ahead] = plane_shift(noise_of([ahead])[0], ahead)
    rest = noise_of(others)
    for by, value in zip(others, rest):
        near[by] = plane_shift(value, by) if by else value
    far = [lax.ppermute(value, "mode", sample_swap) for value in near]
    noise = (*near, *far)

    outgoing = pl.pallas_call(
        outgoing_kernel,
        grid=(planes,),
        in_specs=[
            pl.BlockSpec((samples, 1, rows, width), lambda p: (0, p, 0, 0)),
            full(width, width),
        ],
        out_specs=pl.BlockSpec((1, samples, cores, rows, half), lambda p: (p, 0, 0, 0, 0)),
        out_shape=shape_of(planes, samples, cores, rows, half),
        compiler_params=params(1, 56),
        name="outgoing",
    )(right_side, basis_second)
    arrived = lax.all_to_all(
        outgoing.reshape(groups, rows, half), "mode", split_axis=0, concat_axis=0, tiled=True
    )

    eigen = eigen_second.reshape(1, -1)
    for reach in (1, cores):
        other = lax.ppermute(eigen, "mode", [(at, at ^ reach) for at in range(groups)])
        low = (index // reach) % 2 == 0
        eigen = jnp.where(
            low,
            jnp.concatenate([eigen, other], axis=1),
            jnp.concatenate([other, eigen], axis=1),
        )
    eigen = pl.pallas_call(
        follow_kernel,
        in_specs=[pl.BlockSpec(memory_space=pltpu.VMEM)]
        + [pl.BlockSpec(memory_space=pl.ANY)] * (planes - 1),
        out_specs=pl.BlockSpec(memory_space=pltpu.VMEM),
        out_shape=shape_of(*eigen.shape),
        compiler_params=pltpu.CompilerParams(vmem_limit_bytes=1024 * 1024),
        name="follow",
    )(eigen, *near[1:])
    shifted = [eigen] + [
        lax.ppermute(eigen, "mode", [(at, (at + by * unit) % groups) for at in range(groups)])
        for by in range(1, planes)
    ]
    bf16_square = jax.ShapeDtypeStruct((height, height), BF16)
    turned, high, low, tall_eigen = pl.pallas_call(
        prepare_kernel,
        grid=(1,),
        in_specs=[full(height, height), full(width, width), full(width, width), full(1, height)]
        + [pl.BlockSpec(memory_space=pl.ANY)],
        out_specs=[whole_out(height, height)] * 3 + [whole_out(height, 128)],
        out_shape=[bf16_square] * 3 + [shape_of(height, 128)],
        compiler_params=params(1, 24),
        name="prepare",
    )(basis_first, basis_second, kernel_second, eigen_first.reshape(1, -1), eigen)

    def swap(value):
        return lax.ppermute(value, "mode", core_swap)

    def call(kernel, inputs, shapes, scratch_shape, specs=None, more=(), mebibytes=12):
        return pl.pallas_call(
            kernel,
            grid=(1,),
            in_specs=specs or [smem] + [full(*value.shape) for value in inputs[1:]],
            out_specs=[whole_out(*shape) for shape in shapes],
            out_shape=[shape_of(*shape) for shape in shapes],
            scratch_shapes=[*([pltpu.VMEM(scratch_shape, F32)] if scratch_shape else []), *more],
            compiler_params=params(1, mebibytes),
        )(*inputs)

    tile = (height, half)
    piece = (blocks, rows, half)
    whole = (blocks, rows, width)
    by_rows = (blocks, cores, rows, half)
    flat = (blocks * rows, width)
    sums_shape = (8, 128)

    spectral, weights, column, keep, send, sum_one = call(
        first_column_kernel,
        (
            place,
            noise_table,
            in_hbm(arrived),
            in_hbm(turned),
            in_hbm(basis_first),
            tall_eigen,
            *shifted,
        ),
        (tile, tile, tile, piece, piece, sums_shape),
        by_rows,
        [smem, smem]
        + [pl.BlockSpec(memory_space=pltpu.HBM)] * 3
        + [full(height, 128)]
        + [full(*value.shape) for value in shifted],
        [
            pltpu.VMEM((groups, rows, half), F32),
            pltpu.VMEM((height, height), BF16),
            pltpu.VMEM((height, height), BF16),
            pltpu.SemaphoreType.DMA((4,)),
        ],
        18,
    )
    got = swap(send)
    image_keep, image_send = call(
        column_image_kernel, (place, column, kernel_first), (piece, piece), by_rows
    )
    image_got = swap(image_send)
    (z_field,) = call(row_kernel, (place, keep, got, basis_second), (whole,), flat)
    inputs = (place, image_keep, image_got, high, low, z_field)
    image, noise = call(
        first_image_kernel,
        (*inputs, *(in_hbm(value) for value in noise)),
        (whole, whole),
        flat,
        [smem]
        + [full(*value.shape) for value in inputs[1:]]
        + [pl.BlockSpec(memory_space=pltpu.HBM)] * len(noise),
        [pltpu.SemaphoreType.DMA((len(noise),))],
    )

    def give_back(whose):
        kernel = functools.partial(return_kernel, whose)
        return call(kernel, (place, image, basis_second), (piece,), None)[0]

    back_send = give_back(1)
    back_keep = give_back(0)
    back_got = swap(back_send)

    column, keep, send, sum_two = call(
        next_column_kernel,
        (place, back_keep, back_got, spectral, weights, turned, basis_first),
        (tile, piece, piece, sums_shape),
        by_rows,
    )
    got = swap(send)
    image_keep, image_send = call(
        column_image_kernel, (place, column, kernel_first), (piece, piece), by_rows
    )
    image_got = swap(image_send)
    (f_field,) = call(row_kernel, (place, keep, got, basis_second), (whole,), flat)
    f_image, sums = call(
        last_image_kernel,
        (
            place,
            image_keep,
            image_got,
            f_field,
            noise,
            high,
            low,
            sum_one,
            sum_two,
        ),
        (whole, (groups, 8, 128)),
        flat,
    )
    sums = lax.all_to_all(sums, "mode", split_axis=0, concat_axis=0, tiled=True)

    few = blocks // 4
    few_spec = pl.BlockSpec((few, rows, width), lambda i: (i, 0, 0))
    answer = pl.pallas_call(
        combine_kernel,
        grid=(4,),
        in_specs=[full(groups, 8, 128)] + [few_spec] * 4,
        out_specs=pl.BlockSpec((few, 2 * rows, width), lambda i: (i, 0, 0)),
        out_shape=shape_of(blocks, 2 * rows, width),
        compiler_params=params(1, 6),
        name="combine",
    )(sums, z_field, image, f_field, f_image)
    answer = lax.all_to_all(
        answer,
        "mode",
        split_axis=0,
        concat_axis=0,
        axis_index_groups=[list(range(at, groups, cores)) for at in range(cores)],
        tiled=True,
    )

    block = pl.BlockSpec((samples, 1, rows, width), lambda p: (0, p, 0, 0))
    return tuple(
        pl.pallas_call(
            finish_kernel,
            grid=(planes,),
            in_specs=[
                pl.BlockSpec((samples, 2 * rows, width), lambda p: (p, 0, 0)),
                block,
            ],
            out_specs=[block, block],
            out_shape=[shape_of(*right_side.shape)] * 2,
            compiler_params=params(1, 10),
            name="finish",
        )(answer, right_side)
    )


def body(right_side, classes, *rest):
    groups = lax.axis_size("mode")
    samples, planes, rows, width = right_side.shape
    paired = (
        groups == 2 * samples * planes
        and samples == 2
        and rows % 8 == 0
        and width % 512 == 0
        and planes % 2 == 0
    )
    chosen = paired_body if paired else general_body
    return chosen(right_side, classes, *rest)


def solution(mesh):
    in_specs = (
        P(None, "blocks", "mode", None),
        P("blocks", "mode", None),
        P(),
        P(),
        P(),
        P(),
        P(),
        P(),
        P("mode"),
    )
    out_specs = (P(None, "blocks", "mode", None), P(None, "blocks", "mode", None))
    return jax.shard_map(body, mesh=mesh, in_specs=in_specs, out_specs=out_specs, check_vma=False)
```

```python
import functools

import jax
import jax.numpy as jnp
from jax import lax
from jax.experimental import pallas as pl
from jax.experimental.pallas import tpu as pltpu
from jax.sharding import PartitionSpec as P


NCLASS = 8
ITERS = 2
F32 = jnp.float32
BF16 = jnp.bfloat16


def along_rows(matrix, field):
    return jnp.einsum("jk,sprk->sprj", matrix, field, precision=lax.Precision.HIGHEST)


def rows_to_send(matrix, field, groups):
    result = jnp.einsum("kj,sprk->jspr", matrix, field, precision=lax.Precision.HIGHEST)
    return result.reshape(groups, -1)


def received_to_columns(matrix, received, shape5):
    groups, _, _, _, rows = shape5
    block = received.reshape(shape5)
    reshaped = matrix.reshape(groups, rows, matrix.shape[1])
    return jnp.einsum("mri,mcspr->cspi", reshaped, block, precision=lax.Precision.HIGHEST)


def along_columns(matrix, columns):
    return jnp.einsum("ik,cspk->cspi", matrix, columns, precision=lax.Precision.HIGHEST)


def columns_to_send(matrix, columns, groups, rows):
    reshaped = matrix.reshape(groups, rows, matrix.shape[1])
    result = jnp.einsum("mrk,cspk->mcspr", reshaped, columns, precision=lax.Precision.HIGHEST)
    return result.reshape(groups, -1)


def received_to_rows(matrix, received, shape5):
    groups, cols, _, _, _ = shape5
    block = received.reshape(shape5)
    reshaped = matrix.reshape(matrix.shape[0], groups, cols)
    return jnp.einsum("jmc,mcspr->sprj", reshaped, block, precision=lax.Precision.HIGHEST)


def general_body(
    right_side,
    classes,
    noise_table,
    kernel_first,
    kernel_second,
    basis_first,
    basis_second,
    eigen_first,
    eigen_second,
):
    groups = lax.axis_size("mode")
    samples, planes, rows, _ = right_side.shape
    cols = eigen_second.shape[0]
    shape5 = (groups, cols, samples, planes, rows)
    kern_one = kernel_first.astype(F32)
    kern_two = kernel_second.astype(F32)
    base_one = basis_first.astype(F32)
    base_two = basis_second.astype(F32)
    noise = jnp.zeros(classes.shape, F32)
    for level in range(NCLASS):
        noise = noise + jnp.where(classes == level, noise_table[level], 0.0)
    noise = noise[None]
    mean_noise = jnp.mean(noise_table)
    col_weights = 1.0 / (eigen_second[:, None] * eigen_first[None, :] + mean_noise)
    col_weights = col_weights[:, None, None, :]

    def exchange(outgoing):
        return lax.all_to_all(outgoing, "mode", split_axis=0, concat_axis=0, tiled=True)

    def precond_apply(field):
        incoming = exchange(rows_to_send(base_two, field, groups))
        weighted = received_to_columns(base_one, incoming, shape5) * col_weights
        columns = along_columns(base_one, weighted)
        back = exchange(columns_to_send(base_one, weighted, groups, rows))
        kernel_back = exchange(columns_to_send(kern_one, columns, groups, rows))
        z_field = received_to_rows(base_two, back, shape5)
        image = (
            along_rows(kern_two, received_to_rows(base_two, kernel_back, shape5)) + noise * z_field
        )
        return (z_field, image)

    def inner(left, right):
        return lax.psum(jnp.sum(left * right), "mode")

    solution_field = jnp.zeros_like(right_side)
    residual = right_side
    z_field, image = precond_apply(residual)
    direction, along = (z_field, image)
    gamma = inner(residual, z_field)
    for step in range(ITERS):
        alpha = gamma / inner(direction, along)
        solution_field = solution_field + alpha * direction
        residual = residual - alpha * along
        if step + 1 < ITERS:
            z_field, image = precond_apply(residual)
            gamma_new = inner(residual, z_field)
            ratio = gamma_new / gamma
            direction = z_field + ratio * direction
            along = image + ratio * along
            gamma = gamma_new
    return (solution_field, residual)


def split(value):
    high = value.astype(BF16)
    low = (value - high.astype(F32)).astype(BF16)
    return high, low


def times_right(value, matrix, contract):
    high, low = split(value)
    dims = (((1,), (contract,)), ((), ()))
    both = jnp.concatenate([high, low], axis=0)
    result = lax.dot_general(both, matrix, dims, preferred_element_type=F32)
    return result[: value.shape[0]] + result[value.shape[0] :]


def times_left(matrix, value):
    high, low = split(value)
    dims = (((1,), (0,)), ((), ()))
    both = jnp.concatenate([high, low], axis=1)
    result = lax.dot_general(matrix, both, dims, preferred_element_type=F32)
    return result[:, : value.shape[1]] + result[:, value.shape[1] :]


def fold(value):
    total = jnp.sum(value, axis=0, keepdims=True)
    return functools.reduce(
        jnp.add, [total[:, at : at + 128] for at in range(0, total.shape[1], 128)]
    )


def params(dims, mebibytes):
    return pltpu.CompilerParams(
        dimension_semantics=("arbitrary",) * dims, vmem_limit_bytes=mebibytes * 1024 * 1024
    )


def noise_kernel(shifts, unit, table_ref, class_hbm, *refs):
    out_refs, (class_ref, done) = refs[:-2], refs[-2:]
    planes = class_hbm.shape[0]
    plane = lax.axis_index("mode") // unit
    copies = [
        pltpu.make_async_copy(class_hbm.at[(plane + by) % planes], class_ref.at[at], done.at[at])
        for at, by in enumerate(shifts)
    ]
    for copy in copies:
        copy.start()
    for at, copy in enumerate(copies):
        copy.wait()
        level = class_ref[at]
        noise = jnp.full(level.shape, table_ref[0], F32)
        for index in range(1, NCLASS):
            noise = jnp.where(level == index, table_ref[index], noise)
        out_refs[at][...] = noise


def follow_kernel(value_ref, *refs):
    refs[-1][...] = value_ref[...]


def prepare_kernel(
    first_ref, second_ref, kernel_ref, eigen_ref, _, turned_ref, high_ref, low_ref, tall_ref
):
    turned_ref[...] = first_ref[...].T
    tall_ref[...] = jnp.broadcast_to(eigen_ref[...], tall_ref.shape[::-1]).T
    dims = (((1,), (0,)), ((), ()))
    product = lax.dot_general(
        kernel_ref[...], second_ref[...], dims, preferred_element_type=F32
    )
    high_ref[...], low_ref[...] = split(product)


def outgoing_kernel(right_ref, basis_ref, out_ref):
    samples, _, rows, width = right_ref.shape
    cores = out_ref.shape[2]
    half = width // cores
    field = right_ref[...].reshape(samples * rows, width)
    mapped = times_right(field, basis_ref[...], 0)
    for sample in range(samples):
        for core in range(cores):
            out_ref[0, sample, core] = mapped[
                sample * rows : (sample + 1) * rows, core * half : (core + 1) * half
            ]


def both_shares(place_ref, share):
    core = place_ref[0]
    mine = pl.ds(pl.multiple_of(core * share, share), share)
    theirs = pl.ds(pl.multiple_of((1 - core) * share, share), share)
    return mine, theirs


def split_rows(place_ref, value, scratch_ref, keep_ref, send_ref):
    core = place_ref[0]
    scratch_ref[...] = value.reshape(scratch_ref.shape)
    keep_ref[...] = scratch_ref[:, core]
    send_ref[...] = scratch_ref[:, 1 - core]


def store_sums(sum_ref, sums):
    rows = sum_ref.shape[0]
    sum_ref[...] = jnp.concatenate(sums + [jnp.zeros((rows - len(sums), 128), F32)], axis=0)


def first_column_kernel(
    place_ref,
    table_ref,
    field_hbm,
    turned_hbm,
    basis_hbm,
    tall_ref,
    *refs,
):
    wide_refs, refs, local = refs[:-11], refs[-11:-4], refs[-4:]
    start_ref, weight_ref, column_ref, keep_ref, send_ref, sum_ref, scratch_ref = refs
    field_ref, turned_ref, basis_ref, done = local
    middle = turned_ref.shape[0] // 2
    upper, lower = pl.ds(0, middle), pl.ds(middle, middle)
    pairs = (
        (field_hbm, field_ref),
        (turned_hbm.at[upper], turned_ref.at[upper]),
        (turned_hbm.at[lower], turned_ref.at[lower]),
        (basis_hbm, basis_ref),
    )
    copies = [
        pltpu.make_async_copy(source, target, done.at[at])
        for at, (source, target) in enumerate(pairs)
    ]
    for copy in copies:
        copy.start()
    mean = functools.reduce(jnp.add, [table_ref[at] for at in range(NCLASS)]) * (1.0 / NCLASS)
    height, width = start_ref.shape
    planes = len(wide_refs)
    part = wide_refs[0].shape[1]
    for block in range(width // part):
        wanted = place_ref[0] * (width // part) + block
        wide = jnp.zeros((1, part), F32)
        for by, wide_ref in enumerate(wide_refs):
            here = (place_ref[2] + planes - by) % planes == wanted
            wide = jnp.where(here, wide_ref[...], wide)
        for at in range(0, part, 128):
            lanes = slice(block * part + at, block * part + at + 128)
            weight_ref[:, lanes] = 1.0 / (tall_ref[...] * wide[:, at : at + 128] + mean)
    copies[0].wait()
    field = field_ref[...].reshape(height, width)
    copies[1].wait()
    above = times_left(turned_ref[:middle], field)
    copies[2].wait()
    spectral = jnp.concatenate([above, times_left(turned_ref[middle:], field)], axis=0)
    weighted = spectral * weight_ref[...]
    start_ref[...] = field
    store_sums(sum_ref, [fold(spectral * weighted)])
    copies[3].wait()
    column = times_left(basis_ref[...], weighted)
    column_ref[...] = column
    split_rows(place_ref, column, scratch_ref, keep_ref, send_ref)


def next_column_kernel(
    place_ref,
    held_ref,
    got_ref,
    start_ref,
    weight_ref,
    turned_ref,
    basis_ref,
    own_ref,
    other_ref,
    column_ref,
    keep_ref,
    send_ref,
    sum_ref,
    scratch_ref,
):
    core = place_ref[0]
    scratch_ref[:, core] = held_ref[...]
    scratch_ref[:, 1 - core] = got_ref[...]
    total = jnp.sum(own_ref[...] + other_ref[...], axis=1, keepdims=True)
    gamma, curvature = total[0:1], total[1:2]
    proper = (gamma > 0) & (curvature > 0)
    step = jnp.where(proper, gamma / jnp.where(proper, curvature, 1.0), 1.0)
    field = start_ref[...] - step * scratch_ref[...].reshape(start_ref.shape)
    spectral = times_left(turned_ref[...], field)
    weighted = spectral * weight_ref[...]
    store_sums(sum_ref, [fold(spectral * weighted), jnp.broadcast_to(step, (1, 128))])
    column = times_left(basis_ref[...], weighted)
    column_ref[...] = column
    split_rows(place_ref, column, scratch_ref, keep_ref, send_ref)


def column_image_kernel(place_ref, column_ref, kernel_ref, keep_ref, send_ref, scratch_ref):
    image = times_left(kernel_ref[...], column_ref[...])
    split_rows(place_ref, image, scratch_ref, keep_ref, send_ref)


def join_columns(place_ref, scratch_ref, keep_ref, got_ref):
    height, width = scratch_ref.shape
    mine, theirs = both_shares(place_ref, width // 2)
    scratch_ref[:, mine] = keep_ref[...].reshape(height, width // 2)
    scratch_ref[:, theirs] = got_ref[...].reshape(height, width // 2)
    return scratch_ref[...]


def row_kernel(place_ref, keep_ref, got_ref, basis_ref, z_ref, scratch_ref):
    field = join_columns(place_ref, scratch_ref, keep_ref, got_ref)
    z_ref[...] = times_right(field, basis_ref[...], 1).reshape(z_ref.shape)


def row_image(place_ref, keep_ref, got_ref, high_ref, low_ref, scratch_ref):
    field = join_columns(place_ref, scratch_ref, keep_ref, got_ref)
    high, low = split(field)
    dims = (((1,), (1,)), ((), ()))
    both = jnp.concatenate([high, low], axis=0)
    result = lax.dot_general(both, high_ref[...], dims, preferred_element_type=F32)
    small = lax.dot_general(high, low_ref[...], dims, preferred_element_type=F32)
    return result[: field.shape[0]] + (result[field.shape[0] :] + small)


def first_row_kernel(place_ref, keep_ref, got_ref, basis_ref, *refs):
    parts, (z_ref, noise_ref, scratch_ref, done) = refs[:-4], refs[-4:]
    planes = len(parts) // 2
    samples = z_ref.shape[0] // planes
    copies = []
    for by in range(planes):
        row = (place_ref[2] + planes - by) % planes
        for at, part in enumerate((parts[by], parts[planes + by])):
            block = row * samples + (place_ref[1] + at) % samples
            here = done.at[2 * by + at]
            copies.append(pltpu.make_async_copy(part, noise_ref.at[block], here))
    for copy in copies:
        copy.start()
    row_kernel(place_ref, keep_ref, got_ref, basis_ref, z_ref, scratch_ref)
    for copy in copies:
        copy.wait()


def full_image(place_ref, keep_ref, got_ref, z_ref, noise_ref, high_ref, low_ref, image_ref, scratch_ref):
    image = row_image(place_ref, keep_ref, got_ref, high_ref, low_ref, scratch_ref)
    field = z_ref[...].reshape(image.shape)
    image = image + noise_ref[...].reshape(image.shape) * field
    image_ref[...] = image.reshape(image_ref.shape)
    return fold(field * image)


def first_image_kernel(
    place_ref,
    keep_ref,
    got_ref,
    z_ref,
    noise_ref,
    high_ref,
    low_ref,
    one_ref,
    image_ref,
    sum_ref,
    scratch_ref,
):
    refs = (place_ref, keep_ref, got_ref, z_ref, noise_ref, high_ref, low_ref)
    store_sums(sum_ref, [one_ref[0:1], full_image(*refs, image_ref, scratch_ref)])


def return_kernel(whose, place_ref, image_ref, basis_ref, out_ref):
    lanes = both_shares(place_ref, out_ref.shape[2])[whose]
    image = image_ref[...].reshape(-1, basis_ref.shape[0])
    out_ref[...] = times_right(image, basis_ref[:, lanes], 0).reshape(out_ref.shape)


def last_image_kernel(
    place_ref,
    keep_ref,
    got_ref,
    z_ref,
    noise_ref,
    high_ref,
    low_ref,
    one_ref,
    two_ref,
    image_ref,
    sum_ref,
    scratch_ref,
):
    refs = (place_ref, keep_ref, got_ref, z_ref, noise_ref, high_ref, low_ref)
    last = full_image(*refs, image_ref, scratch_ref)
    rows = [one_ref[0:2], two_ref[0:1], last, two_ref[1:2], jnp.zeros((3, 128), F32)]
    sum_ref[...] = jnp.broadcast_to(jnp.concatenate(rows, axis=0)[None], sum_ref.shape)


def combine_kernel(place_ref, sum_ref, z_ref, image_ref, f_ref, f_image_ref, out_ref):
    devices, kinds, lanes = sum_ref.shape
    pairs = devices // 2
    total = jnp.sum(sum_ref[...], axis=2, keepdims=True)
    total = jnp.sum(total.reshape(pairs, 2, kinds, 1), axis=1)
    g00, g01, g11, h11, step = (total[:, at : at + 1] for at in range(5))
    step = step * (1.0 / (2 * lanes))

    def over_pairs(value):
        return jnp.sum(value, axis=0, keepdims=True)

    gamma = over_pairs(g00)
    alpha = gamma / over_pairs(g01)
    theta = alpha / step
    rest = 1.0 - theta
    gamma_new = over_pairs(rest * rest * g00 + theta * theta * g11)
    turn = rest + gamma_new / gamma
    curvature = over_pairs(
        turn * turn * g01 - 2.0 * theta * turn * g11 / step + theta * theta * h11
    )
    alpha_new = gamma_new / curvature
    own = lax.broadcasted_iota(jnp.int32, theta.shape, 0) == place_ref[3]
    on_z = over_pairs(jnp.where(own, alpha + alpha_new * turn, 0.0))
    on_f = over_pairs(jnp.where(own, alpha_new * theta, 0.0))
    share = z_ref.shape[1]
    out_ref[:, :share, :] = on_z * z_ref[...] + on_f * f_ref[...]
    out_ref[:, share:, :] = on_z * image_ref[...] + on_f * f_image_ref[...]


def finish_kernel(got_ref, right_ref, solution_ref, residual_ref):
    samples = got_ref.shape[0]
    rows = got_ref.shape[1] // 2
    for sample in range(samples):
        solution_ref[sample, 0] = got_ref[sample, :rows, :]
        residual_ref[sample, 0] = right_ref[sample, 0] - got_ref[sample, rows:, :]


def paired_body(
    right_side,
    classes,
    noise_table,
    kernel_first,
    kernel_second,
    basis_first,
    basis_second,
    eigen_first,
    eigen_second,
):
    groups = lax.axis_size("mode")
    samples, planes, rows, width = right_side.shape
    height = groups * rows
    cores = 2
    half = width // cores
    blocks = groups // cores
    unit = cores * samples
    index = lax.axis_index("mode")
    core = index % cores
    sample = (index // cores) % samples
    plane = index // unit
    place = jnp.stack([core, sample, plane, index // cores]).astype(jnp.int32)

    def shape_of(*shape):
        return jax.ShapeDtypeStruct(shape, F32)

    smem = pl.BlockSpec(memory_space=pltpu.SMEM)

    def full(*shape):
        return pl.BlockSpec(
            shape, lambda *at: (0,) * len(shape), pipeline_mode=pl.Buffered(1)
        )

    def whole_out(*shape):
        return pl.BlockSpec(shape, lambda *at: (0,) * len(shape))

    core_swap = [(at, at ^ 1) for at in range(groups)]
    sample_swap = [(at, at ^ cores) for at in range(groups)]

    def in_hbm(value):
        return pltpu.with_memory_space_constraint(value, pltpu.HBM)

    def noise_of(shifts):
        return pl.pallas_call(
            functools.partial(noise_kernel, shifts, unit),
            grid=(1,),
            in_specs=[smem, pl.BlockSpec(memory_space=pltpu.HBM)],
            out_specs=[whole_out(rows, width)] * len(shifts),
            out_shape=[shape_of(rows, width)] * len(shifts),
            scratch_shapes=[
                pltpu.VMEM((len(shifts), rows, width), jnp.int32),
                pltpu.SemaphoreType.DMA((len(shifts),)),
            ],
            compiler_params=params(1, 4),
        )(noise_table, in_hbm(classes))

    def plane_shift(value, by):
        pairs = [(at, (at + by * unit) % groups) for at in range(groups)]
        return lax.ppermute(value, "mode", pairs)

    ahead = planes // 2
    others = [by for by in range(planes) if by != ahead]
    near = [None] * planes
    near[ahead] = plane_shift(noise_of([ahead])[0], ahead)
    rest = noise_of(others)
    for by, value in zip(others, rest):
        near[by] = plane_shift(value, by) if by else value
    far = [lax.ppermute(value, "mode", sample_swap) for value in near]
    noise = (*near, *far)

    outgoing = pl.pallas_call(
        outgoing_kernel,
        grid=(planes,),
        in_specs=[
            pl.BlockSpec((samples, 1, rows, width), lambda p: (0, p, 0, 0)),
            full(width, width),
        ],
        out_specs=pl.BlockSpec((1, samples, cores, rows, half), lambda p: (p, 0, 0, 0, 0)),
        out_shape=shape_of(planes, samples, cores, rows, half),
        compiler_params=params(1, 56),
        name="outgoing",
    )(right_side, basis_second)
    arrived = lax.all_to_all(
        outgoing.reshape(groups, rows, half), "mode", split_axis=0, concat_axis=0, tiled=True
    )

    eigen = eigen_second.reshape(1, -1)
    for reach in (1, cores):
        other = lax.ppermute(eigen, "mode", [(at, at ^ reach) for at in range(groups)])
        low = (index // reach) % 2 == 0
        eigen = jnp.where(
            low,
            jnp.concatenate([eigen, other], axis=1),
            jnp.concatenate([other, eigen], axis=1),
        )
    eigen = pl.pallas_call(
        follow_kernel,
        in_specs=[pl.BlockSpec(memory_space=pltpu.VMEM)]
        + [pl.BlockSpec(memory_space=pl.ANY)] * (planes - 1),
        out_specs=pl.BlockSpec(memory_space=pltpu.VMEM),
        out_shape=shape_of(*eigen.shape),
        compiler_params=pltpu.CompilerParams(vmem_limit_bytes=1024 * 1024),
        name="follow",
    )(eigen, *near[1:])
    shifted = [eigen] + [
        lax.ppermute(eigen, "mode", [(at, (at + by * unit) % groups) for at in range(groups)])
        for by in range(1, planes)
    ]
    bf16_square = jax.ShapeDtypeStruct((height, height), BF16)
    turned, high, low, tall_eigen = pl.pallas_call(
        prepare_kernel,
        grid=(1,),
        in_specs=[full(height, height), full(width, width), full(width, width), full(1, height)]
        + [pl.BlockSpec(memory_space=pl.ANY)],
        out_specs=[whole_out(height, height)] * 3 + [whole_out(height, 128)],
        out_shape=[bf16_square] * 3 + [shape_of(height, 128)],
        compiler_params=params(1, 24),
        name="prepare",
    )(basis_first, basis_second, kernel_second, eigen_first.reshape(1, -1), eigen)

    def swap(value):
        return lax.ppermute(value, "mode", core_swap)

    def call(kernel, inputs, shapes, scratch_shape, specs=None, more=(), mebibytes=12):
        return pl.pallas_call(
            kernel,
            grid=(1,),
            in_specs=specs or [smem] + [full(*value.shape) for value in inputs[1:]],
            out_specs=[whole_out(*shape) for shape in shapes],
            out_shape=[shape_of(*shape) for shape in shapes],
            scratch_shapes=[*([pltpu.VMEM(scratch_shape, F32)] if scratch_shape else []), *more],
            compiler_params=params(1, mebibytes),
        )(*inputs)

    tile = (height, half)
    piece = (blocks, rows, half)
    whole = (blocks, rows, width)
    by_rows = (blocks, cores, rows, half)
    flat = (blocks * rows, width)
    sums_shape = (8, 128)

    start, weights, column, keep, send, sum_one = call(
        first_column_kernel,
        (
            place,
            noise_table,
            in_hbm(arrived),
            in_hbm(turned),
            in_hbm(basis_first),
            tall_eigen,
            *shifted,
        ),
        (tile, tile, tile, piece, piece, sums_shape),
        by_rows,
        [smem, smem]
        + [pl.BlockSpec(memory_space=pltpu.HBM)] * 3
        + [full(height, 128)]
        + [full(*value.shape) for value in shifted],
        [
            pltpu.VMEM((groups, rows, half), F32),
            pltpu.VMEM((height, height), BF16),
            pltpu.VMEM((height, height), BF16),
            pltpu.SemaphoreType.DMA((4,)),
        ],
        18,
    )
    got = swap(send)
    image_keep, image_send = call(
        column_image_kernel, (place, column, kernel_first), (piece, piece), by_rows
    )
    image_got = swap(image_send)
    inputs = (place, keep, got, basis_second)
    z_field, noise = call(
        first_row_kernel,
        (*inputs, *(in_hbm(value) for value in noise)),
        (whole, whole),
        flat,
        [smem]
        + [full(*value.shape) for value in inputs[1:]]
        + [pl.BlockSpec(memory_space=pltpu.HBM)] * len(noise),
        [pltpu.SemaphoreType.DMA((len(noise),))],
    )
    image, pair_sum = call(
        first_image_kernel,
        (place, image_keep, image_got, z_field, noise, high, low, sum_one),
        (whole, sums_shape),
        flat,
    )
    pair_other = swap(pair_sum)

    def give_back(whose):
        kernel = functools.partial(return_kernel, whose)
        return call(kernel, (place, image, basis_second), (piece,), None)[0]

    back_send = give_back(1)
    back_keep = give_back(0)
    back_got = swap(back_send)

    column, keep, send, sum_two = call(
        next_column_kernel,
        (
            place,
            back_keep,
            back_got,
            start,
            weights,
            turned,
            basis_first,
            pair_sum,
            pair_other,
        ),
        (tile, piece, piece, sums_shape),
        by_rows,
    )
    got = swap(send)
    image_keep, image_send = call(
        column_image_kernel, (place, column, kernel_first), (piece, piece), by_rows
    )
    image_got = swap(image_send)
    (f_field,) = call(row_kernel, (place, keep, got, basis_second), (whole,), flat)
    f_image, sums = call(
        last_image_kernel,
        (
            place,
            image_keep,
            image_got,
            f_field,
            noise,
            high,
            low,
            pair_sum,
            sum_two,
        ),
        (whole, (groups, 8, 128)),
        flat,
    )
    sums = lax.all_to_all(sums, "mode", split_axis=0, concat_axis=0, tiled=True)

    few = blocks // 4
    few_spec = pl.BlockSpec((few, rows, width), lambda i: (i, 0, 0))
    answer = pl.pallas_call(
        combine_kernel,
        grid=(4,),
        in_specs=[smem, full(groups, 8, 128)] + [few_spec] * 4,
        out_specs=pl.BlockSpec((few, 2 * rows, width), lambda i: (i, 0, 0)),
        out_shape=shape_of(blocks, 2 * rows, width),
        compiler_params=params(1, 6),
        name="combine",
    )(place, sums, z_field, image, f_field, f_image)
    answer = lax.all_to_all(
        answer,
        "mode",
        split_axis=0,
        concat_axis=0,
        axis_index_groups=[list(range(at, groups, cores)) for at in range(cores)],
        tiled=True,
    )

    block = pl.BlockSpec((samples, 1, rows, width), lambda p: (0, p, 0, 0))
    return tuple(
        pl.pallas_call(
            finish_kernel,
            grid=(planes,),
            in_specs=[
                pl.BlockSpec((samples, 2 * rows, width), lambda p: (p, 0, 0)),
                block,
            ],
            out_specs=[block, block],
            out_shape=[shape_of(*right_side.shape)] * 2,
            compiler_params=params(1, 10),
            name="finish",
        )(answer, right_side)
    )


def body(right_side, classes, *rest):
    groups = lax.axis_size("mode")
    samples, planes, rows, width = right_side.shape
    paired = (
        groups == 2 * samples * planes
        and samples == 2
        and rows % 8 == 0
        and width % 512 == 0
        and planes % 2 == 0
    )
    chosen = paired_body if paired else general_body
    return chosen(right_side, classes, *rest)


def solution(mesh):
    in_specs = (
        P(None, "blocks", "mode", None),
        P("blocks", "mode", None),
        P(),
        P(),
        P(),
        P(),
        P(),
        P(),
        P("mode"),
    )
    out_specs = (P(None, "blocks", "mode", None), P(None, "blocks", "mode", None))
    return jax.shard_map(body, mesh=mesh, in_specs=in_specs, out_specs=out_specs, check_vma=False)
```

```python
import functools

import jax
import jax.numpy as jnp
from jax import lax
from jax.experimental import pallas as pl
from jax.experimental.pallas import tpu as pltpu
from jax.sharding import PartitionSpec as P


NCLASS = 8
ITERS = 2
F32 = jnp.float32
BF16 = jnp.bfloat16


def along_rows(matrix, field):
    return jnp.einsum("jk,sprk->sprj", matrix, field, precision=lax.Precision.HIGHEST)


def rows_to_send(matrix, field, groups):
    result = jnp.einsum("kj,sprk->jspr", matrix, field, precision=lax.Precision.HIGHEST)
    return result.reshape(groups, -1)


def received_to_columns(matrix, received, shape5):
    groups, _, _, _, rows = shape5
    block = received.reshape(shape5)
    reshaped = matrix.reshape(groups, rows, matrix.shape[1])
    return jnp.einsum("mri,mcspr->cspi", reshaped, block, precision=lax.Precision.HIGHEST)


def along_columns(matrix, columns):
    return jnp.einsum("ik,cspk->cspi", matrix, columns, precision=lax.Precision.HIGHEST)


def columns_to_send(matrix, columns, groups, rows):
    reshaped = matrix.reshape(groups, rows, matrix.shape[1])
    result = jnp.einsum("mrk,cspk->mcspr", reshaped, columns, precision=lax.Precision.HIGHEST)
    return result.reshape(groups, -1)


def received_to_rows(matrix, received, shape5):
    groups, cols, _, _, _ = shape5
    block = received.reshape(shape5)
    reshaped = matrix.reshape(matrix.shape[0], groups, cols)
    return jnp.einsum("jmc,mcspr->sprj", reshaped, block, precision=lax.Precision.HIGHEST)


def general_body(
    right_side,
    classes,
    noise_table,
    kernel_first,
    kernel_second,
    basis_first,
    basis_second,
    eigen_first,
    eigen_second,
):
    groups = lax.axis_size("mode")
    samples, planes, rows, _ = right_side.shape
    cols = eigen_second.shape[0]
    shape5 = (groups, cols, samples, planes, rows)
    kern_one = kernel_first.astype(F32)
    kern_two = kernel_second.astype(F32)
    base_one = basis_first.astype(F32)
    base_two = basis_second.astype(F32)
    noise = jnp.zeros(classes.shape, F32)
    for level in range(NCLASS):
        noise = noise + jnp.where(classes == level, noise_table[level], 0.0)
    noise = noise[None]
    mean_noise = jnp.mean(noise_table)
    col_weights = 1.0 / (eigen_second[:, None] * eigen_first[None, :] + mean_noise)
    col_weights = col_weights[:, None, None, :]

    def exchange(outgoing):
        return lax.all_to_all(outgoing, "mode", split_axis=0, concat_axis=0, tiled=True)

    def precond_apply(field):
        incoming = exchange(rows_to_send(base_two, field, groups))
        weighted = received_to_columns(base_one, incoming, shape5) * col_weights
        columns = along_columns(base_one, weighted)
        back = exchange(columns_to_send(base_one, weighted, groups, rows))
        kernel_back = exchange(columns_to_send(kern_one, columns, groups, rows))
        z_field = received_to_rows(base_two, back, shape5)
        image = (
            along_rows(kern_two, received_to_rows(base_two, kernel_back, shape5)) + noise * z_field
        )
        return (z_field, image)

    def inner(left, right):
        return lax.psum(jnp.sum(left * right), "mode")

    solution_field = jnp.zeros_like(right_side)
    residual = right_side
    z_field, image = precond_apply(residual)
    direction, along = (z_field, image)
    gamma = inner(residual, z_field)
    for step in range(ITERS):
        alpha = gamma / inner(direction, along)
        solution_field = solution_field + alpha * direction
        residual = residual - alpha * along
        if step + 1 < ITERS:
            z_field, image = precond_apply(residual)
            gamma_new = inner(residual, z_field)
            ratio = gamma_new / gamma
            direction = z_field + ratio * direction
            along = image + ratio * along
            gamma = gamma_new
    return (solution_field, residual)


def split(value):
    high = value.astype(BF16)
    low = (value - high.astype(F32)).astype(BF16)
    return high, low


def times_right(value, matrix, contract):
    high, low = split(value)
    dims = (((1,), (contract,)), ((), ()))
    both = jnp.concatenate([high, low], axis=0)
    result = lax.dot_general(both, matrix, dims, preferred_element_type=F32)
    return result[: value.shape[0]] + result[value.shape[0] :]


def times_left(matrix, value):
    high, low = split(value)
    dims = (((1,), (0,)), ((), ()))
    both = jnp.concatenate([high, low], axis=1)
    result = lax.dot_general(matrix, both, dims, preferred_element_type=F32)
    return result[:, : value.shape[1]] + result[:, value.shape[1] :]


def fold(value):
    total = jnp.sum(value, axis=0, keepdims=True)
    return functools.reduce(
        jnp.add, [total[:, at : at + 128] for at in range(0, total.shape[1], 128)]
    )


def params(dims, mebibytes):
    return pltpu.CompilerParams(
        dimension_semantics=("arbitrary",) * dims, vmem_limit_bytes=mebibytes * 1024 * 1024
    )


def noise_kernel(shifts, unit, table_ref, class_hbm, *refs):
    out_refs, (class_ref, done) = refs[:-2], refs[-2:]
    planes = class_hbm.shape[0]
    plane = lax.axis_index("mode") // unit
    copies = [
        pltpu.make_async_copy(class_hbm.at[(plane + by) % planes], class_ref.at[at], done.at[at])
        for at, by in enumerate(shifts)
    ]
    for copy in copies:
        copy.start()
    for at, copy in enumerate(copies):
        copy.wait()
        level = class_ref[at]
        noise = jnp.full(level.shape, table_ref[0], F32)
        for index in range(1, NCLASS):
            noise = jnp.where(level == index, table_ref[index], noise)
        out_refs[at][...] = noise


def follow_kernel(value_ref, *refs):
    refs[-1][...] = value_ref[...]


def prepare_kernel(
    first_ref, second_ref, kernel_ref, eigen_ref, _, turned_ref, high_ref, low_ref, tall_ref
):
    turned_ref[...] = first_ref[...].T
    tall_ref[...] = jnp.broadcast_to(eigen_ref[...], tall_ref.shape[::-1]).T
    dims = (((1,), (0,)), ((), ()))
    product = lax.dot_general(
        kernel_ref[...], second_ref[...], dims, preferred_element_type=F32
    )
    high_ref[...], low_ref[...] = split(product)


def outgoing_kernel(right_ref, basis_ref, out_ref):
    samples, _, rows, width = right_ref.shape
    cores = out_ref.shape[2]
    half = width // cores
    field = right_ref[...].reshape(samples * rows, width)
    mapped = times_right(field, basis_ref[...], 0)
    for sample in range(samples):
        for core in range(cores):
            out_ref[0, sample, core] = mapped[
                sample * rows : (sample + 1) * rows, core * half : (core + 1) * half
            ]


def both_shares(place_ref, share):
    core = place_ref[0]
    mine = pl.ds(pl.multiple_of(core * share, share), share)
    theirs = pl.ds(pl.multiple_of((1 - core) * share, share), share)
    return mine, theirs


def split_rows(place_ref, value, scratch_ref, keep_ref, send_ref):
    core = place_ref[0]
    scratch_ref[...] = value.reshape(scratch_ref.shape)
    keep_ref[...] = scratch_ref[:, core]
    send_ref[...] = scratch_ref[:, 1 - core]


def store_sums(sum_ref, sums):
    rows = sum_ref.shape[0]
    sum_ref[...] = jnp.concatenate(sums + [jnp.zeros((rows - len(sums), 128), F32)], axis=0)


def copy_into(pairs, done):
    return [
        pltpu.make_async_copy(source, target, done.at[at])
        for at, (source, target) in enumerate(pairs)
    ]


def first_column_kernel(
    place_ref,
    table_ref,
    field_hbm,
    turned_hbm,
    basis_hbm,
    kernel_hbm,
    second_hbm,
    tall_ref,
    *refs,
):
    wide_refs, refs, outs = refs[:-13], refs[-7:], refs[-13:-7]
    start_ref, weight_ref, column_ref, keep_ref, send_ref, sum_ref = outs
    turned_ref, basis_ref, kernel_ref, second_ref, scratch_ref, field_ref, done = refs
    middle = turned_ref.shape[0] // 2
    upper, lower = pl.ds(0, middle), pl.ds(middle, middle)
    copies = copy_into(
        (
            (field_hbm, field_ref),
            (turned_hbm.at[upper], turned_ref.at[upper]),
            (turned_hbm.at[lower], turned_ref.at[lower]),
            (basis_hbm, basis_ref),
            (kernel_hbm, kernel_ref),
            (second_hbm, second_ref),
        ),
        done,
    )
    for copy in copies[:3]:
        copy.start()
    mean = functools.reduce(jnp.add, [table_ref[at] for at in range(NCLASS)]) * (1.0 / NCLASS)
    height, width = start_ref.shape
    planes = len(wide_refs)
    part = wide_refs[0].shape[1]
    for block in range(width // part):
        wanted = place_ref[0] * (width // part) + block
        wide = jnp.zeros((1, part), F32)
        for by, wide_ref in enumerate(wide_refs):
            here = (place_ref[2] + planes - by) % planes == wanted
            wide = jnp.where(here, wide_ref[...], wide)
        for at in range(0, part, 128):
            lanes = slice(block * part + at, block * part + at + 128)
            weight_ref[:, lanes] = 1.0 / (tall_ref[...] * wide[:, at : at + 128] + mean)
    copies[0].wait()
    field = field_ref[...].reshape(height, width)
    copies[1].wait()
    copies[2].wait()
    for copy in copies[3:]:
        copy.start()
    spectral = times_left(turned_ref[...], field)
    weighted = spectral * weight_ref[...]
    start_ref[...] = field
    store_sums(sum_ref, [fold(spectral * weighted)])
    copies[3].wait()
    column = times_left(basis_ref[...], weighted)
    column_ref[...] = column
    split_rows(place_ref, column, scratch_ref, keep_ref, send_ref)
    copies[4].wait()
    copies[5].wait()


def next_column_kernel(
    place_ref,
    held_ref,
    got_ref,
    start_ref,
    weight_ref,
    turned_ref,
    basis_ref,
    own_ref,
    other_ref,
    column_ref,
    keep_ref,
    send_ref,
    sum_ref,
    scratch_ref,
):
    core = place_ref[0]
    scratch_ref[:, core] = held_ref[...]
    scratch_ref[:, 1 - core] = got_ref[...]
    total = jnp.sum(own_ref[...] + other_ref[...], axis=1, keepdims=True)
    gamma, curvature = total[0:1], total[1:2]
    proper = (gamma > 0) & (curvature > 0)
    step = jnp.where(proper, gamma / jnp.where(proper, curvature, 1.0), 1.0)
    field = start_ref[...] - step * scratch_ref[...].reshape(start_ref.shape)
    spectral = times_left(turned_ref[...], field)
    weighted = spectral * weight_ref[...]
    store_sums(sum_ref, [fold(spectral * weighted), jnp.broadcast_to(step, (1, 128))])
    column = times_left(basis_ref[...], weighted)
    column_ref[...] = column
    split_rows(place_ref, column, scratch_ref, keep_ref, send_ref)


def column_image_kernel(place_ref, column_ref, kernel_ref, keep_ref, send_ref, scratch_ref):
    image = times_left(kernel_ref[...], column_ref[...])
    split_rows(place_ref, image, scratch_ref, keep_ref, send_ref)


def first_column_image_kernel(place_ref, column_ref, kernel_ref, high_hbm, low_hbm, *refs):
    keep_ref, send_ref, high_ref, low_ref, scratch_ref, done = refs
    copies = copy_into(((high_hbm, high_ref), (low_hbm, low_ref)), done)
    for copy in copies:
        copy.start()
    column_image_kernel(place_ref, column_ref, kernel_ref, keep_ref, send_ref, scratch_ref)
    for copy in copies:
        copy.wait()


def join_columns(place_ref, scratch_ref, keep_ref, got_ref):
    height, width = scratch_ref.shape
    mine, theirs = both_shares(place_ref, width // 2)
    scratch_ref[:, mine] = keep_ref[...].reshape(height, width // 2)
    scratch_ref[:, theirs] = got_ref[...].reshape(height, width // 2)
    return scratch_ref[...]


def row_kernel(place_ref, keep_ref, got_ref, basis_ref, z_ref, scratch_ref):
    field = join_columns(place_ref, scratch_ref, keep_ref, got_ref)
    z_ref[...] = times_right(field, basis_ref[...], 1).reshape(z_ref.shape)


def row_image(place_ref, keep_ref, got_ref, high_ref, low_ref, scratch_ref):
    field = join_columns(place_ref, scratch_ref, keep_ref, got_ref)
    high, low = split(field)
    dims = (((1,), (1,)), ((), ()))
    both = jnp.concatenate([high, low], axis=0)
    result = lax.dot_general(both, high_ref[...], dims, preferred_element_type=F32)
    small = lax.dot_general(high, low_ref[...], dims, preferred_element_type=F32)
    return result[: field.shape[0]] + (result[field.shape[0] :] + small)


def first_row_kernel(place_ref, keep_ref, got_ref, basis_ref, *refs):
    parts, (z_ref, noise_ref, scratch_ref, done) = refs[:-4], refs[-4:]
    planes = len(parts) // 2
    samples = z_ref.shape[0] // planes
    copies = []
    for by in range(planes):
        row = (place_ref[2] + planes - by) % planes
        for at, part in enumerate((parts[by], parts[planes + by])):
            block = row * samples + (place_ref[1] + at) % samples
            here = done.at[2 * by + at]
            copies.append(pltpu.make_async_copy(part, noise_ref.at[block], here))
    for copy in copies:
        copy.start()
    row_kernel(place_ref, keep_ref, got_ref, basis_ref, z_ref, scratch_ref)
    for copy in copies:
        copy.wait()


def full_image(place_ref, keep_ref, got_ref, z_ref, noise_ref, high_ref, low_ref, image_ref, scratch_ref):
    image = row_image(place_ref, keep_ref, got_ref, high_ref, low_ref, scratch_ref)
    field = z_ref[...].reshape(image.shape)
    image = image + noise_ref[...].reshape(image.shape) * field
    image_ref[...] = image.reshape(image_ref.shape)
    return fold(field * image)


def first_image_kernel(
    place_ref,
    keep_ref,
    got_ref,
    z_ref,
    noise_ref,
    high_ref,
    low_ref,
    one_ref,
    image_ref,
    sum_ref,
    scratch_ref,
):
    refs = (place_ref, keep_ref, got_ref, z_ref, noise_ref, high_ref, low_ref)
    store_sums(sum_ref, [one_ref[0:1], full_image(*refs, image_ref, scratch_ref)])


def return_kernel(whose, place_ref, image_ref, basis_ref, out_ref):
    lanes = both_shares(place_ref, out_ref.shape[2])[whose]
    image = image_ref[...].reshape(-1, basis_ref.shape[0])
    out_ref[...] = times_right(image, basis_ref[:, lanes], 0).reshape(out_ref.shape)


def last_image_kernel(
    place_ref,
    keep_ref,
    got_ref,
    z_ref,
    noise_ref,
    high_ref,
    low_ref,
    one_ref,
    two_ref,
    image_ref,
    sum_ref,
    scratch_ref,
):
    refs = (place_ref, keep_ref, got_ref, z_ref, noise_ref, high_ref, low_ref)
    last = full_image(*refs, image_ref, scratch_ref)
    rows = [one_ref[0:2], two_ref[0:1], last, two_ref[1:2], jnp.zeros((3, 128), F32)]
    sum_ref[...] = jnp.broadcast_to(jnp.concatenate(rows, axis=0)[None], sum_ref.shape)


def combine_kernel(place_ref, sum_ref, z_ref, image_ref, f_ref, f_image_ref, out_ref):
    devices, kinds, lanes = sum_ref.shape
    pairs = devices // 2
    total = jnp.sum(sum_ref[...], axis=2, keepdims=True)
    total = jnp.sum(total.reshape(pairs, 2, kinds, 1), axis=1)
    g00, g01, g11, h11, step = (total[:, at : at + 1] for at in range(5))
    step = step * (1.0 / (2 * lanes))

    def over_pairs(value):
        return jnp.sum(value, axis=0, keepdims=True)

    gamma = over_pairs(g00)
    alpha = gamma / over_pairs(g01)
    theta = alpha / step
    rest = 1.0 - theta
    gamma_new = over_pairs(rest * rest * g00 + theta * theta * g11)
    turn = rest + gamma_new / gamma
    curvature = over_pairs(
        turn * turn * g01 - 2.0 * theta * turn * g11 / step + theta * theta * h11
    )
    alpha_new = gamma_new / curvature
    own = lax.broadcasted_iota(jnp.int32, theta.shape, 0) == place_ref[3]
    on_z = over_pairs(jnp.where(own, alpha + alpha_new * turn, 0.0))
    on_f = over_pairs(jnp.where(own, alpha_new * theta, 0.0))
    share = z_ref.shape[1]
    out_ref[:, :share, :] = on_z * z_ref[...] + on_f * f_ref[...]
    out_ref[:, share:, :] = on_z * image_ref[...] + on_f * f_image_ref[...]


def finish_kernel(got_ref, right_ref, solution_ref, residual_ref):
    samples = got_ref.shape[0]
    rows = got_ref.shape[1] // 2
    for sample in range(samples):
        solution_ref[sample, 0] = got_ref[sample, :rows, :]
        residual_ref[sample, 0] = right_ref[sample, 0] - got_ref[sample, rows:, :]


def paired_body(
    right_side,
    classes,
    noise_table,
    kernel_first,
    kernel_second,
    basis_first,
    basis_second,
    eigen_first,
    eigen_second,
):
    groups = lax.axis_size("mode")
    samples, planes, rows, width = right_side.shape
    height = groups * rows
    cores = 2
    half = width // cores
    blocks = groups // cores
    unit = cores * samples
    index = lax.axis_index("mode")
    core = index % cores
    sample = (index // cores) % samples
    plane = index // unit
    place = jnp.stack([core, sample, plane, index // cores]).astype(jnp.int32)

    def shape_of(*shape):
        return jax.ShapeDtypeStruct(shape, F32)

    smem = pl.BlockSpec(memory_space=pltpu.SMEM)

    hbm = pl.BlockSpec(memory_space=pltpu.HBM)

    def full(*shape):
        return pl.BlockSpec(
            shape, lambda *at: (0,) * len(shape), pipeline_mode=pl.Buffered(1)
        )

    def whole_out(*shape):
        return pl.BlockSpec(shape, lambda *at: (0,) * len(shape))

    core_swap = [(at, at ^ 1) for at in range(groups)]
    sample_swap = [(at, at ^ cores) for at in range(groups)]

    def in_hbm(value):
        return pltpu.with_memory_space_constraint(value, pltpu.HBM)

    def noise_of(shifts):
        return pl.pallas_call(
            functools.partial(noise_kernel, shifts, unit),
            grid=(1,),
            in_specs=[smem, pl.BlockSpec(memory_space=pltpu.HBM)],
            out_specs=[whole_out(rows, width)] * len(shifts),
            out_shape=[shape_of(rows, width)] * len(shifts),
            scratch_shapes=[
                pltpu.VMEM((len(shifts), rows, width), jnp.int32),
                pltpu.SemaphoreType.DMA((len(shifts),)),
            ],
            compiler_params=params(1, 4),
        )(in_hbm(noise_table), in_hbm(classes))

    def plane_shift(value, by):
        pairs = [(at, (at + by * unit) % groups) for at in range(groups)]
        return lax.ppermute(value, "mode", pairs)

    ahead = planes // 2
    others = [by for by in range(planes) if by != ahead]
    near = [None] * planes
    near[ahead] = plane_shift(noise_of([ahead])[0], ahead)
    rest = noise_of(others)
    for by, value in zip(others, rest):
        near[by] = plane_shift(value, by) if by else value
    far = [lax.ppermute(value, "mode", sample_swap) for value in near]
    noise = (*near, *far)

    outgoing = pl.pallas_call(
        outgoing_kernel,
        grid=(planes,),
        in_specs=[
            pl.BlockSpec((samples, 1, rows, width), lambda p: (0, p, 0, 0)),
            full(width, width),
        ],
        out_specs=pl.BlockSpec((1, samples, cores, rows, half), lambda p: (p, 0, 0, 0, 0)),
        out_shape=shape_of(planes, samples, cores, rows, half),
        compiler_params=params(1, 56),
        name="outgoing",
    )(right_side, basis_second)
    arrived = lax.all_to_all(
        outgoing.reshape(groups, rows, half), "mode", split_axis=0, concat_axis=0, tiled=True
    )

    eigen = eigen_second.reshape(1, -1)
    for reach in (1, cores):
        other = lax.ppermute(eigen, "mode", [(at, at ^ reach) for at in range(groups)])
        low = (index // reach) % 2 == 0
        eigen = jnp.where(
            low,
            jnp.concatenate([eigen, other], axis=1),
            jnp.concatenate([other, eigen], axis=1),
        )
    eigen = pl.pallas_call(
        follow_kernel,
        in_specs=[pl.BlockSpec(memory_space=pltpu.VMEM)]
        + [pl.BlockSpec(memory_space=pl.ANY)] * (planes - 1),
        out_specs=pl.BlockSpec(memory_space=pltpu.VMEM),
        out_shape=shape_of(*eigen.shape),
        compiler_params=pltpu.CompilerParams(vmem_limit_bytes=1024 * 1024),
        name="follow",
    )(eigen, *near[1:])
    shifted = [eigen] + [
        lax.ppermute(eigen, "mode", [(at, (at + by * unit) % groups) for at in range(groups)])
        for by in range(1, planes)
    ]
    bf16_square = jax.ShapeDtypeStruct((height, height), BF16)
    turned, high, low, tall_eigen = pl.pallas_call(
        prepare_kernel,
        grid=(1,),
        in_specs=[full(height, height), full(width, width), full(width, width), full(1, height)]
        + [pl.BlockSpec(memory_space=pl.ANY)],
        out_specs=[whole_out(height, height)] * 3 + [whole_out(height, 128)],
        out_shape=[bf16_square] * 3 + [shape_of(height, 128)],
        compiler_params=params(1, 24),
        name="prepare",
    )(basis_first, basis_second, kernel_second, eigen_first.reshape(1, -1), eigen)

    def swap(value):
        return lax.ppermute(value, "mode", core_swap)

    def call(kernel, inputs, shapes, scratch_shape, specs=None, more=(), mebibytes=12, matrices=0):
        return pl.pallas_call(
            kernel,
            grid=(1,),
            in_specs=specs or [smem] + [full(*value.shape) for value in inputs[1:]],
            out_specs=[whole_out(*shape) for shape in shapes]
            + [whole_out(height, height)] * matrices,
            out_shape=[shape_of(*shape) for shape in shapes] + [bf16_square] * matrices,
            scratch_shapes=[*([pltpu.VMEM(scratch_shape, F32)] if scratch_shape else []), *more],
            compiler_params=params(1, mebibytes),
        )(*inputs)

    tile = (height, half)
    piece = (blocks, rows, half)
    whole = (blocks, rows, width)
    by_rows = (blocks, cores, rows, half)
    flat = (blocks * rows, width)
    sums_shape = (8, 128)

    (start, weights, column, keep, send, sum_one, turned, *squares) = call(
        first_column_kernel,
        (
            place,
            noise_table,
            *(
                in_hbm(value)
                for value in (arrived, turned, basis_first, kernel_first, basis_second)
            ),
            tall_eigen,
            *shifted,
        ),
        (tile, tile, tile, piece, piece, sums_shape),
        by_rows,
        [smem, smem]
        + [hbm] * 5
        + [full(height, 128)]
        + [full(*value.shape) for value in shifted],
        [pltpu.VMEM((groups, rows, half), F32), pltpu.SemaphoreType.DMA((6,))],
        16,
        4,
    )
    basis_first, kernel_first, basis_second = squares
    got = swap(send)
    image_keep, image_send, high, low = call(
        first_column_image_kernel,
        (place, column, kernel_first, in_hbm(high), in_hbm(low)),
        (piece, piece),
        by_rows,
        [smem, full(*tile), full(height, height), hbm, hbm],
        [pltpu.SemaphoreType.DMA((2,))],
        matrices=2,
    )
    image_got = swap(image_send)
    inputs = (place, keep, got, basis_second)
    z_field, noise = call(
        first_row_kernel,
        (*inputs, *(in_hbm(value) for value in noise)),
        (whole, whole),
        flat,
        [smem]
        + [full(*value.shape) for value in inputs[1:]]
        + [hbm] * len(noise),
        [pltpu.SemaphoreType.DMA((len(noise),))],
    )
    image, pair_sum = call(
        first_image_kernel,
        (place, image_keep, image_got, z_field, noise, high, low, sum_one),
        (whole, sums_shape),
        flat,
    )
    pair_other = swap(pair_sum)

    def give_back(whose):
        kernel = functools.partial(return_kernel, whose)
        return call(kernel, (place, image, basis_second), (piece,), None)[0]

    back_send = give_back(1)
    back_keep = give_back(0)
    back_got = swap(back_send)

    column, keep, send, sum_two = call(
        next_column_kernel,
        (
            place,
            back_keep,
            back_got,
            start,
            weights,
            turned,
            basis_first,
            pair_sum,
            pair_other,
        ),
        (tile, piece, piece, sums_shape),
        by_rows,
    )
    got = swap(send)
    image_keep, image_send = call(
        column_image_kernel, (place, column, kernel_first), (piece, piece), by_rows
    )
    image_got = swap(image_send)
    (f_field,) = call(row_kernel, (place, keep, got, basis_second), (whole,), flat)
    f_image, sums = call(
        last_image_kernel,
        (
            place,
            image_keep,
            image_got,
            f_field,
            noise,
            high,
            low,
            pair_sum,
            sum_two,
        ),
        (whole, (groups, 8, 128)),
        flat,
    )
    sums = lax.all_to_all(sums, "mode", split_axis=0, concat_axis=0, tiled=True)

    few = blocks
    few_spec = pl.BlockSpec((few, rows, width), lambda i: (i, 0, 0))
    answer = pl.pallas_call(
        combine_kernel,
        grid=(1,),
        in_specs=[smem, full(groups, 8, 128)] + [few_spec] * 4,
        out_specs=pl.BlockSpec((few, 2 * rows, width), lambda i: (i, 0, 0)),
        out_shape=shape_of(blocks, 2 * rows, width),
        compiler_params=params(1, 6),
        name="combine",
    )(place, sums, z_field, image, f_field, f_image)
    answer = lax.all_to_all(
        answer,
        "mode",
        split_axis=0,
        concat_axis=0,
        axis_index_groups=[list(range(at, groups, cores)) for at in range(cores)],
        tiled=True,
    )

    block = pl.BlockSpec((samples, 1, rows, width), lambda p: (0, p, 0, 0))
    return tuple(
        pl.pallas_call(
            finish_kernel,
            grid=(planes,),
            in_specs=[
                pl.BlockSpec((samples, 2 * rows, width), lambda p: (p, 0, 0)),
                block,
            ],
            out_specs=[block, block],
            out_shape=[shape_of(*right_side.shape)] * 2,
            compiler_params=params(1, 10),
            name="finish",
        )(answer, right_side)
    )


def body(right_side, classes, *rest):
    groups = lax.axis_size("mode")
    samples, planes, rows, width = right_side.shape
    paired = (
        groups == 2 * samples * planes
        and samples == 2
        and rows % 8 == 0
        and width % 512 == 0
        and planes % 2 == 0
    )
    chosen = paired_body if paired else general_body
    return chosen(right_side, classes, *rest)


def solution(mesh):
    in_specs = (
        P(None, "blocks", "mode", None),
        P("blocks", "mode", None),
        P(),
        P(),
        P(),
        P(),
        P(),
        P(),
        P("mode"),
    )
    out_specs = (P(None, "blocks", "mode", None), P(None, "blocks", "mode", None))
    return jax.shard_map(body, mesh=mesh, in_specs=in_specs, out_specs=out_specs, check_vma=False)
```

```python
import functools

import jax
import jax.numpy as jnp
from jax import lax
from jax.experimental import pallas as pl
from jax.experimental.pallas import tpu as pltpu
from jax.sharding import PartitionSpec as P


NCLASS = 8
ITERS = 2
F32 = jnp.float32
BF16 = jnp.bfloat16


def along_rows(matrix, field):
    return jnp.einsum("jk,sprk->sprj", matrix, field, precision=lax.Precision.HIGHEST)


def rows_to_send(matrix, field, groups):
    result = jnp.einsum("kj,sprk->jspr", matrix, field, precision=lax.Precision.HIGHEST)
    return result.reshape(groups, -1)


def received_to_columns(matrix, received, shape5):
    groups, _, _, _, rows = shape5
    block = received.reshape(shape5)
    reshaped = matrix.reshape(groups, rows, matrix.shape[1])
    return jnp.einsum("mri,mcspr->cspi", reshaped, block, precision=lax.Precision.HIGHEST)


def along_columns(matrix, columns):
    return jnp.einsum("ik,cspk->cspi", matrix, columns, precision=lax.Precision.HIGHEST)


def columns_to_send(matrix, columns, groups, rows):
    reshaped = matrix.reshape(groups, rows, matrix.shape[1])
    result = jnp.einsum("mrk,cspk->mcspr", reshaped, columns, precision=lax.Precision.HIGHEST)
    return result.reshape(groups, -1)


def received_to_rows(matrix, received, shape5):
    groups, cols, _, _, _ = shape5
    block = received.reshape(shape5)
    reshaped = matrix.reshape(matrix.shape[0], groups, cols)
    return jnp.einsum("jmc,mcspr->sprj", reshaped, block, precision=lax.Precision.HIGHEST)


def general_body(
    right_side,
    classes,
    noise_table,
    kernel_first,
    kernel_second,
    basis_first,
    basis_second,
    eigen_first,
    eigen_second,
):
    groups = lax.axis_size("mode")
    samples, planes, rows, _ = right_side.shape
    cols = eigen_second.shape[0]
    shape5 = (groups, cols, samples, planes, rows)
    kern_one = kernel_first.astype(F32)
    kern_two = kernel_second.astype(F32)
    base_one = basis_first.astype(F32)
    base_two = basis_second.astype(F32)
    noise = jnp.zeros(classes.shape, F32)
    for level in range(NCLASS):
        noise = noise + jnp.where(classes == level, noise_table[level], 0.0)
    noise = noise[None]
    mean_noise = jnp.mean(noise_table)
    col_weights = 1.0 / (eigen_second[:, None] * eigen_first[None, :] + mean_noise)
    col_weights = col_weights[:, None, None, :]

    def exchange(outgoing):
        return lax.all_to_all(outgoing, "mode", split_axis=0, concat_axis=0, tiled=True)

    def precond_apply(field):
        incoming = exchange(rows_to_send(base_two, field, groups))
        weighted = received_to_columns(base_one, incoming, shape5) * col_weights
        columns = along_columns(base_one, weighted)
        back = exchange(columns_to_send(base_one, weighted, groups, rows))
        kernel_back = exchange(columns_to_send(kern_one, columns, groups, rows))
        z_field = received_to_rows(base_two, back, shape5)
        image = (
            along_rows(kern_two, received_to_rows(base_two, kernel_back, shape5)) + noise * z_field
        )
        return (z_field, image)

    def inner(left, right):
        return lax.psum(jnp.sum(left * right), "mode")

    solution_field = jnp.zeros_like(right_side)
    residual = right_side
    z_field, image = precond_apply(residual)
    direction, along = (z_field, image)
    gamma = inner(residual, z_field)
    for step in range(ITERS):
        alpha = gamma / inner(direction, along)
        solution_field = solution_field + alpha * direction
        residual = residual - alpha * along
        if step + 1 < ITERS:
            z_field, image = precond_apply(residual)
            gamma_new = inner(residual, z_field)
            ratio = gamma_new / gamma
            direction = z_field + ratio * direction
            along = image + ratio * along
            gamma = gamma_new
    return (solution_field, residual)


def split(value):
    high = value.astype(BF16)
    low = (value - high.astype(F32)).astype(BF16)
    return high, low


def times_right(value, matrix, contract):
    high, low = split(value)
    dims = (((1,), (contract,)), ((), ()))
    both = jnp.concatenate([high, low], axis=0)
    result = lax.dot_general(both, matrix, dims, preferred_element_type=F32)
    return result[: value.shape[0]] + result[value.shape[0] :]


def side_by_side(value):
    return jnp.concatenate(split(value), axis=1)


def times_both(matrix, both):
    width = both.shape[1] // 2
    dims = (((1,), (0,)), ((), ()))
    result = lax.dot_general(matrix, both, dims, preferred_element_type=F32)
    return result[:, :width] + result[:, width:]


def times_left(matrix, value):
    return times_both(matrix, side_by_side(value))


def fold(value):
    total = jnp.sum(value, axis=0, keepdims=True)
    return functools.reduce(
        jnp.add, [total[:, at : at + 128] for at in range(0, total.shape[1], 128)]
    )


def params(dims, mebibytes):
    return pltpu.CompilerParams(
        dimension_semantics=("arbitrary",) * dims, vmem_limit_bytes=mebibytes * 1024 * 1024
    )


def noise_kernel(shifts, unit, table_ref, class_hbm, *refs):
    out_refs, (class_ref, done) = refs[:-2], refs[-2:]
    planes = class_hbm.shape[0]
    plane = lax.axis_index("mode") // unit
    copies = [
        pltpu.make_async_copy(class_hbm.at[(plane + by) % planes], class_ref.at[at], done.at[at])
        for at, by in enumerate(shifts)
    ]
    for copy in copies:
        copy.start()
    for at, copy in enumerate(copies):
        copy.wait()
        level = class_ref[at]
        noise = jnp.full(level.shape, table_ref[0], F32)
        for index in range(1, NCLASS):
            noise = jnp.where(level == index, table_ref[index], noise)
        out_refs[at][...] = noise


def follow_kernel(value_ref, *refs):
    refs[-1][...] = value_ref[...]


def prepare_kernel(
    first_ref, second_ref, kernel_ref, eigen_ref, _, turned_ref, high_ref, low_ref, tall_ref
):
    turned_ref[...] = first_ref[...].T
    tall_ref[...] = jnp.broadcast_to(eigen_ref[...], tall_ref.shape[::-1]).T
    dims = (((1,), (0,)), ((), ()))
    product = lax.dot_general(
        kernel_ref[...], second_ref[...], dims, preferred_element_type=F32
    )
    high_ref[...], low_ref[...] = split(product)


def outgoing_kernel(right_ref, basis_ref, out_ref):
    samples, _, rows, width = right_ref.shape
    cores = out_ref.shape[2]
    half = width // cores
    field = right_ref[...].reshape(samples * rows, width)
    mapped = times_right(field, basis_ref[...], 0)
    for sample in range(samples):
        for core in range(cores):
            out_ref[0, sample, core] = mapped[
                sample * rows : (sample + 1) * rows, core * half : (core + 1) * half
            ]


def both_shares(place_ref, share):
    core = place_ref[0]
    mine = pl.ds(pl.multiple_of(core * share, share), share)
    theirs = pl.ds(pl.multiple_of((1 - core) * share, share), share)
    return mine, theirs


def split_rows(place_ref, value, scratch_ref, keep_ref, send_ref):
    core = place_ref[0]
    scratch_ref[...] = value.reshape(scratch_ref.shape)
    keep_ref[...] = scratch_ref[:, core]
    send_ref[...] = scratch_ref[:, 1 - core]


def store_sums(sum_ref, sums):
    rows = sum_ref.shape[0]
    sum_ref[...] = jnp.concatenate(sums + [jnp.zeros((rows - len(sums), 128), F32)], axis=0)


def copy_into(pairs, done):
    return [
        pltpu.make_async_copy(source, target, done.at[at])
        for at, (source, target) in enumerate(pairs)
    ]


def first_column_kernel(
    place_ref,
    table_ref,
    field_hbm,
    turned_hbm,
    basis_hbm,
    kernel_hbm,
    second_hbm,
    tall_ref,
    *refs,
):
    wide_refs, refs, outs = refs[:-13], refs[-7:], refs[-13:-7]
    start_ref, weight_ref, column_ref, keep_ref, send_ref, sum_ref = outs
    turned_ref, basis_ref, kernel_ref, second_ref, scratch_ref, field_ref, done = refs
    quarter = turned_ref.shape[0] // 4
    quarters = [pl.ds(at * quarter, quarter) for at in range(4)]
    copies = copy_into(
        (
            (field_hbm, field_ref),
            *((turned_hbm.at[rows], turned_ref.at[rows]) for rows in quarters),
            (basis_hbm, basis_ref),
            (kernel_hbm, kernel_ref),
            (second_hbm, second_ref),
        ),
        done,
    )
    for copy in copies[:5]:
        copy.start()
    mean = functools.reduce(jnp.add, [table_ref[at] for at in range(NCLASS)]) * (1.0 / NCLASS)
    height, width = start_ref.shape
    planes = len(wide_refs)
    part = wide_refs[0].shape[1]
    for block in range(width // part):
        wanted = place_ref[0] * (width // part) + block
        wide = jnp.zeros((1, part), F32)
        for by, wide_ref in enumerate(wide_refs):
            here = (place_ref[2] + planes - by) % planes == wanted
            wide = jnp.where(here, wide_ref[...], wide)
        for at in range(0, part, 128):
            lanes = slice(block * part + at, block * part + at + 128)
            weight_ref[:, lanes] = 1.0 / (tall_ref[...] * wide[:, at : at + 128] + mean)
    copies[0].wait()
    field = field_ref[...].reshape(height, width)
    both = side_by_side(field)
    parts = []
    for copy, rows in zip(copies[1:5], quarters):
        copy.wait()
        parts.append(times_both(turned_ref[rows, :], both))
    for copy in copies[5:]:
        copy.start()
    spectral = jnp.concatenate(parts, axis=0)
    weighted = spectral * weight_ref[...]
    start_ref[...] = field
    store_sums(sum_ref, [fold(spectral * weighted)])
    copies[5].wait()
    column = times_left(basis_ref[...], weighted)
    column_ref[...] = column
    split_rows(place_ref, column, scratch_ref, keep_ref, send_ref)
    copies[6].wait()
    copies[7].wait()


def next_column_kernel(
    place_ref,
    held_ref,
    got_ref,
    start_ref,
    weight_ref,
    turned_ref,
    basis_ref,
    own_ref,
    other_ref,
    column_ref,
    keep_ref,
    send_ref,
    sum_ref,
    scratch_ref,
):
    core = place_ref[0]
    scratch_ref[:, core] = held_ref[...]
    scratch_ref[:, 1 - core] = got_ref[...]
    total = jnp.sum(own_ref[...] + other_ref[...], axis=1, keepdims=True)
    gamma, curvature = total[0:1], total[1:2]
    proper = (gamma > 0) & (curvature > 0)
    step = jnp.where(proper, gamma / jnp.where(proper, curvature, 1.0), 1.0)
    field = start_ref[...] - step * scratch_ref[...].reshape(start_ref.shape)
    spectral = times_left(turned_ref[...], field)
    weighted = spectral * weight_ref[...]
    store_sums(sum_ref, [fold(spectral * weighted), jnp.broadcast_to(step, (1, 128))])
    column = times_left(basis_ref[...], weighted)
    column_ref[...] = column
    split_rows(place_ref, column, scratch_ref, keep_ref, send_ref)


def column_image_kernel(place_ref, column_ref, kernel_ref, keep_ref, send_ref, scratch_ref):
    image = times_left(kernel_ref[...], column_ref[...])
    split_rows(place_ref, image, scratch_ref, keep_ref, send_ref)


def first_column_image_kernel(place_ref, column_ref, kernel_ref, *refs):
    parts, (keep_ref, send_ref, noise_ref, scratch_ref, done) = refs[:-5], refs[-5:]
    planes = len(parts) // 2
    samples = noise_ref.shape[0] // planes
    pairs = []
    for by in range(planes):
        row = (place_ref[2] + planes - by) % planes
        for at, part in enumerate((parts[by], parts[planes + by])):
            block = row * samples + (place_ref[1] + at) % samples
            pairs.append((part, noise_ref.at[block]))
    copies = copy_into(pairs, done)
    for copy in copies:
        copy.start()
    column_image_kernel(place_ref, column_ref, kernel_ref, keep_ref, send_ref, scratch_ref)
    for copy in copies:
        copy.wait()


def join_columns(place_ref, scratch_ref, keep_ref, got_ref):
    height, width = scratch_ref.shape
    mine, theirs = both_shares(place_ref, width // 2)
    scratch_ref[:, mine] = keep_ref[...].reshape(height, width // 2)
    scratch_ref[:, theirs] = got_ref[...].reshape(height, width // 2)
    return scratch_ref[...]


def row_kernel(place_ref, keep_ref, got_ref, basis_ref, z_ref, scratch_ref):
    field = join_columns(place_ref, scratch_ref, keep_ref, got_ref)
    z_ref[...] = times_right(field, basis_ref[...], 1).reshape(z_ref.shape)


def row_image(place_ref, keep_ref, got_ref, high_ref, low_ref, scratch_ref):
    field = join_columns(place_ref, scratch_ref, keep_ref, got_ref)
    high, low = split(field)
    dims = (((1,), (1,)), ((), ()))
    both = jnp.concatenate([high, low], axis=0)
    result = lax.dot_general(both, high_ref[...], dims, preferred_element_type=F32)
    small = lax.dot_general(high, low_ref[...], dims, preferred_element_type=F32)
    return result[: field.shape[0]] + (result[field.shape[0] :] + small)


def first_row_kernel(place_ref, keep_ref, got_ref, basis_ref, high_hbm, low_hbm, *refs):
    z_ref, high_ref, low_ref, scratch_ref, done = refs
    copies = copy_into(((high_hbm, high_ref), (low_hbm, low_ref)), done)
    for copy in copies:
        copy.start()
    row_kernel(place_ref, keep_ref, got_ref, basis_ref, z_ref, scratch_ref)
    for copy in copies:
        copy.wait()


def full_image(place_ref, keep_ref, got_ref, z_ref, noise_ref, high_ref, low_ref, image_ref, scratch_ref):
    image = row_image(place_ref, keep_ref, got_ref, high_ref, low_ref, scratch_ref)
    field = z_ref[...].reshape(image.shape)
    image = image + noise_ref[...].reshape(image.shape) * field
    image_ref[...] = image.reshape(image_ref.shape)
    return fold(field * image)


def first_image_kernel(
    place_ref,
    keep_ref,
    got_ref,
    z_ref,
    noise_ref,
    high_ref,
    low_ref,
    one_ref,
    image_ref,
    sum_ref,
    scratch_ref,
):
    refs = (place_ref, keep_ref, got_ref, z_ref, noise_ref, high_ref, low_ref)
    store_sums(sum_ref, [one_ref[0:1], full_image(*refs, image_ref, scratch_ref)])


def return_kernel(whose, place_ref, image_ref, basis_ref, out_ref):
    lanes = both_shares(place_ref, out_ref.shape[2])[whose]
    image = image_ref[...].reshape(-1, basis_ref.shape[0])
    out_ref[...] = times_right(image, basis_ref[:, lanes], 0).reshape(out_ref.shape)


def last_image_kernel(
    place_ref,
    keep_ref,
    got_ref,
    z_ref,
    noise_ref,
    high_ref,
    low_ref,
    one_ref,
    two_ref,
    image_ref,
    sum_ref,
    scratch_ref,
):
    refs = (place_ref, keep_ref, got_ref, z_ref, noise_ref, high_ref, low_ref)
    last = full_image(*refs, image_ref, scratch_ref)
    rows = [one_ref[0:2], two_ref[0:1], last, two_ref[1:2], jnp.zeros((3, 128), F32)]
    sum_ref[...] = jnp.broadcast_to(jnp.concatenate(rows, axis=0)[None], sum_ref.shape)


def combine_kernel(place_ref, sum_ref, z_ref, image_ref, f_ref, f_image_ref, out_ref):
    devices, kinds, lanes = sum_ref.shape
    pairs = devices // 2
    total = jnp.sum(sum_ref[...], axis=2, keepdims=True)
    total = jnp.sum(total.reshape(pairs, 2, kinds, 1), axis=1)
    g00, g01, g11, h11, step = (total[:, at : at + 1] for at in range(5))
    step = step * (1.0 / (2 * lanes))

    def over_pairs(value):
        return jnp.sum(value, axis=0, keepdims=True)

    gamma = over_pairs(g00)
    alpha = gamma / over_pairs(g01)
    theta = alpha / step
    rest = 1.0 - theta
    gamma_new = over_pairs(rest * rest * g00 + theta * theta * g11)
    turn = rest + gamma_new / gamma
    curvature = over_pairs(
        turn * turn * g01 - 2.0 * theta * turn * g11 / step + theta * theta * h11
    )
    alpha_new = gamma_new / curvature
    own = lax.broadcasted_iota(jnp.int32, theta.shape, 0) == place_ref[3]
    on_z = over_pairs(jnp.where(own, alpha + alpha_new * turn, 0.0))
    on_f = over_pairs(jnp.where(own, alpha_new * theta, 0.0))
    share = z_ref.shape[1]
    out_ref[:, :share, :] = on_z * z_ref[...] + on_f * f_ref[...]
    out_ref[:, share:, :] = on_z * image_ref[...] + on_f * f_image_ref[...]


def finish_kernel(got_ref, right_ref, solution_ref, residual_ref):
    samples = got_ref.shape[0]
    rows = got_ref.shape[1] // 2
    for sample in range(samples):
        solution_ref[sample, 0] = got_ref[sample, :rows, :]
        residual_ref[sample, 0] = right_ref[sample, 0] - got_ref[sample, rows:, :]


def paired_body(
    right_side,
    classes,
    noise_table,
    kernel_first,
    kernel_second,
    basis_first,
    basis_second,
    eigen_first,
    eigen_second,
):
    groups = lax.axis_size("mode")
    samples, planes, rows, width = right_side.shape
    height = groups * rows
    cores = 2
    half = width // cores
    blocks = groups // cores
    unit = cores * samples
    index = lax.axis_index("mode")
    core = index % cores
    sample = (index // cores) % samples
    plane = index // unit
    place = jnp.stack([core, sample, plane, index // cores]).astype(jnp.int32)

    def shape_of(*shape):
        return jax.ShapeDtypeStruct(shape, F32)

    smem = pl.BlockSpec(memory_space=pltpu.SMEM)

    hbm = pl.BlockSpec(memory_space=pltpu.HBM)

    def full(*shape):
        return pl.BlockSpec(
            shape, lambda *at: (0,) * len(shape), pipeline_mode=pl.Buffered(1)
        )

    def whole_out(*shape):
        return pl.BlockSpec(shape, lambda *at: (0,) * len(shape))

    core_swap = [(at, at ^ 1) for at in range(groups)]
    sample_swap = [(at, at ^ cores) for at in range(groups)]

    def in_hbm(value):
        return pltpu.with_memory_space_constraint(value, pltpu.HBM)

    def noise_of(shifts):
        return pl.pallas_call(
            functools.partial(noise_kernel, shifts, unit),
            grid=(1,),
            in_specs=[smem, pl.BlockSpec(memory_space=pltpu.HBM)],
            out_specs=[whole_out(rows, width)] * len(shifts),
            out_shape=[shape_of(rows, width)] * len(shifts),
            scratch_shapes=[
                pltpu.VMEM((len(shifts), rows, width), jnp.int32),
                pltpu.SemaphoreType.DMA((len(shifts),)),
            ],
            compiler_params=params(1, 4),
        )(in_hbm(noise_table), in_hbm(classes))

    def plane_shift(value, by):
        pairs = [(at, (at + by * unit) % groups) for at in range(groups)]
        return lax.ppermute(value, "mode", pairs)

    ahead = planes // 2
    others = [by for by in range(planes) if by != ahead]
    near = [None] * planes
    near[ahead] = plane_shift(noise_of([ahead])[0], ahead)
    rest = noise_of(others)
    for by, value in zip(others, rest):
        near[by] = plane_shift(value, by) if by else value
    far = [lax.ppermute(value, "mode", sample_swap) for value in near]
    noise = (*near, *far)

    outgoing = pl.pallas_call(
        outgoing_kernel,
        grid=(planes,),
        in_specs=[
            pl.BlockSpec((samples, 1, rows, width), lambda p: (0, p, 0, 0)),
            full(width, width),
        ],
        out_specs=pl.BlockSpec((1, samples, cores, rows, half), lambda p: (p, 0, 0, 0, 0)),
        out_shape=shape_of(planes, samples, cores, rows, half),
        compiler_params=params(1, 56),
        name="outgoing",
    )(right_side, basis_second)
    arrived = lax.all_to_all(
        outgoing.reshape(groups, rows, half), "mode", split_axis=0, concat_axis=0, tiled=True
    )

    eigen = eigen_second.reshape(1, -1)
    for reach in (1, cores):
        other = lax.ppermute(eigen, "mode", [(at, at ^ reach) for at in range(groups)])
        low = (index // reach) % 2 == 0
        eigen = jnp.where(
            low,
            jnp.concatenate([eigen, other], axis=1),
            jnp.concatenate([other, eigen], axis=1),
        )
    eigen = pl.pallas_call(
        follow_kernel,
        in_specs=[pl.BlockSpec(memory_space=pltpu.VMEM)]
        + [pl.BlockSpec(memory_space=pl.ANY)] * (planes - 1),
        out_specs=pl.BlockSpec(memory_space=pltpu.VMEM),
        out_shape=shape_of(*eigen.shape),
        compiler_params=pltpu.CompilerParams(vmem_limit_bytes=1024 * 1024),
        name="follow",
    )(eigen, *near[1:])
    shifted = [eigen] + [
        lax.ppermute(eigen, "mode", [(at, (at + by * unit) % groups) for at in range(groups)])
        for by in range(1, planes)
    ]
    bf16_square = jax.ShapeDtypeStruct((height, height), BF16)
    turned, high, low, tall_eigen = pl.pallas_call(
        prepare_kernel,
        grid=(1,),
        in_specs=[full(height, height), full(width, width), full(width, width), full(1, height)]
        + [pl.BlockSpec(memory_space=pl.ANY)],
        out_specs=[whole_out(height, height)] * 3 + [whole_out(height, 128)],
        out_shape=[bf16_square] * 3 + [shape_of(height, 128)],
        compiler_params=params(1, 24),
        name="prepare",
    )(basis_first, basis_second, kernel_second, eigen_first.reshape(1, -1), eigen)

    def swap(value):
        return lax.ppermute(value, "mode", core_swap)

    def call(kernel, inputs, shapes, scratch_shape, specs=None, more=(), mebibytes=12, matrices=0):
        return pl.pallas_call(
            kernel,
            grid=(1,),
            in_specs=specs or [smem] + [full(*value.shape) for value in inputs[1:]],
            out_specs=[whole_out(*shape) for shape in shapes]
            + [whole_out(height, height)] * matrices,
            out_shape=[shape_of(*shape) for shape in shapes] + [bf16_square] * matrices,
            scratch_shapes=[*([pltpu.VMEM(scratch_shape, F32)] if scratch_shape else []), *more],
            compiler_params=params(1, mebibytes),
        )(*inputs)

    tile = (height, half)
    piece = (blocks, rows, half)
    whole = (blocks, rows, width)
    by_rows = (blocks, cores, rows, half)
    flat = (blocks * rows, width)
    sums_shape = (8, 128)

    (start, weights, column, keep, send, sum_one, turned, *squares) = call(
        first_column_kernel,
        (
            place,
            noise_table,
            *(
                in_hbm(value)
                for value in (arrived, turned, basis_first, kernel_first, basis_second)
            ),
            tall_eigen,
            *shifted,
        ),
        (tile, tile, tile, piece, piece, sums_shape),
        by_rows,
        [smem, smem]
        + [hbm] * 5
        + [full(height, 128)]
        + [full(*value.shape) for value in shifted],
        [pltpu.VMEM((groups, rows, half), F32), pltpu.SemaphoreType.DMA((8,))],
        16,
        4,
    )
    basis_first, kernel_first, basis_second = squares
    got = swap(send)
    image_keep, image_send, noise = call(
        first_column_image_kernel,
        (place, column, kernel_first, *(in_hbm(value) for value in noise)),
        (piece, piece, whole),
        by_rows,
        [smem, full(*tile), full(height, height)] + [hbm] * len(noise),
        [pltpu.SemaphoreType.DMA((len(noise),))],
    )
    image_got = swap(image_send)
    inputs = (place, keep, got, basis_second)
    z_field, high, low = call(
        first_row_kernel,
        (*inputs, in_hbm(high), in_hbm(low)),
        (whole,),
        flat,
        [smem] + [full(*value.shape) for value in inputs[1:]] + [hbm] * 2,
        [pltpu.SemaphoreType.DMA((2,))],
        matrices=2,
    )
    image, pair_sum = call(
        first_image_kernel,
        (place, image_keep, image_got, z_field, noise, high, low, sum_one),
        (whole, sums_shape),
        flat,
    )
    pair_other = swap(pair_sum)

    def give_back(whose):
        kernel = functools.partial(return_kernel, whose)
        return call(kernel, (place, image, basis_second), (piece,), None)[0]

    back_send = give_back(1)
    back_keep = give_back(0)
    back_got = swap(back_send)

    column, keep, send, sum_two = call(
        next_column_kernel,
        (
            place,
            back_keep,
            back_got,
            start,
            weights,
            turned,
            basis_first,
            pair_sum,
            pair_other,
        ),
        (tile, piece, piece, sums_shape),
        by_rows,
    )
    got = swap(send)
    image_keep, image_send = call(
        column_image_kernel, (place, column, kernel_first), (piece, piece), by_rows
    )
    image_got = swap(image_send)
    (f_field,) = call(row_kernel, (place, keep, got, basis_second), (whole,), flat)
    f_image, sums = call(
        last_image_kernel,
        (
            place,
            image_keep,
            image_got,
            f_field,
            noise,
            high,
            low,
            pair_sum,
            sum_two,
        ),
        (whole, (groups, 8, 128)),
        flat,
    )
    sums = lax.all_to_all(sums, "mode", split_axis=0, concat_axis=0, tiled=True)

    few = blocks
    few_spec = pl.BlockSpec((few, rows, width), lambda i: (i, 0, 0))
    answer = pl.pallas_call(
        combine_kernel,
        grid=(1,),
        in_specs=[smem, full(groups, 8, 128)] + [few_spec] * 4,
        out_specs=pl.BlockSpec((few, 2 * rows, width), lambda i: (i, 0, 0)),
        out_shape=shape_of(blocks, 2 * rows, width),
        compiler_params=params(1, 6),
        name="combine",
    )(place, sums, z_field, image, f_field, f_image)
    answer = lax.all_to_all(
        answer,
        "mode",
        split_axis=0,
        concat_axis=0,
        axis_index_groups=[list(range(at, groups, cores)) for at in range(cores)],
        tiled=True,
    )

    block = pl.BlockSpec((samples, 1, rows, width), lambda p: (0, p, 0, 0))
    return tuple(
        pl.pallas_call(
            finish_kernel,
            grid=(planes,),
            in_specs=[
                pl.BlockSpec((samples, 2 * rows, width), lambda p: (p, 0, 0)),
                block,
            ],
            out_specs=[block, block],
            out_shape=[shape_of(*right_side.shape)] * 2,
            compiler_params=params(1, 10),
            name="finish",
        )(answer, right_side)
    )


def body(right_side, classes, *rest):
    groups = lax.axis_size("mode")
    samples, planes, rows, width = right_side.shape
    paired = (
        groups == 2 * samples * planes
        and samples == 2
        and rows % 8 == 0
        and width % 512 == 0
        and planes % 2 == 0
    )
    chosen = paired_body if paired else general_body
    return chosen(right_side, classes, *rest)


def solution(mesh):
    in_specs = (
        P(None, "blocks", "mode", None),
        P("blocks", "mode", None),
        P(),
        P(),
        P(),
        P(),
        P(),
        P(),
        P("mode"),
    )
    out_specs = (P(None, "blocks", "mode", None), P(None, "blocks", "mode", None))
    return jax.shard_map(body, mesh=mesh, in_specs=in_specs, out_specs=out_specs, check_vma=False)
```

```python
import functools

import jax
import jax.numpy as jnp
from jax import lax
from jax.experimental import pallas as pl
from jax.experimental.pallas import tpu as pltpu
from jax.sharding import PartitionSpec as P


NCLASS = 8
ITERS = 2
F32 = jnp.float32
BF16 = jnp.bfloat16


def along_rows(matrix, field):
    return jnp.einsum("jk,sprk->sprj", matrix, field, precision=lax.Precision.HIGHEST)


def rows_to_send(matrix, field, groups):
    result = jnp.einsum("kj,sprk->jspr", matrix, field, precision=lax.Precision.HIGHEST)
    return result.reshape(groups, -1)


def received_to_columns(matrix, received, shape5):
    groups, _, _, _, rows = shape5
    block = received.reshape(shape5)
    reshaped = matrix.reshape(groups, rows, matrix.shape[1])
    return jnp.einsum("mri,mcspr->cspi", reshaped, block, precision=lax.Precision.HIGHEST)


def along_columns(matrix, columns):
    return jnp.einsum("ik,cspk->cspi", matrix, columns, precision=lax.Precision.HIGHEST)


def columns_to_send(matrix, columns, groups, rows):
    reshaped = matrix.reshape(groups, rows, matrix.shape[1])
    result = jnp.einsum("mrk,cspk->mcspr", reshaped, columns, precision=lax.Precision.HIGHEST)
    return result.reshape(groups, -1)


def received_to_rows(matrix, received, shape5):
    groups, cols, _, _, _ = shape5
    block = received.reshape(shape5)
    reshaped = matrix.reshape(matrix.shape[0], groups, cols)
    return jnp.einsum("jmc,mcspr->sprj", reshaped, block, precision=lax.Precision.HIGHEST)


def general_body(
    right_side,
    classes,
    noise_table,
    kernel_first,
    kernel_second,
    basis_first,
    basis_second,
    eigen_first,
    eigen_second,
):
    groups = lax.axis_size("mode")
    samples, planes, rows, _ = right_side.shape
    cols = eigen_second.shape[0]
    shape5 = (groups, cols, samples, planes, rows)
    kern_one = kernel_first.astype(F32)
    kern_two = kernel_second.astype(F32)
    base_one = basis_first.astype(F32)
    base_two = basis_second.astype(F32)
    noise = jnp.zeros(classes.shape, F32)
    for level in range(NCLASS):
        noise = noise + jnp.where(classes == level, noise_table[level], 0.0)
    noise = noise[None]
    mean_noise = jnp.mean(noise_table)
    col_weights = 1.0 / (eigen_second[:, None] * eigen_first[None, :] + mean_noise)
    col_weights = col_weights[:, None, None, :]

    def exchange(outgoing):
        return lax.all_to_all(outgoing, "mode", split_axis=0, concat_axis=0, tiled=True)

    def precond_apply(field):
        incoming = exchange(rows_to_send(base_two, field, groups))
        weighted = received_to_columns(base_one, incoming, shape5) * col_weights
        columns = along_columns(base_one, weighted)
        back = exchange(columns_to_send(base_one, weighted, groups, rows))
        kernel_back = exchange(columns_to_send(kern_one, columns, groups, rows))
        z_field = received_to_rows(base_two, back, shape5)
        image = (
            along_rows(kern_two, received_to_rows(base_two, kernel_back, shape5)) + noise * z_field
        )
        return (z_field, image)

    def inner(left, right):
        return lax.psum(jnp.sum(left * right), "mode")

    solution_field = jnp.zeros_like(right_side)
    residual = right_side
    z_field, image = precond_apply(residual)
    direction, along = (z_field, image)
    gamma = inner(residual, z_field)
    for step in range(ITERS):
        alpha = gamma / inner(direction, along)
        solution_field = solution_field + alpha * direction
        residual = residual - alpha * along
        if step + 1 < ITERS:
            z_field, image = precond_apply(residual)
            gamma_new = inner(residual, z_field)
            ratio = gamma_new / gamma
            direction = z_field + ratio * direction
            along = image + ratio * along
            gamma = gamma_new
    return (solution_field, residual)


def split(value):
    high = value.astype(BF16)
    low = (value - high.astype(F32)).astype(BF16)
    return high, low


def times_right(value, matrix, contract):
    high, low = split(value)
    dims = (((1,), (contract,)), ((), ()))
    both = jnp.concatenate([high, low], axis=0)
    result = lax.dot_general(both, matrix, dims, preferred_element_type=F32)
    return result[: value.shape[0]] + result[value.shape[0] :]


def times_left(matrix, value):
    high, low = split(value)
    dims = (((1,), (0,)), ((), ()))
    both = jnp.concatenate([high, low], axis=1)
    result = lax.dot_general(matrix, both, dims, preferred_element_type=F32)
    return result[:, : value.shape[1]] + result[:, value.shape[1] :]


def fold(value):
    total = jnp.sum(value, axis=0, keepdims=True)
    return functools.reduce(
        jnp.add, [total[:, at : at + 128] for at in range(0, total.shape[1], 128)]
    )


def params(dims, mebibytes):
    return pltpu.CompilerParams(
        dimension_semantics=("arbitrary",) * dims, vmem_limit_bytes=mebibytes * 1024 * 1024
    )


def noise_kernel(shifts, unit, table_ref, class_hbm, *refs):
    out_refs, (class_ref, done) = refs[:-2], refs[-2:]
    planes = class_hbm.shape[0]
    plane = lax.axis_index("mode") // unit
    copies = [
        pltpu.make_async_copy(class_hbm.at[(plane + by) % planes], class_ref.at[at], done.at[at])
        for at, by in enumerate(shifts)
    ]
    for copy in copies:
        copy.start()
    for at, copy in enumerate(copies):
        copy.wait()
        level = class_ref[at]
        noise = jnp.full(level.shape, table_ref[0], F32)
        for index in range(1, NCLASS):
            noise = jnp.where(level == index, table_ref[index], noise)
        out_refs[at][...] = noise


def join_kernel(place_ref, value_ref, *refs):
    parts, (joined_ref, out_ref) = refs[:-2], refs[-2:]
    planes = len(parts)
    for by, part in enumerate(parts):
        joined_ref[(place_ref[2] + planes - by) % planes] = part[...]
    out_ref[...] = value_ref[...]


def prepare_kernel(
    first_ref, second_ref, kernel_ref, eigen_ref, _, turned_ref, high_ref, low_ref, tall_ref
):
    turned_ref[...] = first_ref[...].T
    tall_ref[...] = jnp.broadcast_to(eigen_ref[...], tall_ref.shape[::-1]).T
    dims = (((1,), (0,)), ((), ()))
    product = lax.dot_general(
        kernel_ref[...], second_ref[...], dims, preferred_element_type=F32
    )
    high_ref[...], low_ref[...] = split(product)


def outgoing_kernel(right_ref, basis_ref, out_ref):
    samples, _, rows, width = right_ref.shape
    cores = out_ref.shape[2]
    half = width // cores
    field = right_ref[...].reshape(samples * rows, width)
    mapped = times_right(field, basis_ref[...], 0)
    for sample in range(samples):
        for core in range(cores):
            out_ref[0, sample, core] = mapped[
                sample * rows : (sample + 1) * rows, core * half : (core + 1) * half
            ]


def both_shares(place_ref, share):
    core = place_ref[0]
    mine = pl.ds(pl.multiple_of(core * share, share), share)
    theirs = pl.ds(pl.multiple_of((1 - core) * share, share), share)
    return mine, theirs


def split_rows(place_ref, value, scratch_ref, keep_ref, send_ref):
    core = place_ref[0]
    scratch_ref[...] = value.reshape(scratch_ref.shape)
    keep_ref[...] = scratch_ref[:, core]
    send_ref[...] = scratch_ref[:, 1 - core]


def store_sums(sum_ref, sums):
    rows = sum_ref.shape[0]
    sum_ref[...] = jnp.concatenate(sums + [jnp.zeros((rows - len(sums), 128), F32)], axis=0)


def copy_into(pairs, done):
    return [
        pltpu.make_async_copy(source, target, done.at[at])
        for at, (source, target) in enumerate(pairs)
    ]


def first_column_kernel(
    place_ref,
    table_ref,
    field_hbm,
    turned_hbm,
    basis_hbm,
    kernel_hbm,
    second_hbm,
    tall_ref,
    *refs,
):
    wide_refs, refs, outs = refs[:-13], refs[-7:], refs[-13:-7]
    start_ref, weight_ref, column_ref, keep_ref, send_ref, sum_ref = outs
    turned_ref, basis_ref, kernel_ref, second_ref, scratch_ref, field_ref, done = refs
    copies = copy_into(
        (
            (field_hbm, field_ref),
            (turned_hbm, turned_ref),
            (basis_hbm, basis_ref),
            (kernel_hbm, kernel_ref),
            (second_hbm, second_ref),
        ),
        done,
    )
    for copy in copies[:2]:
        copy.start()
    mean = functools.reduce(jnp.add, [table_ref[at] for at in range(NCLASS)]) * (1.0 / NCLASS)
    height, width = start_ref.shape
    planes = len(wide_refs)
    part = wide_refs[0].shape[1]
    for block in range(width // part):
        wanted = place_ref[0] * (width // part) + block
        wide = jnp.zeros((1, part), F32)
        for by, wide_ref in enumerate(wide_refs):
            here = (place_ref[2] + planes - by) % planes == wanted
            wide = jnp.where(here, wide_ref[...], wide)
        for at in range(0, part, 128):
            lanes = slice(block * part + at, block * part + at + 128)
            weight_ref[:, lanes] = 1.0 / (tall_ref[...] * wide[:, at : at + 128] + mean)
    copies[0].wait()
    field = field_ref[...].reshape(height, width)
    copies[1].wait()
    for copy in copies[2:]:
        copy.start()
    spectral = times_left(turned_ref[...], field)
    weighted = spectral * weight_ref[...]
    start_ref[...] = field
    store_sums(sum_ref, [fold(spectral * weighted)])
    copies[2].wait()
    column = times_left(basis_ref[...], weighted)
    column_ref[...] = column
    split_rows(place_ref, column, scratch_ref, keep_ref, send_ref)
    copies[3].wait()
    copies[4].wait()


def next_column_kernel(
    place_ref,
    held_ref,
    got_ref,
    start_ref,
    weight_ref,
    turned_ref,
    basis_ref,
    own_ref,
    other_ref,
    column_ref,
    keep_ref,
    send_ref,
    sum_ref,
    scratch_ref,
):
    core = place_ref[0]
    scratch_ref[:, core] = held_ref[...]
    scratch_ref[:, 1 - core] = got_ref[...]
    total = jnp.sum(own_ref[...] + other_ref[...], axis=1, keepdims=True)
    gamma, curvature = total[0:1], total[1:2]
    proper = (gamma > 0) & (curvature > 0)
    step = jnp.where(proper, gamma / jnp.where(proper, curvature, 1.0), 1.0)
    field = start_ref[...] - step * scratch_ref[...].reshape(start_ref.shape)
    spectral = times_left(turned_ref[...], field)
    weighted = spectral * weight_ref[...]
    store_sums(sum_ref, [fold(spectral * weighted), jnp.broadcast_to(step, (1, 128))])
    column = times_left(basis_ref[...], weighted)
    column_ref[...] = column
    split_rows(place_ref, column, scratch_ref, keep_ref, send_ref)


def column_image_kernel(place_ref, column_ref, kernel_ref, keep_ref, send_ref, scratch_ref):
    image = times_left(kernel_ref[...], column_ref[...])
    split_rows(place_ref, image, scratch_ref, keep_ref, send_ref)


def first_column_image_kernel(place_ref, column_ref, kernel_ref, high_hbm, low_hbm, *refs):
    keep_ref, send_ref, high_ref, low_ref, scratch_ref, done = refs
    copies = copy_into(((high_hbm, high_ref), (low_hbm, low_ref)), done)
    for copy in copies:
        copy.start()
    column_image_kernel(place_ref, column_ref, kernel_ref, keep_ref, send_ref, scratch_ref)
    for copy in copies:
        copy.wait()


def join_columns(place_ref, scratch_ref, keep_ref, got_ref):
    height, width = scratch_ref.shape
    mine, theirs = both_shares(place_ref, width // 2)
    scratch_ref[:, mine] = keep_ref[...].reshape(height, width // 2)
    scratch_ref[:, theirs] = got_ref[...].reshape(height, width // 2)
    return scratch_ref[...]


def row_kernel(place_ref, keep_ref, got_ref, basis_ref, z_ref, scratch_ref):
    field = join_columns(place_ref, scratch_ref, keep_ref, got_ref)
    z_ref[...] = times_right(field, basis_ref[...], 1).reshape(z_ref.shape)


def row_image(place_ref, keep_ref, got_ref, high_ref, low_ref, scratch_ref):
    field = join_columns(place_ref, scratch_ref, keep_ref, got_ref)
    high, low = split(field)
    dims = (((1,), (1,)), ((), ()))
    both = jnp.concatenate([high, low], axis=0)
    result = lax.dot_general(both, high_ref[...], dims, preferred_element_type=F32)
    small = lax.dot_general(high, low_ref[...], dims, preferred_element_type=F32)
    return result[: field.shape[0]] + (result[field.shape[0] :] + small)


def first_row_kernel(place_ref, keep_ref, got_ref, basis_ref, near_hbm, far_hbm, *refs):
    z_ref, noise_ref, scratch_ref, done = refs
    sample = place_ref[1]
    copies = copy_into(
        ((near_hbm, noise_ref.at[:, sample]), (far_hbm, noise_ref.at[:, 1 - sample])), done
    )
    for copy in copies:
        copy.start()
    row_kernel(place_ref, keep_ref, got_ref, basis_ref, z_ref, scratch_ref)
    for copy in copies:
        copy.wait()


def full_image(place_ref, keep_ref, got_ref, z_ref, noise_ref, high_ref, low_ref, image_ref, scratch_ref):
    image = row_image(place_ref, keep_ref, got_ref, high_ref, low_ref, scratch_ref)
    field = z_ref[...].reshape(image.shape)
    image = image + noise_ref[...].reshape(image.shape) * field
    image_ref[...] = image.reshape(image_ref.shape)
    return fold(field * image)


def first_image_kernel(
    place_ref,
    keep_ref,
    got_ref,
    z_ref,
    noise_ref,
    high_ref,
    low_ref,
    one_ref,
    image_ref,
    sum_ref,
    scratch_ref,
):
    refs = (place_ref, keep_ref, got_ref, z_ref, noise_ref, high_ref, low_ref)
    store_sums(sum_ref, [one_ref[0:1], full_image(*refs, image_ref, scratch_ref)])


def return_kernel(whose, place_ref, image_ref, basis_ref, out_ref):
    lanes = both_shares(place_ref, out_ref.shape[2])[whose]
    image = image_ref[...].reshape(-1, basis_ref.shape[0])
    out_ref[...] = times_right(image, basis_ref[:, lanes], 0).reshape(out_ref.shape)


def last_image_kernel(
    place_ref,
    keep_ref,
    got_ref,
    z_ref,
    noise_ref,
    high_ref,
    low_ref,
    one_ref,
    two_ref,
    image_ref,
    sum_ref,
    scratch_ref,
):
    refs = (place_ref, keep_ref, got_ref, z_ref, noise_ref, high_ref, low_ref)
    last = full_image(*refs, image_ref, scratch_ref)
    rows = [one_ref[0:2], two_ref[0:1], last, two_ref[1:2], jnp.zeros((3, 128), F32)]
    sum_ref[...] = jnp.broadcast_to(jnp.concatenate(rows, axis=0)[None], sum_ref.shape)


def combine_kernel(place_ref, sum_ref, z_ref, image_ref, f_ref, f_image_ref, out_ref):
    devices, kinds, lanes = sum_ref.shape
    pairs = devices // 2
    total = jnp.sum(sum_ref[...], axis=2, keepdims=True)
    total = jnp.sum(total.reshape(pairs, 2, kinds, 1), axis=1)
    g00, g01, g11, h11, step = (total[:, at : at + 1] for at in range(5))
    step = step * (1.0 / (2 * lanes))

    def over_pairs(value):
        return jnp.sum(value, axis=0, keepdims=True)

    gamma = over_pairs(g00)
    alpha = gamma / over_pairs(g01)
    theta = alpha / step
    rest = 1.0 - theta
    gamma_new = over_pairs(rest * rest * g00 + theta * theta * g11)
    turn = rest + gamma_new / gamma
    curvature = over_pairs(
        turn * turn * g01 - 2.0 * theta * turn * g11 / step + theta * theta * h11
    )
    alpha_new = gamma_new / curvature
    own = lax.broadcasted_iota(jnp.int32, theta.shape, 0) == place_ref[3]
    on_z = over_pairs(jnp.where(own, alpha + alpha_new * turn, 0.0))
    on_f = over_pairs(jnp.where(own, alpha_new * theta, 0.0))
    share = z_ref.shape[1]
    out_ref[:, :share, :] = on_z * z_ref[...] + on_f * f_ref[...]
    out_ref[:, share:, :] = on_z * image_ref[...] + on_f * f_image_ref[...]


def finish_kernel(got_ref, right_ref, solution_ref, residual_ref):
    samples = got_ref.shape[0]
    rows = got_ref.shape[1] // 2
    for sample in range(samples):
        solution_ref[sample, 0] = got_ref[sample, :rows, :]
        residual_ref[sample, 0] = right_ref[sample, 0] - got_ref[sample, rows:, :]


def paired_body(
    right_side,
    classes,
    noise_table,
    kernel_first,
    kernel_second,
    basis_first,
    basis_second,
    eigen_first,
    eigen_second,
):
    groups = lax.axis_size("mode")
    samples, planes, rows, width = right_side.shape
    height = groups * rows
    cores = 2
    half = width // cores
    blocks = groups // cores
    unit = cores * samples
    index = lax.axis_index("mode")
    core = index % cores
    sample = (index // cores) % samples
    plane = index // unit
    place = jnp.stack([core, sample, plane, index // cores]).astype(jnp.int32)

    def shape_of(*shape):
        return jax.ShapeDtypeStruct(shape, F32)

    smem = pl.BlockSpec(memory_space=pltpu.SMEM)

    hbm = pl.BlockSpec(memory_space=pltpu.HBM)

    def full(*shape):
        return pl.BlockSpec(
            shape, lambda *at: (0,) * len(shape), pipeline_mode=pl.Buffered(1)
        )

    def whole_out(*shape):
        return pl.BlockSpec(shape, lambda *at: (0,) * len(shape))

    core_swap = [(at, at ^ 1) for at in range(groups)]
    sample_swap = [(at, at ^ cores) for at in range(groups)]

    def in_hbm(value):
        return pltpu.with_memory_space_constraint(value, pltpu.HBM)

    def noise_of(shifts):
        return pl.pallas_call(
            functools.partial(noise_kernel, shifts, unit),
            grid=(1,),
            in_specs=[smem, pl.BlockSpec(memory_space=pltpu.HBM)],
            out_specs=[whole_out(rows, width)] * len(shifts),
            out_shape=[shape_of(rows, width)] * len(shifts),
            scratch_shapes=[
                pltpu.VMEM((len(shifts), rows, width), jnp.int32),
                pltpu.SemaphoreType.DMA((len(shifts),)),
            ],
            compiler_params=params(1, 4),
        )(in_hbm(noise_table), in_hbm(classes))

    def plane_shift(value, by):
        pairs = [(at, (at + by * unit) % groups) for at in range(groups)]
        return lax.ppermute(value, "mode", pairs)

    ahead = planes // 2
    others = [by for by in range(planes) if by != ahead]
    near = [None] * planes
    near[ahead] = plane_shift(noise_of([ahead])[0], ahead)
    rest = noise_of(others)
    for by, value in zip(others, rest):
        near[by] = plane_shift(value, by) if by else value

    outgoing = pl.pallas_call(
        outgoing_kernel,
        grid=(planes,),
        in_specs=[
            pl.BlockSpec((samples, 1, rows, width), lambda p: (0, p, 0, 0)),
            full(width, width),
        ],
        out_specs=pl.BlockSpec((1, samples, cores, rows, half), lambda p: (p, 0, 0, 0, 0)),
        out_shape=shape_of(planes, samples, cores, rows, half),
        compiler_params=params(1, 56),
        name="outgoing",
    )(right_side, basis_second)
    arrived = lax.all_to_all(
        outgoing.reshape(groups, rows, half), "mode", split_axis=0, concat_axis=0, tiled=True
    )

    eigen = eigen_second.reshape(1, -1)
    for reach in (1, cores):
        other = lax.ppermute(eigen, "mode", [(at, at ^ reach) for at in range(groups)])
        low = (index // reach) % 2 == 0
        eigen = jnp.where(
            low,
            jnp.concatenate([eigen, other], axis=1),
            jnp.concatenate([other, eigen], axis=1),
        )
    near, eigen = pl.pallas_call(
        join_kernel,
        grid=(1,),
        in_specs=[smem, full(*eigen.shape)] + [full(rows, width)] * planes,
        out_specs=[whole_out(planes, rows, width), whole_out(*eigen.shape)],
        out_shape=[shape_of(planes, rows, width), shape_of(*eigen.shape)],
        compiler_params=params(1, 58),
        name="join",
    )(place, eigen, *near)
    far = lax.ppermute(near, "mode", sample_swap)
    shifted = [eigen] + [
        lax.ppermute(eigen, "mode", [(at, (at + by * unit) % groups) for at in range(groups)])
        for by in range(1, planes)
    ]
    bf16_square = jax.ShapeDtypeStruct((height, height), BF16)
    prepare = pl.pallas_call(
        prepare_kernel,
        grid=(1,),
        in_specs=[full(height, height), full(width, width), full(width, width), full(1, height)]
        + [pl.BlockSpec(memory_space=pl.ANY)],
        out_specs=[whole_out(height, height)] * 3 + [whole_out(height, 128)],
        out_shape=[bf16_square] * 3 + [shape_of(height, 128)],
        compiler_params=params(1, 24),
        name="prepare",
    )
    turned, high, low, tall_eigen = prepare(
        basis_first, basis_second, kernel_second, eigen_first.reshape(1, -1), eigen
    )

    def swap(value):
        return lax.ppermute(value, "mode", core_swap)

    def call(kernel, inputs, shapes, scratch_shape, specs=None, more=(), mebibytes=12, matrices=0):
        return pl.pallas_call(
            kernel,
            grid=(1,),
            in_specs=specs or [smem] + [full(*value.shape) for value in inputs[1:]],
            out_specs=[whole_out(*shape) for shape in shapes]
            + [whole_out(height, height)] * matrices,
            out_shape=[shape_of(*shape) for shape in shapes] + [bf16_square] * matrices,
            scratch_shapes=[*([pltpu.VMEM(scratch_shape, F32)] if scratch_shape else []), *more],
            compiler_params=params(1, mebibytes),
        )(*inputs)

    tile = (height, half)
    piece = (blocks, rows, half)
    whole = (blocks, rows, width)
    by_rows = (blocks, cores, rows, half)
    flat = (blocks * rows, width)
    sums_shape = (8, 128)

    (start, weights, column, keep, send, sum_one, turned, *squares) = call(
        first_column_kernel,
        (
            place,
            noise_table,
            *(
                in_hbm(value)
                for value in (arrived, turned, basis_first, kernel_first, basis_second)
            ),
            tall_eigen,
            *shifted,
        ),
        (tile, tile, tile, piece, piece, sums_shape),
        by_rows,
        [smem, smem]
        + [hbm] * 5
        + [full(height, 128)]
        + [full(*value.shape) for value in shifted],
        [pltpu.VMEM((groups, rows, half), F32), pltpu.SemaphoreType.DMA((5,))],
        16,
        4,
    )
    basis_first, kernel_first, basis_second = squares
    got = swap(send)
    image_keep, image_send, high, low = call(
        first_column_image_kernel,
        (place, column, kernel_first, in_hbm(high), in_hbm(low)),
        (piece, piece),
        by_rows,
        [smem, full(*tile), full(height, height), hbm, hbm],
        [pltpu.SemaphoreType.DMA((2,))],
        matrices=2,
    )
    image_got = swap(image_send)
    inputs = (place, keep, got, basis_second)
    z_field, noise = call(
        first_row_kernel,
        (*inputs, in_hbm(near), in_hbm(far)),
        (whole, (planes, samples, rows, width)),
        flat,
        [smem] + [full(*value.shape) for value in inputs[1:]] + [hbm] * 2,
        [pltpu.SemaphoreType.DMA((2,))],
    )
    image, pair_sum = call(
        first_image_kernel,
        (place, image_keep, image_got, z_field, noise, high, low, sum_one),
        (whole, sums_shape),
        flat,
    )
    pair_other = swap(pair_sum)

    def give_back(whose):
        kernel = functools.partial(return_kernel, whose)
        return call(kernel, (place, image, basis_second), (piece,), None)[0]

    back_send = give_back(1)
    back_keep = give_back(0)
    back_got = swap(back_send)

    column, keep, send, sum_two = call(
        next_column_kernel,
        (
            place,
            back_keep,
            back_got,
            start,
            weights,
            turned,
            basis_first,
            pair_sum,
            pair_other,
        ),
        (tile, piece, piece, sums_shape),
        by_rows,
    )
    got = swap(send)
    image_keep, image_send = call(
        column_image_kernel, (place, column, kernel_first), (piece, piece), by_rows
    )
    image_got = swap(image_send)
    (f_field,) = call(row_kernel, (place, keep, got, basis_second), (whole,), flat)
    f_image, sums = call(
        last_image_kernel,
        (
            place,
            image_keep,
            image_got,
            f_field,
            noise,
            high,
            low,
            pair_sum,
            sum_two,
        ),
        (whole, (groups, 8, 128)),
        flat,
    )
    sums = lax.all_to_all(sums, "mode", split_axis=0, concat_axis=0, tiled=True)

    few = blocks
    few_spec = pl.BlockSpec((few, rows, width), lambda i: (i, 0, 0))
    answer = pl.pallas_call(
        combine_kernel,
        grid=(1,),
        in_specs=[smem, full(groups, 8, 128)] + [few_spec] * 4,
        out_specs=pl.BlockSpec((few, 2 * rows, width), lambda i: (i, 0, 0)),
        out_shape=shape_of(blocks, 2 * rows, width),
        compiler_params=params(1, 6),
        name="combine",
    )(place, sums, z_field, image, f_field, f_image)
    answer = lax.all_to_all(
        answer,
        "mode",
        split_axis=0,
        concat_axis=0,
        axis_index_groups=[list(range(at, groups, cores)) for at in range(cores)],
        tiled=True,
    )

    block = pl.BlockSpec((samples, 1, rows, width), lambda p: (0, p, 0, 0))
    return tuple(
        pl.pallas_call(
            finish_kernel,
            grid=(planes,),
            in_specs=[
                pl.BlockSpec((samples, 2 * rows, width), lambda p: (p, 0, 0)),
                block,
            ],
            out_specs=[block, block],
            out_shape=[shape_of(*right_side.shape)] * 2,
            compiler_params=params(1, 10),
            name="finish",
        )(answer, right_side)
    )


def body(right_side, classes, *rest):
    groups = lax.axis_size("mode")
    samples, planes, rows, width = right_side.shape
    paired = (
        groups == 2 * samples * planes
        and samples == 2
        and rows % 8 == 0
        and width % 512 == 0
        and planes % 2 == 0
    )
    chosen = paired_body if paired else general_body
    return chosen(right_side, classes, *rest)


def solution(mesh):
    in_specs = (
        P(None, "blocks", "mode", None),
        P("blocks", "mode", None),
        P(),
        P(),
        P(),
        P(),
        P(),
        P(),
        P("mode"),
    )
    out_specs = (P(None, "blocks", "mode", None), P(None, "blocks", "mode", None))
    return jax.shard_map(body, mesh=mesh, in_specs=in_specs, out_specs=out_specs, check_vma=False)
```

```python
import functools

import jax
import jax.numpy as jnp
from jax import lax
from jax.experimental import pallas as pl
from jax.experimental.pallas import tpu as pltpu
from jax.sharding import PartitionSpec as P


NCLASS = 8
ITERS = 2
F32 = jnp.float32
BF16 = jnp.bfloat16


def along_rows(matrix, field):
    return jnp.einsum("jk,sprk->sprj", matrix, field, precision=lax.Precision.HIGHEST)


def rows_to_send(matrix, field, groups):
    result = jnp.einsum("kj,sprk->jspr", matrix, field, precision=lax.Precision.HIGHEST)
    return result.reshape(groups, -1)


def received_to_columns(matrix, received, shape5):
    groups, _, _, _, rows = shape5
    block = received.reshape(shape5)
    reshaped = matrix.reshape(groups, rows, matrix.shape[1])
    return jnp.einsum("mri,mcspr->cspi", reshaped, block, precision=lax.Precision.HIGHEST)


def along_columns(matrix, columns):
    return jnp.einsum("ik,cspk->cspi", matrix, columns, precision=lax.Precision.HIGHEST)


def columns_to_send(matrix, columns, groups, rows):
    reshaped = matrix.reshape(groups, rows, matrix.shape[1])
    result = jnp.einsum("mrk,cspk->mcspr", reshaped, columns, precision=lax.Precision.HIGHEST)
    return result.reshape(groups, -1)


def received_to_rows(matrix, received, shape5):
    groups, cols, _, _, _ = shape5
    block = received.reshape(shape5)
    reshaped = matrix.reshape(matrix.shape[0], groups, cols)
    return jnp.einsum("jmc,mcspr->sprj", reshaped, block, precision=lax.Precision.HIGHEST)


def general_body(
    right_side,
    classes,
    noise_table,
    kernel_first,
    kernel_second,
    basis_first,
    basis_second,
    eigen_first,
    eigen_second,
):
    groups = lax.axis_size("mode")
    samples, planes, rows, _ = right_side.shape
    cols = eigen_second.shape[0]
    shape5 = (groups, cols, samples, planes, rows)
    kern_one = kernel_first.astype(F32)
    kern_two = kernel_second.astype(F32)
    base_one = basis_first.astype(F32)
    base_two = basis_second.astype(F32)
    noise = jnp.zeros(classes.shape, F32)
    for level in range(NCLASS):
        noise = noise + jnp.where(classes == level, noise_table[level], 0.0)
    noise = noise[None]
    mean_noise = jnp.mean(noise_table)
    col_weights = 1.0 / (eigen_second[:, None] * eigen_first[None, :] + mean_noise)
    col_weights = col_weights[:, None, None, :]

    def exchange(outgoing):
        return lax.all_to_all(outgoing, "mode", split_axis=0, concat_axis=0, tiled=True)

    def precond_apply(field):
        incoming = exchange(rows_to_send(base_two, field, groups))
        weighted = received_to_columns(base_one, incoming, shape5) * col_weights
        columns = along_columns(base_one, weighted)
        back = exchange(columns_to_send(base_one, weighted, groups, rows))
        kernel_back = exchange(columns_to_send(kern_one, columns, groups, rows))
        z_field = received_to_rows(base_two, back, shape5)
        image = (
            along_rows(kern_two, received_to_rows(base_two, kernel_back, shape5)) + noise * z_field
        )
        return (z_field, image)

    def inner(left, right):
        return lax.psum(jnp.sum(left * right), "mode")

    solution_field = jnp.zeros_like(right_side)
    residual = right_side
    z_field, image = precond_apply(residual)
    direction, along = (z_field, image)
    gamma = inner(residual, z_field)
    for step in range(ITERS):
        alpha = gamma / inner(direction, along)
        solution_field = solution_field + alpha * direction
        residual = residual - alpha * along
        if step + 1 < ITERS:
            z_field, image = precond_apply(residual)
            gamma_new = inner(residual, z_field)
            ratio = gamma_new / gamma
            direction = z_field + ratio * direction
            along = image + ratio * along
            gamma = gamma_new
    return (solution_field, residual)


def split(value):
    high = value.astype(BF16)
    low = (value - high.astype(F32)).astype(BF16)
    return high, low


def times_right(value, matrix, contract):
    high, low = split(value)
    dims = (((1,), (contract,)), ((), ()))
    both = jnp.concatenate([high, low], axis=0)
    result = lax.dot_general(both, matrix, dims, preferred_element_type=F32)
    return result[: value.shape[0]] + result[value.shape[0] :]


def side_by_side(value):
    return jnp.concatenate(split(value), axis=1)


def times_both(matrix, both):
    width = both.shape[1] // 2
    dims = (((1,), (0,)), ((), ()))
    result = lax.dot_general(matrix, both, dims, preferred_element_type=F32)
    return result[:, :width] + result[:, width:]


def times_left(matrix, value):
    return times_both(matrix, side_by_side(value))


def fold(value):
    total = jnp.sum(value, axis=0, keepdims=True)
    return functools.reduce(
        jnp.add, [total[:, at : at + 128] for at in range(0, total.shape[1], 128)]
    )


def params(dims, mebibytes):
    return pltpu.CompilerParams(
        dimension_semantics=("arbitrary",) * dims, vmem_limit_bytes=mebibytes * 1024 * 1024
    )


def noise_kernel(shifts, unit, table_ref, class_hbm, *refs):
    out_refs, (class_ref, done) = refs[:-2], refs[-2:]
    planes = class_hbm.shape[0]
    plane = lax.axis_index("mode") // unit
    copies = [
        pltpu.make_async_copy(class_hbm.at[(plane + by) % planes], class_ref.at[at], done.at[at])
        for at, by in enumerate(shifts)
    ]
    for copy in copies:
        copy.start()
    for at, copy in enumerate(copies):
        copy.wait()
        level = class_ref[at]
        noise = jnp.full(level.shape, table_ref[0], F32)
        for index in range(1, NCLASS):
            noise = jnp.where(level == index, table_ref[index], noise)
        out_refs[at][...] = noise


def join_kernel(place_ref, value_ref, *refs):
    parts, (joined_ref, out_ref) = refs[:-2], refs[-2:]
    planes = len(parts)
    for by, part in enumerate(parts):
        joined_ref[(place_ref[2] + planes - by) % planes] = part[...]
    out_ref[...] = value_ref[...]


def prepare_kernel(
    first_ref,
    second_ref,
    kernel_ref,
    _,
    upper_ref,
    lower_ref,
    high_ref,
    low_ref,
):
    turned = first_ref[...].T
    middle = upper_ref.shape[0]
    upper_ref[...] = turned[:middle]
    lower_ref[...] = turned[middle:]
    dims = (((1,), (0,)), ((), ()))
    product = lax.dot_general(
        kernel_ref[...], second_ref[...], dims, preferred_element_type=F32
    )
    high_ref[...], low_ref[...] = split(product)


def outgoing_kernel(right_ref, basis_ref, out_ref):
    samples, _, rows, width = right_ref.shape
    cores = out_ref.shape[2]
    half = width // cores
    field = right_ref[...].reshape(samples * rows, width)
    mapped = times_right(field, basis_ref[...], 0)
    for sample in range(samples):
        for core in range(cores):
            out_ref[0, sample, core] = mapped[
                sample * rows : (sample + 1) * rows, core * half : (core + 1) * half
            ]


def both_shares(place_ref, share):
    core = place_ref[0]
    mine = pl.ds(pl.multiple_of(core * share, share), share)
    theirs = pl.ds(pl.multiple_of((1 - core) * share, share), share)
    return mine, theirs


def split_rows(place_ref, value, scratch_ref, keep_ref, send_ref):
    core = place_ref[0]
    scratch_ref[...] = value.reshape(scratch_ref.shape)
    keep_ref[...] = scratch_ref[:, core]
    send_ref[...] = scratch_ref[:, 1 - core]


def store_sums(sum_ref, sums):
    rows = sum_ref.shape[0]
    sum_ref[...] = jnp.concatenate(sums + [jnp.zeros((rows - len(sums), 128), F32)], axis=0)


def copy_into(pairs, done):
    return [
        pltpu.make_async_copy(source, target, done.at[at])
        for at, (source, target) in enumerate(pairs)
    ]


def first_column_kernel(
    place_ref,
    table_ref,
    field_hbm,
    lower_hbm,
    basis_hbm,
    kernel_hbm,
    second_hbm,
    upper_ref,
    eigen_ref,
    *refs,
):
    wide_refs, refs, outs = refs[:-13], refs[-7:], refs[-13:-7]
    start_ref, weight_ref, column_ref, keep_ref, send_ref, sum_ref = outs
    lower_ref, basis_ref, kernel_ref, second_ref, scratch_ref, field_ref, done = refs
    copies = copy_into(
        (
            (field_hbm, field_ref),
            (lower_hbm, lower_ref),
            (basis_hbm, basis_ref),
            (kernel_hbm, kernel_ref),
            (second_hbm, second_ref),
        ),
        done,
    )
    for copy in copies[:2]:
        copy.start()
    mean = functools.reduce(jnp.add, [table_ref[at] for at in range(NCLASS)]) * (1.0 / NCLASS)
    height, width = start_ref.shape
    tall = jnp.broadcast_to(eigen_ref[...], (128, height)).T
    planes = len(wide_refs)
    part = wide_refs[0].shape[1]
    for block in range(width // part):
        wanted = place_ref[0] * (width // part) + block
        wide = jnp.zeros((1, part), F32)
        for by, wide_ref in enumerate(wide_refs):
            here = (place_ref[2] + planes - by) % planes == wanted
            wide = jnp.where(here, wide_ref[...], wide)
        for at in range(0, part, 128):
            lanes = slice(block * part + at, block * part + at + 128)
            weight_ref[:, lanes] = 1.0 / (tall * wide[:, at : at + 128] + mean)
    copies[0].wait()
    field = field_ref[...].reshape(height, width)
    both = side_by_side(field)
    above = times_both(upper_ref[...], both)
    copies[1].wait()
    for copy in copies[2:]:
        copy.start()
    spectral = jnp.concatenate([above, times_both(lower_ref[...], both)], axis=0)
    weighted = spectral * weight_ref[...]
    start_ref[...] = field
    store_sums(sum_ref, [fold(spectral * weighted)])
    copies[2].wait()
    column = times_left(basis_ref[...], weighted)
    column_ref[...] = column
    split_rows(place_ref, column, scratch_ref, keep_ref, send_ref)
    copies[3].wait()
    copies[4].wait()


def next_column_kernel(
    place_ref,
    held_ref,
    got_ref,
    start_ref,
    weight_ref,
    upper_ref,
    lower_ref,
    basis_ref,
    own_ref,
    other_ref,
    column_ref,
    keep_ref,
    send_ref,
    sum_ref,
    scratch_ref,
):
    core = place_ref[0]
    scratch_ref[:, core] = held_ref[...]
    scratch_ref[:, 1 - core] = got_ref[...]
    total = jnp.sum(own_ref[...] + other_ref[...], axis=1, keepdims=True)
    gamma, curvature = total[0:1], total[1:2]
    proper = (gamma > 0) & (curvature > 0)
    step = jnp.where(proper, gamma / jnp.where(proper, curvature, 1.0), 1.0)
    field = start_ref[...] - step * scratch_ref[...].reshape(start_ref.shape)
    both = side_by_side(field)
    halves = [times_both(half_ref[...], both) for half_ref in (upper_ref, lower_ref)]
    spectral = jnp.concatenate(halves, axis=0)
    weighted = spectral * weight_ref[...]
    store_sums(sum_ref, [fold(spectral * weighted), jnp.broadcast_to(step, (1, 128))])
    column = times_left(basis_ref[...], weighted)
    column_ref[...] = column
    split_rows(place_ref, column, scratch_ref, keep_ref, send_ref)


def column_image_kernel(place_ref, column_ref, kernel_ref, keep_ref, send_ref, scratch_ref):
    image = times_left(kernel_ref[...], column_ref[...])
    split_rows(place_ref, image, scratch_ref, keep_ref, send_ref)


def first_column_image_kernel(place_ref, column_ref, kernel_ref, high_hbm, low_hbm, *refs):
    keep_ref, send_ref, high_ref, low_ref, scratch_ref, done = refs
    copies = copy_into(((high_hbm, high_ref), (low_hbm, low_ref)), done)
    for copy in copies:
        copy.start()
    column_image_kernel(place_ref, column_ref, kernel_ref, keep_ref, send_ref, scratch_ref)
    for copy in copies:
        copy.wait()


def join_columns(place_ref, scratch_ref, keep_ref, got_ref):
    height, width = scratch_ref.shape
    mine, theirs = both_shares(place_ref, width // 2)
    scratch_ref[:, mine] = keep_ref[...].reshape(height, width // 2)
    scratch_ref[:, theirs] = got_ref[...].reshape(height, width // 2)
    return scratch_ref[...]


def row_kernel(place_ref, keep_ref, got_ref, basis_ref, z_ref, scratch_ref):
    field = join_columns(place_ref, scratch_ref, keep_ref, got_ref)
    z_ref[...] = times_right(field, basis_ref[...], 1).reshape(z_ref.shape)


def row_image(place_ref, keep_ref, got_ref, high_ref, low_ref, scratch_ref):
    field = join_columns(place_ref, scratch_ref, keep_ref, got_ref)
    high, low = split(field)
    dims = (((1,), (1,)), ((), ()))
    both = jnp.concatenate([high, low], axis=0)
    result = lax.dot_general(both, high_ref[...], dims, preferred_element_type=F32)
    small = lax.dot_general(high, low_ref[...], dims, preferred_element_type=F32)
    return result[: field.shape[0]] + (result[field.shape[0] :] + small)


def first_row_kernel(place_ref, keep_ref, got_ref, basis_ref, near_hbm, far_hbm, *refs):
    z_ref, noise_ref, scratch_ref, done = refs
    sample = place_ref[1]
    copies = copy_into(
        ((near_hbm, noise_ref.at[:, sample]), (far_hbm, noise_ref.at[:, 1 - sample])), done
    )
    for copy in copies:
        copy.start()
    row_kernel(place_ref, keep_ref, got_ref, basis_ref, z_ref, scratch_ref)
    for copy in copies:
        copy.wait()


def full_image(place_ref, keep_ref, got_ref, z_ref, noise_ref, high_ref, low_ref, image_ref, scratch_ref):
    image = row_image(place_ref, keep_ref, got_ref, high_ref, low_ref, scratch_ref)
    field = z_ref[...].reshape(image.shape)
    image = image + noise_ref[...].reshape(image.shape) * field
    image_ref[...] = image.reshape(image_ref.shape)
    return fold(field * image)


def first_image_kernel(
    place_ref,
    keep_ref,
    got_ref,
    z_ref,
    noise_ref,
    high_ref,
    low_ref,
    one_ref,
    image_ref,
    sum_ref,
    scratch_ref,
):
    refs = (place_ref, keep_ref, got_ref, z_ref, noise_ref, high_ref, low_ref)
    store_sums(sum_ref, [one_ref[0:1], full_image(*refs, image_ref, scratch_ref)])


def return_kernel(whose, place_ref, image_ref, basis_ref, out_ref):
    lanes = both_shares(place_ref, out_ref.shape[2])[whose]
    image = image_ref[...].reshape(-1, basis_ref.shape[0])
    out_ref[...] = times_right(image, basis_ref[:, lanes], 0).reshape(out_ref.shape)


def last_image_kernel(
    place_ref,
    keep_ref,
    got_ref,
    z_ref,
    noise_ref,
    high_ref,
    low_ref,
    one_ref,
    two_ref,
    image_ref,
    sum_ref,
    scratch_ref,
):
    refs = (place_ref, keep_ref, got_ref, z_ref, noise_ref, high_ref, low_ref)
    last = full_image(*refs, image_ref, scratch_ref)
    rows = [one_ref[0:2], two_ref[0:1], last, two_ref[1:2], jnp.zeros((3, 128), F32)]
    sum_ref[...] = jnp.broadcast_to(jnp.concatenate(rows, axis=0)[None], sum_ref.shape)


def combine_kernel(place_ref, sum_ref, z_ref, image_ref, f_ref, f_image_ref, out_ref):
    devices, kinds, lanes = sum_ref.shape
    pairs = devices // 2
    total = jnp.sum(sum_ref[...], axis=2, keepdims=True)
    total = jnp.sum(total.reshape(pairs, 2, kinds, 1), axis=1)
    g00, g01, g11, h11, step = (total[:, at : at + 1] for at in range(5))
    step = step * (1.0 / (2 * lanes))

    def over_pairs(value):
        return jnp.sum(value, axis=0, keepdims=True)

    gamma = over_pairs(g00)
    alpha = gamma / over_pairs(g01)
    theta = alpha / step
    rest = 1.0 - theta
    gamma_new = over_pairs(rest * rest * g00 + theta * theta * g11)
    turn = rest + gamma_new / gamma
    curvature = over_pairs(
        turn * turn * g01 - 2.0 * theta * turn * g11 / step + theta * theta * h11
    )
    alpha_new = gamma_new / curvature
    own = lax.broadcasted_iota(jnp.int32, theta.shape, 0) == place_ref[3]
    on_z = over_pairs(jnp.where(own, alpha + alpha_new * turn, 0.0))
    on_f = over_pairs(jnp.where(own, alpha_new * theta, 0.0))
    share = z_ref.shape[1]
    out_ref[:, :share, :] = on_z * z_ref[...] + on_f * f_ref[...]
    out_ref[:, share:, :] = on_z * image_ref[...] + on_f * f_image_ref[...]


def finish_kernel(got_ref, right_ref, solution_ref, residual_ref):
    samples = got_ref.shape[0]
    rows = got_ref.shape[1] // 2
    for sample in range(samples):
        solution_ref[sample, 0] = got_ref[sample, :rows, :]
        residual_ref[sample, 0] = right_ref[sample, 0] - got_ref[sample, rows:, :]


def paired_body(
    right_side,
    classes,
    noise_table,
    kernel_first,
    kernel_second,
    basis_first,
    basis_second,
    eigen_first,
    eigen_second,
):
    groups = lax.axis_size("mode")
    samples, planes, rows, width = right_side.shape
    height = groups * rows
    cores = 2
    half = width // cores
    blocks = groups // cores
    unit = cores * samples
    index = lax.axis_index("mode")
    core = index % cores
    sample = (index // cores) % samples
    plane = index // unit
    place = jnp.stack([core, sample, plane, index // cores]).astype(jnp.int32)

    def shape_of(*shape):
        return jax.ShapeDtypeStruct(shape, F32)

    smem = pl.BlockSpec(memory_space=pltpu.SMEM)

    hbm = pl.BlockSpec(memory_space=pltpu.HBM)

    def full(*shape):
        return pl.BlockSpec(
            shape, lambda *at: (0,) * len(shape), pipeline_mode=pl.Buffered(1)
        )

    def whole_out(*shape):
        return pl.BlockSpec(shape, lambda *at: (0,) * len(shape))

    core_swap = [(at, at ^ 1) for at in range(groups)]
    sample_swap = [(at, at ^ cores) for at in range(groups)]

    def in_hbm(value):
        return pltpu.with_memory_space_constraint(value, pltpu.HBM)

    def noise_of(shifts):
        return pl.pallas_call(
            functools.partial(noise_kernel, shifts, unit),
            grid=(1,),
            in_specs=[smem, pl.BlockSpec(memory_space=pltpu.HBM)],
            out_specs=[whole_out(rows, width)] * len(shifts),
            out_shape=[shape_of(rows, width)] * len(shifts),
            scratch_shapes=[
                pltpu.VMEM((len(shifts), rows, width), jnp.int32),
                pltpu.SemaphoreType.DMA((len(shifts),)),
            ],
            compiler_params=params(1, 4),
        )(in_hbm(noise_table), in_hbm(classes))

    def plane_shift(value, by):
        pairs = [(at, (at + by * unit) % groups) for at in range(groups)]
        return lax.ppermute(value, "mode", pairs)

    ahead = planes // 2
    others = [by for by in range(planes) if by != ahead]
    near = [None] * planes
    near[ahead] = plane_shift(noise_of([ahead])[0], ahead)
    rest = noise_of(others)
    for by, value in zip(others, rest):
        near[by] = plane_shift(value, by) if by else value

    outgoing = pl.pallas_call(
        outgoing_kernel,
        grid=(planes,),
        in_specs=[
            pl.BlockSpec((samples, 1, rows, width), lambda p: (0, p, 0, 0)),
            full(width, width),
        ],
        out_specs=pl.BlockSpec((1, samples, cores, rows, half), lambda p: (p, 0, 0, 0, 0)),
        out_shape=shape_of(planes, samples, cores, rows, half),
        compiler_params=params(1, 56),
        name="outgoing",
    )(right_side, basis_second)
    arrived = lax.all_to_all(
        outgoing.reshape(groups, rows, half), "mode", split_axis=0, concat_axis=0, tiled=True
    )

    eigen = eigen_second.reshape(1, -1)
    for reach in (1, cores):
        other = lax.ppermute(eigen, "mode", [(at, at ^ reach) for at in range(groups)])
        low = (index // reach) % 2 == 0
        eigen = jnp.where(
            low,
            jnp.concatenate([eigen, other], axis=1),
            jnp.concatenate([other, eigen], axis=1),
        )
    near, eigen = pl.pallas_call(
        join_kernel,
        grid=(1,),
        in_specs=[smem, full(*eigen.shape)] + [full(rows, width)] * planes,
        out_specs=[whole_out(planes, rows, width), whole_out(*eigen.shape)],
        out_shape=[shape_of(planes, rows, width), shape_of(*eigen.shape)],
        compiler_params=params(1, 58),
        name="join",
    )(place, eigen, *near)
    far = lax.ppermute(near, "mode", sample_swap)
    shifted = [eigen] + [
        lax.ppermute(eigen, "mode", [(at, (at + by * unit) % groups) for at in range(groups)])
        for by in range(1, planes)
    ]
    bf16_square = jax.ShapeDtypeStruct((height, height), BF16)
    bf16_half = jax.ShapeDtypeStruct((height // 2, height), BF16)
    prepare = pl.pallas_call(
        prepare_kernel,
        grid=(1,),
        in_specs=[full(height, height), full(width, width), full(width, width)]
        + [pl.BlockSpec(memory_space=pl.ANY)],
        out_specs=[whole_out(height // 2, height)] * 2 + [whole_out(height, height)] * 2,
        out_shape=[bf16_half] * 2 + [bf16_square] * 2,
        compiler_params=params(1, 24),
        name="prepare",
    )
    upper, lower, high, low = prepare(basis_first, basis_second, kernel_second, eigen)

    def swap(value):
        return lax.ppermute(value, "mode", core_swap)

    def call(kernel, inputs, shapes, scratch_shape, specs=None, more=(), mebibytes=12, matrices=()):
        return pl.pallas_call(
            kernel,
            grid=(1,),
            in_specs=specs or [smem] + [full(*value.shape) for value in inputs[1:]],
            out_specs=[whole_out(*shape) for shape in shapes]
            + [whole_out(*value.shape) for value in matrices],
            out_shape=[shape_of(*shape) for shape in shapes] + list(matrices),
            scratch_shapes=[*([pltpu.VMEM(scratch_shape, F32)] if scratch_shape else []), *more],
            compiler_params=params(1, mebibytes),
        )(*inputs)

    tile = (height, half)
    piece = (blocks, rows, half)
    whole = (blocks, rows, width)
    by_rows = (blocks, cores, rows, half)
    flat = (blocks * rows, width)
    sums_shape = (8, 128)

    (start, weights, column, keep, send, sum_one, lower, *squares) = call(
        first_column_kernel,
        (
            place,
            noise_table,
            *(in_hbm(value) for value in (arrived, lower, basis_first, kernel_first, basis_second)),
            upper,
            eigen_first.reshape(1, -1),
            *shifted,
        ),
        (tile, tile, tile, piece, piece, sums_shape),
        by_rows,
        [smem, smem]
        + [hbm] * 5
        + [full(height // 2, height), full(1, height)]
        + [full(*value.shape) for value in shifted],
        [pltpu.VMEM((groups, rows, half), F32), pltpu.SemaphoreType.DMA((5,))],
        16,
        [bf16_half] + [bf16_square] * 3,
    )
    basis_first, kernel_first, basis_second = squares
    got = swap(send)
    image_keep, image_send, high, low = call(
        first_column_image_kernel,
        (place, column, kernel_first, in_hbm(high), in_hbm(low)),
        (piece, piece),
        by_rows,
        [smem, full(*tile), full(height, height), hbm, hbm],
        [pltpu.SemaphoreType.DMA((2,))],
        matrices=[bf16_square] * 2,
    )
    image_got = swap(image_send)
    inputs = (place, keep, got, basis_second)
    z_field, noise = call(
        first_row_kernel,
        (*inputs, in_hbm(near), in_hbm(far)),
        (whole, (planes, samples, rows, width)),
        flat,
        [smem] + [full(*value.shape) for value in inputs[1:]] + [hbm] * 2,
        [pltpu.SemaphoreType.DMA((2,))],
    )
    image, pair_sum = call(
        first_image_kernel,
        (place, image_keep, image_got, z_field, noise, high, low, sum_one),
        (whole, sums_shape),
        flat,
    )
    pair_other = swap(pair_sum)

    def give_back(whose):
        kernel = functools.partial(return_kernel, whose)
        return call(kernel, (place, image, basis_second), (piece,), None)[0]

    back_send = give_back(1)
    back_keep = give_back(0)
    back_got = swap(back_send)

    column, keep, send, sum_two = call(
        next_column_kernel,
        (
            place,
            back_keep,
            back_got,
            start,
            weights,
            upper,
            lower,
            basis_first,
            pair_sum,
            pair_other,
        ),
        (tile, piece, piece, sums_shape),
        by_rows,
    )
    got = swap(send)
    image_keep, image_send = call(
        column_image_kernel, (place, column, kernel_first), (piece, piece), by_rows
    )
    image_got = swap(image_send)
    (f_field,) = call(row_kernel, (place, keep, got, basis_second), (whole,), flat)
    f_image, sums = call(
        last_image_kernel,
        (
            place,
            image_keep,
            image_got,
            f_field,
            noise,
            high,
            low,
            pair_sum,
            sum_two,
        ),
        (whole, (groups, 8, 128)),
        flat,
    )
    sums = lax.all_to_all(sums, "mode", split_axis=0, concat_axis=0, tiled=True)

    few = blocks
    few_spec = pl.BlockSpec((few, rows, width), lambda i: (i, 0, 0))
    answer = pl.pallas_call(
        combine_kernel,
        grid=(1,),
        in_specs=[smem, full(groups, 8, 128)] + [few_spec] * 4,
        out_specs=pl.BlockSpec((few, 2 * rows, width), lambda i: (i, 0, 0)),
        out_shape=shape_of(blocks, 2 * rows, width),
        compiler_params=params(1, 6),
        name="combine",
    )(place, sums, z_field, image, f_field, f_image)
    answer = lax.all_to_all(
        answer,
        "mode",
        split_axis=0,
        concat_axis=0,
        axis_index_groups=[list(range(at, groups, cores)) for at in range(cores)],
        tiled=True,
    )

    block = pl.BlockSpec((samples, 1, rows, width), lambda p: (0, p, 0, 0))
    return tuple(
        pl.pallas_call(
            finish_kernel,
            grid=(planes,),
            in_specs=[
                pl.BlockSpec((samples, 2 * rows, width), lambda p: (p, 0, 0)),
                block,
            ],
            out_specs=[block, block],
            out_shape=[shape_of(*right_side.shape)] * 2,
            compiler_params=params(1, 10),
            name="finish",
        )(answer, right_side)
    )


def body(right_side, classes, *rest):
    groups = lax.axis_size("mode")
    samples, planes, rows, width = right_side.shape
    paired = (
        groups == 2 * samples * planes
        and samples == 2
        and rows % 8 == 0
        and width % 512 == 0
        and planes % 2 == 0
    )
    chosen = paired_body if paired else general_body
    return chosen(right_side, classes, *rest)


def solution(mesh):
    in_specs = (
        P(None, "blocks", "mode", None),
        P("blocks", "mode", None),
        P(),
        P(),
        P(),
        P(),
        P(),
        P(),
        P("mode"),
    )
    out_specs = (P(None, "blocks", "mode", None), P(None, "blocks", "mode", None))
    return jax.shard_map(body, mesh=mesh, in_specs=in_specs, out_specs=out_specs, check_vma=False)
```

```python
import functools

import jax
import jax.numpy as jnp
from jax import lax
from jax.experimental import pallas as pl
from jax.experimental.pallas import tpu as pltpu
from jax.sharding import PartitionSpec as P


NCLASS = 8
ITERS = 2
F32 = jnp.float32
BF16 = jnp.bfloat16


def along_rows(matrix, field):
    return jnp.einsum("jk,sprk->sprj", matrix, field, precision=lax.Precision.HIGHEST)


def rows_to_send(matrix, field, groups):
    result = jnp.einsum("kj,sprk->jspr", matrix, field, precision=lax.Precision.HIGHEST)
    return result.reshape(groups, -1)


def received_to_columns(matrix, received, shape5):
    groups, _, _, _, rows = shape5
    block = received.reshape(shape5)
    reshaped = matrix.reshape(groups, rows, matrix.shape[1])
    return jnp.einsum("mri,mcspr->cspi", reshaped, block, precision=lax.Precision.HIGHEST)


def along_columns(matrix, columns):
    return jnp.einsum("ik,cspk->cspi", matrix, columns, precision=lax.Precision.HIGHEST)


def columns_to_send(matrix, columns, groups, rows):
    reshaped = matrix.reshape(groups, rows, matrix.shape[1])
    result = jnp.einsum("mrk,cspk->mcspr", reshaped, columns, precision=lax.Precision.HIGHEST)
    return result.reshape(groups, -1)


def received_to_rows(matrix, received, shape5):
    groups, cols, _, _, _ = shape5
    block = received.reshape(shape5)
    reshaped = matrix.reshape(matrix.shape[0], groups, cols)
    return jnp.einsum("jmc,mcspr->sprj", reshaped, block, precision=lax.Precision.HIGHEST)


def general_body(
    right_side,
    classes,
    noise_table,
    kernel_first,
    kernel_second,
    basis_first,
    basis_second,
    eigen_first,
    eigen_second,
):
    groups = lax.axis_size("mode")
    samples, planes, rows, _ = right_side.shape
    cols = eigen_second.shape[0]
    shape5 = (groups, cols, samples, planes, rows)
    kern_one = kernel_first.astype(F32)
    kern_two = kernel_second.astype(F32)
    base_one = basis_first.astype(F32)
    base_two = basis_second.astype(F32)
    noise = jnp.zeros(classes.shape, F32)
    for level in range(NCLASS):
        noise = noise + jnp.where(classes == level, noise_table[level], 0.0)
    noise = noise[None]
    mean_noise = jnp.mean(noise_table)
    col_weights = 1.0 / (eigen_second[:, None] * eigen_first[None, :] + mean_noise)
    col_weights = col_weights[:, None, None, :]

    def exchange(outgoing):
        return lax.all_to_all(outgoing, "mode", split_axis=0, concat_axis=0, tiled=True)

    def precond_apply(field):
        incoming = exchange(rows_to_send(base_two, field, groups))
        weighted = received_to_columns(base_one, incoming, shape5) * col_weights
        columns = along_columns(base_one, weighted)
        back = exchange(columns_to_send(base_one, weighted, groups, rows))
        kernel_back = exchange(columns_to_send(kern_one, columns, groups, rows))
        z_field = received_to_rows(base_two, back, shape5)
        image = (
            along_rows(kern_two, received_to_rows(base_two, kernel_back, shape5)) + noise * z_field
        )
        return (z_field, image)

    def inner(left, right):
        return lax.psum(jnp.sum(left * right), "mode")

    solution_field = jnp.zeros_like(right_side)
    residual = right_side
    z_field, image = precond_apply(residual)
    direction, along = (z_field, image)
    gamma = inner(residual, z_field)
    for step in range(ITERS):
        alpha = gamma / inner(direction, along)
        solution_field = solution_field + alpha * direction
        residual = residual - alpha * along
        if step + 1 < ITERS:
            z_field, image = precond_apply(residual)
            gamma_new = inner(residual, z_field)
            ratio = gamma_new / gamma
            direction = z_field + ratio * direction
            along = image + ratio * along
            gamma = gamma_new
    return (solution_field, residual)


def split(value):
    high = value.astype(BF16)
    low = (value - high.astype(F32)).astype(BF16)
    return high, low


def times_right(value, matrix, contract):
    high, low = split(value)
    dims = (((1,), (contract,)), ((), ()))
    both = jnp.concatenate([high, low], axis=0)
    result = lax.dot_general(both, matrix, dims, preferred_element_type=F32)
    return result[: value.shape[0]] + result[value.shape[0] :]


def side_by_side(value):
    return jnp.concatenate(split(value), axis=1)


def times_both(matrix, both):
    width = both.shape[1] // 2
    dims = (((1,), (0,)), ((), ()))
    result = lax.dot_general(matrix, both, dims, preferred_element_type=F32)
    return result[:, :width] + result[:, width:]


def times_left(matrix, value):
    return times_both(matrix, side_by_side(value))


def fold(value):
    total = jnp.sum(value, axis=0, keepdims=True)
    return functools.reduce(
        jnp.add, [total[:, at : at + 128] for at in range(0, total.shape[1], 128)]
    )


def params(dims, mebibytes):
    return pltpu.CompilerParams(
        dimension_semantics=("arbitrary",) * dims, vmem_limit_bytes=mebibytes * 1024 * 1024
    )


def noise_kernel(shifts, unit, table_ref, class_hbm, *refs):
    out_refs, (class_ref, done) = refs[:-2], refs[-2:]
    planes = class_hbm.shape[0]
    plane = lax.axis_index("mode") // unit
    copies = [
        pltpu.make_async_copy(class_hbm.at[(plane + by) % planes], class_ref.at[at], done.at[at])
        for at, by in enumerate(shifts)
    ]
    for copy in copies:
        copy.start()
    for at, copy in enumerate(copies):
        copy.wait()
        level = class_ref[at]
        noise = jnp.full(level.shape, table_ref[0], F32)
        for index in range(1, NCLASS):
            noise = jnp.where(level == index, table_ref[index], noise)
        out_refs[at][...] = noise


def join_kernel(place_ref, value_ref, *refs):
    parts, (joined_ref, out_ref) = refs[:-2], refs[-2:]
    planes = len(parts)
    for by, part in enumerate(parts):
        joined_ref[(place_ref[2] + planes - by) % planes] = part[...]
    out_ref[...] = value_ref[...]


def prepare_kernel(
    first_ref,
    second_ref,
    kernel_ref,
    _,
    upper_ref,
    lower_ref,
    high_ref,
    low_ref,
):
    turned = first_ref[...].T
    middle = upper_ref.shape[0]
    upper_ref[...] = turned[:middle]
    lower_ref[...] = turned[middle:]
    dims = (((1,), (0,)), ((), ()))
    product = lax.dot_general(
        kernel_ref[...], second_ref[...], dims, preferred_element_type=F32
    )
    high_ref[...], low_ref[...] = split(product)


def outgoing_kernel(right_ref, basis_ref, out_ref):
    samples, _, rows, width = right_ref.shape
    cores = out_ref.shape[2]
    half = width // cores
    field = right_ref[...].reshape(samples * rows, width)
    mapped = times_right(field, basis_ref[...], 0)
    for sample in range(samples):
        for core in range(cores):
            out_ref[0, sample, core] = mapped[
                sample * rows : (sample + 1) * rows, core * half : (core + 1) * half
            ]


def both_shares(place_ref, share):
    core = place_ref[0]
    mine = pl.ds(pl.multiple_of(core * share, share), share)
    theirs = pl.ds(pl.multiple_of((1 - core) * share, share), share)
    return mine, theirs


def split_rows(place_ref, value, scratch_ref, keep_ref, send_ref):
    core = place_ref[0]
    scratch_ref[...] = value.reshape(scratch_ref.shape)
    keep_ref[...] = scratch_ref[:, core]
    send_ref[...] = scratch_ref[:, 1 - core]


def store_sums(sum_ref, sums):
    rows = sum_ref.shape[0]
    sum_ref[...] = jnp.concatenate(sums + [jnp.zeros((rows - len(sums), 128), F32)], axis=0)


def copy_into(pairs, done):
    return [
        pltpu.make_async_copy(source, target, done.at[at])
        for at, (source, target) in enumerate(pairs)
    ]


def first_column_kernel(
    place_ref,
    table_ref,
    field_hbm,
    lower_hbm,
    basis_hbm,
    kernel_hbm,
    second_hbm,
    upper_ref,
    eigen_ref,
    *refs,
):
    wide_refs, refs, outs = refs[:-13], refs[-7:], refs[-13:-7]
    start_ref, weight_ref, column_ref, keep_ref, send_ref, sum_ref = outs
    lower_ref, basis_ref, kernel_ref, second_ref, scratch_ref, field_ref, done = refs
    copies = copy_into(
        (
            (field_hbm, field_ref),
            (lower_hbm, lower_ref),
            (basis_hbm, basis_ref),
            (kernel_hbm, kernel_ref),
            (second_hbm, second_ref),
        ),
        done,
    )
    for copy in copies[:2]:
        copy.start()
    mean = functools.reduce(jnp.add, [table_ref[at] for at in range(NCLASS)]) * (1.0 / NCLASS)
    height, width = start_ref.shape
    tall = jnp.broadcast_to(eigen_ref[...], (128, height)).T
    planes = len(wide_refs)
    part = wide_refs[0].shape[1]
    for block in range(width // part):
        wanted = place_ref[0] * (width // part) + block
        wide = jnp.zeros((1, part), F32)
        for by, wide_ref in enumerate(wide_refs):
            here = (place_ref[2] + planes - by) % planes == wanted
            wide = jnp.where(here, wide_ref[...], wide)
        for at in range(0, part, 128):
            lanes = slice(block * part + at, block * part + at + 128)
            weight_ref[:, lanes] = 1.0 / (tall * wide[:, at : at + 128] + mean)
    copies[0].wait()
    field = field_ref[...].reshape(height, width)
    for copy in copies[2:]:
        copy.start()
    both = side_by_side(field)
    above = times_both(upper_ref[...], both)
    copies[1].wait()
    spectral = jnp.concatenate([above, times_both(lower_ref[...], both)], axis=0)
    weighted = spectral * weight_ref[...]
    start_ref[...] = field
    store_sums(sum_ref, [fold(spectral * weighted)])
    copies[2].wait()
    column = times_left(basis_ref[...], weighted)
    column_ref[...] = column
    split_rows(place_ref, column, scratch_ref, keep_ref, send_ref)
    copies[3].wait()
    copies[4].wait()


def next_column_kernel(
    place_ref,
    held_ref,
    got_ref,
    start_ref,
    weight_ref,
    upper_ref,
    lower_ref,
    basis_ref,
    own_ref,
    column_ref,
    keep_ref,
    send_ref,
    sum_ref,
    scratch_ref,
):
    core = place_ref[0]
    tall = got_ref.shape[0] - own_ref.shape[0]
    scratch_ref[:, core] = held_ref[...]
    scratch_ref[:, 1 - core] = got_ref[:tall, :].reshape(held_ref.shape)
    total = jnp.sum(own_ref[...] + got_ref[tall:, :128], axis=1, keepdims=True)
    gamma, curvature = total[0:1], total[1:2]
    proper = (gamma > 0) & (curvature > 0)
    step = jnp.where(proper, gamma / jnp.where(proper, curvature, 1.0), 1.0)
    field = start_ref[...] - step * scratch_ref[...].reshape(start_ref.shape)
    both = side_by_side(field)
    halves = [times_both(half_ref[...], both) for half_ref in (upper_ref, lower_ref)]
    spectral = jnp.concatenate(halves, axis=0)
    weighted = spectral * weight_ref[...]
    store_sums(sum_ref, [fold(spectral * weighted), jnp.broadcast_to(step, (1, 128))])
    column = times_left(basis_ref[...], weighted)
    column_ref[...] = column
    split_rows(place_ref, column, scratch_ref, keep_ref, send_ref)


def column_image_kernel(place_ref, column_ref, kernel_ref, keep_ref, send_ref, scratch_ref):
    image = times_left(kernel_ref[...], column_ref[...])
    split_rows(place_ref, image, scratch_ref, keep_ref, send_ref)


def first_column_image_kernel(place_ref, column_ref, kernel_ref, high_hbm, low_hbm, *refs):
    keep_ref, send_ref, high_ref, low_ref, scratch_ref, done = refs
    copies = copy_into(((high_hbm, high_ref), (low_hbm, low_ref)), done)
    for copy in copies:
        copy.start()
    column_image_kernel(place_ref, column_ref, kernel_ref, keep_ref, send_ref, scratch_ref)
    for copy in copies:
        copy.wait()


def join_columns(place_ref, scratch_ref, keep_ref, got_ref):
    height, width = scratch_ref.shape
    mine, theirs = both_shares(place_ref, width // 2)
    scratch_ref[:, mine] = keep_ref[...].reshape(height, width // 2)
    scratch_ref[:, theirs] = got_ref[...].reshape(height, width // 2)
    return scratch_ref[...]


def row_kernel(place_ref, keep_ref, got_ref, basis_ref, z_ref, scratch_ref):
    field = join_columns(place_ref, scratch_ref, keep_ref, got_ref)
    z_ref[...] = times_right(field, basis_ref[...], 1).reshape(z_ref.shape)


def row_image(place_ref, keep_ref, got_ref, high_ref, low_ref, scratch_ref):
    field = join_columns(place_ref, scratch_ref, keep_ref, got_ref)
    high, low = split(field)
    dims = (((1,), (1,)), ((), ()))
    both = jnp.concatenate([high, low], axis=0)
    result = lax.dot_general(both, high_ref[...], dims, preferred_element_type=F32)
    small = lax.dot_general(high, low_ref[...], dims, preferred_element_type=F32)
    return result[: field.shape[0]] + (result[field.shape[0] :] + small)


def first_row_kernel(place_ref, keep_ref, got_ref, basis_ref, near_hbm, far_hbm, *refs):
    z_ref, noise_ref, scratch_ref, done = refs
    sample = place_ref[1]
    copies = copy_into(
        ((near_hbm, noise_ref.at[:, sample]), (far_hbm, noise_ref.at[:, 1 - sample])), done
    )
    for copy in copies:
        copy.start()
    row_kernel(place_ref, keep_ref, got_ref, basis_ref, z_ref, scratch_ref)
    for copy in copies:
        copy.wait()


def full_image(place_ref, keep_ref, got_ref, z_ref, noise_ref, high_ref, low_ref, image_ref, scratch_ref):
    image = row_image(place_ref, keep_ref, got_ref, high_ref, low_ref, scratch_ref)
    field = z_ref[...].reshape(image.shape)
    image = image + noise_ref[...].reshape(image.shape) * field
    image_ref[...] = image.reshape(image_ref.shape)
    return fold(field * image)


def first_image_kernel(
    place_ref,
    keep_ref,
    got_ref,
    z_ref,
    noise_ref,
    high_ref,
    low_ref,
    one_ref,
    image_ref,
    sum_ref,
    scratch_ref,
):
    refs = (place_ref, keep_ref, got_ref, z_ref, noise_ref, high_ref, low_ref)
    store_sums(sum_ref, [one_ref[0:1], full_image(*refs, image_ref, scratch_ref)])


def returned(place_ref, image_ref, basis_ref, whose, half):
    lanes = both_shares(place_ref, half)[whose]
    image = image_ref[...].reshape(-1, basis_ref.shape[0])
    return times_right(image, basis_ref[:, lanes], 0)


def return_theirs_kernel(place_ref, image_ref, basis_ref, sum_ref, out_ref):
    part = returned(place_ref, image_ref, basis_ref, 1, out_ref.shape[1])
    out_ref[: part.shape[0], :] = part
    out_ref[part.shape[0] :, :] = jnp.concatenate(
        [sum_ref[...]] * (out_ref.shape[1] // 128), axis=1
    )


def return_mine_kernel(place_ref, image_ref, basis_ref, out_ref):
    part = returned(place_ref, image_ref, basis_ref, 0, out_ref.shape[2])
    out_ref[...] = part.reshape(out_ref.shape)


def last_image_kernel(
    place_ref,
    keep_ref,
    got_ref,
    z_ref,
    noise_ref,
    high_ref,
    low_ref,
    one_ref,
    two_ref,
    image_ref,
    sum_ref,
    scratch_ref,
):
    refs = (place_ref, keep_ref, got_ref, z_ref, noise_ref, high_ref, low_ref)
    last = full_image(*refs, image_ref, scratch_ref)
    rows = [one_ref[0:2], two_ref[0:1], last, two_ref[1:2], jnp.zeros((3, 128), F32)]
    sum_ref[...] = jnp.broadcast_to(jnp.concatenate(rows, axis=0)[None], sum_ref.shape)


def combine_kernel(place_ref, sum_ref, z_ref, image_ref, f_ref, f_image_ref, out_ref):
    devices, kinds, lanes = sum_ref.shape
    pairs = devices // 2
    total = jnp.sum(sum_ref[...], axis=2, keepdims=True)
    total = jnp.sum(total.reshape(pairs, 2, kinds, 1), axis=1)
    g00, g01, g11, h11, step = (total[:, at : at + 1] for at in range(5))
    step = step * (1.0 / (2 * lanes))

    def over_pairs(value):
        return jnp.sum(value, axis=0, keepdims=True)

    gamma = over_pairs(g00)
    alpha = gamma / over_pairs(g01)
    theta = alpha / step
    rest = 1.0 - theta
    gamma_new = over_pairs(rest * rest * g00 + theta * theta * g11)
    turn = rest + gamma_new / gamma
    curvature = over_pairs(
        turn * turn * g01 - 2.0 * theta * turn * g11 / step + theta * theta * h11
    )
    alpha_new = gamma_new / curvature
    own = lax.broadcasted_iota(jnp.int32, theta.shape, 0) == place_ref[3]
    on_z = over_pairs(jnp.where(own, alpha + alpha_new * turn, 0.0))
    on_f = over_pairs(jnp.where(own, alpha_new * theta, 0.0))
    share = z_ref.shape[1]
    out_ref[:, :share, :] = on_z * z_ref[...] + on_f * f_ref[...]
    out_ref[:, share:, :] = on_z * image_ref[...] + on_f * f_image_ref[...]


def finish_kernel(got_ref, right_ref, solution_ref, residual_ref):
    samples = got_ref.shape[0]
    rows = got_ref.shape[1] // 2
    for sample in range(samples):
        solution_ref[sample, 0] = got_ref[sample, :rows, :]
        residual_ref[sample, 0] = right_ref[sample, 0] - got_ref[sample, rows:, :]


def paired_body(
    right_side,
    classes,
    noise_table,
    kernel_first,
    kernel_second,
    basis_first,
    basis_second,
    eigen_first,
    eigen_second,
):
    groups = lax.axis_size("mode")
    samples, planes, rows, width = right_side.shape
    height = groups * rows
    cores = 2
    half = width // cores
    blocks = groups // cores
    unit = cores * samples
    index = lax.axis_index("mode")
    core = index % cores
    sample = (index // cores) % samples
    plane = index // unit
    place = jnp.stack([core, sample, plane, index // cores]).astype(jnp.int32)

    def shape_of(*shape):
        return jax.ShapeDtypeStruct(shape, F32)

    smem = pl.BlockSpec(memory_space=pltpu.SMEM)

    hbm = pl.BlockSpec(memory_space=pltpu.HBM)

    def full(*shape):
        return pl.BlockSpec(
            shape, lambda *at: (0,) * len(shape), pipeline_mode=pl.Buffered(1)
        )

    def whole_out(*shape):
        return pl.BlockSpec(shape, lambda *at: (0,) * len(shape))

    core_swap = [(at, at ^ 1) for at in range(groups)]
    sample_swap = [(at, at ^ cores) for at in range(groups)]

    def in_hbm(value):
        return pltpu.with_memory_space_constraint(value, pltpu.HBM)

    def noise_of(shifts):
        return pl.pallas_call(
            functools.partial(noise_kernel, shifts, unit),
            grid=(1,),
            in_specs=[smem, pl.BlockSpec(memory_space=pltpu.HBM)],
            out_specs=[whole_out(rows, width)] * len(shifts),
            out_shape=[shape_of(rows, width)] * len(shifts),
            scratch_shapes=[
                pltpu.VMEM((len(shifts), rows, width), jnp.int32),
                pltpu.SemaphoreType.DMA((len(shifts),)),
            ],
            compiler_params=params(1, 4),
        )(in_hbm(noise_table), in_hbm(classes))

    def plane_shift(value, by):
        pairs = [(at, (at + by * unit) % groups) for at in range(groups)]
        return lax.ppermute(value, "mode", pairs)

    ahead = planes // 2
    others = [by for by in range(planes) if by != ahead]
    near = [None] * planes
    near[ahead] = plane_shift(noise_of([ahead])[0], ahead)
    rest = noise_of(others)
    for by, value in zip(others, rest):
        near[by] = plane_shift(value, by) if by else value

    outgoing = pl.pallas_call(
        outgoing_kernel,
        grid=(planes,),
        in_specs=[
            pl.BlockSpec((samples, 1, rows, width), lambda p: (0, p, 0, 0)),
            full(width, width),
        ],
        out_specs=pl.BlockSpec((1, samples, cores, rows, half), lambda p: (p, 0, 0, 0, 0)),
        out_shape=shape_of(planes, samples, cores, rows, half),
        compiler_params=params(1, 56),
        name="outgoing",
    )(right_side, basis_second)
    arrived = lax.all_to_all(
        outgoing.reshape(groups, rows, half), "mode", split_axis=0, concat_axis=0, tiled=True
    )

    eigen = eigen_second.reshape(1, -1)
    for reach in (1, cores):
        other = lax.ppermute(eigen, "mode", [(at, at ^ reach) for at in range(groups)])
        low = (index // reach) % 2 == 0
        eigen = jnp.where(
            low,
            jnp.concatenate([eigen, other], axis=1),
            jnp.concatenate([other, eigen], axis=1),
        )
    near, eigen = pl.pallas_call(
        join_kernel,
        grid=(1,),
        in_specs=[smem, full(*eigen.shape)] + [full(rows, width)] * planes,
        out_specs=[whole_out(planes, rows, width), whole_out(*eigen.shape)],
        out_shape=[shape_of(planes, rows, width), shape_of(*eigen.shape)],
        compiler_params=params(1, 58),
        name="join",
    )(place, eigen, *near)
    far = lax.ppermute(near, "mode", sample_swap)
    shifted = [eigen] + [
        lax.ppermute(eigen, "mode", [(at, (at + by * unit) % groups) for at in range(groups)])
        for by in range(1, planes)
    ]
    bf16_square = jax.ShapeDtypeStruct((height, height), BF16)
    bf16_half = jax.ShapeDtypeStruct((height // 2, height), BF16)
    prepare = pl.pallas_call(
        prepare_kernel,
        grid=(1,),
        in_specs=[full(height, height), full(width, width), full(width, width)]
        + [pl.BlockSpec(memory_space=pl.ANY)],
        out_specs=[whole_out(height // 2, height)] * 2 + [whole_out(height, height)] * 2,
        out_shape=[bf16_half] * 2 + [bf16_square] * 2,
        compiler_params=params(1, 24),
        name="prepare",
    )
    upper, lower, high, low = prepare(basis_first, basis_second, kernel_second, eigen)

    def swap(value):
        return lax.ppermute(value, "mode", core_swap)

    def call(kernel, inputs, shapes, scratch_shape, specs=None, more=(), mebibytes=12, matrices=()):
        return pl.pallas_call(
            kernel,
            grid=(1,),
            in_specs=specs or [smem] + [full(*value.shape) for value in inputs[1:]],
            out_specs=[whole_out(*shape) for shape in shapes]
            + [whole_out(*value.shape) for value in matrices],
            out_shape=[shape_of(*shape) for shape in shapes] + list(matrices),
            scratch_shapes=[*([pltpu.VMEM(scratch_shape, F32)] if scratch_shape else []), *more],
            compiler_params=params(1, mebibytes),
        )(*inputs)

    tile = (height, half)
    piece = (blocks, rows, half)
    whole = (blocks, rows, width)
    by_rows = (blocks, cores, rows, half)
    flat = (blocks * rows, width)
    sums_shape = (8, 128)

    (start, weights, column, keep, send, sum_one, lower, *squares) = call(
        first_column_kernel,
        (
            place,
            noise_table,
            *(in_hbm(value) for value in (arrived, lower, basis_first, kernel_first, basis_second)),
            upper,
            eigen_first.reshape(1, -1),
            *shifted,
        ),
        (tile, tile, tile, piece, piece, sums_shape),
        by_rows,
        [smem, smem]
        + [hbm] * 5
        + [full(height // 2, height), full(1, height)]
        + [full(*value.shape) for value in shifted],
        [pltpu.VMEM((groups, rows, half), F32), pltpu.SemaphoreType.DMA((5,))],
        16,
        [bf16_half] + [bf16_square] * 3,
    )
    basis_first, kernel_first, basis_second = squares
    got = swap(send)
    image_keep, image_send, high, low = call(
        first_column_image_kernel,
        (place, column, kernel_first, in_hbm(high), in_hbm(low)),
        (piece, piece),
        by_rows,
        [smem, full(*tile), full(height, height), hbm, hbm],
        [pltpu.SemaphoreType.DMA((2,))],
        matrices=[bf16_square] * 2,
    )
    image_got = swap(image_send)
    inputs = (place, keep, got, basis_second)
    z_field, noise = call(
        first_row_kernel,
        (*inputs, in_hbm(near), in_hbm(far)),
        (whole, (planes, samples, rows, width)),
        flat,
        [smem] + [full(*value.shape) for value in inputs[1:]] + [hbm] * 2,
        [pltpu.SemaphoreType.DMA((2,))],
    )
    image, pair_sum = call(
        first_image_kernel,
        (place, image_keep, image_got, z_field, noise, high, low, sum_one),
        (whole, sums_shape),
        flat,
    )

    (back_send,) = call(
        return_theirs_kernel, (place, image, basis_second, pair_sum), ((flat[0] + 8, half),), None
    )
    (back_keep,) = call(return_mine_kernel, (place, image, basis_second), (piece,), None)
    back_got = swap(back_send)

    column, keep, send, sum_two = call(
        next_column_kernel,
        (
            place,
            back_keep,
            back_got,
            start,
            weights,
            upper,
            lower,
            basis_first,
            pair_sum,
        ),
        (tile, piece, piece, sums_shape),
        by_rows,
    )
    got = swap(send)
    image_keep, image_send = call(
        column_image_kernel, (place, column, kernel_first), (piece, piece), by_rows
    )
    image_got = swap(image_send)
    (f_field,) = call(row_kernel, (place, keep, got, basis_second), (whole,), flat)
    f_image, sums = call(
        last_image_kernel,
        (
            place,
            image_keep,
            image_got,
            f_field,
            noise,
            high,
            low,
            pair_sum,
            sum_two,
        ),
        (whole, (groups, 8, 128)),
        flat,
    )
    sums = lax.all_to_all(sums, "mode", split_axis=0, concat_axis=0, tiled=True)

    few = blocks
    few_spec = pl.BlockSpec((few, rows, width), lambda i: (i, 0, 0))
    answer = pl.pallas_call(
        combine_kernel,
        grid=(1,),
        in_specs=[smem, full(groups, 8, 128)] + [few_spec] * 4,
        out_specs=pl.BlockSpec((few, 2 * rows, width), lambda i: (i, 0, 0)),
        out_shape=shape_of(blocks, 2 * rows, width),
        compiler_params=params(1, 6),
        name="combine",
    )(place, sums, z_field, image, f_field, f_image)
    answer = lax.all_to_all(
        answer,
        "mode",
        split_axis=0,
        concat_axis=0,
        axis_index_groups=[list(range(at, groups, cores)) for at in range(cores)],
        tiled=True,
    )

    block = pl.BlockSpec((samples, 1, rows, width), lambda p: (0, p, 0, 0))
    return tuple(
        pl.pallas_call(
            finish_kernel,
            grid=(planes,),
            in_specs=[
                pl.BlockSpec((samples, 2 * rows, width), lambda p: (p, 0, 0)),
                block,
            ],
            out_specs=[block, block],
            out_shape=[shape_of(*right_side.shape)] * 2,
            compiler_params=params(1, 10),
            name="finish",
        )(answer, right_side)
    )


def body(right_side, classes, *rest):
    groups = lax.axis_size("mode")
    samples, planes, rows, width = right_side.shape
    paired = (
        groups == 2 * samples * planes
        and samples == 2
        and rows % 8 == 0
        and width % 512 == 0
        and planes % 2 == 0
    )
    chosen = paired_body if paired else general_body
    return chosen(right_side, classes, *rest)


def solution(mesh):
    in_specs = (
        P(None, "blocks", "mode", None),
        P("blocks", "mode", None),
        P(),
        P(),
        P(),
        P(),
        P(),
        P(),
        P("mode"),
    )
    out_specs = (P(None, "blocks", "mode", None), P(None, "blocks", "mode", None))
    return jax.shard_map(body, mesh=mesh, in_specs=in_specs, out_specs=out_specs, check_vma=False)
```

```python
import functools

import jax
import jax.numpy as jnp
from jax import lax
from jax.experimental import pallas as pl
from jax.experimental.pallas import tpu as pltpu
from jax.sharding import PartitionSpec as P


NCLASS = 8
ITERS = 2
F32 = jnp.float32
BF16 = jnp.bfloat16


def along_rows(matrix, field):
    return jnp.einsum("jk,sprk->sprj", matrix, field, precision=lax.Precision.HIGHEST)


def rows_to_send(matrix, field, groups):
    result = jnp.einsum("kj,sprk->jspr", matrix, field, precision=lax.Precision.HIGHEST)
    return result.reshape(groups, -1)


def received_to_columns(matrix, received, shape5):
    groups, _, _, _, rows = shape5
    block = received.reshape(shape5)
    reshaped = matrix.reshape(groups, rows, matrix.shape[1])
    return jnp.einsum("mri,mcspr->cspi", reshaped, block, precision=lax.Precision.HIGHEST)


def along_columns(matrix, columns):
    return jnp.einsum("ik,cspk->cspi", matrix, columns, precision=lax.Precision.HIGHEST)


def columns_to_send(matrix, columns, groups, rows):
    reshaped = matrix.reshape(groups, rows, matrix.shape[1])
    result = jnp.einsum("mrk,cspk->mcspr", reshaped, columns, precision=lax.Precision.HIGHEST)
    return result.reshape(groups, -1)


def received_to_rows(matrix, received, shape5):
    groups, cols, _, _, _ = shape5
    block = received.reshape(shape5)
    reshaped = matrix.reshape(matrix.shape[0], groups, cols)
    return jnp.einsum("jmc,mcspr->sprj", reshaped, block, precision=lax.Precision.HIGHEST)


def general_body(
    right_side,
    classes,
    noise_table,
    kernel_first,
    kernel_second,
    basis_first,
    basis_second,
    eigen_first,
    eigen_second,
):
    groups = lax.axis_size("mode")
    samples, planes, rows, _ = right_side.shape
    cols = eigen_second.shape[0]
    shape5 = (groups, cols, samples, planes, rows)
    kern_one = kernel_first.astype(F32)
    kern_two = kernel_second.astype(F32)
    base_one = basis_first.astype(F32)
    base_two = basis_second.astype(F32)
    noise = jnp.zeros(classes.shape, F32)
    for level in range(NCLASS):
        noise = noise + jnp.where(classes == level, noise_table[level], 0.0)
    noise = noise[None]
    mean_noise = jnp.mean(noise_table)
    col_weights = 1.0 / (eigen_second[:, None] * eigen_first[None, :] + mean_noise)
    col_weights = col_weights[:, None, None, :]

    def exchange(outgoing):
        return lax.all_to_all(outgoing, "mode", split_axis=0, concat_axis=0, tiled=True)

    def precond_apply(field):
        incoming = exchange(rows_to_send(base_two, field, groups))
        weighted = received_to_columns(base_one, incoming, shape5) * col_weights
        columns = along_columns(base_one, weighted)
        back = exchange(columns_to_send(base_one, weighted, groups, rows))
        kernel_back = exchange(columns_to_send(kern_one, columns, groups, rows))
        z_field = received_to_rows(base_two, back, shape5)
        image = (
            along_rows(kern_two, received_to_rows(base_two, kernel_back, shape5)) + noise * z_field
        )
        return (z_field, image)

    def inner(left, right):
        return lax.psum(jnp.sum(left * right), "mode")

    solution_field = jnp.zeros_like(right_side)
    residual = right_side
    z_field, image = precond_apply(residual)
    direction, along = (z_field, image)
    gamma = inner(residual, z_field)
    for step in range(ITERS):
        alpha = gamma / inner(direction, along)
        solution_field = solution_field + alpha * direction
        residual = residual - alpha * along
        if step + 1 < ITERS:
            z_field, image = precond_apply(residual)
            gamma_new = inner(residual, z_field)
            ratio = gamma_new / gamma
            direction = z_field + ratio * direction
            along = image + ratio * along
            gamma = gamma_new
    return (solution_field, residual)


def split(value):
    high = value.astype(BF16)
    low = (value - high.astype(F32)).astype(BF16)
    return high, low


def times_right(value, matrix, contract):
    high, low = split(value)
    dims = (((1,), (contract,)), ((), ()))
    both = jnp.concatenate([high, low], axis=0)
    result = lax.dot_general(both, matrix, dims, preferred_element_type=F32)
    return result[: value.shape[0]] + result[value.shape[0] :]


def side_by_side(value):
    return jnp.concatenate(split(value), axis=1)


def times_both(matrix, both):
    width = both.shape[1] // 2
    dims = (((1,), (0,)), ((), ()))
    result = lax.dot_general(matrix, both, dims, preferred_element_type=F32)
    return result[:, :width] + result[:, width:]


def times_left(matrix, value):
    return times_both(matrix, side_by_side(value))


def fold(value):
    total = jnp.sum(value, axis=0, keepdims=True)
    return functools.reduce(
        jnp.add, [total[:, at : at + 128] for at in range(0, total.shape[1], 128)]
    )


def params(dims, mebibytes):
    return pltpu.CompilerParams(
        dimension_semantics=("arbitrary",) * dims, vmem_limit_bytes=mebibytes * 1024 * 1024
    )


def look_up(table_ref, level):
    noise = jnp.full(level.shape, table_ref[0], F32)
    for index in range(1, NCLASS):
        noise = jnp.where(level == index, table_ref[index], noise)
    return noise


def pick_kernel(by, unit, class_hbm, out_ref, done):
    plane = lax.axis_index("mode") // unit
    copy = pltpu.make_async_copy(class_hbm.at[(plane + by) % class_hbm.shape[0]], out_ref, done)
    copy.start()
    copy.wait()


def noise_kernel(shifts, unit, table_ref, class_hbm, *refs):
    out_refs, (class_ref, done) = refs[:-2], refs[-2:]
    planes = class_hbm.shape[0]
    plane = lax.axis_index("mode") // unit
    pairs = [(class_hbm.at[(plane + by) % planes], class_ref.at[at]) for at, by in enumerate(shifts)]
    copies = copy_into(pairs, done)
    for copy in copies:
        copy.start()
    for at, copy in enumerate(copies):
        copy.wait()
        out_refs[at][...] = look_up(table_ref, class_ref[at])


def join_kernel(ahead, place_ref, table_ref, value_ref, *refs):
    parts, (joined_ref, out_ref) = refs[:-2], refs[-2:]
    planes = len(parts)
    for by, part in enumerate(parts):
        noise = look_up(table_ref, part[...]) if by == ahead else part[...]
        joined_ref[(place_ref[2] + planes - by) % planes] = noise
    out_ref[...] = value_ref[...]


def prepare_kernel(
    first_ref,
    second_ref,
    kernel_ref,
    _,
    upper_ref,
    lower_ref,
    high_ref,
    low_ref,
):
    turned = first_ref[...].T
    middle = upper_ref.shape[0]
    upper_ref[...] = turned[:middle]
    lower_ref[...] = turned[middle:]
    dims = (((1,), (0,)), ((), ()))
    product = lax.dot_general(
        kernel_ref[...], second_ref[...], dims, preferred_element_type=F32
    )
    high_ref[...], low_ref[...] = split(product)


def outgoing_kernel(right_ref, basis_ref, out_ref):
    samples, _, rows, width = right_ref.shape
    cores = out_ref.shape[2]
    half = width // cores
    field = right_ref[...].reshape(samples * rows, width)
    mapped = times_right(field, basis_ref[...], 0)
    for sample in range(samples):
        for core in range(cores):
            out_ref[0, sample, core] = mapped[
                sample * rows : (sample + 1) * rows, core * half : (core + 1) * half
            ]


def both_shares(place_ref, share):
    core = place_ref[0]
    mine = pl.ds(pl.multiple_of(core * share, share), share)
    theirs = pl.ds(pl.multiple_of((1 - core) * share, share), share)
    return mine, theirs


def split_rows(place_ref, value, scratch_ref, keep_ref, send_ref):
    core = place_ref[0]
    scratch_ref[...] = value.reshape(scratch_ref.shape)
    keep_ref[...] = scratch_ref[:, core]
    send_ref[...] = scratch_ref[:, 1 - core]


def store_sums(sum_ref, sums):
    rows = sum_ref.shape[0]
    sum_ref[...] = jnp.concatenate(sums + [jnp.zeros((rows - len(sums), 128), F32)], axis=0)


def copy_into(pairs, done):
    return [
        pltpu.make_async_copy(source, target, done.at[at])
        for at, (source, target) in enumerate(pairs)
    ]


def first_column_kernel(
    place_ref,
    table_ref,
    field_hbm,
    lower_hbm,
    basis_hbm,
    kernel_hbm,
    second_hbm,
    upper_ref,
    eigen_ref,
    *refs,
):
    wide_refs, refs, outs = refs[:-13], refs[-7:], refs[-13:-7]
    start_ref, weight_ref, column_ref, keep_ref, send_ref, sum_ref = outs
    lower_ref, basis_ref, kernel_ref, second_ref, scratch_ref, field_ref, done = refs
    copies = copy_into(
        (
            (field_hbm, field_ref),
            (lower_hbm, lower_ref),
            (basis_hbm, basis_ref),
            (kernel_hbm, kernel_ref),
            (second_hbm, second_ref),
        ),
        done,
    )
    for copy in copies[:2]:
        copy.start()
    mean = functools.reduce(jnp.add, [table_ref[at] for at in range(NCLASS)]) * (1.0 / NCLASS)
    height, width = start_ref.shape
    tall = jnp.broadcast_to(eigen_ref[...], (128, height)).T
    planes = len(wide_refs)
    part = wide_refs[0].shape[1]
    for block in range(width // part):
        wanted = place_ref[0] * (width // part) + block
        wide = jnp.zeros((1, part), F32)
        for by, wide_ref in enumerate(wide_refs):
            here = (place_ref[2] + planes - by) % planes == wanted
            wide = jnp.where(here, wide_ref[...], wide)
        for at in range(0, part, 128):
            lanes = slice(block * part + at, block * part + at + 128)
            weight_ref[:, lanes] = 1.0 / (tall * wide[:, at : at + 128] + mean)
    copies[0].wait()
    field = field_ref[...].reshape(height, width)
    for copy in copies[2:]:
        copy.start()
    both = side_by_side(field)
    above = times_both(upper_ref[...], both)
    copies[1].wait()
    spectral = jnp.concatenate([above, times_both(lower_ref[...], both)], axis=0)
    weighted = spectral * weight_ref[...]
    start_ref[...] = field
    store_sums(sum_ref, [fold(spectral * weighted)])
    copies[2].wait()
    column = times_left(basis_ref[...], weighted)
    column_ref[...] = column
    split_rows(place_ref, column, scratch_ref, keep_ref, send_ref)
    copies[3].wait()
    copies[4].wait()


def next_column_kernel(
    place_ref,
    held_ref,
    got_ref,
    start_ref,
    weight_ref,
    upper_ref,
    lower_ref,
    basis_ref,
    own_ref,
    column_ref,
    keep_ref,
    send_ref,
    sum_ref,
    scratch_ref,
):
    core = place_ref[0]
    tall = got_ref.shape[0] - own_ref.shape[0]
    scratch_ref[:, core] = held_ref[...]
    scratch_ref[:, 1 - core] = got_ref[:tall, :].reshape(held_ref.shape)
    total = jnp.sum(own_ref[...] + got_ref[tall:, :128], axis=1, keepdims=True)
    gamma, curvature = total[0:1], total[1:2]
    proper = (gamma > 0) & (curvature > 0)
    step = jnp.where(proper, gamma / jnp.where(proper, curvature, 1.0), 1.0)
    field = start_ref[...] - step * scratch_ref[...].reshape(start_ref.shape)
    both = side_by_side(field)
    halves = [times_both(half_ref[...], both) for half_ref in (upper_ref, lower_ref)]
    spectral = jnp.concatenate(halves, axis=0)
    weighted = spectral * weight_ref[...]
    store_sums(sum_ref, [fold(spectral * weighted), jnp.broadcast_to(step, (1, 128))])
    column = times_left(basis_ref[...], weighted)
    column_ref[...] = column
    split_rows(place_ref, column, scratch_ref, keep_ref, send_ref)


def column_image_kernel(place_ref, column_ref, kernel_ref, keep_ref, send_ref, scratch_ref):
    image = times_left(kernel_ref[...], column_ref[...])
    split_rows(place_ref, image, scratch_ref, keep_ref, send_ref)


def first_column_image_kernel(place_ref, column_ref, kernel_ref, high_hbm, low_hbm, *refs):
    keep_ref, send_ref, high_ref, low_ref, scratch_ref, done = refs
    copies = copy_into(((high_hbm, high_ref), (low_hbm, low_ref)), done)
    for copy in copies:
        copy.start()
    column_image_kernel(place_ref, column_ref, kernel_ref, keep_ref, send_ref, scratch_ref)
    for copy in copies:
        copy.wait()


def join_columns(place_ref, scratch_ref, keep_ref, got_ref):
    height, width = scratch_ref.shape
    mine, theirs = both_shares(place_ref, width // 2)
    scratch_ref[:, mine] = keep_ref[...].reshape(height, width // 2)
    scratch_ref[:, theirs] = got_ref[...].reshape(height, width // 2)
    return scratch_ref[...]


def row_kernel(place_ref, keep_ref, got_ref, basis_ref, z_ref, scratch_ref):
    field = join_columns(place_ref, scratch_ref, keep_ref, got_ref)
    z_ref[...] = times_right(field, basis_ref[...], 1).reshape(z_ref.shape)


def row_image(place_ref, keep_ref, got_ref, high_ref, low_ref, scratch_ref):
    field = join_columns(place_ref, scratch_ref, keep_ref, got_ref)
    high, low = split(field)
    dims = (((1,), (1,)), ((), ()))
    both = jnp.concatenate([high, low], axis=0)
    result = lax.dot_general(both, high_ref[...], dims, preferred_element_type=F32)
    small = lax.dot_general(high, low_ref[...], dims, preferred_element_type=F32)
    return result[: field.shape[0]] + (result[field.shape[0] :] + small)


def first_row_kernel(place_ref, keep_ref, got_ref, basis_ref, near_hbm, far_hbm, *refs):
    z_ref, noise_ref, scratch_ref, done = refs
    sample = place_ref[1]
    copies = copy_into(
        ((near_hbm, noise_ref.at[:, sample]), (far_hbm, noise_ref.at[:, 1 - sample])), done
    )
    for copy in copies:
        copy.start()
    row_kernel(place_ref, keep_ref, got_ref, basis_ref, z_ref, scratch_ref)
    for copy in copies:
        copy.wait()


def full_image(place_ref, keep_ref, got_ref, z_ref, noise_ref, high_ref, low_ref, image_ref, scratch_ref):
    image = row_image(place_ref, keep_ref, got_ref, high_ref, low_ref, scratch_ref)
    field = z_ref[...].reshape(image.shape)
    image = image + noise_ref[...].reshape(image.shape) * field
    image_ref[...] = image.reshape(image_ref.shape)
    return fold(field * image)


def first_image_kernel(
    place_ref,
    keep_ref,
    got_ref,
    z_ref,
    noise_ref,
    high_ref,
    low_ref,
    one_ref,
    image_ref,
    sum_ref,
    scratch_ref,
):
    refs = (place_ref, keep_ref, got_ref, z_ref, noise_ref, high_ref, low_ref)
    store_sums(sum_ref, [one_ref[0:1], full_image(*refs, image_ref, scratch_ref)])


def returned(place_ref, image_ref, basis_ref, whose, half):
    lanes = both_shares(place_ref, half)[whose]
    image = image_ref[...].reshape(-1, basis_ref.shape[0])
    return times_right(image, basis_ref[:, lanes], 0)


def return_theirs_kernel(place_ref, image_ref, basis_ref, sum_ref, out_ref):
    part = returned(place_ref, image_ref, basis_ref, 1, out_ref.shape[1])
    out_ref[: part.shape[0], :] = part
    out_ref[part.shape[0] :, :] = jnp.concatenate(
        [sum_ref[...]] * (out_ref.shape[1] // 128), axis=1
    )


def return_mine_kernel(place_ref, image_ref, basis_ref, out_ref):
    part = returned(place_ref, image_ref, basis_ref, 0, out_ref.shape[2])
    out_ref[...] = part.reshape(out_ref.shape)


def last_image_kernel(
    place_ref,
    keep_ref,
    got_ref,
    z_ref,
    noise_ref,
    high_ref,
    low_ref,
    one_ref,
    two_ref,
    image_ref,
    sum_ref,
    scratch_ref,
):
    refs = (place_ref, keep_ref, got_ref, z_ref, noise_ref, high_ref, low_ref)
    last = full_image(*refs, image_ref, scratch_ref)
    rows = [one_ref[0:2], two_ref[0:1], last, two_ref[1:2], jnp.zeros((3, 128), F32)]
    sum_ref[...] = jnp.broadcast_to(jnp.concatenate(rows, axis=0)[None], sum_ref.shape)


def combine_kernel(place_ref, sum_ref, z_ref, image_ref, f_ref, f_image_ref, out_ref):
    devices, kinds, lanes = sum_ref.shape
    pairs = devices // 2
    total = jnp.sum(sum_ref[...], axis=2, keepdims=True)
    total = jnp.sum(total.reshape(pairs, 2, kinds, 1), axis=1)
    g00, g01, g11, h11, step = (total[:, at : at + 1] for at in range(5))
    step = step * (1.0 / (2 * lanes))

    def over_pairs(value):
        return jnp.sum(value, axis=0, keepdims=True)

    gamma = over_pairs(g00)
    alpha = gamma / over_pairs(g01)
    theta = alpha / step
    rest = 1.0 - theta
    gamma_new = over_pairs(rest * rest * g00 + theta * theta * g11)
    turn = rest + gamma_new / gamma
    curvature = over_pairs(
        turn * turn * g01 - 2.0 * theta * turn * g11 / step + theta * theta * h11
    )
    alpha_new = gamma_new / curvature
    own = lax.broadcasted_iota(jnp.int32, theta.shape, 0) == place_ref[3]
    on_z = over_pairs(jnp.where(own, alpha + alpha_new * turn, 0.0))
    on_f = over_pairs(jnp.where(own, alpha_new * theta, 0.0))
    share = z_ref.shape[1]
    out_ref[:, :share, :] = on_z * z_ref[...] + on_f * f_ref[...]
    out_ref[:, share:, :] = on_z * image_ref[...] + on_f * f_image_ref[...]


def finish_kernel(got_ref, right_ref, solution_ref, residual_ref):
    samples = got_ref.shape[0]
    rows = got_ref.shape[1] // 2
    for sample in range(samples):
        solution_ref[sample, 0] = got_ref[sample, :rows, :]
        residual_ref[sample, 0] = right_ref[sample, 0] - got_ref[sample, rows:, :]


def paired_body(
    right_side,
    classes,
    noise_table,
    kernel_first,
    kernel_second,
    basis_first,
    basis_second,
    eigen_first,
    eigen_second,
):
    groups = lax.axis_size("mode")
    samples, planes, rows, width = right_side.shape
    height = groups * rows
    cores = 2
    half = width // cores
    blocks = groups // cores
    unit = cores * samples
    index = lax.axis_index("mode")
    core = index % cores
    sample = (index // cores) % samples
    plane = index // unit
    place = jnp.stack([core, sample, plane, index // cores]).astype(jnp.int32)

    def shape_of(*shape):
        return jax.ShapeDtypeStruct(shape, F32)

    smem = pl.BlockSpec(memory_space=pltpu.SMEM)

    hbm = pl.BlockSpec(memory_space=pltpu.HBM)

    def full(*shape):
        return pl.BlockSpec(
            shape, lambda *at: (0,) * len(shape), pipeline_mode=pl.Buffered(1)
        )

    def whole_out(*shape):
        return pl.BlockSpec(shape, lambda *at: (0,) * len(shape))

    core_swap = [(at, at ^ 1) for at in range(groups)]
    sample_swap = [(at, at ^ cores) for at in range(groups)]

    def in_hbm(value):
        return pltpu.with_memory_space_constraint(value, pltpu.HBM)

    def noise_of(shifts):
        return pl.pallas_call(
            functools.partial(noise_kernel, shifts, unit),
            grid=(1,),
            in_specs=[smem, pl.BlockSpec(memory_space=pltpu.HBM)],
            out_specs=[whole_out(rows, width)] * len(shifts),
            out_shape=[shape_of(rows, width)] * len(shifts),
            scratch_shapes=[
                pltpu.VMEM((len(shifts), rows, width), jnp.int32),
                pltpu.SemaphoreType.DMA((len(shifts),)),
            ],
            compiler_params=params(1, 4),
        )(in_hbm(noise_table), in_hbm(classes))

    def plane_shift(value, by):
        pairs = [(at, (at + by * unit) % groups) for at in range(groups)]
        return lax.ppermute(value, "mode", pairs)

    ahead = planes // 2
    others = [by for by in range(planes) if by != ahead]
    near = [None] * planes
    picked = pl.pallas_call(
        functools.partial(pick_kernel, ahead, unit),
        in_specs=[hbm],
        out_specs=pl.BlockSpec(memory_space=pltpu.VMEM),
        out_shape=jax.ShapeDtypeStruct((rows, width), jnp.int32),
        scratch_shapes=[pltpu.SemaphoreType.DMA],
        compiler_params=pltpu.CompilerParams(vmem_limit_bytes=1024 * 1024),
        name="pick",
    )(in_hbm(classes))
    near[ahead] = plane_shift(picked, ahead)
    rest = noise_of(others)
    for by, value in zip(others, rest):
        near[by] = plane_shift(value, by) if by else value

    outgoing = pl.pallas_call(
        outgoing_kernel,
        grid=(planes,),
        in_specs=[
            pl.BlockSpec((samples, 1, rows, width), lambda p: (0, p, 0, 0)),
            full(width, width),
        ],
        out_specs=pl.BlockSpec((1, samples, cores, rows, half), lambda p: (p, 0, 0, 0, 0)),
        out_shape=shape_of(planes, samples, cores, rows, half),
        compiler_params=params(1, 56),
        name="outgoing",
    )(right_side, basis_second)
    arrived = lax.all_to_all(
        outgoing.reshape(groups, rows, half), "mode", split_axis=0, concat_axis=0, tiled=True
    )

    eigen = eigen_second.reshape(1, -1)
    for reach in (1, cores):
        other = lax.ppermute(eigen, "mode", [(at, at ^ reach) for at in range(groups)])
        low = (index // reach) % 2 == 0
        eigen = jnp.where(
            low,
            jnp.concatenate([eigen, other], axis=1),
            jnp.concatenate([other, eigen], axis=1),
        )
    near, eigen = pl.pallas_call(
        functools.partial(join_kernel, ahead),
        grid=(1,),
        in_specs=[smem, smem, full(*eigen.shape)] + [full(rows, width)] * planes,
        out_specs=[whole_out(planes, rows, width), whole_out(*eigen.shape)],
        out_shape=[shape_of(planes, rows, width), shape_of(*eigen.shape)],
        compiler_params=params(1, 58),
        name="join",
    )(place, noise_table, eigen, *near)
    far = lax.ppermute(near, "mode", sample_swap)
    shifted = [eigen] + [
        lax.ppermute(eigen, "mode", [(at, (at + by * unit) % groups) for at in range(groups)])
        for by in range(1, planes)
    ]
    bf16_square = jax.ShapeDtypeStruct((height, height), BF16)
    bf16_half = jax.ShapeDtypeStruct((height // 2, height), BF16)
    prepare = pl.pallas_call(
        prepare_kernel,
        grid=(1,),
        in_specs=[full(height, height), full(width, width), full(width, width)]
        + [pl.BlockSpec(memory_space=pl.ANY)],
        out_specs=[whole_out(height // 2, height)] * 2 + [whole_out(height, height)] * 2,
        out_shape=[bf16_half] * 2 + [bf16_square] * 2,
        compiler_params=params(1, 24),
        name="prepare",
    )
    upper, lower, high, low = prepare(basis_first, basis_second, kernel_second, eigen)

    def swap(value):
        return lax.ppermute(value, "mode", core_swap)

    def call(kernel, inputs, shapes, scratch_shape, specs=None, more=(), mebibytes=12, matrices=()):
        return pl.pallas_call(
            kernel,
            grid=(1,),
            in_specs=specs or [smem] + [full(*value.shape) for value in inputs[1:]],
            out_specs=[whole_out(*shape) for shape in shapes]
            + [whole_out(*value.shape) for value in matrices],
            out_shape=[shape_of(*shape) for shape in shapes] + list(matrices),
            scratch_shapes=[*([pltpu.VMEM(scratch_shape, F32)] if scratch_shape else []), *more],
            compiler_params=params(1, mebibytes),
        )(*inputs)

    tile = (height, half)
    piece = (blocks, rows, half)
    whole = (blocks, rows, width)
    by_rows = (blocks, cores, rows, half)
    flat = (blocks * rows, width)
    sums_shape = (8, 128)

    (start, weights, column, keep, send, sum_one, lower, *squares) = call(
        first_column_kernel,
        (
            place,
            noise_table,
            *(in_hbm(value) for value in (arrived, lower, basis_first, kernel_first, basis_second)),
            upper,
            eigen_first.reshape(1, -1),
            *shifted,
        ),
        (tile, tile, tile, piece, piece, sums_shape),
        by_rows,
        [smem, smem]
        + [hbm] * 5
        + [full(height // 2, height), full(1, height)]
        + [full(*value.shape) for value in shifted],
        [pltpu.VMEM((groups, rows, half), F32), pltpu.SemaphoreType.DMA((5,))],
        16,
        [bf16_half] + [bf16_square] * 3,
    )
    basis_first, kernel_first, basis_second = squares
    got = swap(send)
    image_keep, image_send, high, low = call(
        first_column_image_kernel,
        (place, column, kernel_first, in_hbm(high), in_hbm(low)),
        (piece, piece),
        by_rows,
        [smem, full(*tile), full(height, height), hbm, hbm],
        [pltpu.SemaphoreType.DMA((2,))],
        matrices=[bf16_square] * 2,
    )
    image_got = swap(image_send)
    inputs = (place, keep, got, basis_second)
    z_field, noise = call(
        first_row_kernel,
        (*inputs, in_hbm(near), in_hbm(far)),
        (whole, (planes, samples, rows, width)),
        flat,
        [smem] + [full(*value.shape) for value in inputs[1:]] + [hbm] * 2,
        [pltpu.SemaphoreType.DMA((2,))],
    )
    image, pair_sum = call(
        first_image_kernel,
        (place, image_keep, image_got, z_field, noise, high, low, sum_one),
        (whole, sums_shape),
        flat,
    )

    (back_send,) = call(
        return_theirs_kernel, (place, image, basis_second, pair_sum), ((flat[0] + 8, half),), None
    )
    (back_keep,) = call(return_mine_kernel, (place, image, basis_second), (piece,), None)
    back_got = swap(back_send)

    column, keep, send, sum_two = call(
        next_column_kernel,
        (
            place,
            back_keep,
            back_got,
            start,
            weights,
            upper,
            lower,
            basis_first,
            pair_sum,
        ),
        (tile, piece, piece, sums_shape),
        by_rows,
    )
    got = swap(send)
    image_keep, image_send = call(
        column_image_kernel, (place, column, kernel_first), (piece, piece), by_rows
    )
    image_got = swap(image_send)
    (f_field,) = call(row_kernel, (place, keep, got, basis_second), (whole,), flat)
    f_image, sums = call(
        last_image_kernel,
        (
            place,
            image_keep,
            image_got,
            f_field,
            noise,
            high,
            low,
            pair_sum,
            sum_two,
        ),
        (whole, (groups, 8, 128)),
        flat,
    )
    sums = lax.all_to_all(sums, "mode", split_axis=0, concat_axis=0, tiled=True)

    few = blocks
    few_spec = pl.BlockSpec((few, rows, width), lambda i: (i, 0, 0))
    answer = pl.pallas_call(
        combine_kernel,
        grid=(1,),
        in_specs=[smem, full(groups, 8, 128)] + [few_spec] * 4,
        out_specs=pl.BlockSpec((few, 2 * rows, width), lambda i: (i, 0, 0)),
        out_shape=shape_of(blocks, 2 * rows, width),
        compiler_params=params(1, 6),
        name="combine",
    )(place, sums, z_field, image, f_field, f_image)
    answer = lax.all_to_all(
        answer,
        "mode",
        split_axis=0,
        concat_axis=0,
        axis_index_groups=[list(range(at, groups, cores)) for at in range(cores)],
        tiled=True,
    )

    block = pl.BlockSpec((samples, 1, rows, width), lambda p: (0, p, 0, 0))
    return tuple(
        pl.pallas_call(
            finish_kernel,
            grid=(planes,),
            in_specs=[
                pl.BlockSpec((samples, 2 * rows, width), lambda p: (p, 0, 0)),
                block,
            ],
            out_specs=[block, block],
            out_shape=[shape_of(*right_side.shape)] * 2,
            compiler_params=params(1, 10),
            name="finish",
        )(answer, right_side)
    )


def body(right_side, classes, *rest):
    groups = lax.axis_size("mode")
    samples, planes, rows, width = right_side.shape
    paired = (
        groups == 2 * samples * planes
        and samples == 2
        and rows % 8 == 0
        and width % 512 == 0
        and planes % 2 == 0
    )
    chosen = paired_body if paired else general_body
    return chosen(right_side, classes, *rest)


def solution(mesh):
    in_specs = (
        P(None, "blocks", "mode", None),
        P("blocks", "mode", None),
        P(),
        P(),
        P(),
        P(),
        P(),
        P(),
        P("mode"),
    )
    out_specs = (P(None, "blocks", "mode", None), P(None, "blocks", "mode", None))
    return jax.shard_map(body, mesh=mesh, in_specs=in_specs, out_specs=out_specs, check_vma=False)
```

```python
import functools

import jax
import jax.numpy as jnp
from jax import lax
from jax.experimental import pallas as pl
from jax.experimental.pallas import tpu as pltpu
from jax.sharding import PartitionSpec as P


NCLASS = 8
ITERS = 2
F32 = jnp.float32
BF16 = jnp.bfloat16


def along_rows(matrix, field):
    return jnp.einsum("jk,sprk->sprj", matrix, field, precision=lax.Precision.HIGHEST)


def rows_to_send(matrix, field, groups):
    result = jnp.einsum("kj,sprk->jspr", matrix, field, precision=lax.Precision.HIGHEST)
    return result.reshape(groups, -1)


def received_to_columns(matrix, received, shape5):
    groups, _, _, _, rows = shape5
    block = received.reshape(shape5)
    reshaped = matrix.reshape(groups, rows, matrix.shape[1])
    return jnp.einsum("mri,mcspr->cspi", reshaped, block, precision=lax.Precision.HIGHEST)


def along_columns(matrix, columns):
    return jnp.einsum("ik,cspk->cspi", matrix, columns, precision=lax.Precision.HIGHEST)


def columns_to_send(matrix, columns, groups, rows):
    reshaped = matrix.reshape(groups, rows, matrix.shape[1])
    result = jnp.einsum("mrk,cspk->mcspr", reshaped, columns, precision=lax.Precision.HIGHEST)
    return result.reshape(groups, -1)


def received_to_rows(matrix, received, shape5):
    groups, cols, _, _, _ = shape5
    block = received.reshape(shape5)
    reshaped = matrix.reshape(matrix.shape[0], groups, cols)
    return jnp.einsum("jmc,mcspr->sprj", reshaped, block, precision=lax.Precision.HIGHEST)


def general_body(
    right_side,
    classes,
    noise_table,
    kernel_first,
    kernel_second,
    basis_first,
    basis_second,
    eigen_first,
    eigen_second,
):
    groups = lax.axis_size("mode")
    samples, planes, rows, _ = right_side.shape
    cols = eigen_second.shape[0]
    shape5 = (groups, cols, samples, planes, rows)
    kern_one = kernel_first.astype(F32)
    kern_two = kernel_second.astype(F32)
    base_one = basis_first.astype(F32)
    base_two = basis_second.astype(F32)
    noise = jnp.zeros(classes.shape, F32)
    for level in range(NCLASS):
        noise = noise + jnp.where(classes == level, noise_table[level], 0.0)
    noise = noise[None]
    mean_noise = jnp.mean(noise_table)
    col_weights = 1.0 / (eigen_second[:, None] * eigen_first[None, :] + mean_noise)
    col_weights = col_weights[:, None, None, :]

    def exchange(outgoing):
        return lax.all_to_all(outgoing, "mode", split_axis=0, concat_axis=0, tiled=True)

    def precond_apply(field):
        incoming = exchange(rows_to_send(base_two, field, groups))
        weighted = received_to_columns(base_one, incoming, shape5) * col_weights
        columns = along_columns(base_one, weighted)
        back = exchange(columns_to_send(base_one, weighted, groups, rows))
        kernel_back = exchange(columns_to_send(kern_one, columns, groups, rows))
        z_field = received_to_rows(base_two, back, shape5)
        image = (
            along_rows(kern_two, received_to_rows(base_two, kernel_back, shape5)) + noise * z_field
        )
        return (z_field, image)

    def inner(left, right):
        return lax.psum(jnp.sum(left * right), "mode")

    solution_field = jnp.zeros_like(right_side)
    residual = right_side
    z_field, image = precond_apply(residual)
    direction, along = (z_field, image)
    gamma = inner(residual, z_field)
    for step in range(ITERS):
        alpha = gamma / inner(direction, along)
        solution_field = solution_field + alpha * direction
        residual = residual - alpha * along
        if step + 1 < ITERS:
            z_field, image = precond_apply(residual)
            gamma_new = inner(residual, z_field)
            ratio = gamma_new / gamma
            direction = z_field + ratio * direction
            along = image + ratio * along
            gamma = gamma_new
    return (solution_field, residual)


def split(value):
    high = value.astype(BF16)
    low = (value - high.astype(F32)).astype(BF16)
    return high, low


def times_right(value, matrix, contract):
    high, low = split(value)
    dims = (((1,), (contract,)), ((), ()))
    both = jnp.concatenate([high, low], axis=0)
    result = lax.dot_general(both, matrix, dims, preferred_element_type=F32)
    return result[: value.shape[0]] + result[value.shape[0] :]


def side_by_side(value):
    return jnp.concatenate(split(value), axis=1)


def times_both(matrix, both):
    width = both.shape[1] // 2
    dims = (((1,), (0,)), ((), ()))
    result = lax.dot_general(matrix, both, dims, preferred_element_type=F32)
    return result[:, :width] + result[:, width:]


def times_left(matrix, value):
    return times_both(matrix, side_by_side(value))


def fold(value):
    total = jnp.sum(value, axis=0, keepdims=True)
    return functools.reduce(
        jnp.add, [total[:, at : at + 128] for at in range(0, total.shape[1], 128)]
    )


def params(dims, mebibytes):
    return pltpu.CompilerParams(
        dimension_semantics=("arbitrary",) * dims, vmem_limit_bytes=mebibytes * 1024 * 1024
    )


def look_up(table_ref, level):
    noise = jnp.full(level.shape, table_ref[0], F32)
    for index in range(1, NCLASS):
        noise = jnp.where(level == index, table_ref[index], noise)
    return noise


def pick_kernel(by, unit, class_hbm, out_ref, done):
    plane = lax.axis_index("mode") // unit
    copy = pltpu.make_async_copy(class_hbm.at[(plane + by) % class_hbm.shape[0]], out_ref, done)
    copy.start()
    copy.wait()


def noise_kernel(shifts, unit, table_ref, class_hbm, *refs):
    out_refs, (class_ref, done) = refs[:-2], refs[-2:]
    planes = class_hbm.shape[0]
    plane = lax.axis_index("mode") // unit
    pairs = [(class_hbm.at[(plane + by) % planes], class_ref.at[at]) for at, by in enumerate(shifts)]
    copies = copy_into(pairs, done)
    for copy in copies:
        copy.start()
    for at, copy in enumerate(copies):
        copy.wait()
        out_refs[at][...] = look_up(table_ref, class_ref[at])


def join_kernel(ahead, place_ref, table_ref, value_ref, *refs):
    parts, (joined_ref, out_ref) = refs[:-2], refs[-2:]
    planes = len(parts)
    for by, part in enumerate(parts):
        noise = look_up(table_ref, part[...]) if by == ahead else part[...]
        joined_ref[(place_ref[2] + planes - by) % planes] = noise
    out_ref[...] = value_ref[...]


def prepare_kernel(
    first_ref,
    second_ref,
    kernel_ref,
    _,
    upper_ref,
    lower_ref,
    high_ref,
    low_ref,
):
    turned = first_ref[...].T
    middle = upper_ref.shape[0]
    upper_ref[...] = turned[:middle]
    lower_ref[...] = turned[middle:]
    dims = (((1,), (0,)), ((), ()))
    product = lax.dot_general(
        kernel_ref[...], second_ref[...], dims, preferred_element_type=F32
    )
    high_ref[...], low_ref[...] = split(product)


def outgoing_kernel(right_ref, basis_ref, out_ref):
    samples, _, rows, width = right_ref.shape
    cores = out_ref.shape[2]
    half = width // cores
    field = right_ref[...].reshape(samples * rows, width)
    mapped = times_right(field, basis_ref[...], 0)
    for sample in range(samples):
        for core in range(cores):
            out_ref[0, sample, core] = mapped[
                sample * rows : (sample + 1) * rows, core * half : (core + 1) * half
            ]


def both_shares(place_ref, share):
    core = place_ref[0]
    mine = pl.ds(pl.multiple_of(core * share, share), share)
    theirs = pl.ds(pl.multiple_of((1 - core) * share, share), share)
    return mine, theirs


def split_rows(place_ref, value, scratch_ref, keep_ref, send_ref):
    core = place_ref[0]
    scratch_ref[...] = value.reshape(scratch_ref.shape)
    keep_ref[...] = scratch_ref[:, core]
    send_ref[...] = scratch_ref[:, 1 - core]


def store_sums(sum_ref, sums):
    rows = sum_ref.shape[0]
    sum_ref[...] = jnp.concatenate(sums + [jnp.zeros((rows - len(sums), 128), F32)], axis=0)


def copy_into(pairs, done):
    return [
        pltpu.make_async_copy(source, target, done.at[at])
        for at, (source, target) in enumerate(pairs)
    ]


def first_column_kernel(
    place_ref,
    table_ref,
    field_hbm,
    lower_hbm,
    basis_hbm,
    kernel_hbm,
    second_hbm,
    upper_ref,
    eigen_ref,
    *refs,
):
    wide_refs, refs, outs = refs[:-13], refs[-7:], refs[-13:-7]
    start_ref, weight_ref, column_ref, keep_ref, send_ref, sum_ref = outs
    lower_ref, basis_ref, kernel_ref, second_ref, scratch_ref, field_ref, done = refs
    groups = field_ref.shape[0]
    first, second = pl.ds(0, groups // 2), pl.ds(groups // 2, groups // 2)
    copies = copy_into(
        (
            (field_hbm.at[first], field_ref.at[first]),
            (field_hbm.at[second], field_ref.at[second]),
            (lower_hbm, lower_ref),
            (basis_hbm, basis_ref),
            (kernel_hbm, kernel_ref),
            (second_hbm, second_ref),
        ),
        done,
    )
    for copy in copies[:3]:
        copy.start()
    mean = functools.reduce(jnp.add, [table_ref[at] for at in range(NCLASS)]) * (1.0 / NCLASS)
    height, width = start_ref.shape
    tall = jnp.broadcast_to(eigen_ref[...], (128, height)).T
    planes = len(wide_refs)
    part = wide_refs[0].shape[1]
    for block in range(width // part):
        wanted = place_ref[0] * (width // part) + block
        wide = jnp.zeros((1, part), F32)
        for by, wide_ref in enumerate(wide_refs):
            here = (place_ref[2] + planes - by) % planes == wanted
            wide = jnp.where(here, wide_ref[...], wide)
        for at in range(0, part, 128):
            lanes = slice(block * part + at, block * part + at + 128)
            weight_ref[:, lanes] = 1.0 / (tall * wide[:, at : at + 128] + mean)
    middle = height // 2
    copies[0].wait()
    start = side_by_side(field_ref[: groups // 2].reshape(middle, width))
    above = times_both(upper_ref[:, :middle], start)
    copies[1].wait()
    for copy in copies[3:]:
        copy.start()
    end = side_by_side(field_ref[groups // 2 :].reshape(middle, width))
    above = above + times_both(upper_ref[:, middle:], end)
    copies[2].wait()
    below = times_both(lower_ref[...], jnp.concatenate([start, end], axis=0))
    spectral = jnp.concatenate([above, below], axis=0)
    weighted = spectral * weight_ref[...]
    start_ref[...] = field_ref[...].reshape(height, width)
    store_sums(sum_ref, [fold(spectral * weighted)])
    copies[3].wait()
    column = times_left(basis_ref[...], weighted)
    column_ref[...] = column
    split_rows(place_ref, column, scratch_ref, keep_ref, send_ref)
    copies[4].wait()
    copies[5].wait()


def next_column_kernel(
    place_ref,
    held_ref,
    got_ref,
    start_ref,
    weight_ref,
    upper_ref,
    lower_ref,
    basis_ref,
    own_ref,
    column_ref,
    keep_ref,
    send_ref,
    sum_ref,
    scratch_ref,
):
    core = place_ref[0]
    tall = got_ref.shape[0] - own_ref.shape[0]
    scratch_ref[:, core] = held_ref[...]
    scratch_ref[:, 1 - core] = got_ref[:tall, :].reshape(held_ref.shape)
    total = jnp.sum(own_ref[...] + got_ref[tall:, :128], axis=1, keepdims=True)
    gamma, curvature = total[0:1], total[1:2]
    proper = (gamma > 0) & (curvature > 0)
    step = jnp.where(proper, gamma / jnp.where(proper, curvature, 1.0), 1.0)
    field = start_ref[...] - step * scratch_ref[...].reshape(start_ref.shape)
    both = side_by_side(field)
    halves = [times_both(half_ref[...], both) for half_ref in (upper_ref, lower_ref)]
    spectral = jnp.concatenate(halves, axis=0)
    weighted = spectral * weight_ref[...]
    store_sums(sum_ref, [fold(spectral * weighted), jnp.broadcast_to(step, (1, 128))])
    column = times_left(basis_ref[...], weighted)
    column_ref[...] = column
    split_rows(place_ref, column, scratch_ref, keep_ref, send_ref)


def column_image_kernel(place_ref, column_ref, kernel_ref, keep_ref, send_ref, scratch_ref):
    image = times_left(kernel_ref[...], column_ref[...])
    split_rows(place_ref, image, scratch_ref, keep_ref, send_ref)


def first_column_image_kernel(place_ref, column_ref, kernel_ref, high_hbm, low_hbm, *refs):
    keep_ref, send_ref, high_ref, low_ref, scratch_ref, done = refs
    copies = copy_into(((high_hbm, high_ref), (low_hbm, low_ref)), done)
    for copy in copies:
        copy.start()
    column_image_kernel(place_ref, column_ref, kernel_ref, keep_ref, send_ref, scratch_ref)
    for copy in copies:
        copy.wait()


def join_columns(place_ref, scratch_ref, keep_ref, got_ref):
    height, width = scratch_ref.shape
    mine, theirs = both_shares(place_ref, width // 2)
    scratch_ref[:, mine] = keep_ref[...].reshape(height, width // 2)
    scratch_ref[:, theirs] = got_ref[...].reshape(height, width // 2)
    return scratch_ref[...]


def row_kernel(place_ref, keep_ref, got_ref, basis_ref, z_ref, scratch_ref):
    field = join_columns(place_ref, scratch_ref, keep_ref, got_ref)
    z_ref[...] = times_right(field, basis_ref[...], 1).reshape(z_ref.shape)


def row_image(place_ref, keep_ref, got_ref, high_ref, low_ref, scratch_ref):
    field = join_columns(place_ref, scratch_ref, keep_ref, got_ref)
    high, low = split(field)
    dims = (((1,), (1,)), ((), ()))
    both = jnp.concatenate([high, low], axis=0)
    result = lax.dot_general(both, high_ref[...], dims, preferred_element_type=F32)
    small = lax.dot_general(high, low_ref[...], dims, preferred_element_type=F32)
    return result[: field.shape[0]] + (result[field.shape[0] :] + small)


def first_row_kernel(place_ref, keep_ref, got_ref, basis_ref, near_hbm, far_hbm, *refs):
    z_ref, noise_ref, scratch_ref, done = refs
    sample = place_ref[1]
    copies = copy_into(
        ((near_hbm, noise_ref.at[:, sample]), (far_hbm, noise_ref.at[:, 1 - sample])), done
    )
    for copy in copies:
        copy.start()
    row_kernel(place_ref, keep_ref, got_ref, basis_ref, z_ref, scratch_ref)
    for copy in copies:
        copy.wait()


def full_image(place_ref, keep_ref, got_ref, z_ref, noise_ref, high_ref, low_ref, image_ref, scratch_ref):
    image = row_image(place_ref, keep_ref, got_ref, high_ref, low_ref, scratch_ref)
    field = z_ref[...].reshape(image.shape)
    image = image + noise_ref[...].reshape(image.shape) * field
    image_ref[...] = image.reshape(image_ref.shape)
    return fold(field * image)


def first_image_kernel(
    place_ref,
    keep_ref,
    got_ref,
    z_ref,
    noise_ref,
    high_ref,
    low_ref,
    one_ref,
    image_ref,
    sum_ref,
    scratch_ref,
):
    refs = (place_ref, keep_ref, got_ref, z_ref, noise_ref, high_ref, low_ref)
    store_sums(sum_ref, [one_ref[0:1], full_image(*refs, image_ref, scratch_ref)])


def returned(place_ref, image_ref, basis_ref, whose, half):
    lanes = both_shares(place_ref, half)[whose]
    image = image_ref[...].reshape(-1, basis_ref.shape[0])
    return times_right(image, basis_ref[:, lanes], 0)


def return_theirs_kernel(place_ref, image_ref, basis_ref, sum_ref, out_ref):
    part = returned(place_ref, image_ref, basis_ref, 1, out_ref.shape[1])
    out_ref[: part.shape[0], :] = part
    out_ref[part.shape[0] :, :] = jnp.concatenate(
        [sum_ref[...]] * (out_ref.shape[1] // 128), axis=1
    )


def return_mine_kernel(place_ref, image_ref, basis_ref, out_ref):
    part = returned(place_ref, image_ref, basis_ref, 0, out_ref.shape[2])
    out_ref[...] = part.reshape(out_ref.shape)


def last_image_kernel(
    place_ref,
    keep_ref,
    got_ref,
    z_ref,
    noise_ref,
    high_ref,
    low_ref,
    one_ref,
    two_ref,
    image_ref,
    sum_ref,
    scratch_ref,
):
    refs = (place_ref, keep_ref, got_ref, z_ref, noise_ref, high_ref, low_ref)
    last = full_image(*refs, image_ref, scratch_ref)
    rows = [one_ref[0:2], two_ref[0:1], last, two_ref[1:2], jnp.zeros((3, 128), F32)]
    sum_ref[...] = jnp.broadcast_to(jnp.concatenate(rows, axis=0)[None], sum_ref.shape)


def combine_kernel(place_ref, sum_ref, z_ref, image_ref, f_ref, f_image_ref, out_ref):
    devices, kinds, lanes = sum_ref.shape
    pairs = devices // 2
    total = jnp.sum(sum_ref[...], axis=2, keepdims=True)
    total = jnp.sum(total.reshape(pairs, 2, kinds, 1), axis=1)
    g00, g01, g11, h11, step = (total[:, at : at + 1] for at in range(5))
    step = step * (1.0 / (2 * lanes))

    def over_pairs(value):
        return jnp.sum(value, axis=0, keepdims=True)

    gamma = over_pairs(g00)
    alpha = gamma / over_pairs(g01)
    theta = alpha / step
    rest = 1.0 - theta
    gamma_new = over_pairs(rest * rest * g00 + theta * theta * g11)
    turn = rest + gamma_new / gamma
    curvature = over_pairs(
        turn * turn * g01 - 2.0 * theta * turn * g11 / step + theta * theta * h11
    )
    alpha_new = gamma_new / curvature
    own = lax.broadcasted_iota(jnp.int32, theta.shape, 0) == place_ref[3]
    on_z = over_pairs(jnp.where(own, alpha + alpha_new * turn, 0.0))
    on_f = over_pairs(jnp.where(own, alpha_new * theta, 0.0))
    share = z_ref.shape[1]
    out_ref[:, :share, :] = on_z * z_ref[...] + on_f * f_ref[...]
    out_ref[:, share:, :] = on_z * image_ref[...] + on_f * f_image_ref[...]


def finish_kernel(got_ref, right_ref, solution_ref, residual_ref):
    samples = got_ref.shape[0]
    rows = got_ref.shape[1] // 2
    for sample in range(samples):
        solution_ref[sample, 0] = got_ref[sample, :rows, :]
        residual_ref[sample, 0] = right_ref[sample, 0] - got_ref[sample, rows:, :]


def paired_body(
    right_side,
    classes,
    noise_table,
    kernel_first,
    kernel_second,
    basis_first,
    basis_second,
    eigen_first,
    eigen_second,
):
    groups = lax.axis_size("mode")
    samples, planes, rows, width = right_side.shape
    height = groups * rows
    cores = 2
    half = width // cores
    blocks = groups // cores
    unit = cores * samples
    index = lax.axis_index("mode")
    core = index % cores
    sample = (index // cores) % samples
    plane = index // unit
    place = jnp.stack([core, sample, plane, index // cores]).astype(jnp.int32)

    def shape_of(*shape):
        return jax.ShapeDtypeStruct(shape, F32)

    smem = pl.BlockSpec(memory_space=pltpu.SMEM)

    hbm = pl.BlockSpec(memory_space=pltpu.HBM)

    def full(*shape):
        return pl.BlockSpec(
            shape, lambda *at: (0,) * len(shape), pipeline_mode=pl.Buffered(1)
        )

    def whole_out(*shape):
        return pl.BlockSpec(shape, lambda *at: (0,) * len(shape))

    core_swap = [(at, at ^ 1) for at in range(groups)]
    sample_swap = [(at, at ^ cores) for at in range(groups)]

    def in_hbm(value):
        return pltpu.with_memory_space_constraint(value, pltpu.HBM)

    def noise_of(shifts):
        return pl.pallas_call(
            functools.partial(noise_kernel, shifts, unit),
            grid=(1,),
            in_specs=[smem, pl.BlockSpec(memory_space=pltpu.HBM)],
            out_specs=[whole_out(rows, width)] * len(shifts),
            out_shape=[shape_of(rows, width)] * len(shifts),
            scratch_shapes=[
                pltpu.VMEM((len(shifts), rows, width), jnp.int32),
                pltpu.SemaphoreType.DMA((len(shifts),)),
            ],
            compiler_params=params(1, 4),
        )(in_hbm(noise_table), in_hbm(classes))

    def plane_shift(value, by):
        pairs = [(at, (at + by * unit) % groups) for at in range(groups)]
        return lax.ppermute(value, "mode", pairs)

    ahead = planes // 2
    others = [by for by in range(planes) if by != ahead]
    near = [None] * planes
    picked = pl.pallas_call(
        functools.partial(pick_kernel, ahead, unit),
        in_specs=[hbm],
        out_specs=pl.BlockSpec(memory_space=pltpu.VMEM),
        out_shape=jax.ShapeDtypeStruct((rows, width), jnp.int32),
        scratch_shapes=[pltpu.SemaphoreType.DMA],
        compiler_params=pltpu.CompilerParams(vmem_limit_bytes=1024 * 1024),
        name="pick",
    )(in_hbm(classes))
    near[ahead] = plane_shift(picked, ahead)
    rest = noise_of(others)
    for by, value in zip(others, rest):
        near[by] = plane_shift(value, by) if by else value

    outgoing = pl.pallas_call(
        outgoing_kernel,
        grid=(planes,),
        in_specs=[
            pl.BlockSpec((samples, 1, rows, width), lambda p: (0, p, 0, 0)),
            full(width, width),
        ],
        out_specs=pl.BlockSpec((1, samples, cores, rows, half), lambda p: (p, 0, 0, 0, 0)),
        out_shape=shape_of(planes, samples, cores, rows, half),
        compiler_params=params(1, 56),
        name="outgoing",
    )(right_side, basis_second)
    arrived = lax.all_to_all(
        outgoing.reshape(groups, rows, half), "mode", split_axis=0, concat_axis=0, tiled=True
    )

    eigen = eigen_second.reshape(1, -1)
    for reach in (1, cores):
        other = lax.ppermute(eigen, "mode", [(at, at ^ reach) for at in range(groups)])
        low = (index // reach) % 2 == 0
        eigen = jnp.where(
            low,
            jnp.concatenate([eigen, other], axis=1),
            jnp.concatenate([other, eigen], axis=1),
        )
    near, eigen = pl.pallas_call(
        functools.partial(join_kernel, ahead),
        grid=(1,),
        in_specs=[smem, smem, full(*eigen.shape)] + [full(rows, width)] * planes,
        out_specs=[whole_out(planes, rows, width), whole_out(*eigen.shape)],
        out_shape=[shape_of(planes, rows, width), shape_of(*eigen.shape)],
        compiler_params=params(1, 58),
        name="join",
    )(place, noise_table, eigen, *near)
    far = lax.ppermute(near, "mode", sample_swap)
    shifted = [eigen] + [
        lax.ppermute(eigen, "mode", [(at, (at + by * unit) % groups) for at in range(groups)])
        for by in range(1, planes)
    ]
    bf16_square = jax.ShapeDtypeStruct((height, height), BF16)
    bf16_half = jax.ShapeDtypeStruct((height // 2, height), BF16)
    prepare = pl.pallas_call(
        prepare_kernel,
        grid=(1,),
        in_specs=[full(height, height), full(width, width), full(width, width)]
        + [pl.BlockSpec(memory_space=pl.ANY)],
        out_specs=[whole_out(height // 2, height)] * 2 + [whole_out(height, height)] * 2,
        out_shape=[bf16_half] * 2 + [bf16_square] * 2,
        compiler_params=params(1, 24),
        name="prepare",
    )
    upper, lower, high, low = prepare(basis_first, basis_second, kernel_second, eigen)

    def swap(value):
        return lax.ppermute(value, "mode", core_swap)

    def call(kernel, inputs, shapes, scratch_shape, specs=None, more=(), mebibytes=12, matrices=()):
        return pl.pallas_call(
            kernel,
            grid=(1,),
            in_specs=specs or [smem] + [full(*value.shape) for value in inputs[1:]],
            out_specs=[whole_out(*shape) for shape in shapes]
            + [whole_out(*value.shape) for value in matrices],
            out_shape=[shape_of(*shape) for shape in shapes] + list(matrices),
            scratch_shapes=[*([pltpu.VMEM(scratch_shape, F32)] if scratch_shape else []), *more],
            compiler_params=params(1, mebibytes),
        )(*inputs)

    tile = (height, half)
    piece = (blocks, rows, half)
    whole = (blocks, rows, width)
    by_rows = (blocks, cores, rows, half)
    flat = (blocks * rows, width)
    sums_shape = (8, 128)

    (start, weights, column, keep, send, sum_one, lower, *squares) = call(
        first_column_kernel,
        (
            place,
            noise_table,
            *(in_hbm(value) for value in (arrived, lower, basis_first, kernel_first, basis_second)),
            upper,
            eigen_first.reshape(1, -1),
            *shifted,
        ),
        (tile, tile, tile, piece, piece, sums_shape),
        by_rows,
        [smem, smem]
        + [hbm] * 5
        + [full(height // 2, height), full(1, height)]
        + [full(*value.shape) for value in shifted],
        [pltpu.VMEM((groups, rows, half), F32), pltpu.SemaphoreType.DMA((6,))],
        16,
        [bf16_half] + [bf16_square] * 3,
    )
    basis_first, kernel_first, basis_second = squares
    got = swap(send)
    image_keep, image_send, high, low = call(
        first_column_image_kernel,
        (place, column, kernel_first, in_hbm(high), in_hbm(low)),
        (piece, piece),
        by_rows,
        [smem, full(*tile), full(height, height), hbm, hbm],
        [pltpu.SemaphoreType.DMA((2,))],
        matrices=[bf16_square] * 2,
    )
    image_got = swap(image_send)
    inputs = (place, keep, got, basis_second)
    z_field, noise = call(
        first_row_kernel,
        (*inputs, in_hbm(near), in_hbm(far)),
        (whole, (planes, samples, rows, width)),
        flat,
        [smem] + [full(*value.shape) for value in inputs[1:]] + [hbm] * 2,
        [pltpu.SemaphoreType.DMA((2,))],
    )
    image, pair_sum = call(
        first_image_kernel,
        (place, image_keep, image_got, z_field, noise, high, low, sum_one),
        (whole, sums_shape),
        flat,
    )

    (back_send,) = call(
        return_theirs_kernel, (place, image, basis_second, pair_sum), ((flat[0] + 8, half),), None
    )
    (back_keep,) = call(return_mine_kernel, (place, image, basis_second), (piece,), None)
    back_got = swap(back_send)

    column, keep, send, sum_two = call(
        next_column_kernel,
        (
            place,
            back_keep,
            back_got,
            start,
            weights,
            upper,
            lower,
            basis_first,
            pair_sum,
        ),
        (tile, piece, piece, sums_shape),
        by_rows,
    )
    got = swap(send)
    image_keep, image_send = call(
        column_image_kernel, (place, column, kernel_first), (piece, piece), by_rows
    )
    image_got = swap(image_send)
    (f_field,) = call(row_kernel, (place, keep, got, basis_second), (whole,), flat)
    f_image, sums = call(
        last_image_kernel,
        (
            place,
            image_keep,
            image_got,
            f_field,
            noise,
            high,
            low,
            pair_sum,
            sum_two,
        ),
        (whole, (groups, 8, 128)),
        flat,
    )
    sums = lax.all_to_all(sums, "mode", split_axis=0, concat_axis=0, tiled=True)

    few = blocks
    few_spec = pl.BlockSpec((few, rows, width), lambda i: (i, 0, 0))
    answer = pl.pallas_call(
        combine_kernel,
        grid=(1,),
        in_specs=[smem, full(groups, 8, 128)] + [few_spec] * 4,
        out_specs=pl.BlockSpec((few, 2 * rows, width), lambda i: (i, 0, 0)),
        out_shape=shape_of(blocks, 2 * rows, width),
        compiler_params=params(1, 6),
        name="combine",
    )(place, sums, z_field, image, f_field, f_image)
    answer = lax.all_to_all(
        answer,
        "mode",
        split_axis=0,
        concat_axis=0,
        axis_index_groups=[list(range(at, groups, cores)) for at in range(cores)],
        tiled=True,
    )

    block = pl.BlockSpec((samples, 1, rows, width), lambda p: (0, p, 0, 0))
    return tuple(
        pl.pallas_call(
            finish_kernel,
            grid=(planes,),
            in_specs=[
                pl.BlockSpec((samples, 2 * rows, width), lambda p: (p, 0, 0)),
                block,
            ],
            out_specs=[block, block],
            out_shape=[shape_of(*right_side.shape)] * 2,
            compiler_params=params(1, 10),
            name="finish",
        )(answer, right_side)
    )


def body(right_side, classes, *rest):
    groups = lax.axis_size("mode")
    samples, planes, rows, width = right_side.shape
    paired = (
        groups == 2 * samples * planes
        and samples == 2
        and rows % 8 == 0
        and width % 512 == 0
        and planes % 2 == 0
    )
    chosen = paired_body if paired else general_body
    return chosen(right_side, classes, *rest)


def solution(mesh):
    in_specs = (
        P(None, "blocks", "mode", None),
        P("blocks", "mode", None),
        P(),
        P(),
        P(),
        P(),
        P(),
        P(),
        P("mode"),
    )
    out_specs = (P(None, "blocks", "mode", None), P(None, "blocks", "mode", None))
    return jax.shard_map(body, mesh=mesh, in_specs=in_specs, out_specs=out_specs, check_vma=False)
```

```python
import functools

import jax
import jax.numpy as jnp
from jax import lax
from jax.experimental import pallas as pl
from jax.experimental.pallas import tpu as pltpu
from jax.sharding import PartitionSpec as P


NCLASS = 8
ITERS = 2
F32 = jnp.float32
BF16 = jnp.bfloat16


def along_rows(matrix, field):
    return jnp.einsum("jk,sprk->sprj", matrix, field, precision=lax.Precision.HIGHEST)


def rows_to_send(matrix, field, groups):
    result = jnp.einsum("kj,sprk->jspr", matrix, field, precision=lax.Precision.HIGHEST)
    return result.reshape(groups, -1)


def received_to_columns(matrix, received, shape5):
    groups, _, _, _, rows = shape5
    block = received.reshape(shape5)
    reshaped = matrix.reshape(groups, rows, matrix.shape[1])
    return jnp.einsum("mri,mcspr->cspi", reshaped, block, precision=lax.Precision.HIGHEST)


def along_columns(matrix, columns):
    return jnp.einsum("ik,cspk->cspi", matrix, columns, precision=lax.Precision.HIGHEST)


def columns_to_send(matrix, columns, groups, rows):
    reshaped = matrix.reshape(groups, rows, matrix.shape[1])
    result = jnp.einsum("mrk,cspk->mcspr", reshaped, columns, precision=lax.Precision.HIGHEST)
    return result.reshape(groups, -1)


def received_to_rows(matrix, received, shape5):
    groups, cols, _, _, _ = shape5
    block = received.reshape(shape5)
    reshaped = matrix.reshape(matrix.shape[0], groups, cols)
    return jnp.einsum("jmc,mcspr->sprj", reshaped, block, precision=lax.Precision.HIGHEST)


def general_body(
    right_side,
    classes,
    noise_table,
    kernel_first,
    kernel_second,
    basis_first,
    basis_second,
    eigen_first,
    eigen_second,
):
    groups = lax.axis_size("mode")
    samples, planes, rows, _ = right_side.shape
    cols = eigen_second.shape[0]
    shape5 = (groups, cols, samples, planes, rows)
    kern_one = kernel_first.astype(F32)
    kern_two = kernel_second.astype(F32)
    base_one = basis_first.astype(F32)
    base_two = basis_second.astype(F32)
    noise = jnp.zeros(classes.shape, F32)
    for level in range(NCLASS):
        noise = noise + jnp.where(classes == level, noise_table[level], 0.0)
    noise = noise[None]
    mean_noise = jnp.mean(noise_table)
    col_weights = 1.0 / (eigen_second[:, None] * eigen_first[None, :] + mean_noise)
    col_weights = col_weights[:, None, None, :]

    def exchange(outgoing):
        return lax.all_to_all(outgoing, "mode", split_axis=0, concat_axis=0, tiled=True)

    def precond_apply(field):
        incoming = exchange(rows_to_send(base_two, field, groups))
        weighted = received_to_columns(base_one, incoming, shape5) * col_weights
        columns = along_columns(base_one, weighted)
        back = exchange(columns_to_send(base_one, weighted, groups, rows))
        kernel_back = exchange(columns_to_send(kern_one, columns, groups, rows))
        z_field = received_to_rows(base_two, back, shape5)
        image = (
            along_rows(kern_two, received_to_rows(base_two, kernel_back, shape5)) + noise * z_field
        )
        return (z_field, image)

    def inner(left, right):
        return lax.psum(jnp.sum(left * right), "mode")

    solution_field = jnp.zeros_like(right_side)
    residual = right_side
    z_field, image = precond_apply(residual)
    direction, along = (z_field, image)
    gamma = inner(residual, z_field)
    for step in range(ITERS):
        alpha = gamma / inner(direction, along)
        solution_field = solution_field + alpha * direction
        residual = residual - alpha * along
        if step + 1 < ITERS:
            z_field, image = precond_apply(residual)
            gamma_new = inner(residual, z_field)
            ratio = gamma_new / gamma
            direction = z_field + ratio * direction
            along = image + ratio * along
            gamma = gamma_new
    return (solution_field, residual)


def split(value):
    high = value.astype(BF16)
    low = (value - high.astype(F32)).astype(BF16)
    return high, low


def times_right(value, matrix, contract):
    high, low = split(value)
    dims = (((1,), (contract,)), ((), ()))
    both = jnp.concatenate([high, low], axis=0)
    result = lax.dot_general(both, matrix, dims, preferred_element_type=F32)
    return result[: value.shape[0]] + result[value.shape[0] :]


def side_by_side(value):
    return jnp.concatenate(split(value), axis=1)


def times_both(matrix, both):
    width = both.shape[1] // 2
    dims = (((1,), (0,)), ((), ()))
    result = lax.dot_general(matrix, both, dims, preferred_element_type=F32)
    return result[:, :width] + result[:, width:]


def times_left(matrix, value):
    return times_both(matrix, side_by_side(value))


def fold(value):
    total = jnp.sum(value, axis=0, keepdims=True)
    return functools.reduce(
        jnp.add, [total[:, at : at + 128] for at in range(0, total.shape[1], 128)]
    )


def params(dims, mebibytes):
    return pltpu.CompilerParams(
        dimension_semantics=("arbitrary",) * dims, vmem_limit_bytes=mebibytes * 1024 * 1024
    )


def look_up(table_ref, level):
    noise = jnp.full(level.shape, table_ref[0], F32)
    for index in range(1, NCLASS):
        noise = jnp.where(level == index, table_ref[index], noise)
    return noise


def pick_kernel(by, unit, class_hbm, out_ref, done):
    plane = lax.axis_index("mode") // unit
    copy = pltpu.make_async_copy(class_hbm.at[(plane + by) % class_hbm.shape[0]], out_ref, done)
    copy.start()
    copy.wait()


def noise_kernel(shifts, unit, table_ref, class_hbm, *refs):
    out_refs, (class_ref, done) = refs[:-2], refs[-2:]
    planes = class_hbm.shape[0]
    plane = lax.axis_index("mode") // unit
    pairs = [(class_hbm.at[(plane + by) % planes], class_ref.at[at]) for at, by in enumerate(shifts)]
    copies = copy_into(pairs, done)
    for copy in copies:
        copy.start()
    for at, copy in enumerate(copies):
        copy.wait()
        out_refs[at][...] = look_up(table_ref, class_ref[at])


def join_kernel(ahead, place_ref, table_ref, value_ref, *refs):
    parts, (joined_ref, out_ref) = refs[:-2], refs[-2:]
    planes = len(parts)
    for by, part in enumerate(parts):
        noise = look_up(table_ref, part[...]) if by == ahead else part[...]
        joined_ref[(place_ref[2] + planes - by) % planes] = noise
    out_ref[...] = value_ref[...]


def prepare_kernel(
    first_ref,
    second_ref,
    kernel_ref,
    _,
    upper_ref,
    lower_ref,
    high_ref,
    low_ref,
):
    turned = first_ref[...].T
    middle = upper_ref.shape[0]
    upper_ref[...] = turned[:middle]
    lower_ref[...] = turned[middle:]
    dims = (((1,), (0,)), ((), ()))
    product = lax.dot_general(
        kernel_ref[...], second_ref[...], dims, preferred_element_type=F32
    )
    high_ref[...], low_ref[...] = split(product)


def outgoing_kernel(right_ref, basis_ref, out_ref):
    samples, _, rows, width = right_ref.shape
    cores = out_ref.shape[2]
    half = width // cores
    field = right_ref[...].reshape(samples * rows, width)
    mapped = times_right(field, basis_ref[...], 0)
    for sample in range(samples):
        for core in range(cores):
            out_ref[0, sample, core] = mapped[
                sample * rows : (sample + 1) * rows, core * half : (core + 1) * half
            ]


def both_shares(place_ref, share):
    core = place_ref[0]
    mine = pl.ds(pl.multiple_of(core * share, share), share)
    theirs = pl.ds(pl.multiple_of((1 - core) * share, share), share)
    return mine, theirs


def split_rows(place_ref, value, scratch_ref, keep_ref, send_ref):
    core = place_ref[0]
    scratch_ref[...] = value.reshape(scratch_ref.shape)
    keep_ref[...] = scratch_ref[:, core]
    send_ref[...] = scratch_ref[:, 1 - core]


def store_sums(sum_ref, sums):
    rows = sum_ref.shape[0]
    sum_ref[...] = jnp.concatenate(sums + [jnp.zeros((rows - len(sums), 128), F32)], axis=0)


def copy_into(pairs, done):
    return [
        pltpu.make_async_copy(source, target, done.at[at])
        for at, (source, target) in enumerate(pairs)
    ]


def first_column_kernel(
    place_ref,
    table_ref,
    field_hbm,
    lower_hbm,
    basis_hbm,
    kernel_hbm,
    second_hbm,
    upper_ref,
    eigen_ref,
    *refs,
):
    wide_refs, refs, outs = refs[:-13], refs[-7:], refs[-13:-7]
    start_ref, weight_ref, column_ref, keep_ref, send_ref, sum_ref = outs
    lower_ref, basis_ref, kernel_ref, second_ref, scratch_ref, field_ref, done = refs
    groups = field_ref.shape[0]
    first, second = pl.ds(0, groups // 2), pl.ds(groups // 2, groups // 2)
    copies = copy_into(
        (
            (field_hbm.at[first], field_ref.at[first]),
            (field_hbm.at[second], field_ref.at[second]),
            (lower_hbm, lower_ref),
            (basis_hbm, basis_ref),
            (kernel_hbm, kernel_ref),
            (second_hbm, second_ref),
        ),
        done,
    )
    for copy in copies[:3]:
        copy.start()
    mean = functools.reduce(jnp.add, [table_ref[at] for at in range(NCLASS)]) * (1.0 / NCLASS)
    height, width = start_ref.shape
    tall = jnp.broadcast_to(eigen_ref[...], (128, height)).T
    planes = len(wide_refs)
    part = wide_refs[0].shape[1]
    for block in range(width // part):
        wanted = place_ref[0] * (width // part) + block
        wide = jnp.zeros((1, part), F32)
        for by, wide_ref in enumerate(wide_refs):
            here = (place_ref[2] + planes - by) % planes == wanted
            wide = jnp.where(here, wide_ref[...], wide)
        for at in range(0, part, 128):
            lanes = slice(block * part + at, block * part + at + 128)
            weight_ref[:, lanes] = 1.0 / (tall * wide[:, at : at + 128] + mean)
    middle = height // 2
    copies[0].wait()
    start = side_by_side(field_ref[: groups // 2].reshape(middle, width))
    above = times_both(upper_ref[:, :middle], start)
    copies[1].wait()
    for copy in copies[3:]:
        copy.start()
    end = side_by_side(field_ref[groups // 2 :].reshape(middle, width))
    above = above + times_both(upper_ref[:, middle:], end)
    copies[2].wait()
    below = times_both(lower_ref[...], jnp.concatenate([start, end], axis=0))
    spectral = jnp.concatenate([above, below], axis=0)
    weighted = spectral * weight_ref[...]
    start_ref[...] = field_ref[...].reshape(height, width)
    store_sums(sum_ref, [fold(spectral * weighted)])
    copies[3].wait()
    column = times_left(basis_ref[...], weighted)
    column_ref[...] = column
    split_rows(place_ref, column, scratch_ref, keep_ref, send_ref)
    copies[4].wait()
    copies[5].wait()


def next_column_kernel(
    place_ref,
    held_ref,
    got_ref,
    start_ref,
    weight_ref,
    upper_ref,
    lower_ref,
    basis_ref,
    own_ref,
    column_ref,
    keep_ref,
    send_ref,
    sum_ref,
    scratch_ref,
):
    core = place_ref[0]
    tall = got_ref.shape[0] - own_ref.shape[0]
    scratch_ref[:, core] = held_ref[...]
    scratch_ref[:, 1 - core] = got_ref[:tall, :].reshape(held_ref.shape)
    total = jnp.sum(own_ref[...] + got_ref[tall:, :128], axis=1, keepdims=True)
    gamma, curvature = total[0:1], total[1:2]
    proper = (gamma > 0) & (curvature > 0)
    step = jnp.where(proper, gamma / jnp.where(proper, curvature, 1.0), 1.0)
    field = start_ref[...] - step * scratch_ref[...].reshape(start_ref.shape)
    both = side_by_side(field)
    halves = [times_both(half_ref[...], both) for half_ref in (upper_ref, lower_ref)]
    spectral = jnp.concatenate(halves, axis=0)
    weighted = spectral * weight_ref[...]
    store_sums(sum_ref, [fold(spectral * weighted), jnp.broadcast_to(step, (1, 128))])
    column = times_left(basis_ref[...], weighted)
    column_ref[...] = column
    split_rows(place_ref, column, scratch_ref, keep_ref, send_ref)


def column_image_kernel(place_ref, column_ref, kernel_ref, keep_ref, send_ref, scratch_ref):
    image = times_left(kernel_ref[...], column_ref[...])
    split_rows(place_ref, image, scratch_ref, keep_ref, send_ref)


def first_column_image_kernel(place_ref, column_ref, kernel_ref, high_hbm, low_hbm, *refs):
    keep_ref, send_ref, high_ref, low_ref, scratch_ref, done = refs
    copies = copy_into(((high_hbm, high_ref), (low_hbm, low_ref)), done)
    for copy in copies:
        copy.start()
    column_image_kernel(place_ref, column_ref, kernel_ref, keep_ref, send_ref, scratch_ref)
    for copy in copies:
        copy.wait()


def join_columns(place_ref, scratch_ref, keep_ref, got_ref):
    height, width = scratch_ref.shape
    mine, theirs = both_shares(place_ref, width // 2)
    scratch_ref[:, mine] = keep_ref[...].reshape(height, width // 2)
    scratch_ref[:, theirs] = got_ref[...].reshape(height, width // 2)
    return scratch_ref[...]


def row_kernel(place_ref, keep_ref, got_ref, basis_ref, z_ref, scratch_ref):
    field = join_columns(place_ref, scratch_ref, keep_ref, got_ref)
    z_ref[...] = times_right(field, basis_ref[...], 1).reshape(z_ref.shape)


def row_image(place_ref, keep_ref, got_ref, high_ref, low_ref, scratch_ref):
    field = join_columns(place_ref, scratch_ref, keep_ref, got_ref)
    high, low = split(field)
    dims = (((1,), (1,)), ((), ()))
    both = jnp.concatenate([high, low], axis=0)
    result = lax.dot_general(both, high_ref[...], dims, preferred_element_type=F32)
    small = lax.dot_general(high, low_ref[...], dims, preferred_element_type=F32)
    return result[: field.shape[0]] + (result[field.shape[0] :] + small)


def first_row_kernel(place_ref, keep_ref, got_ref, basis_ref, near_hbm, far_hbm, *refs):
    z_ref, noise_ref, scratch_ref, done = refs
    sample = place_ref[1]
    copies = copy_into(
        ((near_hbm, noise_ref.at[:, sample]), (far_hbm, noise_ref.at[:, 1 - sample])), done
    )
    for copy in copies:
        copy.start()
    row_kernel(place_ref, keep_ref, got_ref, basis_ref, z_ref, scratch_ref)
    for copy in copies:
        copy.wait()


def full_image(place_ref, keep_ref, got_ref, z_ref, noise_ref, high_ref, low_ref, image_ref, scratch_ref):
    image = row_image(place_ref, keep_ref, got_ref, high_ref, low_ref, scratch_ref)
    field = z_ref[...].reshape(image.shape)
    image = image + noise_ref[...].reshape(image.shape) * field
    image_ref[...] = image.reshape(image_ref.shape)
    return fold(field * image)


def first_image_kernel(
    place_ref,
    keep_ref,
    got_ref,
    z_ref,
    noise_ref,
    high_ref,
    low_ref,
    one_ref,
    image_ref,
    sum_ref,
    scratch_ref,
):
    refs = (place_ref, keep_ref, got_ref, z_ref, noise_ref, high_ref, low_ref)
    store_sums(sum_ref, [one_ref[0:1], full_image(*refs, image_ref, scratch_ref)])


def returned(place_ref, image_ref, basis_ref, whose, half):
    lanes = both_shares(place_ref, half)[whose]
    image = image_ref[...].reshape(-1, basis_ref.shape[0])
    return times_right(image, basis_ref[:, lanes], 0)


def return_theirs_kernel(place_ref, image_ref, basis_ref, sum_ref, out_ref):
    part = returned(place_ref, image_ref, basis_ref, 1, out_ref.shape[1])
    out_ref[: part.shape[0], :] = part
    out_ref[part.shape[0] :, :] = jnp.concatenate(
        [sum_ref[...]] * (out_ref.shape[1] // 128), axis=1
    )


def return_mine_kernel(place_ref, image_ref, basis_ref, out_ref):
    part = returned(place_ref, image_ref, basis_ref, 0, out_ref.shape[2])
    out_ref[...] = part.reshape(out_ref.shape)


def last_image_kernel(
    place_ref,
    keep_ref,
    got_ref,
    z_ref,
    noise_ref,
    high_ref,
    low_ref,
    one_ref,
    two_ref,
    image_ref,
    sum_ref,
    scratch_ref,
):
    refs = (place_ref, keep_ref, got_ref, z_ref, noise_ref, high_ref, low_ref)
    last = full_image(*refs, image_ref, scratch_ref)
    rows = [one_ref[0:2], two_ref[0:1], last, two_ref[1:2], jnp.zeros((3, 128), F32)]
    sum_ref[...] = jnp.broadcast_to(jnp.concatenate(rows, axis=0)[None], sum_ref.shape)


def combine_kernel(place_ref, sum_ref, z_ref, image_ref, f_ref, f_image_ref, out_ref):
    devices, kinds, lanes = sum_ref.shape
    pairs = devices // 2
    total = jnp.sum(sum_ref[...], axis=2, keepdims=True)
    total = jnp.sum(total.reshape(pairs, 2, kinds, 1), axis=1)
    g00, g01, g11, h11, step = (total[:, at : at + 1] for at in range(5))
    step = step * (1.0 / (2 * lanes))

    def over_pairs(value):
        return jnp.sum(value, axis=0, keepdims=True)

    gamma = over_pairs(g00)
    alpha = gamma / over_pairs(g01)
    theta = alpha / step
    rest = 1.0 - theta
    gamma_new = over_pairs(rest * rest * g00 + theta * theta * g11)
    turn = rest + gamma_new / gamma
    curvature = over_pairs(
        turn * turn * g01 - 2.0 * theta * turn * g11 / step + theta * theta * h11
    )
    alpha_new = gamma_new / curvature
    own = lax.broadcasted_iota(jnp.int32, theta.shape, 0) == place_ref[3]
    on_z = over_pairs(jnp.where(own, alpha + alpha_new * turn, 0.0))
    on_f = over_pairs(jnp.where(own, alpha_new * theta, 0.0))
    share = z_ref.shape[1]
    out_ref[:, :share, :] = on_z * z_ref[...] + on_f * f_ref[...]
    out_ref[:, share:, :] = on_z * image_ref[...] + on_f * f_image_ref[...]


def finish_kernel(got_ref, right_ref, solution_hbm, residual_hbm, residual_ref, done):
    samples, _, rows, _ = right_ref.shape
    kept = [(got_ref.at[:, at, :rows], solution_hbm.at[at]) for at in range(samples)]
    made = [(residual_ref.at[at], residual_hbm.at[at]) for at in range(samples)]
    copies = copy_into(kept + made, done)
    for copy in copies[:samples]:
        copy.start()
    for at in range(samples):
        residual_ref[at] = right_ref[at] - got_ref[:, at, rows:]
        copies[samples + at].start()
    for copy in copies:
        copy.wait()


def paired_body(
    right_side,
    classes,
    noise_table,
    kernel_first,
    kernel_second,
    basis_first,
    basis_second,
    eigen_first,
    eigen_second,
):
    groups = lax.axis_size("mode")
    samples, planes, rows, width = right_side.shape
    height = groups * rows
    cores = 2
    half = width // cores
    blocks = groups // cores
    unit = cores * samples
    index = lax.axis_index("mode")
    core = index % cores
    sample = (index // cores) % samples
    plane = index // unit
    place = jnp.stack([core, sample, plane, index // cores]).astype(jnp.int32)

    def shape_of(*shape):
        return jax.ShapeDtypeStruct(shape, F32)

    smem = pl.BlockSpec(memory_space=pltpu.SMEM)

    hbm = pl.BlockSpec(memory_space=pltpu.HBM)

    def full(*shape):
        return pl.BlockSpec(
            shape, lambda *at: (0,) * len(shape), pipeline_mode=pl.Buffered(1)
        )

    def whole_out(*shape):
        return pl.BlockSpec(shape, lambda *at: (0,) * len(shape))

    core_swap = [(at, at ^ 1) for at in range(groups)]
    sample_swap = [(at, at ^ cores) for at in range(groups)]

    def in_hbm(value):
        return pltpu.with_memory_space_constraint(value, pltpu.HBM)

    def noise_of(shifts):
        return pl.pallas_call(
            functools.partial(noise_kernel, shifts, unit),
            grid=(1,),
            in_specs=[smem, pl.BlockSpec(memory_space=pltpu.HBM)],
            out_specs=[whole_out(rows, width)] * len(shifts),
            out_shape=[shape_of(rows, width)] * len(shifts),
            scratch_shapes=[
                pltpu.VMEM((len(shifts), rows, width), jnp.int32),
                pltpu.SemaphoreType.DMA((len(shifts),)),
            ],
            compiler_params=params(1, 4),
        )(in_hbm(noise_table), in_hbm(classes))

    def plane_shift(value, by):
        pairs = [(at, (at + by * unit) % groups) for at in range(groups)]
        return lax.ppermute(value, "mode", pairs)

    ahead = 1
    others = [by for by in range(planes) if by != ahead]
    near = [None] * planes
    picked = pl.pallas_call(
        functools.partial(pick_kernel, ahead, unit),
        in_specs=[hbm],
        out_specs=pl.BlockSpec(memory_space=pltpu.VMEM),
        out_shape=jax.ShapeDtypeStruct((rows, width), jnp.int32),
        scratch_shapes=[pltpu.SemaphoreType.DMA],
        compiler_params=pltpu.CompilerParams(vmem_limit_bytes=1024 * 1024),
        name="pick",
    )(in_hbm(classes))
    near[ahead] = plane_shift(picked, ahead)
    rest = noise_of(others)
    for by, value in zip(others, rest):
        near[by] = plane_shift(value, by) if by else value

    outgoing = pl.pallas_call(
        outgoing_kernel,
        grid=(planes,),
        in_specs=[
            pl.BlockSpec((samples, 1, rows, width), lambda p: (0, p, 0, 0)),
            full(width, width),
        ],
        out_specs=pl.BlockSpec((1, samples, cores, rows, half), lambda p: (p, 0, 0, 0, 0)),
        out_shape=shape_of(planes, samples, cores, rows, half),
        compiler_params=params(1, 56),
        name="outgoing",
    )(right_side, basis_second)
    arrived = lax.all_to_all(
        outgoing.reshape(groups, rows, half), "mode", split_axis=0, concat_axis=0, tiled=True
    )

    eigen = eigen_second.reshape(1, -1)
    for reach in (1, cores):
        other = lax.ppermute(eigen, "mode", [(at, at ^ reach) for at in range(groups)])
        low = (index // reach) % 2 == 0
        eigen = jnp.where(
            low,
            jnp.concatenate([eigen, other], axis=1),
            jnp.concatenate([other, eigen], axis=1),
        )
    near, eigen = pl.pallas_call(
        functools.partial(join_kernel, ahead),
        grid=(1,),
        in_specs=[smem, smem, full(*eigen.shape)] + [full(rows, width)] * planes,
        out_specs=[whole_out(planes, rows, width), whole_out(*eigen.shape)],
        out_shape=[shape_of(planes, rows, width), shape_of(*eigen.shape)],
        compiler_params=params(1, 58),
        name="join",
    )(place, noise_table, eigen, *near)
    far = lax.ppermute(near, "mode", sample_swap)
    shifted = [eigen] + [
        lax.ppermute(eigen, "mode", [(at, (at + by * unit) % groups) for at in range(groups)])
        for by in range(1, planes)
    ]
    bf16_square = jax.ShapeDtypeStruct((height, height), BF16)
    bf16_half = jax.ShapeDtypeStruct((height // 2, height), BF16)
    prepare = pl.pallas_call(
        prepare_kernel,
        grid=(1,),
        in_specs=[full(height, height), full(width, width), full(width, width)]
        + [pl.BlockSpec(memory_space=pl.ANY)],
        out_specs=[whole_out(height // 2, height)] * 2 + [whole_out(height, height)] * 2,
        out_shape=[bf16_half] * 2 + [bf16_square] * 2,
        compiler_params=params(1, 24),
        name="prepare",
    )
    upper, lower, high, low = prepare(basis_first, basis_second, kernel_second, eigen)

    def swap(value):
        return lax.ppermute(value, "mode", core_swap)

    def call(kernel, inputs, shapes, scratch_shape, specs=None, more=(), mebibytes=12, matrices=()):
        return pl.pallas_call(
            kernel,
            grid=(1,),
            in_specs=specs or [smem] + [full(*value.shape) for value in inputs[1:]],
            out_specs=[whole_out(*shape) for shape in shapes]
            + [whole_out(*value.shape) for value in matrices],
            out_shape=[shape_of(*shape) for shape in shapes] + list(matrices),
            scratch_shapes=[*([pltpu.VMEM(scratch_shape, F32)] if scratch_shape else []), *more],
            compiler_params=params(1, mebibytes),
        )(*inputs)

    tile = (height, half)
    piece = (blocks, rows, half)
    whole = (blocks, rows, width)
    by_rows = (blocks, cores, rows, half)
    flat = (blocks * rows, width)
    sums_shape = (8, 128)

    (start, weights, column, keep, send, sum_one, lower, *squares) = call(
        first_column_kernel,
        (
            place,
            noise_table,
            *(in_hbm(value) for value in (arrived, lower, basis_first, kernel_first, basis_second)),
            upper,
            eigen_first.reshape(1, -1),
            *shifted,
        ),
        (tile, tile, tile, piece, piece, sums_shape),
        by_rows,
        [smem, smem]
        + [hbm] * 5
        + [full(height // 2, height), full(1, height)]
        + [full(*value.shape) for value in shifted],
        [pltpu.VMEM((groups, rows, half), F32), pltpu.SemaphoreType.DMA((6,))],
        16,
        [bf16_half] + [bf16_square] * 3,
    )
    basis_first, kernel_first, basis_second = squares
    got = swap(send)
    image_keep, image_send, high, low = call(
        first_column_image_kernel,
        (place, column, kernel_first, in_hbm(high), in_hbm(low)),
        (piece, piece),
        by_rows,
        [smem, full(*tile), full(height, height), hbm, hbm],
        [pltpu.SemaphoreType.DMA((2,))],
        matrices=[bf16_square] * 2,
    )
    image_got = swap(image_send)
    inputs = (place, keep, got, basis_second)
    z_field, noise = call(
        first_row_kernel,
        (*inputs, in_hbm(near), in_hbm(far)),
        (whole, (planes, samples, rows, width)),
        flat,
        [smem] + [full(*value.shape) for value in inputs[1:]] + [hbm] * 2,
        [pltpu.SemaphoreType.DMA((2,))],
    )
    image, pair_sum = call(
        first_image_kernel,
        (place, image_keep, image_got, z_field, noise, high, low, sum_one),
        (whole, sums_shape),
        flat,
    )

    (back_send,) = call(
        return_theirs_kernel, (place, image, basis_second, pair_sum), ((flat[0] + 8, half),), None
    )
    (back_keep,) = call(return_mine_kernel, (place, image, basis_second), (piece,), None)
    back_got = swap(back_send)

    column, keep, send, sum_two = call(
        next_column_kernel,
        (
            place,
            back_keep,
            back_got,
            start,
            weights,
            upper,
            lower,
            basis_first,
            pair_sum,
        ),
        (tile, piece, piece, sums_shape),
        by_rows,
    )
    got = swap(send)
    image_keep, image_send = call(
        column_image_kernel, (place, column, kernel_first), (piece, piece), by_rows
    )
    image_got = swap(image_send)
    (f_field,) = call(row_kernel, (place, keep, got, basis_second), (whole,), flat)
    f_image, sums = call(
        last_image_kernel,
        (
            place,
            image_keep,
            image_got,
            f_field,
            noise,
            high,
            low,
            pair_sum,
            sum_two,
        ),
        (whole, (groups, 8, 128)),
        flat,
    )
    sums = lax.all_to_all(sums, "mode", split_axis=0, concat_axis=0, tiled=True)

    few = blocks
    few_spec = pl.BlockSpec((few, rows, width), lambda i: (i, 0, 0))
    answer = pl.pallas_call(
        combine_kernel,
        grid=(1,),
        in_specs=[smem, full(groups, 8, 128)] + [few_spec] * 4,
        out_specs=pl.BlockSpec((few, 2 * rows, width), lambda i: (i, 0, 0)),
        out_shape=shape_of(blocks, 2 * rows, width),
        compiler_params=params(1, 6),
        name="combine",
    )(place, sums, z_field, image, f_field, f_image)
    answer = lax.all_to_all(
        answer,
        "mode",
        split_axis=0,
        concat_axis=0,
        axis_index_groups=[list(range(at, groups, cores)) for at in range(cores)],
        tiled=True,
    )

    answer = answer.reshape(planes, samples, 2 * rows, width)
    return tuple(
        pl.pallas_call(
            finish_kernel,
            grid=(1,),
            in_specs=[full(*answer.shape), full(*right_side.shape)],
            out_specs=[hbm, hbm],
            out_shape=[shape_of(*right_side.shape)] * 2,
            scratch_shapes=[
                pltpu.VMEM(right_side.shape, F32),
                pltpu.SemaphoreType.DMA((2 * samples,)),
            ],
            compiler_params=params(1, 10),
            name="finish",
        )(answer, right_side)
    )


def body(right_side, classes, *rest):
    groups = lax.axis_size("mode")
    samples, planes, rows, width = right_side.shape
    paired = (
        groups == 2 * samples * planes
        and samples == 2
        and rows % 8 == 0
        and width % 512 == 0
        and planes % 2 == 0
    )
    chosen = paired_body if paired else general_body
    return chosen(right_side, classes, *rest)


def solution(mesh):
    in_specs = (
        P(None, "blocks", "mode", None),
        P("blocks", "mode", None),
        P(),
        P(),
        P(),
        P(),
        P(),
        P(),
        P("mode"),
    )
    out_specs = (P(None, "blocks", "mode", None), P(None, "blocks", "mode", None))
    return jax.shard_map(body, mesh=mesh, in_specs=in_specs, out_specs=out_specs, check_vma=False)
```
